32 devices in a mesh: shadow: 2 (over y), seq: 4 (over x, core), head: 4 (over z).
Axes of the slice: x: 2, y: 2, z: 4, core: 2. Of those that a mesh axis runs over, the one named last changes fastest.
Arguments:
- token_ids: int32 [4096], P(('shadow', 'seq')), parts along dimension 0, may hold values from 0 to 25599
- target_ids: int32 [4096], P(('shadow', 'seq')), parts along dimension 0, may hold values from 0 to 25599
- doc_start: int32 [8], P(('shadow', 'seq')), parts along dimension 0, may hold values from 0 to 512, as said below
- vocab_table: bfloat16 [51200, 2048], P(('shadow', 'head'), 'seq'), parts along dimension 0, may hold values from -2.25 to 2.25
- norm_gain_one: bfloat16 [4096], P('shadow'), parts along dimension 0, may hold values from 0.25 to 1.75
- lin_qkv: bfloat16 [4096, 2560], P('shadow', 'head'), parts along dimension 0, may hold values from -0.125 to 0.125
- lin_head_gain: bfloat16 [4096], P(('shadow', 'head')), parts along dimension 0, may hold values from 0.25 to 1.75
- lin_out: bfloat16 [4096, 2048], P(('shadow', 'head')), parts along dimension 0, may hold values from -0.125 to 0.125
- norm_gain_two: bfloat16 [4096], P('shadow'), parts along dimension 0, may hold values from 0.25 to 1.75
- win_qkv: bfloat16 [4096, 6144], P('shadow', 'head'), parts along dimension 0, may hold values from -4 to 4
- win_out: bfloat16 [4096, 2048], P(('shadow', 'head')), parts along dimension 0, may hold values from -0.125 to 0.125
- final_gain: bfloat16 [4096], P('shadow'), parts along dimension 0, may hold values from 0.25 to 1.75
Outputs:
- loglik: float32 [4096], P(('shadow', 'seq', 'head')), parts along dimension 0
The draws below stay inside these ranges and needn't reach their ends.
There are 2 independent parts, one for each index of `shadow`. The reference program is written for one: setup_inputs(seed, part) draws one part's arguments, and reference() takes and returns one part's arrays. A program takes and returns all parts, laid end to end along the dimension named above; each array names one. Nothing has to cross between parts.
Inputs may be any that keep to these rules, and one draw needn't show every extreme that they name: `doc_start`: in exactly max(1, B // 4) of the B = 4 blocks a document begins, at this offset within the block; every other entry equals 512, and no document begins in that block.
All inputs are finite; a program needn't handle non-finite values.
Results may differ from the reference program's by a relative error of at most 0.005.
Values may be sent and summed in bfloat16 or wider, within the bound.
No kernel may reach another device: no remote copies, remote signals or barrier semaphores. Data moves between devices by JAX's collectives and lax.ppermute only.
A program may use at most 192 MiB of HBM per device.

```python
import math
import jax
import jax.numpy as jnp
import numpy as np
from jax import lax

D = 2048
HEADS = 16
FEAT = 16
WINDOW = 64
VOCAB = 25600
TOK_DEV = 512
HEAD_DIM = 128
TAYLOR = 273
TOKENS = 2048
N_HEAD = 4


def draw_doc_start(key, part):
    block_count = TOKENS // TOK_DEV
    order = jax.random.permutation(jax.random.fold_in(key, 11), block_count)
    chosen = order < max(1, block_count // 4)
    offsets = jax.random.randint(jax.random.fold_in(key, 12), (block_count,), 0, TOK_DEV, dtype=jnp.int32)
    return jnp.where(chosen, offsets, TOK_DEV).astype(jnp.int32)


def draw_vocab_table(key, part):
    base_key = jax.random.fold_in(key, 21)
    entries = jax.random.truncated_normal(base_key, -6.0, 6.0, (VOCAB, D), jnp.float32)
    return (0.08 * entries).astype(jnp.bfloat16)


def draw_win_qkv(key, part):
    base = jax.random.truncated_normal(jax.random.fold_in(key, 31), -6.0, 6.0, (D, HEADS, 3, HEAD_DIM), jnp.float32) * D ** (-0.5)
    return jnp.clip(base, -4.0, 4.0).reshape(D, HEADS * 3 * HEAD_DIM).astype(jnp.bfloat16)


def with_ends(values, own_key, smallest, largest):
    shape = values.shape
    index_at = [jax.random.randint(jax.random.fold_in(own_key, axis), (), 0, shape[axis]) for axis in range(len(shape))]
    values = values.at[tuple(index_at)].set(smallest)
    longest = shape.index(max(shape))
    index_at[longest] = (index_at[longest] + 1) % shape[longest]
    return values.at[tuple(index_at)].set(largest)


def block_scale(stream_key, dims, pieces, smallest, high):
    def one(dim, shards_of):
        steps = jax.random.uniform(jax.random.fold_in(jax.random.fold_in(stream_key, 6), dim), (shards_of,), jnp.float32, smallest / len(pieces), high / len(pieces))
        return jnp.repeat(jnp.exp(steps), dims[dim] // shards_of).reshape((-1,) + (1,) * (len(dims) - dim - 1))

    level = one(*pieces[0])
    for cut in pieces[1:]:
        level = level * one(*cut)
    return level


def cumulative_ranks(number_of, slope):
    portions = [(1 << 20) // math.isqrt(rank ** slope) + 1 for rank in range(1, number_of + 1)]
    width = 1 + sum(portions) // (1 << 30)
    return np.cumsum(np.array([max(1, weight // width) for weight in portions]))


def skewed_ids(rng, shape, amount, skew):
    grid = cumulative_ranks(amount, skew)
    ticket = jax.random.randint(jax.random.fold_in(rng, 1), shape, 0, int(grid[amount - 1]))
    rank = jnp.searchsorted(jnp.asarray(grid, jnp.int32), ticket, side="right")
    return jax.random.permutation(jax.random.fold_in(rng, 2), amount)[rank].astype(jnp.int32)


def gaussian(stream_key, shape, deviation, reach, shards=(), kind=jnp.bfloat16):
    drawn = deviation * jax.random.normal(stream_key, shape, jnp.float32)
    if shards:
        drawn = drawn * block_scale(stream_key, shape, shards, -0.22, 0.18)
    return jnp.clip(drawn, -reach, reach).astype(kind)


def setup_inputs(seed: int = 0, part: int = 0) -> dict:
    key_of = jax.random.split(jax.random.key(seed), 13)
    part_splits = jax.random.split(jax.random.fold_in(key_of[12], part), 13)
    return {
        "token_ids": with_ends(skewed_ids(part_splits[0], (TOKENS,), VOCAB, 2), jax.random.fold_in(part_splits[0], 3), 0, VOCAB - 1).astype(jnp.int32),
        "target_ids": with_ends(skewed_ids(part_splits[1], (TOKENS,), VOCAB, 2), jax.random.fold_in(part_splits[1], 3), 0, VOCAB - 1).astype(jnp.int32),
        "doc_start": draw_doc_start(jax.random.fold_in(jax.random.fold_in(key_of[12], part), 71), part),
        "vocab_table": draw_vocab_table(jax.random.fold_in(jax.random.fold_in(key_of[12], part), 71), part),
        "norm_gain_one": jnp.clip(1.0 + 0.15 * jax.random.normal(part_splits[4], (D,), jnp.float32), 0.25, 1.75).astype(jnp.bfloat16),
        "lin_qkv": gaussian(part_splits[5], (D, HEADS * (2 * FEAT + HEAD_DIM)), D ** -0.5, 0.125, ((1, 4),)),
        "lin_head_gain": jnp.clip(1.0 + 0.15 * jax.random.normal(part_splits[6], (D,), jnp.float32), 0.25, 1.75).astype(jnp.bfloat16),
        "lin_out": gaussian(part_splits[7], (D, D), D ** -0.5, 0.125, ((0, 4),)),
        "norm_gain_two": jnp.clip(1.0 + 0.15 * jax.random.normal(part_splits[8], (D,), jnp.float32), 0.25, 1.75).astype(jnp.bfloat16),
        "win_qkv": draw_win_qkv(jax.random.fold_in(jax.random.fold_in(key_of[12], part), 71), part),
        "win_out": gaussian(part_splits[10], (D, D), D ** -0.5, 0.125, ((0, 4),)),
        "final_gain": jnp.clip(1.0 + 0.15 * jax.random.normal(part_splits[11], (D,), jnp.float32), 0.25, 1.75).astype(jnp.bfloat16),
    }


EPSILON = 1e-05
NEGATIVE = -1e+30
HIGHEST = lax.Precision.HIGHEST

def normed(values, weight_gain):
    widened = values.astype(jnp.float32)
    factor = lax.rsqrt(lax.optimization_barrier(jnp.mean(widened * widened, axis=-1, keepdims=True)) + EPSILON)
    return (widened * factor * weight_gain.astype(jnp.float32)).astype(jnp.bfloat16)

def taylor(projected):
    scaled = projected * FEAT ** (-0.25)
    squares = (scaled[..., :, None] * scaled[..., None, :]).reshape(scaled.shape[:-1] + (FEAT * FEAT,)) * 0.5 ** 0.5
    leading = jnp.ones(scaled.shape[:-1] + (1,), jnp.float32)
    return jnp.concatenate([leading, scaled, squares], axis=-1).astype(jnp.bfloat16)

def group_sum(inputs, weight):
    group_width = inputs.shape[1] // N_HEAD
    summed = jnp.zeros((inputs.shape[0], weight.shape[1]), jnp.float32)
    for member in range(N_HEAD):
        section = jnp.dot(inputs[:, member * group_width:(member + 1) * group_width], weight[member * group_width:(member + 1) * group_width], preferred_element_type=jnp.float32).astype(jnp.bfloat16)
        summed = summed + lax.optimization_barrier(section).astype(jnp.float32)
    return summed

def reference(token_ids, target_ids, doc_start, vocab_table, norm_gain_one, lin_qkv, lin_head_gain, lin_out, norm_gain_two, win_qkv, win_out, final_gain):
    blocks = TOKENS // TOK_DEV
    places = jnp.arange(TOK_DEV, dtype=jnp.int32)
    every_place = jnp.arange(TOKENS, dtype=jnp.int32)
    block_of = every_place // TOK_DEV
    starts = every_place % TOK_DEV == doc_start[block_of]
    doc_id = jnp.cumsum(starts.astype(jnp.int32), dtype=jnp.int32)
    embedded = jnp.take(vocab_table, token_ids, axis=0)
    units_one = normed(embedded, norm_gain_one)
    projected = jnp.dot(units_one, lin_qkv, preferred_element_type=jnp.float32).reshape(TOKENS, HEADS, 2 * FEAT + HEAD_DIM)
    feat_query = taylor(projected[..., :FEAT])
    feat_key = taylor(projected[..., FEAT:2 * FEAT])
    lin_values = projected[..., 2 * FEAT:].astype(jnp.bfloat16)
    causal = places[:, None] >= places[None, :]

    def lin_step(carried, inputs):
        state_sum, key_sum = carried
        feat_q, feat_k, value_block, boundary = inputs
        query_wide = feat_q.astype(jnp.float32)
        key_wide = feat_k.astype(jnp.float32)
        value_wide = value_block.astype(jnp.float32)
        after_start = places >= boundary
        allowed = causal & (after_start[:, None] == after_start[None, :])
        weights = jnp.einsum('ihf,jhf->hij', query_wide, key_wide, precision=HIGHEST) * allowed[None].astype(jnp.float32)
        numerator = jnp.einsum('hij,jhe->ihe', weights, value_wide, precision=HIGHEST)
        denominator = lax.optimization_barrier(jnp.sum(weights, axis=-1)).T
        before = (places < boundary).astype(jnp.float32)
        numerator = numerator + before[:, None, None] * jnp.einsum('ihf,hfe->ihe', query_wide, state_sum, precision=HIGHEST)
        denominator = denominator + before[:, None] * jnp.einsum('ihf,hf->ih', query_wide, key_sum, precision=HIGHEST)
        mixture = numerator / denominator[..., None]
        no_start = boundary == TOK_DEV
        kept_keys = key_wide * (after_start | no_start).astype(jnp.float32)[:, None, None]
        keep_old = no_start.astype(jnp.float32)
        state_sum = keep_old * state_sum + jnp.einsum('jhf,jhe->hfe', kept_keys, value_wide, precision=HIGHEST)
        key_sum = keep_old * key_sum + lax.optimization_barrier(jnp.sum(kept_keys, axis=0))
        return ((state_sum, key_sum), mixture)
    initial = (jnp.zeros((HEADS, TAYLOR, HEAD_DIM), jnp.float32), jnp.zeros((HEADS, TAYLOR), jnp.float32))
    scanned = (feat_query.reshape(blocks, TOK_DEV, HEADS, TAYLOR), feat_key.reshape(blocks, TOK_DEV, HEADS, TAYLOR), lin_values.reshape(blocks, TOK_DEV, HEADS, HEAD_DIM), doc_start)
    _, mixture = lax.scan(lin_step, initial, scanned)
    mixture = mixture.reshape(TOKENS, HEADS, HEAD_DIM)
    lin_heads = (mixture * lin_head_gain.astype(jnp.float32).reshape(HEADS, HEAD_DIM)).astype(jnp.bfloat16).reshape(TOKENS, D)
    residual_one = (embedded.astype(jnp.float32) + group_sum(lin_heads, lin_out)).astype(jnp.bfloat16)
    units_two = normed(residual_one, norm_gain_two)
    attend_in = jnp.dot(units_two, win_qkv, preferred_element_type=jnp.float32).astype(jnp.bfloat16).reshape(TOKENS, HEADS, 3 * HEAD_DIM)
    reach_back = WINDOW - 1
    padded = jnp.concatenate([jnp.zeros((reach_back, HEADS, 3 * HEAD_DIM), jnp.bfloat16), attend_in], axis=0)
    padded_doc = jnp.concatenate([jnp.full((reach_back,), -1, jnp.int32), doc_id], axis=0)
    key_places = jnp.arange(TOK_DEV + reach_back, dtype=jnp.int32)
    distance = places[:, None] + reach_back - key_places[None, :]
    in_band = (distance >= 0) & (distance < WINDOW)

    def win_block(position):
        first_row = position * TOK_DEV
        key_block = lax.dynamic_slice_in_dim(padded, first_row, TOK_DEV + reach_back, 0)
        key_doc = lax.dynamic_slice_in_dim(padded_doc, first_row, TOK_DEV + reach_back, 0)
        query_doc = lax.dynamic_slice_in_dim(doc_id, first_row, TOK_DEV, 0)
        queries = lax.dynamic_slice_in_dim(attend_in, first_row, TOK_DEV, 0)[..., :HEAD_DIM].astype(jnp.float32)
        key_wide = key_block[..., HEAD_DIM:2 * HEAD_DIM].astype(jnp.float32)
        value_wide = key_block[..., 2 * HEAD_DIM:].astype(jnp.float32)
        scores = jnp.einsum('ihd,jhd->hij', queries, key_wide, precision=HIGHEST) * HEAD_DIM ** (-0.5)
        allowed = in_band & (query_doc[:, None] == key_doc[None, :])
        scores = jnp.where(allowed[None], scores, NEGATIVE)
        highest_score = lax.optimization_barrier(jnp.max(scores, axis=-1, keepdims=True))
        weights = jnp.where(allowed[None], jnp.exp(scores - highest_score), 0.0)
        probabilities = (weights / lax.optimization_barrier(jnp.sum(weights, axis=-1, keepdims=True))).astype(jnp.bfloat16)
        probabilities = lax.optimization_barrier(probabilities).astype(jnp.float32)
        return jnp.einsum('hij,jhe->ihe', probabilities, value_wide, precision=HIGHEST).astype(jnp.bfloat16)
    attended = lax.map(win_block, jnp.arange(blocks, dtype=jnp.int32)).reshape(TOKENS, D)
    residual_two = residual_one.astype(jnp.float32) + group_sum(attended, win_out)
    final_units = normed(residual_two, final_gain)

    def score_block(position):
        row_block = lax.dynamic_slice_in_dim(final_units, position * TOK_DEV, TOK_DEV, 0)
        goal_ids = lax.dynamic_slice_in_dim(target_ids, position * TOK_DEV, TOK_DEV, 0)
        logits = lax.dot_general(row_block, vocab_table, (((1,), (1,)), ((), ())), preferred_element_type=jnp.float32)
        highest_logit = lax.optimization_barrier(jnp.max(logits, axis=-1))
        totals = lax.optimization_barrier(jnp.sum(jnp.exp(logits - highest_logit[:, None]), axis=-1))
        picked = jnp.take_along_axis(logits, goal_ids[:, None], axis=1)[:, 0]
        return picked - (highest_logit + jnp.log(totals))
    return lax.map(score_block, jnp.arange(blocks, dtype=jnp.int32)).reshape(TOKENS)
```

```python
import functools

import jax
import jax.numpy as jnp
import numpy as np
from jax import lax
from jax.experimental import pallas as pl
from jax.experimental.pallas import tpu as pltpu
from jax.sharding import PartitionSpec as P

FEAT = 16
WINDOW = 64
HEAD_DIM = 128
EPSILON = 1e-05
NEGATIVE = -1e30
LANES = 128
WIDE = 256
DISTINCT = 1 + FEAT + FEAT * (FEAT + 1) // 2
STATE_ROWS = 160
BUFFER_ROWS = 176
F32 = jnp.float32
BF16 = jnp.bfloat16
VMEM_BYTES = 56 * 1024 * 1024


def params(**kw):
    return pltpu.CompilerParams(vmem_limit_bytes=VMEM_BYTES, **kw)


def whole():
    return pl.BlockSpec(memory_space=pltpu.VMEM)


def smem():
    return pl.BlockSpec(memory_space=pltpu.SMEM)


def dot(a, b, dims=((1,), (0,))):
    return lax.dot_general(a, b, (dims, ((), ())), preferred_element_type=F32)


def xor_pairs(size, k):
    return [(i, i ^ k) for i in range(size)]


def rms(values, gain):
    factor = lax.rsqrt(jnp.mean(values * values, axis=-1, keepdims=True) + EPSILON)
    return (values * factor * gain.astype(F32)).astype(BF16)


def lookup_kernel(ids_ref, table_ref, out_ref):
    rows = table_ref.shape[0]
    parts, each, width = out_ref.shape[0], out_ref.shape[2], out_ref.shape[3]
    ids = ids_ref[0]
    hot = (lax.broadcasted_iota(jnp.int32, (parts * each, rows), 1) == ids).astype(F32).astype(BF16)
    found = dot(hot, table_ref[...]).astype(BF16)
    for part in range(parts):
        out_ref[part, 0] = found[part * each : (part + 1) * each]


def lookup(local_ids, table, parts):
    blocks, count = local_ids.shape
    rows, width = table.shape
    each = count // parts
    return pl.pallas_call(
        lookup_kernel,
        grid=(blocks,),
        in_specs=[
            pl.BlockSpec((1, count, 1), lambda k: (k, 0, 0)),
            pl.BlockSpec((rows, width), lambda k: (0, 0), pipeline_mode=pl.Buffered(1)),
        ],
        out_specs=pl.BlockSpec((parts, 1, each, width), lambda k: (0, k, 0, 0)),
        out_shape=jax.ShapeDtypeStruct((parts, blocks, each, width), BF16),
        compiler_params=params(),
        name="lookup",
    )(local_ids.reshape(blocks, count, 1), table)


def selectors(heads):
    pairs = [(r, s) for r in range(FEAT) for s in range(r, FEAT)]
    picks = np.zeros((2, heads, 2, LANES, WIDE), np.float32)
    bias = np.zeros((2, WIDE), np.float32)
    scale = 0.5
    bias[:, 0] = 1.0
    for r in range(FEAT):
        bias[1, 1 + r] = 1.0
    for kind in range(2):
        for head in range(heads):
            first = (kind * heads + head) * FEAT
            for r in range(FEAT):
                picks[kind, head, 0, first + r, 1 + r] = scale
            for n, (r, s) in enumerate(pairs):
                picks[kind, head, 0, first + r, 1 + FEAT + n] = scale
                picks[kind, head, 1, first + s, 1 + FEAT + n] = scale
    factor = np.ones((1, WIDE), np.float32)
    for n, (r, s) in enumerate(pairs):
        factor[0, 1 + FEAT + n] = 0.5**0.5 if r == s else 1.0
    doubled = np.concatenate([picks, picks], axis=3)
    return jnp.asarray(doubled, BF16), jnp.asarray(bias), jnp.asarray(factor)


def project_kernel(heads, bound_ref, units_ref, weight_ref, pick_ref, bias_ref, factor_ref, fq_ref, fk_ref, v_ref, state_ref):
    projected = dot(units_ref[...], weight_ref[...])
    count = projected.shape[0]
    width = heads * HEAD_DIM
    values = projected[:, :width].astype(BF16)
    v_ref[...] = values
    narrow = projected[:, width:]
    upper = narrow.astype(BF16)
    lower = (narrow - upper.astype(F32)).astype(BF16)
    both = jnp.concatenate([upper, lower], axis=1)
    bound = bound_ref[0]
    place = lax.broadcasted_iota(jnp.int32, (count, 1), 0)
    kept = ((place >= bound) | (bound == count)).astype(F32)
    ones = jnp.ones((8, count), BF16)
    for head in range(heads):
        feats = []
        for kind in range(2):
            one = dot(both, pick_ref[kind, head, 0]) + bias_ref[0:1]
            two = dot(both, pick_ref[kind, head, 1]) + bias_ref[1:2]
            feats.append(one * two * factor_ref[...])
        fq_ref[head] = feats[0].astype(BF16)
        keys = feats[1].astype(BF16)
        fk_ref[head] = keys
        keys = (keys.astype(F32) * kept).astype(BF16)
        state = dot(keys, values[:, head * HEAD_DIM : (head + 1) * HEAD_DIM], ((0,), (0,)))
        total = dot(ones, keys)
        state_ref[head, 0:STATE_ROWS] = state[0:STATE_ROWS].astype(BF16)
        tail = jnp.concatenate([total[0:1, :LANES], total[0:1, LANES:], jnp.zeros((14, LANES), F32)], axis=0)
        state_ref[head, STATE_ROWS:BUFFER_ROWS] = tail.astype(BF16)


def project(bound, units, weight, heads):
    pick, bias, factor = selectors(heads)
    count = units.shape[0]
    return pl.pallas_call(
        functools.partial(project_kernel, heads),
        in_specs=[smem()] + [whole()] * 5,
        out_specs=[whole()] * 4,
        out_shape=[
            jax.ShapeDtypeStruct((heads, count, WIDE), BF16),
            jax.ShapeDtypeStruct((heads, count, WIDE), BF16),
            jax.ShapeDtypeStruct((count, heads * HEAD_DIM), BF16),
            jax.ShapeDtypeStruct((heads, BUFFER_ROWS, HEAD_DIM), BF16),
        ],
        compiler_params=params(),
        name="project",
    )(bound, units, weight, pick, bias, factor)


def within_kernel(heads, bound_ref, fq_ref, fk_ref, v_ref, num_ref, den_ref):
    count = v_ref.shape[0]
    bound = bound_ref[0]
    step = count // 2
    for first in range(0, count, step):
        reach = first + step
        row = lax.broadcasted_iota(jnp.int32, (step, reach), 0) + first
        col = lax.broadcasted_iota(jnp.int32, (step, reach), 1)
        allowed = (row >= col) & ((row >= bound) == (col >= bound))
        for head in range(heads):
            weights = dot(fq_ref[head, first:reach], fk_ref[head, 0:reach], ((1,), (1,)))
            weights = jnp.where(allowed, weights, 0.0)
            den_ref[head, first:reach] = jnp.broadcast_to(
                jnp.sum(weights, axis=-1, keepdims=True), (step, 8)
            )
            num_ref[head, first:reach] = dot(
                weights.astype(BF16), v_ref[0:reach, head * HEAD_DIM : (head + 1) * HEAD_DIM]
            )


def within(bound, fq, fk, values, heads):
    count = values.shape[0]
    return pl.pallas_call(
        functools.partial(within_kernel, heads),
        in_specs=[smem()] + [whole()] * 3,
        out_specs=[whole()] * 2,
        out_shape=[
            jax.ShapeDtypeStruct((heads, count, HEAD_DIM), F32),
            jax.ShapeDtypeStruct((heads, count, 8), F32),
        ],
        compiler_params=params(),
        name="within",
    )(bound, fq, fk, values)


def across_kernel(heads, earlier, bound_ref, share_ref, fq_ref, num_ref, den_ref, gain_ref, out_ref, *rest):
    states, result_ref = rest[:earlier], rest[earlier]
    count = num_ref.shape[1]
    bound = bound_ref[0]
    before = (lax.broadcasted_iota(jnp.int32, (count, 1), 0) < bound).astype(F32)
    parts = []
    for head in range(heads):
        carried = jnp.zeros((BUFFER_ROWS, HEAD_DIM), F32)
        for n in range(earlier):
            carried = carried + jnp.where(share_ref[n] > 0, states[n][head].astype(F32), 0.0)
        state = jnp.concatenate(
            [carried[0:STATE_ROWS], jnp.zeros((WIDE - STATE_ROWS, HEAD_DIM), F32)], axis=0
        ).astype(BF16)
        total = jnp.concatenate(
            [carried[STATE_ROWS : STATE_ROWS + 1], carried[STATE_ROWS + 1 : STATE_ROWS + 2]], axis=1
        )
        query = fq_ref[head]
        numerator = num_ref[head] + before * dot(query, state)
        more = jnp.sum(query.astype(F32) * total, axis=-1, keepdims=True)
        denominator = den_ref[head][:, 0:1] + before * more
        parts.append(
            (numerator / denominator * gain_ref[:, head * HEAD_DIM : (head + 1) * HEAD_DIM].astype(F32)).astype(BF16)
        )
    mixed = jnp.concatenate(parts, axis=1)
    result_ref[...] = dot(mixed, out_ref[...]).astype(BF16)


def across(bound, share, fq, num, den, gain, weight, states, heads):
    count = num.shape[1]
    return pl.pallas_call(
        functools.partial(across_kernel, heads, len(states)),
        in_specs=[smem(), smem()] + [whole()] * (5 + len(states)),
        out_specs=whole(),
        out_shape=jax.ShapeDtypeStruct((count, weight.shape[1]), BF16),
        compiler_params=params(),
        name="across",
    )(bound, share, fq, num, den, gain, weight, *states)


def matmul_kernel(a_ref, b_ref, o_ref):
    o_ref[...] = dot(a_ref[...], b_ref[...]).astype(BF16)


def matmul(a, b, tile):
    rows, inner = a.shape
    return pl.pallas_call(
        matmul_kernel,
        grid=(b.shape[1] // tile,),
        in_specs=[
            pl.BlockSpec((rows, inner), lambda n: (0, 0), pipeline_mode=pl.Buffered(1)),
            pl.BlockSpec((inner, tile), lambda n: (0, n)),
        ],
        out_specs=pl.BlockSpec((rows, tile), lambda n: (0, n)),
        out_shape=jax.ShapeDtypeStruct((rows, b.shape[1]), BF16),
        compiler_params=params(),
        name="matmul",
    )(a, b)


def window_kernel(heads, bound_ref, qkv_ref, halo_ref, out_ref, result_ref, held):
    count = qkv_ref.shape[0]
    step = 2 * WINDOW
    reach = step + WINDOW
    bound, valid_from = bound_ref[0], bound_ref[1]
    row = lax.broadcasted_iota(jnp.int32, (step, reach), 0)
    col = lax.broadcasted_iota(jnp.int32, (step, reach), 1)
    band = (col > row) & (col <= row + WINDOW)
    for first in range(0, count, step):
        query_place = row + first
        key_place = col + (first - WINDOW)
        allowed = band & ((query_place >= bound) == (key_place >= bound))
        if first == 0:
            allowed = allowed & ((key_place >= 0) | ((key_place + count >= valid_from) & (query_place < bound)))
        for head in range(heads):
            base = head * 3 * HEAD_DIM
            query = qkv_ref[first : first + step, base : base + HEAD_DIM]
            both = []
            for n in (1, 2):
                lanes = slice(base + n * HEAD_DIM, base + (n + 1) * HEAD_DIM)
                if first == 0:
                    both.append(
                        jnp.concatenate([halo_ref[:, lanes], qkv_ref[0:step, lanes]], axis=0)
                    )
                else:
                    both.append(qkv_ref[first - WINDOW : first + step, lanes])
            scores = dot(query, both[0], ((1,), (1,))) * HEAD_DIM ** (-0.5)
            scores = jnp.where(allowed, scores, NEGATIVE)
            peak = jnp.max(scores, axis=-1, keepdims=True)
            weights = jnp.where(allowed, jnp.exp(scores - peak), 0.0)
            probabilities = (weights / jnp.sum(weights, axis=-1, keepdims=True)).astype(BF16)
            held[first : first + step, head * HEAD_DIM : (head + 1) * HEAD_DIM] = dot(
                probabilities, both[1]
            ).astype(BF16)
    result_ref[...] = dot(held[...], out_ref[...]).astype(BF16)


def window(bound, qkv, halo, weight, heads):
    count = qkv.shape[0]
    return pl.pallas_call(
        functools.partial(window_kernel, heads),
        in_specs=[smem()] + [whole()] * 3,
        out_specs=whole(),
        out_shape=jax.ShapeDtypeStruct((count, weight.shape[1]), BF16),
        scratch_shapes=[pltpu.VMEM((count, heads * HEAD_DIM), BF16)],
        compiler_params=params(),
        name="window",
    )(bound, qkv, halo, weight)


def score_kernel(pieces, tile, order_ref, *refs):
    units, tables = refs[:pieces], refs[pieces : 2 * pieces]
    goal_ref, out_ref, peak_ref, total_ref, picked_ref = refs[2 * pieces :]
    step = pl.program_id(0)
    count = goal_ref.shape[0]

    @pl.when(step == 0)
    def _():
        peak_ref[...] = jnp.full_like(peak_ref, NEGATIVE)
        total_ref[...] = jnp.zeros_like(total_ref)
        picked_ref[...] = jnp.zeros_like(picked_ref)

    chunk = 128
    lane = lax.broadcasted_iota(jnp.int32, (chunk, LANES), 1) + step * tile
    for first in range(0, count, chunk):
        rows = slice(first, first + chunk)
        logits = dot(units[0][rows], tables[0][...], ((1,), (1,)))
        for n in range(1, pieces):
            logits = logits + dot(units[n][rows], tables[n][...], ((1,), (1,)))
        goal = goal_ref[rows]
        old = peak_ref[rows]
        peak = old
        for k in range(0, tile, LANES):
            peak = jnp.maximum(peak, logits[:, k : k + LANES])
        total = total_ref[rows] * jnp.exp(old - peak)
        picked = picked_ref[rows]
        for k in range(0, tile, LANES):
            part = logits[:, k : k + LANES]
            total = total + jnp.exp(part - peak)
            picked = picked + jnp.where(lane + k == goal, part, 0.0)
        peak_ref[rows] = peak
        total_ref[rows] = total
        picked_ref[rows] = picked

    @pl.when(step == pl.num_programs(0) - 1)
    def _():
        peak = jnp.max(peak_ref[...], axis=-1, keepdims=True)
        total = jnp.sum(total_ref[...] * jnp.exp(peak_ref[...] - peak), axis=-1, keepdims=True)
        picked = jnp.sum(picked_ref[...], axis=-1, keepdims=True)
        spread = lax.broadcasted_iota(jnp.int32, (count, 8), 1)
        out_ref[...] = jnp.where(spread == 0, peak, jnp.where(spread == 1, total, picked))


def scores(order, units, tables, goal):
    count = units.shape[0]
    pieces = len(tables)
    rows, width = tables[0].shape
    tile = 640
    unit_specs = [
        pl.BlockSpec((count, width), lambda i, order, n=n: (0, order[n]), pipeline_mode=pl.Buffered(1))
        for n in range(pieces)
    ]
    table_specs = [pl.BlockSpec((tile, width), lambda i, order: (i, 0)) for n in range(pieces)]
    return pl.pallas_call(
        functools.partial(score_kernel, pieces, tile),
        grid_spec=pltpu.PrefetchScalarGridSpec(
            num_scalar_prefetch=1,
            grid=(rows // tile,),
            in_specs=unit_specs
            + table_specs
            + [pl.BlockSpec((count, 1), lambda i, order: (0, 0), pipeline_mode=pl.Buffered(1))],
            out_specs=pl.BlockSpec((count, 8), lambda i, order: (0, 0)),
            scratch_shapes=[pltpu.VMEM((count, LANES), F32)] * 3,
        ),
        out_shape=jax.ShapeDtypeStruct((count, 8), F32),
        compiler_params=params(),
        name="scores",
    )(order, *([units] * pieces), *tables, goal)


def shards(
    token_ids,
    target_ids,
    doc_start,
    vocab_table,
    norm_gain_one,
    lin_qkv,
    lin_head_gain,
    lin_out,
    norm_gain_two,
    win_qkv,
    win_out,
    final_gain,
):
    head_count = lax.axis_size("head")
    seq_count = lax.axis_size("seq")
    head_index = lax.axis_index("head")
    seq_index = lax.axis_index("seq")
    tok_count = token_ids.shape[0]
    own_rows = tok_count // head_count
    vocab_rows, table_width = vocab_table.shape
    heads = lin_qkv.shape[1] // (2 * FEAT + HEAD_DIM)
    vocab_first = head_index * vocab_rows

    marks = jnp.concatenate([token_ids, jnp.broadcast_to(doc_start, (LANES,))])
    marks = jnp.stack(
        [marks] + [lax.ppermute(marks, "seq", xor_pairs(seq_count, k)) for k in range(1, seq_count)]
    )
    starts = marks[:, tok_count]
    starts = jnp.stack(
        [lax.dynamic_index_in_dim(starts, seq_index ^ j, 0, False) for j in range(seq_count)]
    )
    bound = doc_start.astype(jnp.int32)
    block = jnp.arange(seq_count, dtype=jnp.int32)

    found = lookup(marks[:, :tok_count] - vocab_first, vocab_table, head_count)
    found = lax.psum_scatter(found, "head", scatter_dimension=0, tiled=True)[0]
    gathered = [found[0]] + [
        lax.ppermute(found[k], "seq", xor_pairs(seq_count, k)) for k in range(1, seq_count)
    ]
    table, gathered = lax.optimization_barrier((vocab_table, gathered))
    gathered = jnp.stack(gathered)
    embedded = jnp.concatenate(
        [lax.dynamic_index_in_dim(gathered, seq_index ^ j, 0, False) for j in range(seq_count)], axis=1
    )

    if seq_count == 4:
        beside = lax.ppermute(table, "seq", xor_pairs(seq_count, 1))
        across_x = lax.ppermute(table, "seq", xor_pairs(seq_count, 2))
        corner = lax.ppermute(across_x, "seq", xor_pairs(seq_count, 1))
        tables = [table, beside, across_x, corner]
        order = seq_index ^ block
    else:
        tables = [lax.all_gather(table, "seq", axis=1, tiled=True)]
        order = jnp.zeros((1,), jnp.int32)

    units_one = rms(embedded.astype(F32), norm_gain_one)
    units_one = lax.all_gather(units_one, "head", axis=0, tiled=True)

    by_head = lin_qkv.reshape(lin_qkv.shape[0], heads, 2 * FEAT + HEAD_DIM)
    pad = LANES - 2 * FEAT * heads
    weight_one = jnp.concatenate(
        [
            by_head[:, :, 2 * FEAT :].reshape(-1, heads * HEAD_DIM),
            by_head[:, :, :FEAT].reshape(-1, heads * FEAT),
            by_head[:, :, FEAT : 2 * FEAT].reshape(-1, heads * FEAT),
            jnp.zeros((lin_qkv.shape[0], pad), BF16),
        ],
        axis=1,
    )
    feat_query, feat_key, values_one, state_here = project(bound, units_one, weight_one, heads)
    states, shares = [], []
    for back in range(1, seq_count):
        states.append(
            lax.ppermute(state_here, "seq", [(i, i + back) for i in range(seq_count - back)])
        )
        between = (block > seq_index - back) & (block < seq_index)
        unbroken = jnp.all(~between | (starts == tok_count))
        shares.append((unbroken & (seq_index >= back)).astype(jnp.int32))
    num, den = within(bound, feat_query, feat_key, values_one, heads)
    partial_one = across(
        bound, jnp.stack(shares), feat_query, num, den, lin_head_gain.reshape(1, -1), lin_out, states, heads
    )
    residual_one = (
        embedded.astype(F32)
        + lax.psum_scatter(partial_one, "head", scatter_dimension=0, tiled=True).astype(F32)
    ).astype(BF16)

    units_two = rms(residual_one.astype(F32), norm_gain_two)
    units_two = lax.all_gather(units_two, "head", axis=0, tiled=True)
    tail = matmul(units_two[tok_count - WINDOW :], win_qkv, 3 * HEAD_DIM)
    halo = lax.ppermute(tail, "seq", [(i, i + 1) for i in range(seq_count - 1)])
    qkv = matmul(units_two, win_qkv, 3 * HEAD_DIM)
    previous = lax.dynamic_index_in_dim(starts, jnp.maximum(seq_index - 1, 0), 0, False)
    valid_from = jnp.where(
        seq_index == 0, tok_count, jnp.where(previous == tok_count, 0, previous)
    ).astype(jnp.int32)
    partial_two = window(
        jnp.concatenate([bound, valid_from.reshape(1)]), qkv, halo, win_out, heads
    )
    residual_two = residual_one.astype(F32) + lax.psum_scatter(
        partial_two, "head", scatter_dimension=0, tiled=True
    ).astype(F32)

    final_units = lax.all_gather(rms(residual_two, final_gain), "head", axis=0, tiled=True)
    found = scores(order, final_units, tables, (target_ids - vocab_first).reshape(tok_count, 1))
    found = found[:, :3].T.reshape(3, head_count, own_rows)

    shares = [lax.dynamic_index_in_dim(found, head_index, 1, False)]
    for step in range(1, head_count):
        leaving = lax.dynamic_index_in_dim(found, (head_index + step) % head_count, 1, False)
        shares.append(
            lax.ppermute(leaving, "head", [(i, (i + step) % head_count) for i in range(head_count)])
        )
    shares = jnp.stack(shares)
    peak = jnp.max(shares[:, 0], axis=0)
    total = jnp.sum(shares[:, 1] * jnp.exp(shares[:, 0] - peak), axis=0)
    return jnp.sum(shares[:, 2], axis=0) - (peak + jnp.log(total))


def solution(mesh):
    return jax.shard_map(
        shards,
        mesh=mesh,
        in_specs=(
            P(("shadow", "seq")),
            P(("shadow", "seq")),
            P(("shadow", "seq")),
            P(("shadow", "head"), "seq"),
            P("shadow"),
            P("shadow", "head"),
            P(("shadow", "head")),
            P(("shadow", "head"), None),
            P("shadow"),
            P("shadow", "head"),
            P(("shadow", "head"), None),
            P("shadow"),
        ),
        out_specs=P(("shadow", "seq", "head")),
        check_vma=False,
    )
```

```python
import functools

import jax
import jax.numpy as jnp
import numpy as np
from jax import lax
from jax.experimental import pallas as pl
from jax.experimental.pallas import tpu as pltpu
from jax.sharding import PartitionSpec as P

FEAT = 16
WINDOW = 64
HEAD_DIM = 128
EPSILON = 1e-05
NEGATIVE = -1e30
LANES = 128
WIDE = 256
STATE_ROWS = 160
BUFFER_ROWS = 176
F32 = jnp.float32
BF16 = jnp.bfloat16
VMEM_BYTES = 56 * 1024 * 1024


def params(**kw):
    return pltpu.CompilerParams(vmem_limit_bytes=VMEM_BYTES, **kw)


def whole():
    return pl.BlockSpec(memory_space=pltpu.VMEM)


def smem():
    return pl.BlockSpec(memory_space=pltpu.SMEM)


def dot(a, b, dims=((1,), (0,))):
    return lax.dot_general(a, b, (dims, ((), ())), preferred_element_type=F32)


def xor_pairs(size, k):
    return [(i, i ^ k) for i in range(size)]


def rms(values, gain):
    factor = lax.rsqrt(jnp.mean(values * values, axis=-1, keepdims=True) + EPSILON)
    return (values * factor * gain.astype(F32)).astype(BF16)


def turned(value, step):
    size = lax.axis_size("head")
    return lax.ppermute(value, "head", [(i, (i + step) % size) for i in range(size)])


def gather_rows(own):
    size = lax.axis_size("head")
    if size != 4:
        full = lax.all_gather(own, "head")
        here = lax.axis_index("head")
        return [[own]] + [
            [lax.dynamic_index_in_dim(full, (here + k) % size, 0, False)] for k in range(1, size)
        ]
    half = own.shape[0] // 2
    before, after = turned(own, 1), turned(own, -1)
    return [[own], [after], [turned(before[:half], 1), turned(after[half:], -1)], [before]]


def add_kernel(next_ref, prev_ref, upper_ref, lower_ref, right_ref, left_ref):
    half = upper_ref.shape[0]
    right_ref[0:half] = (next_ref[0:half].astype(F32) + upper_ref[...].astype(F32)).astype(BF16)
    right_ref[half:] = next_ref[half:]
    left_ref[0:half] = prev_ref[0:half]
    left_ref[half:] = (prev_ref[half:].astype(F32) + lower_ref[...].astype(F32)).astype(BF16)


def scatter_rows(far, near):
    size = lax.axis_size("head")
    if size != 4:
        here = lax.axis_index("head")
        full = jnp.stack([near()[0]] + list(far))
        full = jnp.stack(
            [lax.dynamic_index_in_dim(full, (d - here) % size, 0, False) for d in range(size)]
        )
        return [lax.psum_scatter(full, "head", scatter_dimension=0, tiled=True)[0]]
    upper, lower = turned(far[0], 1), turned(far[1], -1)
    own, after, before = near()
    right, left = pl.pallas_call(
        add_kernel,
        in_specs=[whole()] * 4,
        out_specs=[whole()] * 2,
        out_shape=[jax.ShapeDtypeStruct(own.shape, BF16)] * 2,
        compiler_params=params(),
        name="pass_on",
    )(after, before, upper, lower)
    return [own, turned(right, 1), turned(left, -1)]


def chunk_order(size):
    if size == 4:
        return [[0], [1, 3], [2]]
    return [[k] for k in range(size)]


def lookup_kernel(ids_ref, table_ref, *refs):
    outs, total = refs[:-1], refs[-1]
    step = pl.program_id(0)
    tile = table_ref.shape[0]
    count = ids_ref.shape[1]
    ids = jnp.transpose(jnp.broadcast_to(ids_ref[...], (8, count)))[:, 0:1] - step * tile
    hot = (lax.broadcasted_iota(jnp.int32, (count, tile), 1) == ids).astype(F32).astype(BF16)
    found = dot(hot, table_ref[...])

    @pl.when(step == 0)
    def _():
        total[...] = found

    @pl.when(step > 0)
    def _():
        total[...] += found

    @pl.when(step == pl.num_programs(0) - 1)
    def _():
        rows = outs[0].shape[0]
        for n, out in enumerate(outs):
            out[...] = total[n * rows : (n + 1) * rows].astype(BF16)


def lookup(ids, table, pieces):
    count = ids.shape[0]
    rows, width = table.shape
    tile = rows // 5
    return pl.pallas_call(
        lookup_kernel,
        grid=(rows // tile,),
        in_specs=[
            pl.BlockSpec((1, count), lambda i: (0, 0)),
            pl.BlockSpec((tile, width), lambda i: (i, 0)),
        ],
        out_specs=[pl.BlockSpec((count // pieces, width), lambda i: (0, 0))] * pieces,
        out_shape=[jax.ShapeDtypeStruct((count // pieces, width), BF16)] * pieces,
        scratch_shapes=[pltpu.VMEM((count, width), F32)],
        compiler_params=params(),
        name="lookup",
    )(ids.reshape(1, count), table)


def collect_kernel(parts, *refs):
    ins, outs = refs[:parts], refs[parts:]
    rows = outs[0].shape[0]
    for n, out in enumerate(outs):
        span = slice(n * rows, (n + 1) * rows)
        total = ins[0][span].astype(F32)
        for part in ins[1:]:
            total = total + part[span].astype(F32)
        out[...] = total.astype(BF16)


def collect(parts, pieces):
    rows, width = parts[0].shape
    return pl.pallas_call(
        functools.partial(collect_kernel, len(parts)),
        in_specs=[whole()] * len(parts),
        out_specs=[whole()] * pieces,
        out_shape=[jax.ShapeDtypeStruct((rows // pieces, width), BF16)] * pieces,
        compiler_params=params(),
        name="collect",
    )(*parts)


def begin_kernel(pieces, order_ref, gain_ref, *refs):
    ins, (embedded_ref, units_ref, held) = refs[:pieces], refs[pieces:]
    width = ins[0].shape[1]
    for n in range(pieces):
        held[order_ref[n]] = ins[n][...]
    values = jnp.concatenate([held[n] for n in range(pieces)], axis=1)
    embedded_ref[...] = values
    units_ref[...] = rms(values.astype(F32), gain_ref[...])


def begin(order, gain, pieces):
    rows, width = pieces[0].shape
    full = jax.ShapeDtypeStruct((rows, width * len(pieces)), BF16)
    return pl.pallas_call(
        functools.partial(begin_kernel, len(pieces)),
        in_specs=[smem()] + [whole()] * (1 + len(pieces)),
        out_specs=[whole()] * 2,
        out_shape=[full, full],
        scratch_shapes=[pltpu.VMEM((len(pieces), rows, width), BF16)],
        compiler_params=params(),
        name="begin",
    )(order, gain.reshape(1, -1), *pieces)


def finish_kernel(parts, last, residual_ref, gain_ref, *refs):
    total = refs[0][...].astype(F32)
    for part in refs[1:parts]:
        total = total + part[...].astype(F32)
    total = total + residual_ref[...].astype(F32)
    if not last:
        total = total.astype(BF16)
        refs[parts + 1][...] = total
    refs[parts][...] = rms(total.astype(F32), gain_ref[...])


def finish(residual, gain, parts, last):
    full = jax.ShapeDtypeStruct(residual.shape, BF16)
    return pl.pallas_call(
        functools.partial(finish_kernel, len(parts), last),
        in_specs=[whole()] * (2 + len(parts)),
        out_specs=[whole()] * (1 if last else 2),
        out_shape=[full] * (1 if last else 2),
        compiler_params=params(),
        name="finish",
    )(residual, gain.reshape(1, -1), *parts)


def selectors():
    pairs = [(r, s) for r in range(FEAT) for s in range(r, FEAT)]
    picks = np.zeros((2, 2, LANES, WIDE), np.float32)
    extra = np.zeros((3, WIDE), np.float32)
    extra[0:2, 0] = 1.0
    extra[1, 1 : 1 + FEAT] = 1.0
    extra[2] = 1.0
    for kind in range(2):
        first = kind * FEAT
        for r in range(FEAT):
            picks[kind, 0, first + r, 1 + r] = FEAT ** (-0.25)
        for n, (r, s) in enumerate(pairs):
            picks[kind, 0, first + r, 1 + FEAT + n] = FEAT ** (-0.25)
            picks[kind, 1, first + s, 1 + FEAT + n] = FEAT ** (-0.25)
    for n, (r, s) in enumerate(pairs):
        extra[2, 1 + FEAT + n] = 0.5**0.5 if r == s else 1.0
    return jnp.asarray(np.concatenate([picks, picks], axis=2), BF16), jnp.asarray(extra)


def place_column(places_ref, slots, rows):
    inner = lax.broadcasted_iota(jnp.int32, (rows, 1), 0)
    return jnp.concatenate([inner + places_ref[slot] for slot in slots], axis=0)


def place_row(places_ref, slots, rows):
    inner = lax.broadcasted_iota(jnp.int32, (1, rows), 1)
    return jnp.concatenate([inner + places_ref[slot] for slot in slots], axis=1)


def project_kernel(heads, slots, chunk, count, pieces, more, last, bound_ref, places_ref, *refs):
    units = jnp.concatenate([ref[...] for ref in refs[:pieces]], axis=0)
    weight_ref, pick_ref, extra_ref = refs[pieces : pieces + 3]
    fq_ref, fk_ref, v_ref, state_ref = refs[-4:]
    projected = dot(units, weight_ref[...])
    rows, width = projected.shape
    needed = (heads - 1) * LANES + WIDE
    if needed > width:
        projected = jnp.pad(projected, ((0, 0), (0, needed - width)))
    bound = bound_ref[0]
    place = place_column(places_ref, slots, chunk)
    kept = ((place >= bound) | (bound == count)).astype(F32)
    ones = jnp.ones((8, rows), BF16)
    shift = 2 * FEAT
    for head in range(heads):
        part = projected[:, head * LANES : head * LANES + WIDE]
        narrow = part if head == 0 else pltpu.roll(part, WIDE - shift * head, 1)
        narrow = narrow[:, :LANES]
        values = pltpu.roll(part, WIDE - shift * (head + 1), 1)[:, :HEAD_DIM].astype(BF16)
        v_ref[:, head * HEAD_DIM : (head + 1) * HEAD_DIM] = values
        upper = narrow.astype(BF16)
        lower = (narrow - upper.astype(F32)).astype(BF16)
        both = jnp.concatenate([upper, lower], axis=1)
        feats = []
        for kind in range(2):
            one = dot(both, pick_ref[kind, 0]) + extra_ref[0:1]
            two = dot(both, pick_ref[kind, 1]) + extra_ref[1:2]
            feats.append((one * two * extra_ref[2:3]).astype(BF16))
        fq_ref[head] = feats[0]
        fk_ref[head] = feats[1]
        keys = (feats[1].astype(F32) * kept).astype(BF16)
        state = dot(keys, values, ((0,), (0,)))
        total = dot(ones, keys)
        tail = jnp.concatenate([total[0:1, :LANES], total[0:1, LANES:], jnp.zeros((14, LANES), F32)], axis=0)
        state = jnp.concatenate([state[0:STATE_ROWS], tail], axis=0)
        if more:
            state = state + refs[pieces + 3][head]
        state_ref[head] = state.astype(BF16) if last else state


def project(bound, places, slots, chunk, count, pieces, weight, constants, earlier, last, heads):
    rows = sum(piece.shape[0] for piece in pieces)
    extra = [] if earlier is None else [earlier]
    return pl.pallas_call(
        functools.partial(project_kernel, heads, slots, chunk, count, len(pieces), bool(extra), last),
        in_specs=[smem(), smem()] + [whole()] * (len(pieces) + 3 + len(extra)),
        out_specs=[whole()] * 4,
        out_shape=[
            jax.ShapeDtypeStruct((heads, rows, WIDE), BF16),
            jax.ShapeDtypeStruct((heads, rows, WIDE), BF16),
            jax.ShapeDtypeStruct((rows, heads * HEAD_DIM), BF16),
            jax.ShapeDtypeStruct((heads, BUFFER_ROWS, HEAD_DIM), BF16 if last else F32),
        ],
        compiler_params=params(),
        name="project",
    )(bound, places, *pieces, weight, *constants, *extra)


def within_kernel(heads, slots, chunk, sets, bound_ref, places_ref, *refs):
    fqs, fks, vs = refs[:sets], refs[sets : 2 * sets], refs[2 * sets : 3 * sets]
    num_ref, den_ref = refs[3 * sets :]
    bound = bound_ref[0]
    row = place_column(places_ref, slots, chunk)
    col = place_row(places_ref, slots, chunk)
    allowed = (row >= col) & ((row >= bound) == (col >= bound))
    for head in range(heads):
        query = jnp.concatenate([ref[head] for ref in fqs], axis=0)
        keys = jnp.concatenate([ref[head] for ref in fks], axis=0)
        values = jnp.concatenate(
            [ref[:, head * HEAD_DIM : (head + 1) * HEAD_DIM] for ref in vs], axis=0
        )
        weights = dot(query, keys, ((1,), (1,)))
        weights = jnp.where(allowed, weights, 0.0)
        den_ref[head] = jnp.broadcast_to(
            jnp.sum(weights, axis=-1, keepdims=True), (row.shape[0], 8)
        )
        num_ref[head] = dot(weights.astype(BF16), values)


def within(bound, places, slots, chunk, fqs, fks, vs, heads):
    count = len(slots) * chunk
    return pl.pallas_call(
        functools.partial(within_kernel, heads, slots, chunk, len(fqs)),
        in_specs=[smem(), smem()] + [whole()] * (3 * len(fqs)),
        out_specs=[whole()] * 2,
        out_shape=[
            jax.ShapeDtypeStruct((heads, count, HEAD_DIM), F32),
            jax.ShapeDtypeStruct((heads, count, 8), F32),
        ],
        compiler_params=params(),
        name="within",
    )(bound, places, *fqs, *fks, *vs)


def split_store(total, refs):
    rows = refs[0].shape[0]
    for n, ref in enumerate(refs):
        ref[...] = total[n * rows : (n + 1) * rows].astype(BF16)


def across_kernel(heads, slots, chunk, sets, earlier, near, bound_ref, places_ref, share_ref, *refs):
    fqs, refs = refs[:sets], refs[sets:]
    num_ref, den_ref, gain_ref, weight_ref = refs[:4]
    states, refs = refs[4 : 4 + earlier], refs[4 + earlier :]
    mixed_ref, fars = refs[0], refs[1:]
    bound = bound_ref[0]
    before = (place_column(places_ref, slots, chunk) < bound).astype(F32)
    for head in range(heads):
        carried = jnp.zeros((BUFFER_ROWS, HEAD_DIM), F32)
        for n in range(earlier):
            carried = carried + jnp.where(share_ref[n] > 0, states[n][head].astype(F32), 0.0)
        state = jnp.concatenate(
            [carried[0:STATE_ROWS], jnp.zeros((WIDE - STATE_ROWS, HEAD_DIM), F32)], axis=0
        ).astype(BF16)
        total = jnp.concatenate(
            [carried[STATE_ROWS : STATE_ROWS + 1], carried[STATE_ROWS + 1 : STATE_ROWS + 2]], axis=1
        )
        query = jnp.concatenate([ref[head] for ref in fqs], axis=0)
        numerator = num_ref[head] + before * dot(query, state)
        more = jnp.sum(query.astype(F32) * total, axis=-1, keepdims=True)
        denominator = den_ref[head][:, 0:1] + before * more
        lanes = slice(head * HEAD_DIM, (head + 1) * HEAD_DIM)
        mixed_ref[:, lanes] = (numerator / denominator * gain_ref[:, lanes].astype(F32)).astype(BF16)
    split_store(dot(mixed_ref[near * chunk :], weight_ref[...]), fars)


def across(bound, places, share, slots, chunk, near, far, fqs, num, den, gain, weight, states, heads):
    count = len(slots) * chunk
    rows = (count - near * chunk) // far
    return pl.pallas_call(
        functools.partial(across_kernel, heads, slots, chunk, len(fqs), len(states), near),
        in_specs=[smem()] * 3 + [whole()] * (len(fqs) + 4 + len(states)),
        out_specs=[whole()] * (1 + far),
        out_shape=[jax.ShapeDtypeStruct((count, heads * HEAD_DIM), BF16)]
        + [jax.ShapeDtypeStruct((rows, weight.shape[1]), BF16)] * far,
        compiler_params=params(),
        name="across",
    )(bound, places, share, *fqs, num, den, gain, weight, *states)


def near_kernel(chunk, mixed_ref, weight_ref, *outs):
    split_store(dot(mixed_ref[0 : chunk * len(outs)], weight_ref[...]), outs)


def near_chunks(mixed, weight, near, chunk):
    return pl.pallas_call(
        functools.partial(near_kernel, chunk),
        in_specs=[whole()] * 2,
        out_specs=[whole()] * near,
        out_shape=[jax.ShapeDtypeStruct((chunk, weight.shape[1]), BF16)] * near,
        compiler_params=params(),
        name="near",
    )(mixed, weight)


def matmul_kernel(*refs):
    a = jnp.concatenate([ref[...] for ref in refs[:-2]], axis=0)
    refs[-1][...] = dot(a, refs[-2][...]).astype(BF16)


def matmul(pieces, b, tile):
    rows = sum(piece.shape[0] for piece in pieces)
    inner = b.shape[0]
    return pl.pallas_call(
        matmul_kernel,
        grid=(b.shape[1] // tile,),
        in_specs=[
            pl.BlockSpec(piece.shape, lambda n: (0, 0), pipeline_mode=pl.Buffered(1)) for piece in pieces
        ]
        + [pl.BlockSpec((inner, tile), lambda n: (0, n))],
        out_specs=pl.BlockSpec((rows, tile), lambda n: (0, n)),
        out_shape=jax.ShapeDtypeStruct((rows, b.shape[1]), BF16),
        compiler_params=params(),
        name="matmul",
    )(*pieces, b)


def attend(query, keys, values, allowed):
    scores = dot(query, keys, ((1,), (1,))) * HEAD_DIM ** (-0.5)
    scores = jnp.where(allowed, scores, NEGATIVE)
    peak = jnp.max(scores, axis=-1, keepdims=True)
    weights = jnp.where(allowed, jnp.exp(scores - peak), 0.0)
    probabilities = (weights / jnp.sum(weights, axis=-1, keepdims=True)).astype(BF16)
    return dot(probabilities, values).astype(BF16)


def local_kernel(heads, slots, spots, chunk, sets, bound_ref, places_ref, *refs):
    qkvs, (result_ref, first_ref) = refs[:sets], refs[sets:]
    size = len(slots)
    reach = chunk + WINDOW
    bound = bound_ref[0]
    row = lax.broadcasted_iota(jnp.int32, (chunk, reach), 0)
    col = lax.broadcasted_iota(jnp.int32, (chunk, reach), 1)
    band = (col > row) & (col <= row + WINDOW)
    for slot in range(size):
        k = slots[slot]
        mine, at = spots[k]
        theirs, there = spots[(k - 1) % size]
        base = places_ref[slot]
        query_place = row + base
        key_place = col + (base - WINDOW)
        allowed = band & (key_place >= 0) & ((query_place >= bound) == (key_place >= bound))
        rows = slice(at, at + chunk)
        tail = slice(there + chunk - WINDOW, there + chunk)

        @pl.when(base == 0)
        def _():
            first_ref[...] = qkvs[mine][at : at + WINDOW]

        for head in range(heads):
            lane = head * 3 * HEAD_DIM
            keys, values = [
                jnp.concatenate(
                    [
                        qkvs[theirs][tail, lane + n * HEAD_DIM : lane + (n + 1) * HEAD_DIM],
                        qkvs[mine][rows, lane + n * HEAD_DIM : lane + (n + 1) * HEAD_DIM],
                    ],
                    axis=0,
                )
                for n in (1, 2)
            ]
            result_ref[slot * chunk : (slot + 1) * chunk, head * HEAD_DIM : (head + 1) * HEAD_DIM] = attend(
                qkvs[mine][rows, lane : lane + HEAD_DIM], keys, values, allowed
            )


def local_window(bound, places, slots, spots, chunk, qkvs, heads):
    return pl.pallas_call(
        functools.partial(local_kernel, heads, slots, spots, chunk, len(qkvs)),
        in_specs=[smem(), smem()] + [whole()] * len(qkvs),
        out_specs=[whole()] * 2,
        out_shape=[
            jax.ShapeDtypeStruct((len(slots) * chunk, heads * HEAD_DIM), BF16),
            jax.ShapeDtypeStruct((WINDOW, qkvs[0].shape[1]), BF16),
        ],
        compiler_params=params(),
        name="local_window",
    )(bound, places, *qkvs)


def halo_kernel(heads, count, start, info_ref, local_ref, first_ref, halo_ref, weight_ref, result_ref, *fars):
    result_ref[...] = local_ref[...]
    bound, valid_from, spot = info_ref[0], info_ref[1], info_ref[2]
    row = lax.broadcasted_iota(jnp.int32, (WINDOW, 2 * WINDOW), 0)
    col = lax.broadcasted_iota(jnp.int32, (WINDOW, 2 * WINDOW), 1)
    key_place = col - WINDOW
    allowed = (col > row) & (col <= row + WINDOW) & ((row >= bound) == (key_place >= bound))
    allowed = allowed & ((key_place >= 0) | (key_place + count >= valid_from))
    spot = pl.multiple_of(spot, WINDOW)
    for head in range(heads):
        lane = head * 3 * HEAD_DIM
        keys, values = [
            jnp.concatenate(
                [ref[:, lane + n * HEAD_DIM : lane + (n + 1) * HEAD_DIM] for ref in (halo_ref, first_ref)], axis=0
            )
            for n in (1, 2)
        ]
        result_ref[pl.ds(spot, WINDOW), head * HEAD_DIM : (head + 1) * HEAD_DIM] = attend(
            first_ref[:, lane : lane + HEAD_DIM], keys, values, allowed
        )
    split_store(dot(result_ref[start:], weight_ref[...]), fars)


def halo_window(info, near, chunk, far, local, first, halo, weight, heads):
    count = local.shape[0]
    rows = (count - near * chunk) // far
    return pl.pallas_call(
        functools.partial(halo_kernel, heads, count, near * chunk),
        in_specs=[smem()] + [whole()] * 4,
        out_specs=[whole()] * (1 + far),
        out_shape=[jax.ShapeDtypeStruct(local.shape, BF16)]
        + [jax.ShapeDtypeStruct((rows, weight.shape[1]), BF16)] * far,
        compiler_params=params(),
        name="halo_window",
    )(info, local, first, halo, weight)


def score_kernel(units_count, pieces, first, order_ref, *refs):
    units, refs = refs[:units_count], refs[units_count:]
    tables, (goal_ref, before_ref, out_ref, turned_ref) = refs[:pieces], refs[pieces:]
    step = pl.program_id(0)
    tile, width = tables[0].shape

    @pl.when(step == 0)
    def _():
        rows = jnp.concatenate([ref[...] for ref in units], axis=0)
        turned_ref[...] = jnp.transpose(rows)
        out_ref[...] = before_ref[...]

    logits = None
    for n in range(pieces):
        part = turned_ref[pl.ds(pl.multiple_of(order_ref[n] * width, width), width), :]
        more = dot(tables[n][...], part)
        logits = more if logits is None else logits + more
    count = logits.shape[1]
    logits = logits.reshape(tile // 8, 8, count)
    row = lax.broadcasted_iota(jnp.int32, (tile // 8, 8, count), 0) * 8
    row = row + lax.broadcasted_iota(jnp.int32, (tile // 8, 8, count), 1)
    goal = (goal_ref[...] - (step * tile + first)).reshape(1, 1, count)
    old = out_ref[0]
    peak = jnp.maximum(old, jnp.max(logits, axis=0))
    out_ref[0] = peak
    out_ref[1] = out_ref[1] * jnp.exp(old - peak) + jnp.sum(jnp.exp(logits - peak[None]), axis=0)
    out_ref[2] = out_ref[2] + jnp.sum(jnp.where(row == goal, logits, 0.0), axis=0)


def scores(order, units, tables, goal, before, first):
    count = goal.shape[1]
    tile = 640
    rows, width = tables[-1].shape
    skips = [first // tile if table.shape[0] != rows else 0 for table in tables]
    return pl.pallas_call(
        functools.partial(score_kernel, len(units), len(tables), first),
        in_specs=[smem()]
        + [pl.BlockSpec(piece.shape, lambda i: (0, 0), pipeline_mode=pl.Buffered(1)) for piece in units]
        + [pl.BlockSpec((tile, width), lambda i, skip=skip: (i + skip, 0)) for skip in skips]
        + [
            pl.BlockSpec((1, count), lambda i: (0, 0)),
            pl.BlockSpec((3, 8, count), lambda i: (0, 0, 0)),
        ],
        out_specs=pl.BlockSpec((3, 8, count), lambda i: (0, 0, 0)),
        grid=(rows // tile,),
        out_shape=jax.ShapeDtypeStruct((3, 8, count), F32),
        scratch_shapes=[pltpu.VMEM((units[0].shape[1], count), BF16)],
        compiler_params=params(),
        name="scores",
    )(order, *units, *tables, goal, before)


def shards(
    token_ids,
    target_ids,
    doc_start,
    vocab_table,
    norm_gain_one,
    lin_qkv,
    lin_head_gain,
    lin_out,
    norm_gain_two,
    win_qkv,
    win_out,
    final_gain,
):
    head_count = lax.axis_size("head")
    seq_count = lax.axis_size("seq")
    head_index = lax.axis_index("head")
    seq_index = lax.axis_index("seq")
    tok_count = token_ids.shape[0]
    chunk = tok_count // head_count
    vocab_rows = vocab_table.shape[0]
    heads = lin_qkv.shape[1] // (2 * FEAT + HEAD_DIM)
    vocab_first = head_index * vocab_rows
    calls = chunk_order(head_count)
    slots = [k for call in calls for k in call]
    near = 3 if head_count == 4 else 1
    far = 2 if head_count == 4 else head_count - 1
    spots = {}
    for n, call in enumerate(calls):
        for at, k in enumerate(call):
            spots[k] = (n, at * chunk)
    held_at = (head_index + jnp.asarray(slots, jnp.int32)) % head_count
    places = held_at * chunk

    marks = jnp.concatenate([token_ids, jnp.broadcast_to(doc_start, (LANES,))])
    marks = jnp.stack(
        [marks] + [lax.ppermute(marks, "seq", xor_pairs(seq_count, k)) for k in range(1, seq_count)]
    )
    block = jnp.arange(seq_count, dtype=jnp.int32)
    order = seq_index ^ block
    starts = marks[:, tok_count]
    starts = jnp.sum(jnp.where(order[None, :] == block[:, None], starts[None, :], 0), axis=1)
    bound = doc_start.astype(jnp.int32)

    ids = (marks[:, :tok_count] - vocab_first).reshape(seq_count, head_count, chunk)

    def ids_of(k):
        return lax.dynamic_index_in_dim(ids, (head_index + k) % head_count, 1, False).reshape(-1)

    if head_count == 4:
        outer = lookup(ids_of(2), vocab_table, 2)
        inner = lambda: (
            lookup(ids_of(0), vocab_table, 1)
            + lookup(jnp.concatenate([ids_of(1), ids_of(3)]), vocab_table, 2)
        )
    else:
        outer = [lookup(ids_of(k), vocab_table, 1)[0] for k in range(1, head_count)]
        inner = lambda: lookup(ids_of(0), vocab_table, 1)
    found = collect(scatter_rows(outer, inner), seq_count)
    gathered = [found[0]] + [
        lax.ppermute(found[k], "seq", xor_pairs(seq_count, k)) for k in range(1, seq_count)
    ]
    embedded, units = begin(order, norm_gain_one, gathered)
    chunks = gather_rows(units)

    constants = selectors()
    sets, state = [], None
    for n, call in enumerate(calls):
        pieces = [piece for k in call for piece in chunks[k]]
        first = sum(len(c) for c in calls[:n])
        made = project(
            bound,
            places[first : first + len(call)],
            list(range(len(call))),
            chunk,
            tok_count,
            pieces,
            lin_qkv,
            constants,
            state,
            n == len(calls) - 1,
            heads,
        )
        sets.append(made[:3])
        state = made[3]
    fqs, fks, vs = zip(*sets)
    states, shares = [], []
    for back in range(1, seq_count):
        states.append(
            lax.ppermute(state, "seq", [(i, i + back) for i in range(seq_count - back)])
        )
        between = (block > seq_index - back) & (block < seq_index)
        broken = jnp.sum(jnp.where(between & (starts != tok_count), 1, 0))
        shares.append(((broken == 0) & (seq_index >= back)).astype(jnp.int32))
    position = list(range(head_count))
    num, den = within(bound, places, position, chunk, fqs, fks, vs, heads)
    mixed, *outer = across(
        bound,
        places,
        jnp.stack(shares),
        position,
        chunk,
        near,
        far,
        fqs,
        num,
        den,
        lin_head_gain.reshape(1, -1),
        lin_out,
        states,
        heads,
    )
    parts = scatter_rows(outer, lambda: near_chunks(mixed, lin_out, near, chunk))
    units, residual = finish(embedded, norm_gain_two, parts, False)

    if seq_count == 4:
        lots = [vocab_rows * 3 // 5, vocab_rows * 2 // 5]
        early, _ = lax.optimization_barrier((vocab_table[: lots[0]], states))
        early = lax.ppermute(early, "seq", xor_pairs(seq_count, 2))
        early_corner = lax.ppermute(early, "seq", xor_pairs(seq_count, 1))
        beside = lax.ppermute(vocab_table, "seq", xor_pairs(seq_count, 1))

    chunks = gather_rows(units)
    qkvs = []
    for call in calls:
        qkvs.append(matmul([piece for k in call for piece in chunks[k]], win_qkv, 3 * HEAD_DIM))
    tail = jnp.zeros((WINDOW, win_qkv.shape[1]), BF16)
    for slot, k in enumerate(slots):
        n, at = spots[k]
        tail = jnp.where(
            held_at[slot] == head_count - 1, qkvs[n][at + chunk - WINDOW : at + chunk], tail
        )
    halo = lax.ppermute(tail, "seq", [(i, i + 1) for i in range(seq_count - 1)])
    previous = jnp.sum(jnp.where(block == seq_index - 1, starts, 0))
    valid_from = jnp.where(
        seq_index == 0, tok_count, jnp.where(previous == tok_count, 0, previous)
    ).astype(jnp.int32)
    first_spot = jnp.sum(jnp.where(held_at == 0, jnp.arange(head_count) * chunk, 0)).astype(jnp.int32)
    local, first = local_window(bound, places, slots, spots, chunk, qkvs, heads)
    info = jnp.stack([bound[0], valid_from, first_spot])
    mixed, *outer = halo_window(info, near, chunk, far, local, first, halo, win_out, heads)
    parts = scatter_rows(outer, lambda: near_chunks(mixed, win_out, near, chunk))
    units = finish(residual, final_gain, parts, True)[0]

    if seq_count == 4:
        late, _ = lax.optimization_barrier((vocab_table[lots[0] :], halo))
        late = lax.ppermute(late, "seq", xor_pairs(seq_count, 2))
        late_corner = lax.ppermute(late, "seq", xor_pairs(seq_count, 1))
        lots = [
            (0, [vocab_table, beside, early, early_corner]),
            (lots[0], [vocab_table, beside, late, late_corner]),
        ]
    else:
        lots = [(0, [lax.all_gather(vocab_table, "seq", axis=1, tiled=True)])]
        order = jnp.zeros((1,), jnp.int32)
    chunks = gather_rows(units)
    goals = (target_ids - vocab_first).reshape(head_count, chunk)
    found = {}
    for group in [[0, 3], [1, 2]] if head_count == 4 else [[k] for k in range(head_count)]:
        goal = jnp.concatenate(
            [
                lax.dynamic_index_in_dim(goals, (head_index + k) % head_count, 0, False)
                for k in group
            ]
        ).reshape(1, -1)
        state = jnp.zeros((3, 8, goal.shape[1]), F32).at[0].set(NEGATIVE)
        for first, tables in lots:
            state = scores(
                order, [piece for k in group for piece in chunks[k]], tables, goal, state, first
            )
        peak = jnp.max(state[0], axis=0)
        total = jnp.sum(state[1] * jnp.exp(state[0] - peak), axis=0)
        triple = jnp.stack([peak, total, jnp.sum(state[2], axis=0)])
        for at, k in enumerate(group):
            found[k] = triple[:, at * chunk : (at + 1) * chunk]

    shares = jnp.stack([found[0]] + [turned(found[k], k) for k in range(1, head_count)])
    peak = jnp.max(shares[:, 0], axis=0)
    total = jnp.sum(shares[:, 1] * jnp.exp(shares[:, 0] - peak), axis=0)
    return jnp.sum(shares[:, 2], axis=0) - (peak + jnp.log(total))


def solution(mesh):
    return jax.shard_map(
        shards,
        mesh=mesh,
        in_specs=(
            P(("shadow", "seq")),
            P(("shadow", "seq")),
            P(("shadow", "seq")),
            P(("shadow", "head"), "seq"),
            P("shadow"),
            P("shadow", "head"),
            P(("shadow", "head")),
            P(("shadow", "head"), None),
            P("shadow"),
            P("shadow", "head"),
            P(("shadow", "head"), None),
            P("shadow"),
        ),
        out_specs=P(("shadow", "seq", "head")),
        check_vma=False,
    )
```

```python
import functools

import jax
import jax.numpy as jnp
import numpy as np
from jax import lax
from jax.experimental import pallas as pl
from jax.experimental.pallas import tpu as pltpu
from jax.sharding import PartitionSpec as P

FEAT = 16
WINDOW = 64
HEAD_DIM = 128
EPSILON = 1e-05
NEGATIVE = -1e30
LANES = 128
WIDE = 256
STATE_ROWS = 160
BUFFER_ROWS = 176
F32 = jnp.float32
BF16 = jnp.bfloat16
VMEM_BYTES = 56 * 1024 * 1024


def params(**kw):
    return pltpu.CompilerParams(vmem_limit_bytes=VMEM_BYTES, **kw)


def cost(us):
    return pl.CostEstimate(flops=int(us * 6e8), transcendentals=0, bytes_accessed=int(us * 3e6))


def whole():
    return pl.BlockSpec(memory_space=pltpu.VMEM)


def smem():
    return pl.BlockSpec(memory_space=pltpu.SMEM)


def dot(a, b, dims=((1,), (0,))):
    return lax.dot_general(a, b, (dims, ((), ())), preferred_element_type=F32)


def xor_pairs(size, k):
    return [(i, i ^ k) for i in range(size)]


def rms(values, gain):
    factor = lax.rsqrt(jnp.mean(values * values, axis=-1, keepdims=True) + EPSILON)
    return (values * factor * gain.astype(F32)).astype(BF16)


def turned(value, step):
    size = lax.axis_size("head")
    return lax.ppermute(value, "head", [(i, (i + step) % size) for i in range(size)])


def gather_rows(own):
    size = lax.axis_size("head")
    if size != 4:
        full = lax.all_gather(own, "head")
        here = lax.axis_index("head")
        return [[own]] + [
            [lax.dynamic_index_in_dim(full, (here + k) % size, 0, False)] for k in range(1, size)
        ]
    half = own.shape[0] // 2
    before, after = turned(own, 1), turned(own, -1)
    return [[own], [after], [turned(before[:half], 1), turned(after[half:], -1)], [before]]


def scatter_rows(far, near):
    size = lax.axis_size("head")
    if size != 4:
        here = lax.axis_index("head")
        full = jnp.stack([near()[0]] + list(far))
        full = jnp.stack(
            [lax.dynamic_index_in_dim(full, (d - here) % size, 0, False) for d in range(size)]
        )
        return [[lax.psum_scatter(full, "head", scatter_dimension=0, tiled=True)[0]]]
    from_before, from_after = turned(far[0], 1), turned(far[1], -1)
    own_upper, own_lower, next_upper, next_lower, prev_upper, prev_lower = near()
    lower_right, upper_left = turned(next_lower, 1), turned(prev_upper, -1)
    upper_right = turned(plus(next_upper, from_before), 1)
    lower_left = turned(plus(prev_lower, from_after), -1)
    return [[own_upper, upper_right, upper_left], [own_lower, lower_right, lower_left]]


def plus(one, two):
    return (one.astype(F32) + two.astype(F32)).astype(BF16)


def chunk_order(size):
    if size == 4:
        return [[0], [1, 3], [2]]
    return [[k] for k in range(size)]


def lookup_kernel(ids_ref, table_ref, *refs):
    outs, total = refs[:-1], refs[-1]
    step = pl.program_id(0)
    tile = table_ref.shape[0]
    count = ids_ref.shape[1]
    ids = jnp.transpose(jnp.broadcast_to(ids_ref[...], (8, count)))[:, 0:1] - step * tile
    hot = (lax.broadcasted_iota(jnp.int32, (count, tile), 1) == ids).astype(F32).astype(BF16)
    found = dot(hot, table_ref[...])

    @pl.when(step == 0)
    def _():
        total[...] = found

    @pl.when(step > 0)
    def _():
        total[...] += found

    @pl.when(step == pl.num_programs(0) - 1)
    def _():
        rows = outs[0].shape[0]
        for n, out in enumerate(outs):
            out[...] = total[n * rows : (n + 1) * rows].astype(BF16)


def lookup(ids, table, pieces):
    count = ids.shape[0]
    rows, width = table.shape
    tile = rows // 5
    return pl.pallas_call(
        lookup_kernel,
        grid=(rows // tile,),
        in_specs=[
            pl.BlockSpec((1, count), lambda i: (0, 0)),
            pl.BlockSpec((tile, width), lambda i: (i, 0)),
        ],
        out_specs=[pl.BlockSpec((count // pieces, width), lambda i: (0, 0))] * pieces,
        out_shape=[jax.ShapeDtypeStruct((count // pieces, width), BF16)] * pieces,
        scratch_shapes=[pltpu.VMEM((count, width), F32)],
        compiler_params=params(),
        cost_estimate=cost(8 * count / 512),
        name="lookup",
    )(ids.reshape(1, count), table)


def gathered_sum(refs, sizes):
    rows, at = [], 0
    for size in sizes:
        total = refs[at][...].astype(F32)
        for ref in refs[at + 1 : at + size]:
            total = total + ref[...].astype(F32)
        rows.append(total)
        at += size
    return rows[0] if len(rows) == 1 else jnp.concatenate(rows, axis=0)


def collect_kernel(sizes, *refs):
    ins, outs = refs[: sum(sizes)], refs[sum(sizes) :]
    rows = outs[0].shape[0]
    total = gathered_sum(ins, sizes)
    for n, out in enumerate(outs):
        out[...] = total[n * rows : (n + 1) * rows].astype(BF16)


def collect(terms, pieces):
    sizes = [len(part) for part in terms]
    parts = [term for part in terms for term in part]
    rows, width = sum(part[0].shape[0] for part in terms), parts[0].shape[1]
    return pl.pallas_call(
        functools.partial(collect_kernel, sizes),
        in_specs=[whole()] * len(parts),
        out_specs=[whole()] * pieces,
        out_shape=[jax.ShapeDtypeStruct((rows // pieces, width), BF16)] * pieces,
        compiler_params=params(),
        cost_estimate=cost(2),
        name="collect",
    )(*parts)


def begin_kernel(pieces, order_ref, gain_ref, *refs):
    ins, (embedded_ref, units_ref, held) = refs[:pieces], refs[pieces:]
    width = ins[0].shape[1]
    for n in range(pieces):
        held[order_ref[n]] = ins[n][...]
    values = jnp.concatenate([held[n] for n in range(pieces)], axis=1)
    embedded_ref[...] = values
    units_ref[...] = rms(values.astype(F32), gain_ref[...])


def begin(order, gain, pieces):
    rows, width = pieces[0].shape
    full = jax.ShapeDtypeStruct((rows, width * len(pieces)), BF16)
    return pl.pallas_call(
        functools.partial(begin_kernel, len(pieces)),
        in_specs=[smem()] + [whole()] * (1 + len(pieces)),
        out_specs=[whole()] * 2,
        out_shape=[full, full],
        scratch_shapes=[pltpu.VMEM((len(pieces), rows, width), BF16)],
        compiler_params=params(),
        cost_estimate=cost(2),
        name="begin",
    )(order, gain.reshape(1, -1), *pieces)


def finish_kernel(sizes, last, residual_ref, gain_ref, *refs):
    parts = sum(sizes)
    total = gathered_sum(refs[:parts], sizes) + residual_ref[...].astype(F32)
    if not last:
        total = total.astype(BF16)
        refs[parts + 1][...] = total
    refs[parts][...] = rms(total.astype(F32), gain_ref[...])


def finish(residual, gain, terms, last):
    full = jax.ShapeDtypeStruct(residual.shape, BF16)
    parts = [term for part in terms for term in part]
    return pl.pallas_call(
        functools.partial(finish_kernel, [len(part) for part in terms], last),
        in_specs=[whole()] * (2 + len(parts)),
        out_specs=[whole()] * (1 if last else 2),
        out_shape=[full] * (1 if last else 2),
        compiler_params=params(),
        cost_estimate=cost(2.5),
        name="finish",
    )(residual, gain.reshape(1, -1), *parts)


def selectors():
    pairs = [(r, s) for r in range(FEAT) for s in range(r, FEAT)]
    picks = np.zeros((2, 2, LANES, WIDE), np.float32)
    extra = np.zeros((3, WIDE), np.float32)
    extra[0:2, 0] = 1.0
    extra[1, 1 : 1 + FEAT] = 1.0
    extra[2] = 1.0
    for kind in range(2):
        first = kind * FEAT
        for r in range(FEAT):
            picks[kind, 0, first + r, 1 + r] = FEAT ** (-0.25)
        for n, (r, s) in enumerate(pairs):
            picks[kind, 0, first + r, 1 + FEAT + n] = FEAT ** (-0.25)
            picks[kind, 1, first + s, 1 + FEAT + n] = FEAT ** (-0.25)
    for n, (r, s) in enumerate(pairs):
        extra[2, 1 + FEAT + n] = 0.5**0.5 if r == s else 1.0
    return jnp.asarray(np.concatenate([picks, picks], axis=2), BF16), jnp.asarray(extra)


def place_column(places_ref, slots, rows):
    inner = lax.broadcasted_iota(jnp.int32, (rows, 1), 0)
    return jnp.concatenate([inner + places_ref[slot] for slot in slots], axis=0)


def place_row(places_ref, slots, rows):
    inner = lax.broadcasted_iota(jnp.int32, (1, rows), 1)
    return jnp.concatenate([inner + places_ref[slot] for slot in slots], axis=1)


def project_kernel(heads, slots, chunk, count, pieces, more, last, bound_ref, places_ref, *refs):
    units = jnp.concatenate([ref[...] for ref in refs[:pieces]], axis=0)
    weight_ref, pick_ref, extra_ref = refs[pieces : pieces + 3]
    fq_ref, fk_ref, v_ref, state_ref = refs[-4:]
    projected = dot(units, weight_ref[...])
    rows, width = projected.shape
    needed = (heads - 1) * LANES + WIDE
    if needed > width:
        projected = jnp.pad(projected, ((0, 0), (0, needed - width)))
    bound = bound_ref[0]
    place = place_column(places_ref, slots, chunk)
    kept = ((place >= bound) | (bound == count)).astype(F32)
    ones = jnp.ones((8, rows), BF16)
    shift = 2 * FEAT
    for head in range(heads):
        part = projected[:, head * LANES : head * LANES + WIDE]
        narrow = part if head == 0 else pltpu.roll(part, WIDE - shift * head, 1)
        narrow = narrow[:, :LANES]
        values = pltpu.roll(part, WIDE - shift * (head + 1), 1)[:, :HEAD_DIM].astype(BF16)
        v_ref[:, head * HEAD_DIM : (head + 1) * HEAD_DIM] = values
        upper = narrow.astype(BF16)
        lower = (narrow - upper.astype(F32)).astype(BF16)
        both = jnp.concatenate([upper, lower], axis=1)
        feats = []
        for kind in range(2):
            one = dot(both, pick_ref[kind, 0]) + extra_ref[0:1]
            two = dot(both, pick_ref[kind, 1]) + extra_ref[1:2]
            feats.append((one * two * extra_ref[2:3]).astype(BF16))
        fq_ref[head] = feats[0]
        fk_ref[head] = feats[1]
        keys = (feats[1].astype(F32) * kept).astype(BF16)
        state = dot(keys, values, ((0,), (0,)))
        total = dot(ones, keys)
        tail = jnp.concatenate([total[0:1, :LANES], total[0:1, LANES:], jnp.zeros((14, LANES), F32)], axis=0)
        state = jnp.concatenate([state[0:STATE_ROWS], tail], axis=0)
        if more:
            state = state + refs[pieces + 3][head]
        state_ref[head] = state.astype(BF16) if last else state


def project(bound, places, slots, chunk, count, pieces, weight, constants, earlier, last, heads):
    rows = sum(piece.shape[0] for piece in pieces)
    extra = [] if earlier is None else [earlier]
    return pl.pallas_call(
        functools.partial(project_kernel, heads, slots, chunk, count, len(pieces), bool(extra), last),
        in_specs=[smem(), smem()] + [whole()] * (len(pieces) + 3 + len(extra)),
        out_specs=[whole()] * 4,
        out_shape=[
            jax.ShapeDtypeStruct((heads, rows, WIDE), BF16),
            jax.ShapeDtypeStruct((heads, rows, WIDE), BF16),
            jax.ShapeDtypeStruct((rows, heads * HEAD_DIM), BF16),
            jax.ShapeDtypeStruct((heads, BUFFER_ROWS, HEAD_DIM), BF16 if last else F32),
        ],
        compiler_params=params(),
        cost_estimate=cost(5),
        name="project",
    )(bound, places, *pieces, weight, *constants, *extra)


def within_kernel(heads, slots, chunk, sets, bound_ref, places_ref, *refs):
    fqs, fks, vs = refs[:sets], refs[sets : 2 * sets], refs[2 * sets : 3 * sets]
    num_ref, den_ref = refs[3 * sets :]
    bound = bound_ref[0]
    row = place_column(places_ref, slots, chunk)
    col = place_row(places_ref, slots, chunk)
    allowed = (row >= col) & ((row >= bound) == (col >= bound))
    for head in range(heads):
        query = jnp.concatenate([ref[head] for ref in fqs], axis=0)
        keys = jnp.concatenate([ref[head] for ref in fks], axis=0)
        values = jnp.concatenate(
            [ref[:, head * HEAD_DIM : (head + 1) * HEAD_DIM] for ref in vs], axis=0
        )
        weights = dot(query, keys, ((1,), (1,)))
        weights = jnp.where(allowed, weights, 0.0)
        den_ref[head] = jnp.broadcast_to(
            jnp.sum(weights, axis=-1, keepdims=True), (row.shape[0], 8)
        )
        num_ref[head] = dot(weights.astype(BF16), values)


def within(bound, places, slots, chunk, fqs, fks, vs, heads):
    count = len(slots) * chunk
    return pl.pallas_call(
        functools.partial(within_kernel, heads, slots, chunk, len(fqs)),
        in_specs=[smem(), smem()] + [whole()] * (3 * len(fqs)),
        out_specs=[whole()] * 2,
        out_shape=[
            jax.ShapeDtypeStruct((heads, count, HEAD_DIM), F32),
            jax.ShapeDtypeStruct((heads, count, 8), F32),
        ],
        compiler_params=params(),
        cost_estimate=cost(4.5),
        name="within",
    )(bound, places, *fqs, *fks, *vs)


def split_store(total, refs):
    rows = refs[0].shape[0]
    for n, ref in enumerate(refs):
        ref[...] = total[n * rows : (n + 1) * rows].astype(BF16)


def across_kernel(heads, slots, chunk, sets, earlier, near, bound_ref, places_ref, share_ref, *refs):
    fqs, refs = refs[:sets], refs[sets:]
    num_ref, den_ref, gain_ref, weight_ref = refs[:4]
    states, refs = refs[4 : 4 + earlier], refs[4 + earlier :]
    mixed_ref, fars = refs[0], refs[1:]
    bound = bound_ref[0]
    before = (place_column(places_ref, slots, chunk) < bound).astype(F32)
    for head in range(heads):
        carried = jnp.zeros((BUFFER_ROWS, HEAD_DIM), F32)
        for n in range(earlier):
            carried = carried + jnp.where(share_ref[n] > 0, states[n][head].astype(F32), 0.0)
        state = jnp.concatenate(
            [carried[0:STATE_ROWS], jnp.zeros((WIDE - STATE_ROWS, HEAD_DIM), F32)], axis=0
        ).astype(BF16)
        total = jnp.concatenate(
            [carried[STATE_ROWS : STATE_ROWS + 1], carried[STATE_ROWS + 1 : STATE_ROWS + 2]], axis=1
        )
        query = jnp.concatenate([ref[head] for ref in fqs], axis=0)
        numerator = num_ref[head] + before * dot(query, state)
        more = jnp.sum(query.astype(F32) * total, axis=-1, keepdims=True)
        denominator = den_ref[head][:, 0:1] + before * more
        lanes = slice(head * HEAD_DIM, (head + 1) * HEAD_DIM)
        mixed_ref[:, lanes] = (numerator / denominator * gain_ref[:, lanes].astype(F32)).astype(BF16)
    split_store(dot(mixed_ref[near * chunk :], weight_ref[...]), fars)


def across(bound, places, share, slots, chunk, near, far, fqs, num, den, gain, weight, states, heads):
    count = len(slots) * chunk
    rows = (count - near * chunk) // far
    return pl.pallas_call(
        functools.partial(across_kernel, heads, slots, chunk, len(fqs), len(states), near),
        in_specs=[smem()] * 3 + [whole()] * (len(fqs) + 4 + len(states)),
        out_specs=[whole()] * (1 + far),
        out_shape=[jax.ShapeDtypeStruct((count, heads * HEAD_DIM), BF16)]
        + [jax.ShapeDtypeStruct((rows, weight.shape[1]), BF16)] * far,
        compiler_params=params(),
        cost_estimate=cost(4.5),
        name="across",
    )(bound, places, share, *fqs, num, den, gain, weight, *states)


def near_kernel(rows, mixed_ref, weight_ref, *outs):
    split_store(dot(mixed_ref[0:rows], weight_ref[...]), outs)


def near_chunks(mixed, weight, near, chunk):
    pieces = 2 * near if near > 1 else 1
    rows = near * chunk
    return pl.pallas_call(
        functools.partial(near_kernel, rows),
        in_specs=[whole()] * 2,
        out_specs=[whole()] * pieces,
        out_shape=[jax.ShapeDtypeStruct((rows // pieces, weight.shape[1]), BF16)] * pieces,
        compiler_params=params(),
        cost_estimate=cost(4),
        name="near",
    )(mixed, weight)


def matmul_kernel(*refs):
    a = jnp.concatenate([ref[...] for ref in refs[:-2]], axis=0)
    refs[-1][...] = dot(a, refs[-2][...]).astype(BF16)


def matmul(pieces, b, tile):
    rows = sum(piece.shape[0] for piece in pieces)
    inner = b.shape[0]
    return pl.pallas_call(
        matmul_kernel,
        grid=(b.shape[1] // tile,),
        in_specs=[
            pl.BlockSpec(piece.shape, lambda n: (0, 0), pipeline_mode=pl.Buffered(1)) for piece in pieces
        ]
        + [pl.BlockSpec((inner, tile), lambda n: (0, n))],
        out_specs=pl.BlockSpec((rows, tile), lambda n: (0, n)),
        out_shape=jax.ShapeDtypeStruct((rows, b.shape[1]), BF16),
        compiler_params=params(),
        cost_estimate=cost(5),
        name="matmul",
    )(*pieces, b)


def attend(query, keys, values, allowed):
    scores = dot(query, keys, ((1,), (1,))) * HEAD_DIM ** (-0.5)
    scores = jnp.where(allowed, scores, NEGATIVE)
    peak = jnp.max(scores, axis=-1, keepdims=True)
    weights = jnp.where(allowed, jnp.exp(scores - peak), 0.0)
    probabilities = (weights / jnp.sum(weights, axis=-1, keepdims=True)).astype(BF16)
    return dot(probabilities, values).astype(BF16)


def local_kernel(heads, slots, spots, chunk, sets, bound_ref, places_ref, *refs):
    qkvs, (result_ref, first_ref) = refs[:sets], refs[sets:]
    size = len(slots)
    reach = chunk + WINDOW
    bound = bound_ref[0]
    row = lax.broadcasted_iota(jnp.int32, (chunk, reach), 0)
    col = lax.broadcasted_iota(jnp.int32, (chunk, reach), 1)
    band = (col > row) & (col <= row + WINDOW)
    for slot in range(size):
        k = slots[slot]
        mine, at = spots[k]
        theirs, there = spots[(k - 1) % size]
        base = places_ref[slot]
        query_place = row + base
        key_place = col + (base - WINDOW)
        allowed = band & (key_place >= 0) & ((query_place >= bound) == (key_place >= bound))
        rows = slice(at, at + chunk)
        tail = slice(there + chunk - WINDOW, there + chunk)

        @pl.when(base == 0)
        def _():
            first_ref[...] = qkvs[mine][at : at + WINDOW]

        for head in range(heads):
            lane = head * 3 * HEAD_DIM
            keys, values = [
                jnp.concatenate(
                    [
                        qkvs[theirs][tail, lane + n * HEAD_DIM : lane + (n + 1) * HEAD_DIM],
                        qkvs[mine][rows, lane + n * HEAD_DIM : lane + (n + 1) * HEAD_DIM],
                    ],
                    axis=0,
                )
                for n in (1, 2)
            ]
            result_ref[slot * chunk : (slot + 1) * chunk, head * HEAD_DIM : (head + 1) * HEAD_DIM] = attend(
                qkvs[mine][rows, lane : lane + HEAD_DIM], keys, values, allowed
            )


def local_window(bound, places, slots, spots, chunk, qkvs, heads):
    return pl.pallas_call(
        functools.partial(local_kernel, heads, slots, spots, chunk, len(qkvs)),
        in_specs=[smem(), smem()] + [whole()] * len(qkvs),
        out_specs=[whole()] * 2,
        out_shape=[
            jax.ShapeDtypeStruct((len(slots) * chunk, heads * HEAD_DIM), BF16),
            jax.ShapeDtypeStruct((WINDOW, qkvs[0].shape[1]), BF16),
        ],
        compiler_params=params(),
        cost_estimate=cost(8),
        name="local_window",
    )(bound, places, *qkvs)


def halo_kernel(heads, count, start, info_ref, local_ref, first_ref, halo_ref, weight_ref, result_ref, *fars):
    result_ref[...] = local_ref[...]
    bound, valid_from, spot = info_ref[0], info_ref[1], info_ref[2]
    row = lax.broadcasted_iota(jnp.int32, (WINDOW, 2 * WINDOW), 0)
    col = lax.broadcasted_iota(jnp.int32, (WINDOW, 2 * WINDOW), 1)
    key_place = col - WINDOW
    allowed = (col > row) & (col <= row + WINDOW) & ((row >= bound) == (key_place >= bound))
    allowed = allowed & ((key_place >= 0) | (key_place + count >= valid_from))
    spot = pl.multiple_of(spot, WINDOW)
    for head in range(heads):
        lane = head * 3 * HEAD_DIM
        keys, values = [
            jnp.concatenate(
                [ref[:, lane + n * HEAD_DIM : lane + (n + 1) * HEAD_DIM] for ref in (halo_ref, first_ref)], axis=0
            )
            for n in (1, 2)
        ]
        result_ref[pl.ds(spot, WINDOW), head * HEAD_DIM : (head + 1) * HEAD_DIM] = attend(
            first_ref[:, lane : lane + HEAD_DIM], keys, values, allowed
        )
    split_store(dot(result_ref[start:], weight_ref[...]), fars)


def halo_window(info, near, chunk, far, local, first, halo, weight, heads):
    count = local.shape[0]
    rows = (count - near * chunk) // far
    return pl.pallas_call(
        functools.partial(halo_kernel, heads, count, near * chunk),
        in_specs=[smem()] + [whole()] * 4,
        out_specs=[whole()] * (1 + far),
        out_shape=[jax.ShapeDtypeStruct(local.shape, BF16)]
        + [jax.ShapeDtypeStruct((rows, weight.shape[1]), BF16)] * far,
        compiler_params=params(),
        cost_estimate=cost(4.5),
        name="halo_window",
    )(info, local, first, halo, weight)


def score_kernel(units_count, pieces, first, order_ref, *refs):
    units, refs = refs[:units_count], refs[units_count:]
    tables, (goal_ref, before_ref, out_ref, turned_ref) = refs[:pieces], refs[pieces:]
    step = pl.program_id(0)
    tile, width = tables[0].shape

    @pl.when(step == 0)
    def _():
        rows = jnp.concatenate([ref[...] for ref in units], axis=0)
        turned_ref[...] = jnp.transpose(rows)
        out_ref[...] = before_ref[...]

    logits = None
    for n in range(pieces):
        part = turned_ref[pl.ds(pl.multiple_of(order_ref[n] * width, width), width), :]
        more = dot(tables[n][...], part)
        logits = more if logits is None else logits + more
    count = logits.shape[1]
    logits = logits.reshape(tile // 8, 8, count)
    row = lax.broadcasted_iota(jnp.int32, (tile // 8, 8, count), 0) * 8
    row = row + lax.broadcasted_iota(jnp.int32, (tile // 8, 8, count), 1)
    goal = (goal_ref[...] - (step * tile + first)).reshape(1, 1, count)
    old = out_ref[0]
    peak = jnp.maximum(old, jnp.max(logits, axis=0))
    out_ref[0] = peak
    out_ref[1] = out_ref[1] * jnp.exp(old - peak) + jnp.sum(jnp.exp(logits - peak[None]), axis=0)
    out_ref[2] = out_ref[2] + jnp.sum(jnp.where(row == goal, logits, 0.0), axis=0)


def scores(order, units, tables, goal, before, first):
    count = goal.shape[1]
    tile = 640
    rows, width = tables[-1].shape
    skips = [first // tile if table.shape[0] != rows else 0 for table in tables]
    return pl.pallas_call(
        functools.partial(score_kernel, len(units), len(tables), first),
        in_specs=[smem()]
        + [pl.BlockSpec(piece.shape, lambda i: (0, 0), pipeline_mode=pl.Buffered(1)) for piece in units]
        + [pl.BlockSpec((tile, width), lambda i, skip=skip: (i + skip, 0)) for skip in skips]
        + [
            pl.BlockSpec((1, count), lambda i: (0, 0)),
            pl.BlockSpec((3, 8, count), lambda i: (0, 0, 0)),
        ],
        out_specs=pl.BlockSpec((3, 8, count), lambda i: (0, 0, 0)),
        grid=(rows // tile,),
        out_shape=jax.ShapeDtypeStruct((3, 8, count), F32),
        scratch_shapes=[pltpu.VMEM((units[0].shape[1], count), BF16)],
        compiler_params=params(),
        cost_estimate=cost(9),
        name="scores",
    )(order, *units, *tables, goal, before)


def shards(
    token_ids,
    target_ids,
    doc_start,
    vocab_table,
    norm_gain_one,
    lin_qkv,
    lin_head_gain,
    lin_out,
    norm_gain_two,
    win_qkv,
    win_out,
    final_gain,
):
    head_count = lax.axis_size("head")
    seq_count = lax.axis_size("seq")
    head_index = lax.axis_index("head")
    seq_index = lax.axis_index("seq")
    tok_count = token_ids.shape[0]
    chunk = tok_count // head_count
    vocab_rows = vocab_table.shape[0]
    heads = lin_qkv.shape[1] // (2 * FEAT + HEAD_DIM)
    vocab_first = head_index * vocab_rows
    calls = chunk_order(head_count)
    slots = [k for call in calls for k in call]
    near = 3 if head_count == 4 else 1
    far = 2 if head_count == 4 else head_count - 1
    spots = {}
    for n, call in enumerate(calls):
        for at, k in enumerate(call):
            spots[k] = (n, at * chunk)
    held_at = (head_index + jnp.asarray(slots, jnp.int32)) % head_count
    places = held_at * chunk

    marks = jnp.concatenate([token_ids, jnp.broadcast_to(doc_start, (LANES,))])
    marks = jnp.stack(
        [marks] + [lax.ppermute(marks, "seq", xor_pairs(seq_count, k)) for k in range(1, seq_count)]
    )
    block = jnp.arange(seq_count, dtype=jnp.int32)
    order = seq_index ^ block
    starts = marks[:, tok_count]
    starts = jnp.sum(jnp.where(order[None, :] == block[:, None], starts[None, :], 0), axis=1)
    bound = doc_start.astype(jnp.int32)

    lots = [vocab_rows * 3 // 5, vocab_rows * 2 // 5]
    early, late = vocab_table[: lots[0]], vocab_table[lots[0] :]

    ids = (marks[:, :tok_count] - vocab_first).reshape(seq_count, head_count, chunk)

    def ids_of(k):
        return lax.dynamic_index_in_dim(ids, (head_index + k) % head_count, 1, False).reshape(-1)

    if head_count == 4:
        outer = lookup(ids_of(2), vocab_table, 2)
        inner = lambda: (
            lookup(ids_of(0), vocab_table, 2)
            + lookup(jnp.concatenate([ids_of(1), ids_of(3)]), vocab_table, 4)
        )
    else:
        outer = [lookup(ids_of(k), vocab_table, 1)[0] for k in range(1, head_count)]
        inner = lambda: lookup(ids_of(0), vocab_table, 1)
    found = collect(scatter_rows(outer, inner), seq_count)
    gathered = [found[0]] + [
        lax.ppermute(found[k], "seq", xor_pairs(seq_count, k)) for k in range(1, seq_count)
    ]
    embedded, units = begin(order, norm_gain_one, gathered)
    chunks = gather_rows(units)

    constants = selectors()
    sets, state = [], None
    for n, call in enumerate(calls):
        pieces = [piece for k in call for piece in chunks[k]]
        first = sum(len(c) for c in calls[:n])
        made = project(
            bound,
            places[first : first + len(call)],
            list(range(len(call))),
            chunk,
            tok_count,
            pieces,
            lin_qkv,
            constants,
            state,
            n == len(calls) - 1,
            heads,
        )
        sets.append(made[:3])
        state = made[3]
    fqs, fks, vs = zip(*sets)
    states, shares = [], []
    for back in range(1, seq_count):
        states.append(
            lax.ppermute(state, "seq", [(i, i + back) for i in range(seq_count - back)])
        )
        between = (block > seq_index - back) & (block < seq_index)
        broken = jnp.sum(jnp.where(between & (starts != tok_count), 1, 0))
        shares.append(((broken == 0) & (seq_index >= back)).astype(jnp.int32))
    position = list(range(head_count))
    num, den = within(bound, places, position, chunk, fqs, fks, vs, heads)
    mixed, *outer = across(
        bound,
        places,
        jnp.stack(shares),
        position,
        chunk,
        near,
        far,
        fqs,
        num,
        den,
        lin_head_gain.reshape(1, -1),
        lin_out,
        states,
        heads,
    )
    parts = scatter_rows(outer, lambda: near_chunks(mixed, lin_out, near, chunk))
    units, residual = finish(embedded, norm_gain_two, parts, False)

    if seq_count == 4:
        early, _ = lax.optimization_barrier((early, states))
        early = lax.ppermute(early, "seq", xor_pairs(seq_count, 2))
        early_corner = lax.ppermute(early, "seq", xor_pairs(seq_count, 1))
        beside = lax.ppermute(vocab_table, "seq", xor_pairs(seq_count, 1))

    chunks = gather_rows(units)
    qkvs = []
    for call in calls:
        qkvs.append(matmul([piece for k in call for piece in chunks[k]], win_qkv, 3 * HEAD_DIM))
    tail = jnp.zeros((WINDOW, win_qkv.shape[1]), BF16)
    for slot, k in enumerate(slots):
        n, at = spots[k]
        tail = jnp.where(
            held_at[slot] == head_count - 1, qkvs[n][at + chunk - WINDOW : at + chunk], tail
        )
    late, tail = lax.optimization_barrier((late, tail))
    halo = lax.ppermute(tail, "seq", [(i, i + 1) for i in range(seq_count - 1)])
    previous = jnp.sum(jnp.where(block == seq_index - 1, starts, 0))
    valid_from = jnp.where(
        seq_index == 0, tok_count, jnp.where(previous == tok_count, 0, previous)
    ).astype(jnp.int32)
    first_spot = jnp.sum(jnp.where(held_at == 0, jnp.arange(head_count) * chunk, 0)).astype(jnp.int32)
    local, first = local_window(bound, places, slots, spots, chunk, qkvs, heads)
    info = jnp.stack([bound[0], valid_from, first_spot])
    mixed, *outer = halo_window(info, near, chunk, far, local, first, halo, win_out, heads)
    parts = scatter_rows(outer, lambda: near_chunks(mixed, win_out, near, chunk))
    units = finish(residual, final_gain, parts, True)[0]

    chunks = gather_rows(units)
    if seq_count == 4:
        late = lax.ppermute(late, "seq", xor_pairs(seq_count, 2))
        corner, _ = lax.optimization_barrier((late, (chunks[1][0], chunks[-1][0])))
        late_corner = lax.ppermute(corner, "seq", xor_pairs(seq_count, 1))
        lots = [
            (0, [vocab_table, beside, early, early_corner]),
            (lots[0], [vocab_table, beside, late, late_corner]),
        ]
    else:
        lots = [(0, [lax.all_gather(vocab_table, "seq", axis=1, tiled=True)])]
        order = jnp.zeros((1,), jnp.int32)
    goals = (target_ids - vocab_first).reshape(head_count, chunk)
    found = {}
    for group in [[0, 3], [1, 2]] if head_count == 4 else [[k] for k in range(head_count)]:
        goal = jnp.concatenate(
            [
                lax.dynamic_index_in_dim(goals, (head_index + k) % head_count, 0, False)
                for k in group
            ]
        ).reshape(1, -1)
        state = jnp.zeros((3, 8, goal.shape[1]), F32).at[0].set(NEGATIVE)
        for first, tables in lots:
            state = scores(
                order, [piece for k in group for piece in chunks[k]], tables, goal, state, first
            )
        peak = jnp.max(state[0], axis=0)
        total = jnp.sum(state[1] * jnp.exp(state[0] - peak), axis=0)
        triple = jnp.stack([peak, total, jnp.sum(state[2], axis=0)])
        for at, k in enumerate(group):
            found[k] = triple[:, at * chunk : (at + 1) * chunk]

    shares = jnp.stack([found[0]] + [turned(found[k], k) for k in range(1, head_count)])
    peak = jnp.max(shares[:, 0], axis=0)
    total = jnp.sum(shares[:, 1] * jnp.exp(shares[:, 0] - peak), axis=0)
    return jnp.sum(shares[:, 2], axis=0) - (peak + jnp.log(total))


def solution(mesh):
    return jax.shard_map(
        shards,
        mesh=mesh,
        in_specs=(
            P(("shadow", "seq")),
            P(("shadow", "seq")),
            P(("shadow", "seq")),
            P(("shadow", "head"), "seq"),
            P("shadow"),
            P("shadow", "head"),
            P(("shadow", "head")),
            P(("shadow", "head"), None),
            P("shadow"),
            P("shadow", "head"),
            P(("shadow", "head"), None),
            P("shadow"),
        ),
        out_specs=P(("shadow", "seq", "head")),
        check_vma=False,
    )
```

```python
import functools

import jax
import jax.numpy as jnp
import numpy as np
from jax import lax
from jax.experimental import pallas as pl
from jax.experimental.pallas import tpu as pltpu
from jax.sharding import PartitionSpec as P

FEAT = 16
WINDOW = 64
HEAD_DIM = 128
EPSILON = 1e-05
NEGATIVE = -1e30
LANES = 128
WIDE = 256
STATE_ROWS = 160
BUFFER_ROWS = 176
F32 = jnp.float32
BF16 = jnp.bfloat16
VMEM_BYTES = 56 * 1024 * 1024


def params(**kw):
    return pltpu.CompilerParams(vmem_limit_bytes=VMEM_BYTES, **kw)


def cost(us):
    return pl.CostEstimate(flops=int(us * 6e8), transcendentals=0, bytes_accessed=int(us * 3e6))


def whole():
    return pl.BlockSpec(memory_space=pltpu.VMEM)


def smem():
    return pl.BlockSpec(memory_space=pltpu.SMEM)


def dot(a, b, dims=((1,), (0,))):
    return lax.dot_general(a, b, (dims, ((), ())), preferred_element_type=F32)


def xor_pairs(size, k):
    return [(i, i ^ k) for i in range(size)]


def rms(values, gain):
    factor = lax.rsqrt(jnp.mean(values * values, axis=-1, keepdims=True) + EPSILON)
    return (values * factor * gain.astype(F32)).astype(BF16)


def turned(value, step):
    size = lax.axis_size("head")
    return lax.ppermute(value, "head", [(i, (i + step) % size) for i in range(size)])


def gather_rows(own):
    size = lax.axis_size("head")
    if size != 4:
        full = lax.all_gather(own, "head")
        here = lax.axis_index("head")
        return [[own]] + [
            [lax.dynamic_index_in_dim(full, (here + k) % size, 0, False)] for k in range(1, size)
        ]
    half = own.shape[0] // 2
    before, after = turned(own, 1), turned(own, -1)
    return [[own], [after], [turned(before[:half], 1), turned(after[half:], -1)], [before]]


def scatter_rows(far, near):
    size = lax.axis_size("head")
    if size != 4:
        here = lax.axis_index("head")
        full = jnp.stack([near()[0]] + list(far))
        full = jnp.stack(
            [lax.dynamic_index_in_dim(full, (d - here) % size, 0, False) for d in range(size)]
        )
        return [[lax.psum_scatter(full, "head", scatter_dimension=0, tiled=True)[0]]]
    from_before, from_after = turned(far[0], 1), turned(far[1], -1)
    own_upper, own_lower, next_upper, next_lower, prev_upper, prev_lower = near()
    lower_right, upper_left = turned(next_lower, 1), turned(prev_upper, -1)
    upper_right, lower_left = pass_on(next_upper, from_before, prev_lower, from_after)
    upper_right, lower_left = turned(upper_right, 1), turned(lower_left, -1)
    return [[own_upper, upper_right, upper_left], [own_lower, lower_right, lower_left]]


def pass_on_kernel(next_ref, before_ref, prev_ref, after_ref, right_ref, left_ref):
    right_ref[...] = (next_ref[...].astype(F32) + before_ref[...].astype(F32)).astype(BF16)
    left_ref[...] = (prev_ref[...].astype(F32) + after_ref[...].astype(F32)).astype(BF16)


def pass_on(next_upper, from_before, prev_lower, from_after):
    return pl.pallas_call(
        pass_on_kernel,
        in_specs=[whole()] * 4,
        out_specs=[whole()] * 2,
        out_shape=[jax.ShapeDtypeStruct(next_upper.shape, BF16)] * 2,
        compiler_params=params(),
        cost_estimate=cost(1.5),
        name="pass_on",
    )(next_upper, from_before, prev_lower, from_after)


def chunk_order(size):
    if size == 4:
        return [[0], [1, 3], [2]]
    return [[k] for k in range(size)]


def lookup_kernel(ids_ref, table_ref, *refs):
    outs, total = refs[:-1], refs[-1]
    step = pl.program_id(0)
    tile = table_ref.shape[0]
    count = ids_ref.shape[1]
    ids = jnp.transpose(jnp.broadcast_to(ids_ref[...], (8, count)))[:, 0:1] - step * tile
    hot = (lax.broadcasted_iota(jnp.int32, (count, tile), 1) == ids).astype(F32).astype(BF16)
    found = dot(hot, table_ref[...])

    @pl.when(step == 0)
    def _():
        total[...] = found

    @pl.when(step > 0)
    def _():
        total[...] += found

    @pl.when(step == pl.num_programs(0) - 1)
    def _():
        rows = outs[0].shape[0]
        for n, out in enumerate(outs):
            out[...] = total[n * rows : (n + 1) * rows].astype(BF16)


def lookup(ids, table, pieces):
    count = ids.shape[0]
    rows, width = table.shape
    tile = rows // 5
    return pl.pallas_call(
        lookup_kernel,
        grid=(rows // tile,),
        in_specs=[
            pl.BlockSpec((1, count), lambda i: (0, 0)),
            pl.BlockSpec((tile, width), lambda i: (i, 0)),
        ],
        out_specs=[pl.BlockSpec((count // pieces, width), lambda i: (0, 0))] * pieces,
        out_shape=[jax.ShapeDtypeStruct((count // pieces, width), BF16)] * pieces,
        scratch_shapes=[pltpu.VMEM((count, width), F32)],
        compiler_params=params(),
        cost_estimate=cost(8 * count / 512),
        name="lookup",
    )(ids.reshape(1, count), table)


def gathered_sum(refs, sizes):
    rows, at = [], 0
    for size in sizes:
        total = refs[at][...].astype(F32)
        for ref in refs[at + 1 : at + size]:
            total = total + ref[...].astype(F32)
        rows.append(total)
        at += size
    return rows[0] if len(rows) == 1 else jnp.concatenate(rows, axis=0)


def collect_kernel(sizes, *refs):
    ins, outs = refs[: sum(sizes)], refs[sum(sizes) :]
    rows = outs[0].shape[0]
    total = gathered_sum(ins, sizes)
    for n, out in enumerate(outs):
        out[...] = total[n * rows : (n + 1) * rows].astype(BF16)


def collect(terms, pieces):
    sizes = [len(part) for part in terms]
    parts = [term for part in terms for term in part]
    rows, width = sum(part[0].shape[0] for part in terms), parts[0].shape[1]
    return pl.pallas_call(
        functools.partial(collect_kernel, sizes),
        in_specs=[whole()] * len(parts),
        out_specs=[whole()] * pieces,
        out_shape=[jax.ShapeDtypeStruct((rows // pieces, width), BF16)] * pieces,
        compiler_params=params(),
        cost_estimate=cost(2),
        name="collect",
    )(*parts)


def begin_kernel(pieces, order_ref, gain_ref, *refs):
    ins, (embedded_ref, units_ref, held) = refs[:pieces], refs[pieces:]
    width = ins[0].shape[1]
    for n in range(pieces):
        held[order_ref[n]] = ins[n][...]
    values = jnp.concatenate([held[n] for n in range(pieces)], axis=1)
    embedded_ref[...] = values
    units_ref[...] = rms(values.astype(F32), gain_ref[...])


def begin(order, gain, pieces):
    rows, width = pieces[0].shape
    full = jax.ShapeDtypeStruct((rows, width * len(pieces)), BF16)
    return pl.pallas_call(
        functools.partial(begin_kernel, len(pieces)),
        in_specs=[smem()] + [whole()] * (1 + len(pieces)),
        out_specs=[whole()] * 2,
        out_shape=[full, full],
        scratch_shapes=[pltpu.VMEM((len(pieces), rows, width), BF16)],
        compiler_params=params(),
        cost_estimate=cost(2),
        name="begin",
    )(order, gain.reshape(1, -1), *pieces)


def finish_kernel(sizes, last, residual_ref, gain_ref, *refs):
    parts = sum(sizes)
    total = gathered_sum(refs[:parts], sizes) + residual_ref[...].astype(F32)
    if not last:
        total = total.astype(BF16)
        refs[parts + 1][...] = total
    refs[parts][...] = rms(total.astype(F32), gain_ref[...])


def finish(residual, gain, terms, last):
    full = jax.ShapeDtypeStruct(residual.shape, BF16)
    parts = [term for part in terms for term in part]
    return pl.pallas_call(
        functools.partial(finish_kernel, [len(part) for part in terms], last),
        in_specs=[whole()] * (2 + len(parts)),
        out_specs=[whole()] * (1 if last else 2),
        out_shape=[full] * (1 if last else 2),
        compiler_params=params(),
        cost_estimate=cost(2.5),
        name="finish",
    )(residual, gain.reshape(1, -1), *parts)


def selectors():
    pairs = [(r, s) for r in range(FEAT) for s in range(r, FEAT)]
    picks = np.zeros((2, 2, LANES, WIDE), np.float32)
    extra = np.zeros((3, WIDE), np.float32)
    extra[0:2, 0] = 1.0
    extra[1, 1 : 1 + FEAT] = 1.0
    extra[2] = 1.0
    for kind in range(2):
        first = kind * FEAT
        for r in range(FEAT):
            picks[kind, 0, first + r, 1 + r] = FEAT ** (-0.25)
        for n, (r, s) in enumerate(pairs):
            picks[kind, 0, first + r, 1 + FEAT + n] = FEAT ** (-0.25)
            picks[kind, 1, first + s, 1 + FEAT + n] = FEAT ** (-0.25)
    for n, (r, s) in enumerate(pairs):
        extra[2, 1 + FEAT + n] = 0.5**0.5 if r == s else 1.0
    return jnp.asarray(np.concatenate([picks, picks], axis=2), BF16), jnp.asarray(extra)


def place_column(places_ref, slots, rows):
    inner = lax.broadcasted_iota(jnp.int32, (rows, 1), 0)
    return jnp.concatenate([inner + places_ref[slot] for slot in slots], axis=0)


def place_row(places_ref, slots, rows):
    inner = lax.broadcasted_iota(jnp.int32, (1, rows), 1)
    return jnp.concatenate([inner + places_ref[slot] for slot in slots], axis=1)


def project_kernel(heads, slots, chunk, count, pieces, more, last, bound_ref, places_ref, *refs):
    units = jnp.concatenate([ref[...] for ref in refs[:pieces]], axis=0)
    weight_ref, pick_ref, extra_ref = refs[pieces : pieces + 3]
    fq_ref, fk_ref, v_ref, state_ref = refs[-4:]
    projected = dot(units, weight_ref[...])
    rows, width = projected.shape
    needed = (heads - 1) * LANES + WIDE
    if needed > width:
        projected = jnp.pad(projected, ((0, 0), (0, needed - width)))
    bound = bound_ref[0]
    place = place_column(places_ref, slots, chunk)
    kept = ((place >= bound) | (bound == count)).astype(F32)
    ones = jnp.ones((8, rows), BF16)
    shift = 2 * FEAT
    for head in range(heads):
        part = projected[:, head * LANES : head * LANES + WIDE]
        narrow = part if head == 0 else pltpu.roll(part, WIDE - shift * head, 1)
        narrow = narrow[:, :LANES]
        values = pltpu.roll(part, WIDE - shift * (head + 1), 1)[:, :HEAD_DIM].astype(BF16)
        v_ref[:, head * HEAD_DIM : (head + 1) * HEAD_DIM] = values
        upper = narrow.astype(BF16)
        lower = (narrow - upper.astype(F32)).astype(BF16)
        both = jnp.concatenate([upper, lower], axis=1)
        feats = []
        for kind in range(2):
            one = dot(both, pick_ref[kind, 0]) + extra_ref[0:1]
            two = dot(both, pick_ref[kind, 1]) + extra_ref[1:2]
            feats.append((one * two * extra_ref[2:3]).astype(BF16))
        fq_ref[head] = feats[0]
        fk_ref[head] = feats[1]
        keys = (feats[1].astype(F32) * kept).astype(BF16)
        state = dot(keys, values, ((0,), (0,)))
        total = dot(ones, keys)
        tail = jnp.concatenate([total[0:1, :LANES], total[0:1, LANES:], jnp.zeros((14, LANES), F32)], axis=0)
        state = jnp.concatenate([state[0:STATE_ROWS], tail], axis=0)
        if more:
            state = state + refs[pieces + 3][head]
        state_ref[head] = state.astype(BF16) if last else state


def project(bound, places, slots, chunk, count, pieces, weight, constants, earlier, last, heads):
    rows = sum(piece.shape[0] for piece in pieces)
    extra = [] if earlier is None else [earlier]
    return pl.pallas_call(
        functools.partial(project_kernel, heads, slots, chunk, count, len(pieces), bool(extra), last),
        in_specs=[smem(), smem()] + [whole()] * (len(pieces) + 3 + len(extra)),
        out_specs=[whole()] * 4,
        out_shape=[
            jax.ShapeDtypeStruct((heads, rows, WIDE), BF16),
            jax.ShapeDtypeStruct((heads, rows, WIDE), BF16),
            jax.ShapeDtypeStruct((rows, heads * HEAD_DIM), BF16),
            jax.ShapeDtypeStruct((heads, BUFFER_ROWS, HEAD_DIM), BF16 if last else F32),
        ],
        compiler_params=params(),
        cost_estimate=cost(5),
        name="project",
    )(bound, places, *pieces, weight, *constants, *extra)


def within_kernel(heads, slots, chunk, sets, bound_ref, places_ref, *refs):
    fqs, fks, vs = refs[:sets], refs[sets : 2 * sets], refs[2 * sets : 3 * sets]
    num_ref, den_ref = refs[3 * sets :]
    bound = bound_ref[0]
    row = place_column(places_ref, slots, chunk)
    col = place_row(places_ref, slots, chunk)
    allowed = (row >= col) & ((row >= bound) == (col >= bound))
    for head in range(heads):
        query = jnp.concatenate([ref[head] for ref in fqs], axis=0)
        keys = jnp.concatenate([ref[head] for ref in fks], axis=0)
        values = jnp.concatenate(
            [ref[:, head * HEAD_DIM : (head + 1) * HEAD_DIM] for ref in vs], axis=0
        )
        weights = dot(query, keys, ((1,), (1,)))
        weights = jnp.where(allowed, weights, 0.0)
        den_ref[head] = jnp.broadcast_to(
            jnp.sum(weights, axis=-1, keepdims=True), (row.shape[0], 8)
        )
        num_ref[head] = dot(weights.astype(BF16), values)


def within(bound, places, slots, chunk, fqs, fks, vs, heads):
    count = len(slots) * chunk
    return pl.pallas_call(
        functools.partial(within_kernel, heads, slots, chunk, len(fqs)),
        in_specs=[smem(), smem()] + [whole()] * (3 * len(fqs)),
        out_specs=[whole()] * 2,
        out_shape=[
            jax.ShapeDtypeStruct((heads, count, HEAD_DIM), F32),
            jax.ShapeDtypeStruct((heads, count, 8), F32),
        ],
        compiler_params=params(),
        cost_estimate=cost(4.5),
        name="within",
    )(bound, places, *fqs, *fks, *vs)


def split_store(total, refs):
    rows = refs[0].shape[0]
    for n, ref in enumerate(refs):
        ref[...] = total[n * rows : (n + 1) * rows].astype(BF16)


def across_kernel(heads, slots, chunk, sets, earlier, near, bound_ref, places_ref, share_ref, *refs):
    fqs, refs = refs[:sets], refs[sets:]
    num_ref, den_ref, gain_ref, weight_ref = refs[:4]
    states, refs = refs[4 : 4 + earlier], refs[4 + earlier :]
    mixed_ref, fars = refs[0], refs[1:]
    bound = bound_ref[0]
    before = (place_column(places_ref, slots, chunk) < bound).astype(F32)
    for head in range(heads):
        carried = jnp.zeros((BUFFER_ROWS, HEAD_DIM), F32)
        for n in range(earlier):
            carried = carried + jnp.where(share_ref[n] > 0, states[n][head].astype(F32), 0.0)
        state = jnp.concatenate(
            [carried[0:STATE_ROWS], jnp.zeros((WIDE - STATE_ROWS, HEAD_DIM), F32)], axis=0
        ).astype(BF16)
        total = jnp.concatenate(
            [carried[STATE_ROWS : STATE_ROWS + 1], carried[STATE_ROWS + 1 : STATE_ROWS + 2]], axis=1
        )
        query = jnp.concatenate([ref[head] for ref in fqs], axis=0)
        numerator = num_ref[head] + before * dot(query, state)
        more = jnp.sum(query.astype(F32) * total, axis=-1, keepdims=True)
        denominator = den_ref[head][:, 0:1] + before * more
        lanes = slice(head * HEAD_DIM, (head + 1) * HEAD_DIM)
        mixed_ref[:, lanes] = (numerator / denominator * gain_ref[:, lanes].astype(F32)).astype(BF16)
    split_store(dot(mixed_ref[near * chunk :], weight_ref[...]), fars)


def across(bound, places, share, slots, chunk, near, far, fqs, num, den, gain, weight, states, heads):
    count = len(slots) * chunk
    rows = (count - near * chunk) // far
    return pl.pallas_call(
        functools.partial(across_kernel, heads, slots, chunk, len(fqs), len(states), near),
        in_specs=[smem()] * 3 + [whole()] * (len(fqs) + 4 + len(states)),
        out_specs=[whole()] * (1 + far),
        out_shape=[jax.ShapeDtypeStruct((count, heads * HEAD_DIM), BF16)]
        + [jax.ShapeDtypeStruct((rows, weight.shape[1]), BF16)] * far,
        compiler_params=params(),
        cost_estimate=cost(4.5),
        name="across",
    )(bound, places, share, *fqs, num, den, gain, weight, *states)


def near_kernel(rows, mixed_ref, weight_ref, *outs):
    split_store(dot(mixed_ref[0:rows], weight_ref[...]), outs)


def near_chunks(mixed, weight, near, chunk):
    pieces = 2 * near if near > 1 else 1
    rows = near * chunk
    return pl.pallas_call(
        functools.partial(near_kernel, rows),
        in_specs=[whole()] * 2,
        out_specs=[whole()] * pieces,
        out_shape=[jax.ShapeDtypeStruct((rows // pieces, weight.shape[1]), BF16)] * pieces,
        compiler_params=params(),
        cost_estimate=cost(4),
        name="near",
    )(mixed, weight)


def matmul_kernel(*refs):
    a = jnp.concatenate([ref[...] for ref in refs[:-2]], axis=0)
    refs[-1][...] = dot(a, refs[-2][...]).astype(BF16)


def matmul(pieces, b, tile):
    rows = sum(piece.shape[0] for piece in pieces)
    inner = b.shape[0]
    return pl.pallas_call(
        matmul_kernel,
        grid=(b.shape[1] // tile,),
        in_specs=[
            pl.BlockSpec(piece.shape, lambda n: (0, 0), pipeline_mode=pl.Buffered(1)) for piece in pieces
        ]
        + [pl.BlockSpec((inner, tile), lambda n: (0, n))],
        out_specs=pl.BlockSpec((rows, tile), lambda n: (0, n)),
        out_shape=jax.ShapeDtypeStruct((rows, b.shape[1]), BF16),
        compiler_params=params(),
        cost_estimate=cost(5),
        name="matmul",
    )(*pieces, b)


def attend(query, keys, values, allowed):
    scores = dot(query, keys, ((1,), (1,))) * HEAD_DIM ** (-0.5)
    scores = jnp.where(allowed, scores, NEGATIVE)
    peak = jnp.max(scores, axis=-1, keepdims=True)
    weights = jnp.where(allowed, jnp.exp(scores - peak), 0.0)
    probabilities = (weights / jnp.sum(weights, axis=-1, keepdims=True)).astype(BF16)
    return dot(probabilities, values).astype(BF16)


def local_kernel(heads, slots, spots, chunk, sets, bound_ref, places_ref, *refs):
    qkvs, (result_ref, first_ref) = refs[:sets], refs[sets:]
    size = len(slots)
    reach = chunk + WINDOW
    bound = bound_ref[0]
    row = lax.broadcasted_iota(jnp.int32, (chunk, reach), 0)
    col = lax.broadcasted_iota(jnp.int32, (chunk, reach), 1)
    band = (col > row) & (col <= row + WINDOW)
    for slot in range(size):
        k = slots[slot]
        mine, at = spots[k]
        theirs, there = spots[(k - 1) % size]
        base = places_ref[slot]
        query_place = row + base
        key_place = col + (base - WINDOW)
        allowed = band & (key_place >= 0) & ((query_place >= bound) == (key_place >= bound))
        rows = slice(at, at + chunk)
        tail = slice(there + chunk - WINDOW, there + chunk)

        @pl.when(base == 0)
        def _():
            first_ref[...] = qkvs[mine][at : at + WINDOW]

        for head in range(heads):
            lane = head * 3 * HEAD_DIM
            keys, values = [
                jnp.concatenate(
                    [
                        qkvs[theirs][tail, lane + n * HEAD_DIM : lane + (n + 1) * HEAD_DIM],
                        qkvs[mine][rows, lane + n * HEAD_DIM : lane + (n + 1) * HEAD_DIM],
                    ],
                    axis=0,
                )
                for n in (1, 2)
            ]
            result_ref[slot * chunk : (slot + 1) * chunk, head * HEAD_DIM : (head + 1) * HEAD_DIM] = attend(
                qkvs[mine][rows, lane : lane + HEAD_DIM], keys, values, allowed
            )


def local_window(bound, places, slots, spots, chunk, qkvs, heads):
    return pl.pallas_call(
        functools.partial(local_kernel, heads, slots, spots, chunk, len(qkvs)),
        in_specs=[smem(), smem()] + [whole()] * len(qkvs),
        out_specs=[whole()] * 2,
        out_shape=[
            jax.ShapeDtypeStruct((len(slots) * chunk, heads * HEAD_DIM), BF16),
            jax.ShapeDtypeStruct((WINDOW, qkvs[0].shape[1]), BF16),
        ],
        compiler_params=params(),
        cost_estimate=cost(8),
        name="local_window",
    )(bound, places, *qkvs)


def halo_kernel(heads, count, start, info_ref, local_ref, first_ref, halo_ref, weight_ref, result_ref, *fars):
    result_ref[...] = local_ref[...]
    bound, valid_from, spot = info_ref[0], info_ref[1], info_ref[2]
    row = lax.broadcasted_iota(jnp.int32, (WINDOW, 2 * WINDOW), 0)
    col = lax.broadcasted_iota(jnp.int32, (WINDOW, 2 * WINDOW), 1)
    key_place = col - WINDOW
    allowed = (col > row) & (col <= row + WINDOW) & ((row >= bound) == (key_place >= bound))
    allowed = allowed & ((key_place >= 0) | (key_place + count >= valid_from))
    spot = pl.multiple_of(spot, WINDOW)
    for head in range(heads):
        lane = head * 3 * HEAD_DIM
        keys, values = [
            jnp.concatenate(
                [ref[:, lane + n * HEAD_DIM : lane + (n + 1) * HEAD_DIM] for ref in (halo_ref, first_ref)], axis=0
            )
            for n in (1, 2)
        ]
        result_ref[pl.ds(spot, WINDOW), head * HEAD_DIM : (head + 1) * HEAD_DIM] = attend(
            first_ref[:, lane : lane + HEAD_DIM], keys, values, allowed
        )
    split_store(dot(result_ref[start:], weight_ref[...]), fars)


def halo_window(info, near, chunk, far, local, first, halo, weight, heads):
    count = local.shape[0]
    rows = (count - near * chunk) // far
    return pl.pallas_call(
        functools.partial(halo_kernel, heads, count, near * chunk),
        in_specs=[smem()] + [whole()] * 4,
        out_specs=[whole()] * (1 + far),
        out_shape=[jax.ShapeDtypeStruct(local.shape, BF16)]
        + [jax.ShapeDtypeStruct((rows, weight.shape[1]), BF16)] * far,
        compiler_params=params(),
        cost_estimate=cost(4.5),
        name="halo_window",
    )(info, local, first, halo, weight)


def score_kernel(units_count, pieces, lots, tile, order_ref, *refs):
    units, refs = refs[:units_count], refs[units_count:]
    tables, (goal_ref, out_ref, turned_ref, held) = refs[: len(lots) * pieces], refs[len(lots) * pieces :]
    step = pl.program_id(0)
    width = tables[0].shape[1]
    count = goal_ref.shape[1]
    part = 128

    @pl.when(step == 0)
    def _():
        rows = jnp.concatenate([ref[...] for ref in units], axis=0)
        turned_ref[...] = jnp.transpose(rows)
        held[0] = jnp.full((8, count), NEGATIVE, F32)
        held[1] = jnp.zeros((8, count), F32)
        held[2] = jnp.zeros((8, count), F32)

    def run(mine):
        inner = lax.broadcasted_iota(jnp.int32, (part // 8, 8, count), 0) * 8
        inner = inner + lax.broadcasted_iota(jnp.int32, (part // 8, 8, count), 1)
        peak, total, picked = held[0], held[1], held[2]
        sides = [
            turned_ref[pl.ds(pl.multiple_of(order_ref[n] * width, width), width), :] for n in range(pieces)
        ]
        for at in range(0, tile, part):
            logits = None
            for n in range(pieces):
                more = dot(mine[n][at : at + part], sides[n])
                logits = more if logits is None else logits + more
            logits = logits.reshape(part // 8, 8, count)
            goal = (goal_ref[...] - (step * tile + at)).reshape(1, 1, count)
            old = peak
            peak = jnp.maximum(old, jnp.max(logits, axis=0))
            total = total * jnp.exp(old - peak) + jnp.sum(jnp.exp(logits - peak[None]), axis=0)
            picked = picked + jnp.sum(jnp.where(inner == goal, logits, 0.0), axis=0)
        held[0], held[1], held[2] = peak, total, picked

    for lot, (start, stop) in enumerate(lots):
        pl.when((step >= start) & (step < stop))(
            lambda lot=lot: run(tables[lot * pieces : (lot + 1) * pieces])
        )

    @pl.when(step == pl.num_programs(0) - 1)
    def _():
        peak = jnp.max(held[0], axis=0, keepdims=True)
        total = jnp.sum(held[1] * jnp.exp(held[0] - peak), axis=0, keepdims=True)
        picked = jnp.sum(held[2], axis=0, keepdims=True)
        out_ref[...] = jnp.concatenate([peak, total, picked, jnp.zeros((5, count), F32)], axis=0)


def scores(order, units, lots, goal):
    count = goal.shape[1]
    rows = lots[-1][1]
    tile = 1280 if rows % 1280 == 0 else 640
    pieces = len(lots[0][2])
    specs, steps = [], []
    for first, last, tables in lots:
        start, stop = first // tile, last // tile
        steps.append((start, stop))
        for table in tables:
            shift = 0 if table.shape[0] == rows else start
            specs.append(
                pl.BlockSpec(
                    (tile, table.shape[1]),
                    lambda i, start=start, stop=stop, shift=shift: (jnp.clip(i, start, stop - 1) - shift, 0),
                )
            )
    return pl.pallas_call(
        functools.partial(score_kernel, len(units), pieces, steps, tile),
        in_specs=[smem()]
        + [pl.BlockSpec(piece.shape, lambda i: (0, 0), pipeline_mode=pl.Buffered(1)) for piece in units]
        + specs
        + [pl.BlockSpec((1, count), lambda i: (0, 0))],
        out_specs=pl.BlockSpec((8, count), lambda i: (0, 0)),
        grid=(rows // tile,),
        out_shape=jax.ShapeDtypeStruct((8, count), F32),
        scratch_shapes=[pltpu.VMEM((units[0].shape[1], count), BF16), pltpu.VMEM((3, 8, count), F32)],
        compiler_params=params(),
        cost_estimate=cost(14),
        name="scores",
    )(order, *units, *[table for lot in lots for table in lot[2]], goal)


def shards(
    token_ids,
    target_ids,
    doc_start,
    vocab_table,
    norm_gain_one,
    lin_qkv,
    lin_head_gain,
    lin_out,
    norm_gain_two,
    win_qkv,
    win_out,
    final_gain,
):
    head_count = lax.axis_size("head")
    seq_count = lax.axis_size("seq")
    head_index = lax.axis_index("head")
    seq_index = lax.axis_index("seq")
    tok_count = token_ids.shape[0]
    chunk = tok_count // head_count
    vocab_rows = vocab_table.shape[0]
    heads = lin_qkv.shape[1] // (2 * FEAT + HEAD_DIM)
    vocab_first = head_index * vocab_rows
    calls = chunk_order(head_count)
    slots = [k for call in calls for k in call]
    near = 3 if head_count == 4 else 1
    far = 2 if head_count == 4 else head_count - 1
    spots = {}
    for n, call in enumerate(calls):
        for at, k in enumerate(call):
            spots[k] = (n, at * chunk)
    held_at = (head_index + jnp.asarray(slots, jnp.int32)) % head_count
    places = held_at * chunk

    marks = jnp.concatenate([token_ids, jnp.broadcast_to(doc_start, (LANES,))])
    marks = jnp.stack(
        [marks] + [lax.ppermute(marks, "seq", xor_pairs(seq_count, k)) for k in range(1, seq_count)]
    )
    block = jnp.arange(seq_count, dtype=jnp.int32)
    order = seq_index ^ block
    starts = marks[:, tok_count]
    starts = jnp.sum(jnp.where(order[None, :] == block[:, None], starts[None, :], 0), axis=1)
    bound = doc_start.astype(jnp.int32)

    lots = [vocab_rows * 3 // 5, vocab_rows * 2 // 5]
    early, late = vocab_table[: lots[0]], vocab_table[lots[0] :]

    ids = (marks[:, :tok_count] - vocab_first).reshape(seq_count, head_count, chunk)

    def ids_of(k):
        return lax.dynamic_index_in_dim(ids, (head_index + k) % head_count, 1, False).reshape(-1)

    if head_count == 4:
        outer = lookup(ids_of(2), vocab_table, 2)
        inner = lambda: (
            lookup(ids_of(0), vocab_table, 2)
            + lookup(jnp.concatenate([ids_of(1), ids_of(3)]), vocab_table, 4)
        )
    else:
        outer = [lookup(ids_of(k), vocab_table, 1)[0] for k in range(1, head_count)]
        inner = lambda: lookup(ids_of(0), vocab_table, 1)
    found = collect(scatter_rows(outer, inner), seq_count)
    gathered = [found[0]] + [
        lax.ppermute(found[k], "seq", xor_pairs(seq_count, k)) for k in range(1, seq_count)
    ]
    embedded, units = begin(order, norm_gain_one, gathered)
    chunks = gather_rows(units)

    constants = selectors()
    sets, state = [], None
    for n, call in enumerate(calls):
        pieces = [piece for k in call for piece in chunks[k]]
        first = sum(len(c) for c in calls[:n])
        made = project(
            bound,
            places[first : first + len(call)],
            list(range(len(call))),
            chunk,
            tok_count,
            pieces,
            lin_qkv,
            constants,
            state,
            n == len(calls) - 1,
            heads,
        )
        sets.append(made[:3])
        state = made[3]
    fqs, fks, vs = zip(*sets)
    states, shares = [], []
    for back in range(1, seq_count):
        states.append(
            lax.ppermute(state, "seq", [(i, i + back) for i in range(seq_count - back)])
        )
        between = (block > seq_index - back) & (block < seq_index)
        broken = jnp.sum(jnp.where(between & (starts != tok_count), 1, 0))
        shares.append(((broken == 0) & (seq_index >= back)).astype(jnp.int32))
    position = list(range(head_count))
    num, den = within(bound, places, position, chunk, fqs, fks, vs, heads)
    mixed, *outer = across(
        bound,
        places,
        jnp.stack(shares),
        position,
        chunk,
        near,
        far,
        fqs,
        num,
        den,
        lin_head_gain.reshape(1, -1),
        lin_out,
        states,
        heads,
    )
    parts = scatter_rows(outer, lambda: near_chunks(mixed, lin_out, near, chunk))
    units, residual = finish(embedded, norm_gain_two, parts, False)

    if seq_count == 4:
        early, _ = lax.optimization_barrier((early, states))
        early = lax.ppermute(early, "seq", xor_pairs(seq_count, 2))
        early_corner = lax.ppermute(early, "seq", xor_pairs(seq_count, 1))
        beside = lax.ppermute(vocab_table, "seq", xor_pairs(seq_count, 1))

    chunks = gather_rows(units)
    qkvs = []
    for call in calls:
        qkvs.append(matmul([piece for k in call for piece in chunks[k]], win_qkv, 3 * HEAD_DIM))
    tail = jnp.zeros((WINDOW, win_qkv.shape[1]), BF16)
    for slot, k in enumerate(slots):
        n, at = spots[k]
        tail = jnp.where(
            held_at[slot] == head_count - 1, qkvs[n][at + chunk - WINDOW : at + chunk], tail
        )
    late, tail = lax.optimization_barrier((late, tail))
    halo = lax.ppermute(tail, "seq", [(i, i + 1) for i in range(seq_count - 1)])
    previous = jnp.sum(jnp.where(block == seq_index - 1, starts, 0))
    valid_from = jnp.where(
        seq_index == 0, tok_count, jnp.where(previous == tok_count, 0, previous)
    ).astype(jnp.int32)
    first_spot = jnp.sum(jnp.where(held_at == 0, jnp.arange(head_count) * chunk, 0)).astype(jnp.int32)
    local, first = local_window(bound, places, slots, spots, chunk, qkvs, heads)
    info = jnp.stack([bound[0], valid_from, first_spot])
    mixed, *outer = halo_window(info, near, chunk, far, local, first, halo, win_out, heads)
    parts = scatter_rows(outer, lambda: near_chunks(mixed, win_out, near, chunk))
    units = finish(residual, final_gain, parts, True)[0]

    chunks = gather_rows(units)
    if seq_count == 4:
        late = lax.ppermute(late, "seq", xor_pairs(seq_count, 2))
        corner, _ = lax.optimization_barrier((late, (chunks[1][0], chunks[-1][0])))
        late_corner = lax.ppermute(corner, "seq", xor_pairs(seq_count, 1))
        lots = [
            (0, lots[0], [vocab_table, beside, early, early_corner]),
            (lots[0], vocab_rows, [vocab_table, beside, late, late_corner]),
        ]
    else:
        lots = [(0, vocab_rows, [lax.all_gather(vocab_table, "seq", axis=1, tiled=True)])]
        order = jnp.zeros((1,), jnp.int32)
    goals = (target_ids - vocab_first).reshape(head_count, chunk)
    found = {}
    for group in [[0, 3], [1, 2]] if head_count == 4 else [[k] for k in range(head_count)]:
        goal = jnp.concatenate(
            [
                lax.dynamic_index_in_dim(goals, (head_index + k) % head_count, 0, False)
                for k in group
            ]
        ).reshape(1, -1)
        triple = scores(order, [piece for k in group for piece in chunks[k]], lots, goal)
        for at, k in enumerate(group):
            found[k] = triple[:3, at * chunk : (at + 1) * chunk]

    shares = jnp.stack([found[0]] + [turned(found[k], k) for k in range(1, head_count)])
    peak = jnp.max(shares[:, 0], axis=0)
    total = jnp.sum(shares[:, 1] * jnp.exp(shares[:, 0] - peak), axis=0)
    return jnp.sum(shares[:, 2], axis=0) - (peak + jnp.log(total))


def solution(mesh):
    return jax.shard_map(
        shards,
        mesh=mesh,
        in_specs=(
            P(("shadow", "seq")),
            P(("shadow", "seq")),
            P(("shadow", "seq")),
            P(("shadow", "head"), "seq"),
            P("shadow"),
            P("shadow", "head"),
            P(("shadow", "head")),
            P(("shadow", "head"), None),
            P("shadow"),
            P("shadow", "head"),
            P(("shadow", "head"), None),
            P("shadow"),
        ),
        out_specs=P(("shadow", "seq", "head")),
        check_vma=False,
    )
```

```python
import functools

import jax
import jax.numpy as jnp
import numpy as np
from jax import lax
from jax.experimental import pallas as pl
from jax.experimental.pallas import tpu as pltpu
from jax.sharding import PartitionSpec as P

FEAT = 16
WINDOW = 64
HEAD_DIM = 128
EPSILON = 1e-05
NEGATIVE = -1e30
LANES = 128
WIDE = 256
STATE_ROWS = 160
BUFFER_ROWS = 176
F32 = jnp.float32
BF16 = jnp.bfloat16
VMEM_BYTES = 56 * 1024 * 1024


def params(**kw):
    return pltpu.CompilerParams(vmem_limit_bytes=VMEM_BYTES, **kw)


def cost(us):
    return pl.CostEstimate(flops=int(us * 6e8), transcendentals=0, bytes_accessed=int(us * 3e6))


def whole():
    return pl.BlockSpec(memory_space=pltpu.VMEM)


def smem():
    return pl.BlockSpec(memory_space=pltpu.SMEM)


def dot(a, b, dims=((1,), (0,))):
    return lax.dot_general(a, b, (dims, ((), ())), preferred_element_type=F32)


def xor_pairs(size, k):
    return [(i, i ^ k) for i in range(size)]


def rms(values, gain):
    factor = lax.rsqrt(jnp.mean(values * values, axis=-1, keepdims=True) + EPSILON)
    return (values * factor * gain.astype(F32)).astype(BF16)


def turned(value, step):
    size = lax.axis_size("head")
    return lax.ppermute(value, "head", [(i, (i + step) % size) for i in range(size)])


def gather_rows(own, work=None):
    size = lax.axis_size("head")
    made = None if work is None else work(own)
    if size != 4:
        full = lax.all_gather(own, "head")
        here = lax.axis_index("head")
        return [[own]] + [
            [lax.dynamic_index_in_dim(full, (here + k) % size, 0, False)] for k in range(1, size)
        ], made
    half = own.shape[0] // 2
    before = turned(own, 1)
    if work is not None:
        own, made = lax.optimization_barrier((own, made))
    after = turned(own, -1)
    return [[own], [after], [turned(before[:half], 1), turned(after[half:], -1)], [before]], made


def scatter_rows(far, near):
    size = lax.axis_size("head")
    if size != 4:
        here = lax.axis_index("head")
        full = jnp.stack([near()[0]] + list(far))
        full = jnp.stack(
            [lax.dynamic_index_in_dim(full, (d - here) % size, 0, False) for d in range(size)]
        )
        return [[lax.psum_scatter(full, "head", scatter_dimension=0, tiled=True)[0]]]
    from_before, from_after = turned(far[0], 1), turned(far[1], -1)
    own_upper, own_lower, next_upper, next_lower, prev_upper, prev_lower = near()
    lower_right, upper_left = turned(next_lower, 1), turned(prev_upper, -1)
    upper_right, lower_left = pass_on(next_upper, from_before, prev_lower, from_after)
    upper_right, lower_left = turned(upper_right, 1), turned(lower_left, -1)
    return [[own_upper, upper_right, upper_left], [own_lower, lower_right, lower_left]]


def pass_on_kernel(next_ref, before_ref, prev_ref, after_ref, right_ref, left_ref):
    right_ref[...] = (next_ref[...].astype(F32) + before_ref[...].astype(F32)).astype(BF16)
    left_ref[...] = (prev_ref[...].astype(F32) + after_ref[...].astype(F32)).astype(BF16)


def pass_on(next_upper, from_before, prev_lower, from_after):
    return pl.pallas_call(
        pass_on_kernel,
        in_specs=[whole()] * 4,
        out_specs=[whole()] * 2,
        out_shape=[jax.ShapeDtypeStruct(next_upper.shape, BF16)] * 2,
        compiler_params=params(),
        cost_estimate=cost(1.5),
        name="pass_on",
    )(next_upper, from_before, prev_lower, from_after)


def chunk_order(size):
    if size == 4:
        return [[0], [1, 3], [2]]
    return [[k] for k in range(size)]


def lookup_kernel(ids_ref, table_ref, *refs):
    outs, total = refs[:-1], refs[-1]
    step = pl.program_id(0)
    tile = table_ref.shape[0]
    count = ids_ref.shape[1]
    ids = jnp.transpose(jnp.broadcast_to(ids_ref[...], (8, count)))[:, 0:1] - step * tile
    hot = (lax.broadcasted_iota(jnp.int32, (count, tile), 1) == ids).astype(F32).astype(BF16)
    found = dot(hot, table_ref[...])

    @pl.when(step == 0)
    def _():
        total[...] = found

    @pl.when(step > 0)
    def _():
        total[...] += found

    @pl.when(step == pl.num_programs(0) - 1)
    def _():
        rows = outs[0].shape[0]
        for n, out in enumerate(outs):
            out[...] = total[n * rows : (n + 1) * rows].astype(BF16)


def lookup(ids, table, pieces):
    count = ids.shape[0]
    rows, width = table.shape
    tile = rows // 5
    return pl.pallas_call(
        lookup_kernel,
        grid=(rows // tile,),
        in_specs=[
            pl.BlockSpec((1, count), lambda i: (0, 0)),
            pl.BlockSpec((tile, width), lambda i: (i, 0)),
        ],
        out_specs=[pl.BlockSpec((count // pieces, width), lambda i: (0, 0))] * pieces,
        out_shape=[jax.ShapeDtypeStruct((count // pieces, width), BF16)] * pieces,
        scratch_shapes=[pltpu.VMEM((count, width), F32)],
        compiler_params=params(),
        cost_estimate=cost(8 * count / 512),
        name="lookup",
    )(ids.reshape(1, count), table)


def gathered_sum(refs, sizes):
    rows, at = [], 0
    for size in sizes:
        total = refs[at][...].astype(F32)
        for ref in refs[at + 1 : at + size]:
            total = total + ref[...].astype(F32)
        rows.append(total)
        at += size
    return rows[0] if len(rows) == 1 else jnp.concatenate(rows, axis=0)


def collect_kernel(sizes, *refs):
    ins, outs = refs[: sum(sizes)], refs[sum(sizes) :]
    rows = outs[0].shape[0]
    total = gathered_sum(ins, sizes)
    for n, out in enumerate(outs):
        out[...] = total[n * rows : (n + 1) * rows].astype(BF16)


def collect(terms, pieces):
    sizes = [len(part) for part in terms]
    parts = [term for part in terms for term in part]
    rows, width = sum(part[0].shape[0] for part in terms), parts[0].shape[1]
    return pl.pallas_call(
        functools.partial(collect_kernel, sizes),
        in_specs=[whole()] * len(parts),
        out_specs=[whole()] * pieces,
        out_shape=[jax.ShapeDtypeStruct((rows // pieces, width), BF16)] * pieces,
        compiler_params=params(),
        cost_estimate=cost(2),
        name="collect",
    )(*parts)


def begin_kernel(pieces, order_ref, gain_ref, *refs):
    ins, (embedded_ref, units_ref, held) = refs[:pieces], refs[pieces:]
    width = ins[0].shape[1]
    for n in range(pieces):
        held[order_ref[n]] = ins[n][...]
    values = jnp.concatenate([held[n] for n in range(pieces)], axis=1)
    embedded_ref[...] = values
    units_ref[...] = rms(values.astype(F32), gain_ref[...])


def begin(order, gain, pieces):
    rows, width = pieces[0].shape
    full = jax.ShapeDtypeStruct((rows, width * len(pieces)), BF16)
    return pl.pallas_call(
        functools.partial(begin_kernel, len(pieces)),
        in_specs=[smem()] + [whole()] * (1 + len(pieces)),
        out_specs=[whole()] * 2,
        out_shape=[full, full],
        scratch_shapes=[pltpu.VMEM((len(pieces), rows, width), BF16)],
        compiler_params=params(),
        cost_estimate=cost(2),
        name="begin",
    )(order, gain.reshape(1, -1), *pieces)


def finish_kernel(sizes, last, residual_ref, gain_ref, *refs):
    parts = sum(sizes)
    total = gathered_sum(refs[:parts], sizes) + residual_ref[...].astype(F32)
    if not last:
        total = total.astype(BF16)
        refs[parts + 1][...] = total
    refs[parts][...] = rms(total.astype(F32), gain_ref[...])


def finish(residual, gain, terms, last):
    full = jax.ShapeDtypeStruct(residual.shape, BF16)
    parts = [term for part in terms for term in part]
    return pl.pallas_call(
        functools.partial(finish_kernel, [len(part) for part in terms], last),
        in_specs=[whole()] * (2 + len(parts)),
        out_specs=[whole()] * (1 if last else 2),
        out_shape=[full] * (1 if last else 2),
        compiler_params=params(),
        cost_estimate=cost(2.5),
        name="finish",
    )(residual, gain.reshape(1, -1), *parts)


def selectors():
    pairs = [(r, s) for r in range(FEAT) for s in range(r, FEAT)]
    picks = np.zeros((2, 2, LANES, WIDE), np.float32)
    extra = np.zeros((3, WIDE), np.float32)
    extra[0:2, 0] = 1.0
    extra[1, 1 : 1 + FEAT] = 1.0
    extra[2] = 1.0
    for kind in range(2):
        first = kind * FEAT
        for r in range(FEAT):
            picks[kind, 0, first + r, 1 + r] = FEAT ** (-0.25)
        for n, (r, s) in enumerate(pairs):
            picks[kind, 0, first + r, 1 + FEAT + n] = FEAT ** (-0.25)
            picks[kind, 1, first + s, 1 + FEAT + n] = FEAT ** (-0.25)
    for n, (r, s) in enumerate(pairs):
        extra[2, 1 + FEAT + n] = 0.5**0.5 if r == s else 1.0
    return jnp.asarray(np.concatenate([picks, picks], axis=2), BF16), jnp.asarray(extra)


def place_column(places_ref, slots, rows):
    inner = lax.broadcasted_iota(jnp.int32, (rows, 1), 0)
    return jnp.concatenate([inner + places_ref[slot] for slot in slots], axis=0)


def place_row(places_ref, slots, rows):
    inner = lax.broadcasted_iota(jnp.int32, (1, rows), 1)
    return jnp.concatenate([inner + places_ref[slot] for slot in slots], axis=1)


def project_kernel(heads, slots, chunk, count, pieces, more, last, bound_ref, places_ref, *refs):
    units = jnp.concatenate([ref[...] for ref in refs[:pieces]], axis=0)
    weight_ref, pick_ref, extra_ref = refs[pieces : pieces + 3]
    fq_ref, fk_ref, v_ref, state_ref = refs[-4:]
    projected = dot(units, weight_ref[...])
    rows, width = projected.shape
    needed = (heads - 1) * LANES + WIDE
    if needed > width:
        projected = jnp.pad(projected, ((0, 0), (0, needed - width)))
    bound = bound_ref[0]
    place = place_column(places_ref, slots, chunk)
    kept = ((place >= bound) | (bound == count)).astype(F32)
    ones = jnp.ones((8, rows), BF16)
    shift = 2 * FEAT
    for head in range(heads):
        part = projected[:, head * LANES : head * LANES + WIDE]
        narrow = part if head == 0 else pltpu.roll(part, WIDE - shift * head, 1)
        narrow = narrow[:, :LANES]
        values = pltpu.roll(part, WIDE - shift * (head + 1), 1)[:, :HEAD_DIM].astype(BF16)
        v_ref[:, head * HEAD_DIM : (head + 1) * HEAD_DIM] = values
        upper = narrow.astype(BF16)
        lower = (narrow - upper.astype(F32)).astype(BF16)
        both = jnp.concatenate([upper, lower], axis=1)
        feats = []
        for kind in range(2):
            one = dot(both, pick_ref[kind, 0]) + extra_ref[0:1]
            two = dot(both, pick_ref[kind, 1]) + extra_ref[1:2]
            feats.append((one * two * extra_ref[2:3]).astype(BF16))
        fq_ref[head] = feats[0]
        fk_ref[head] = feats[1]
        keys = (feats[1].astype(F32) * kept).astype(BF16)
        state = dot(keys, values, ((0,), (0,)))
        total = dot(ones, keys)
        tail = jnp.concatenate([total[0:1, :LANES], total[0:1, LANES:], jnp.zeros((14, LANES), F32)], axis=0)
        state = jnp.concatenate([state[0:STATE_ROWS], tail], axis=0)
        if more:
            state = state + refs[pieces + 3][head]
        state_ref[head] = state.astype(BF16) if last else state


def project(bound, places, slots, chunk, count, pieces, weight, constants, earlier, last, heads):
    rows = sum(piece.shape[0] for piece in pieces)
    extra = [] if earlier is None else [earlier]
    return pl.pallas_call(
        functools.partial(project_kernel, heads, slots, chunk, count, len(pieces), bool(extra), last),
        in_specs=[smem(), smem()] + [whole()] * (len(pieces) + 3 + len(extra)),
        out_specs=[whole()] * 4,
        out_shape=[
            jax.ShapeDtypeStruct((heads, rows, WIDE), BF16),
            jax.ShapeDtypeStruct((heads, rows, WIDE), BF16),
            jax.ShapeDtypeStruct((rows, heads * HEAD_DIM), BF16),
            jax.ShapeDtypeStruct((heads, BUFFER_ROWS, HEAD_DIM), BF16 if last else F32),
        ],
        compiler_params=params(),
        cost_estimate=cost(5),
        name="project",
    )(bound, places, *pieces, weight, *constants, *extra)


def within_kernel(heads, slots, chunk, sets, bound_ref, places_ref, *refs):
    fqs, fks, vs = refs[:sets], refs[sets : 2 * sets], refs[2 * sets : 3 * sets]
    num_ref, den_ref = refs[3 * sets :]
    bound = bound_ref[0]
    row = place_column(places_ref, slots, chunk)
    col = place_row(places_ref, slots, chunk)
    allowed = (row >= col) & ((row >= bound) == (col >= bound))
    for head in range(heads):
        query = jnp.concatenate([ref[head] for ref in fqs], axis=0)
        keys = jnp.concatenate([ref[head] for ref in fks], axis=0)
        values = jnp.concatenate(
            [ref[:, head * HEAD_DIM : (head + 1) * HEAD_DIM] for ref in vs], axis=0
        )
        weights = dot(query, keys, ((1,), (1,)))
        weights = jnp.where(allowed, weights, 0.0)
        den_ref[head] = jnp.broadcast_to(
            jnp.sum(weights, axis=-1, keepdims=True), (row.shape[0], 8)
        )
        num_ref[head] = dot(weights.astype(BF16), values)


def within(bound, places, slots, chunk, fqs, fks, vs, heads):
    count = len(slots) * chunk
    return pl.pallas_call(
        functools.partial(within_kernel, heads, slots, chunk, len(fqs)),
        in_specs=[smem(), smem()] + [whole()] * (3 * len(fqs)),
        out_specs=[whole()] * 2,
        out_shape=[
            jax.ShapeDtypeStruct((heads, count, HEAD_DIM), F32),
            jax.ShapeDtypeStruct((heads, count, 8), F32),
        ],
        compiler_params=params(),
        cost_estimate=cost(4.5),
        name="within",
    )(bound, places, *fqs, *fks, *vs)


def split_store(total, refs):
    rows = refs[0].shape[0]
    for n, ref in enumerate(refs):
        ref[...] = total[n * rows : (n + 1) * rows].astype(BF16)


def across_kernel(heads, slots, chunk, sets, earlier, near, bound_ref, places_ref, share_ref, *refs):
    fqs, refs = refs[:sets], refs[sets:]
    num_ref, den_ref, gain_ref, weight_ref = refs[:4]
    states, refs = refs[4 : 4 + earlier], refs[4 + earlier :]
    mixed_ref, fars = refs[0], refs[1:]
    bound = bound_ref[0]
    before = (place_column(places_ref, slots, chunk) < bound).astype(F32)
    for head in range(heads):
        carried = jnp.zeros((BUFFER_ROWS, HEAD_DIM), F32)
        for n in range(earlier):
            carried = carried + jnp.where(share_ref[n] > 0, states[n][head].astype(F32), 0.0)
        state = jnp.concatenate(
            [carried[0:STATE_ROWS], jnp.zeros((WIDE - STATE_ROWS, HEAD_DIM), F32)], axis=0
        ).astype(BF16)
        total = jnp.concatenate(
            [carried[STATE_ROWS : STATE_ROWS + 1], carried[STATE_ROWS + 1 : STATE_ROWS + 2]], axis=1
        )
        query = jnp.concatenate([ref[head] for ref in fqs], axis=0)
        numerator = num_ref[head] + before * dot(query, state)
        more = jnp.sum(query.astype(F32) * total, axis=-1, keepdims=True)
        denominator = den_ref[head][:, 0:1] + before * more
        lanes = slice(head * HEAD_DIM, (head + 1) * HEAD_DIM)
        mixed_ref[:, lanes] = (numerator / denominator * gain_ref[:, lanes].astype(F32)).astype(BF16)
    split_store(dot(mixed_ref[near * chunk :], weight_ref[...]), fars)


def across(bound, places, share, slots, chunk, near, far, fqs, num, den, gain, weight, states, heads):
    count = len(slots) * chunk
    rows = (count - near * chunk) // far
    return pl.pallas_call(
        functools.partial(across_kernel, heads, slots, chunk, len(fqs), len(states), near),
        in_specs=[smem()] * 3 + [whole()] * (len(fqs) + 4 + len(states)),
        out_specs=[whole()] * (1 + far),
        out_shape=[jax.ShapeDtypeStruct((count, heads * HEAD_DIM), BF16)]
        + [jax.ShapeDtypeStruct((rows, weight.shape[1]), BF16)] * far,
        compiler_params=params(),
        cost_estimate=cost(4.5),
        name="across",
    )(bound, places, share, *fqs, num, den, gain, weight, *states)


def near_kernel(rows, mixed_ref, weight_ref, *outs):
    split_store(dot(mixed_ref[0:rows], weight_ref[...]), outs)


def near_chunks(mixed, weight, near, chunk):
    pieces = 2 * near if near > 1 else 1
    rows = near * chunk
    return pl.pallas_call(
        functools.partial(near_kernel, rows),
        in_specs=[whole()] * 2,
        out_specs=[whole()] * pieces,
        out_shape=[jax.ShapeDtypeStruct((rows // pieces, weight.shape[1]), BF16)] * pieces,
        compiler_params=params(),
        cost_estimate=cost(4),
        name="near",
    )(mixed, weight)


def matmul_kernel(*refs):
    a = jnp.concatenate([ref[...] for ref in refs[:-2]], axis=0)
    refs[-1][...] = dot(a, refs[-2][...]).astype(BF16)


def matmul(pieces, b, tile):
    rows = sum(piece.shape[0] for piece in pieces)
    inner = b.shape[0]
    return pl.pallas_call(
        matmul_kernel,
        grid=(b.shape[1] // tile,),
        in_specs=[
            pl.BlockSpec(piece.shape, lambda n: (0, 0), pipeline_mode=pl.Buffered(1)) for piece in pieces
        ]
        + [pl.BlockSpec((inner, tile), lambda n: (0, n))],
        out_specs=pl.BlockSpec((rows, tile), lambda n: (0, n)),
        out_shape=jax.ShapeDtypeStruct((rows, b.shape[1]), BF16),
        compiler_params=params(),
        cost_estimate=cost(5),
        name="matmul",
    )(*pieces, b)


def attend(query, keys, values, allowed):
    scores = dot(query, keys, ((1,), (1,))) * HEAD_DIM ** (-0.5)
    scores = jnp.where(allowed, scores, NEGATIVE)
    peak = jnp.max(scores, axis=-1, keepdims=True)
    weights = jnp.where(allowed, jnp.exp(scores - peak), 0.0)
    probabilities = (weights / jnp.sum(weights, axis=-1, keepdims=True)).astype(BF16)
    return dot(probabilities, values).astype(BF16)


def local_kernel(heads, slots, spots, chunk, sets, bound_ref, places_ref, *refs):
    qkvs, (result_ref, first_ref) = refs[:sets], refs[sets:]
    size = len(slots)
    reach = chunk + WINDOW
    bound = bound_ref[0]
    row = lax.broadcasted_iota(jnp.int32, (chunk, reach), 0)
    col = lax.broadcasted_iota(jnp.int32, (chunk, reach), 1)
    band = (col > row) & (col <= row + WINDOW)
    for slot in range(size):
        k = slots[slot]
        mine, at = spots[k]
        theirs, there = spots[(k - 1) % size]
        base = places_ref[slot]
        query_place = row + base
        key_place = col + (base - WINDOW)
        allowed = band & (key_place >= 0) & ((query_place >= bound) == (key_place >= bound))
        rows = slice(at, at + chunk)
        tail = slice(there + chunk - WINDOW, there + chunk)

        @pl.when(base == 0)
        def _():
            first_ref[...] = qkvs[mine][at : at + WINDOW]

        for head in range(heads):
            lane = head * 3 * HEAD_DIM
            keys, values = [
                jnp.concatenate(
                    [
                        qkvs[theirs][tail, lane + n * HEAD_DIM : lane + (n + 1) * HEAD_DIM],
                        qkvs[mine][rows, lane + n * HEAD_DIM : lane + (n + 1) * HEAD_DIM],
                    ],
                    axis=0,
                )
                for n in (1, 2)
            ]
            result_ref[slot * chunk : (slot + 1) * chunk, head * HEAD_DIM : (head + 1) * HEAD_DIM] = attend(
                qkvs[mine][rows, lane : lane + HEAD_DIM], keys, values, allowed
            )


def local_window(bound, places, slots, spots, chunk, qkvs, heads):
    return pl.pallas_call(
        functools.partial(local_kernel, heads, slots, spots, chunk, len(qkvs)),
        in_specs=[smem(), smem()] + [whole()] * len(qkvs),
        out_specs=[whole()] * 2,
        out_shape=[
            jax.ShapeDtypeStruct((len(slots) * chunk, heads * HEAD_DIM), BF16),
            jax.ShapeDtypeStruct((WINDOW, qkvs[0].shape[1]), BF16),
        ],
        compiler_params=params(),
        cost_estimate=cost(8),
        name="local_window",
    )(bound, places, *qkvs)


def halo_kernel(heads, count, start, info_ref, local_ref, first_ref, halo_ref, weight_ref, result_ref, *fars):
    result_ref[...] = local_ref[...]
    bound, valid_from, spot = info_ref[0], info_ref[1], info_ref[2]
    row = lax.broadcasted_iota(jnp.int32, (WINDOW, 2 * WINDOW), 0)
    col = lax.broadcasted_iota(jnp.int32, (WINDOW, 2 * WINDOW), 1)
    key_place = col - WINDOW
    allowed = (col > row) & (col <= row + WINDOW) & ((row >= bound) == (key_place >= bound))
    allowed = allowed & ((key_place >= 0) | (key_place + count >= valid_from))
    spot = pl.multiple_of(spot, WINDOW)
    for head in range(heads):
        lane = head * 3 * HEAD_DIM
        keys, values = [
            jnp.concatenate(
                [ref[:, lane + n * HEAD_DIM : lane + (n + 1) * HEAD_DIM] for ref in (halo_ref, first_ref)], axis=0
            )
            for n in (1, 2)
        ]
        result_ref[pl.ds(spot, WINDOW), head * HEAD_DIM : (head + 1) * HEAD_DIM] = attend(
            first_ref[:, lane : lane + HEAD_DIM], keys, values, allowed
        )
    split_store(dot(result_ref[start:], weight_ref[...]), fars)


def halo_window(info, near, chunk, far, local, first, halo, weight, heads):
    count = local.shape[0]
    rows = (count - near * chunk) // far
    return pl.pallas_call(
        functools.partial(halo_kernel, heads, count, near * chunk),
        in_specs=[smem()] + [whole()] * 4,
        out_specs=[whole()] * (1 + far),
        out_shape=[jax.ShapeDtypeStruct(local.shape, BF16)]
        + [jax.ShapeDtypeStruct((rows, weight.shape[1]), BF16)] * far,
        compiler_params=params(),
        cost_estimate=cost(4.5),
        name="halo_window",
    )(info, local, first, halo, weight)


def score_kernel(units_count, pieces, lots, tile, order_ref, *refs):
    units, refs = refs[:units_count], refs[units_count:]
    tables, (goal_ref, out_ref, turned_ref, held) = refs[: len(lots) * pieces], refs[len(lots) * pieces :]
    step = pl.program_id(0)
    width = tables[0].shape[1]
    count = goal_ref.shape[1]
    part = 128

    @pl.when(step == 0)
    def _():
        rows = jnp.concatenate([ref[...] for ref in units], axis=0)
        turned_ref[...] = jnp.transpose(rows)
        held[0] = jnp.full((8, count), NEGATIVE, F32)
        held[1] = jnp.zeros((8, count), F32)
        held[2] = jnp.zeros((8, count), F32)

    def run(mine):
        inner = lax.broadcasted_iota(jnp.int32, (part // 8, 8, count), 0) * 8
        inner = inner + lax.broadcasted_iota(jnp.int32, (part // 8, 8, count), 1)
        peak, total, picked = held[0], held[1], held[2]
        sides = [
            turned_ref[pl.ds(pl.multiple_of(order_ref[n] * width, width), width), :] for n in range(pieces)
        ]
        for at in range(0, tile, part):
            logits = None
            for n in range(pieces):
                more = dot(mine[n][at : at + part], sides[n])
                logits = more if logits is None else logits + more
            logits = logits.reshape(part // 8, 8, count)
            goal = (goal_ref[...] - (step * tile + at)).reshape(1, 1, count)
            old = peak
            peak = jnp.maximum(old, jnp.max(logits, axis=0))
            total = total * jnp.exp(old - peak) + jnp.sum(jnp.exp(logits - peak[None]), axis=0)
            picked = picked + jnp.sum(jnp.where(inner == goal, logits, 0.0), axis=0)
        held[0], held[1], held[2] = peak, total, picked

    for lot, (start, stop) in enumerate(lots):
        pl.when((step >= start) & (step < stop))(
            lambda lot=lot: run(tables[lot * pieces : (lot + 1) * pieces])
        )

    @pl.when(step == pl.num_programs(0) - 1)
    def _():
        peak = jnp.max(held[0], axis=0, keepdims=True)
        total = jnp.sum(held[1] * jnp.exp(held[0] - peak), axis=0, keepdims=True)
        picked = jnp.sum(held[2], axis=0, keepdims=True)
        out_ref[...] = jnp.concatenate([peak, total, picked, jnp.zeros((5, count), F32)], axis=0)


def scores(order, units, lots, goal):
    count = goal.shape[1]
    rows = lots[-1][1]
    tile = 1280 if rows % 1280 == 0 else 640
    pieces = len(lots[0][2])
    specs, steps = [], []
    for first, last, tables in lots:
        start, stop = first // tile, last // tile
        steps.append((start, stop))
        for table in tables:
            shift = 0 if table.shape[0] == rows else start
            specs.append(
                pl.BlockSpec(
                    (tile, table.shape[1]),
                    lambda i, start=start, stop=stop, shift=shift: (jnp.clip(i, start, stop - 1) - shift, 0),
                )
            )
    return pl.pallas_call(
        functools.partial(score_kernel, len(units), pieces, steps, tile),
        in_specs=[smem()]
        + [pl.BlockSpec(piece.shape, lambda i: (0, 0), pipeline_mode=pl.Buffered(1)) for piece in units]
        + specs
        + [pl.BlockSpec((1, count), lambda i: (0, 0))],
        out_specs=pl.BlockSpec((8, count), lambda i: (0, 0)),
        grid=(rows // tile,),
        out_shape=jax.ShapeDtypeStruct((8, count), F32),
        scratch_shapes=[pltpu.VMEM((units[0].shape[1], count), BF16), pltpu.VMEM((3, 8, count), F32)],
        compiler_params=params(),
        cost_estimate=cost(14),
        name="scores",
    )(order, *units, *[table for lot in lots for table in lot[2]], goal)


def shards(
    token_ids,
    target_ids,
    doc_start,
    vocab_table,
    norm_gain_one,
    lin_qkv,
    lin_head_gain,
    lin_out,
    norm_gain_two,
    win_qkv,
    win_out,
    final_gain,
):
    head_count = lax.axis_size("head")
    seq_count = lax.axis_size("seq")
    head_index = lax.axis_index("head")
    seq_index = lax.axis_index("seq")
    tok_count = token_ids.shape[0]
    chunk = tok_count // head_count
    vocab_rows = vocab_table.shape[0]
    heads = lin_qkv.shape[1] // (2 * FEAT + HEAD_DIM)
    vocab_first = head_index * vocab_rows
    calls = chunk_order(head_count)
    slots = [k for call in calls for k in call]
    near = 3 if head_count == 4 else 1
    far = 2 if head_count == 4 else head_count - 1
    spots = {}
    for n, call in enumerate(calls):
        for at, k in enumerate(call):
            spots[k] = (n, at * chunk)
    held_at = (head_index + jnp.asarray(slots, jnp.int32)) % head_count
    places = held_at * chunk

    marks = jnp.concatenate([token_ids, jnp.broadcast_to(doc_start, (LANES,))])
    marks = jnp.stack(
        [marks] + [lax.ppermute(marks, "seq", xor_pairs(seq_count, k)) for k in range(1, seq_count)]
    )
    block = jnp.arange(seq_count, dtype=jnp.int32)
    order = seq_index ^ block
    starts = marks[:, tok_count]
    starts = jnp.sum(jnp.where(order[None, :] == block[:, None], starts[None, :], 0), axis=1)
    bound = doc_start.astype(jnp.int32)

    lots = [vocab_rows * 3 // 5, vocab_rows * 2 // 5]
    early, late = vocab_table[: lots[0]], vocab_table[lots[0] :]

    ids = (marks[:, :tok_count] - vocab_first).reshape(seq_count, head_count, chunk)

    def ids_of(k):
        return lax.dynamic_index_in_dim(ids, (head_index + k) % head_count, 1, False).reshape(-1)

    if head_count == 4:
        outer = lookup(ids_of(2), vocab_table, 2)
        inner = lambda: (
            lookup(ids_of(0), vocab_table, 2)
            + lookup(jnp.concatenate([ids_of(1), ids_of(3)]), vocab_table, 4)
        )
    else:
        outer = [lookup(ids_of(k), vocab_table, 1)[0] for k in range(1, head_count)]
        inner = lambda: lookup(ids_of(0), vocab_table, 1)
    found = collect(scatter_rows(outer, inner), seq_count)
    gathered = [found[0]] + [
        lax.ppermute(found[k], "seq", xor_pairs(seq_count, k)) for k in range(1, seq_count)
    ]
    embedded, units = begin(order, norm_gain_one, gathered)

    constants = selectors()
    sets, state = [], None

    def project_call(n, pieces, state):
        first = sum(len(c) for c in calls[:n])
        return project(
            bound,
            places[first : first + len(calls[n])],
            list(range(len(calls[n]))),
            chunk,
            tok_count,
            pieces,
            lin_qkv,
            constants,
            state,
            n == len(calls) - 1,
            heads,
        )

    chunks, made = gather_rows(units, lambda own: project_call(0, [own], None))
    for n, call in enumerate(calls):
        if n:
            made = project_call(n, [piece for k in call for piece in chunks[k]], state)
        sets.append(made[:3])
        state = made[3]
    fqs, fks, vs = zip(*sets)
    states, shares = [], []
    for back in range(1, seq_count):
        states.append(
            lax.ppermute(state, "seq", [(i, i + back) for i in range(seq_count - back)])
        )
        between = (block > seq_index - back) & (block < seq_index)
        broken = jnp.sum(jnp.where(between & (starts != tok_count), 1, 0))
        shares.append(((broken == 0) & (seq_index >= back)).astype(jnp.int32))
    position = list(range(head_count))
    num, den = within(bound, places, position, chunk, fqs, fks, vs, heads)
    mixed, *outer = across(
        bound,
        places,
        jnp.stack(shares),
        position,
        chunk,
        near,
        far,
        fqs,
        num,
        den,
        lin_head_gain.reshape(1, -1),
        lin_out,
        states,
        heads,
    )
    parts = scatter_rows(outer, lambda: near_chunks(mixed, lin_out, near, chunk))
    units, residual = finish(embedded, norm_gain_two, parts, False)

    if seq_count == 4:
        early, _ = lax.optimization_barrier((early, states))
        early = lax.ppermute(early, "seq", xor_pairs(seq_count, 2))
        early_corner = lax.ppermute(early, "seq", xor_pairs(seq_count, 1))
        beside = lax.ppermute(vocab_table, "seq", xor_pairs(seq_count, 1))

    chunks, made = gather_rows(units, lambda own: matmul([own], win_qkv, 3 * HEAD_DIM))
    qkvs = [made]
    for call in calls[1:]:
        qkvs.append(matmul([piece for k in call for piece in chunks[k]], win_qkv, 3 * HEAD_DIM))
    tail = jnp.zeros((WINDOW, win_qkv.shape[1]), BF16)
    for slot, k in enumerate(slots):
        n, at = spots[k]
        tail = jnp.where(
            held_at[slot] == head_count - 1, qkvs[n][at + chunk - WINDOW : at + chunk], tail
        )
    halo = lax.ppermute(tail, "seq", [(i, i + 1) for i in range(seq_count - 1)])
    previous = jnp.sum(jnp.where(block == seq_index - 1, starts, 0))
    valid_from = jnp.where(
        seq_index == 0, tok_count, jnp.where(previous == tok_count, 0, previous)
    ).astype(jnp.int32)
    first_spot = jnp.sum(jnp.where(held_at == 0, jnp.arange(head_count) * chunk, 0)).astype(jnp.int32)
    local, first = local_window(bound, places, slots, spots, chunk, qkvs, heads)
    late, local, halo = lax.optimization_barrier((late, local, halo))
    info = jnp.stack([bound[0], valid_from, first_spot])
    mixed, *outer = halo_window(info, near, chunk, far, local, first, halo, win_out, heads)
    parts = scatter_rows(outer, lambda: near_chunks(mixed, win_out, near, chunk))
    units = finish(residual, final_gain, parts, True)[0]

    chunks, _ = gather_rows(units)
    if seq_count == 4:
        late = lax.ppermute(late, "seq", xor_pairs(seq_count, 2))
        corner, _ = lax.optimization_barrier((late, (chunks[1][0], chunks[-1][0])))
        late_corner = lax.ppermute(corner, "seq", xor_pairs(seq_count, 1))
        lots = [
            (0, lots[0], [vocab_table, beside, early, early_corner]),
            (lots[0], vocab_rows, [vocab_table, beside, late, late_corner]),
        ]
    else:
        lots = [(0, vocab_rows, [lax.all_gather(vocab_table, "seq", axis=1, tiled=True)])]
        order = jnp.zeros((1,), jnp.int32)
    goals = (target_ids - vocab_first).reshape(head_count, chunk)
    found = {}
    for group in [[0, 3], [1, 2]] if head_count == 4 else [[k] for k in range(head_count)]:
        goal = jnp.concatenate(
            [
                lax.dynamic_index_in_dim(goals, (head_index + k) % head_count, 0, False)
                for k in group
            ]
        ).reshape(1, -1)
        triple = scores(order, [piece for k in group for piece in chunks[k]], lots, goal)
        for at, k in enumerate(group):
            found[k] = triple[:3, at * chunk : (at + 1) * chunk]

    shares = jnp.stack([found[0]] + [turned(found[k], k) for k in range(1, head_count)])
    peak = jnp.max(shares[:, 0], axis=0)
    total = jnp.sum(shares[:, 1] * jnp.exp(shares[:, 0] - peak), axis=0)
    return jnp.sum(shares[:, 2], axis=0) - (peak + jnp.log(total))


def solution(mesh):
    return jax.shard_map(
        shards,
        mesh=mesh,
        in_specs=(
            P(("shadow", "seq")),
            P(("shadow", "seq")),
            P(("shadow", "seq")),
            P(("shadow", "head"), "seq"),
            P("shadow"),
            P("shadow", "head"),
            P(("shadow", "head")),
            P(("shadow", "head"), None),
            P("shadow"),
            P("shadow", "head"),
            P(("shadow", "head"), None),
            P("shadow"),
        ),
        out_specs=P(("shadow", "seq", "head")),
        check_vma=False,
    )
```

```python
import functools

import jax
import jax.numpy as jnp
import numpy as np
from jax import lax
from jax.experimental import pallas as pl
from jax.experimental.pallas import tpu as pltpu
from jax.sharding import PartitionSpec as P

FEAT = 16
WINDOW = 64
HEAD_DIM = 128
EPSILON = 1e-05
NEGATIVE = -1e30
LANES = 128
WIDE = 256
STATE_ROWS = 160
BUFFER_ROWS = 176
F32 = jnp.float32
BF16 = jnp.bfloat16
VMEM_BYTES = 56 * 1024 * 1024


def params(**kw):
    return pltpu.CompilerParams(vmem_limit_bytes=VMEM_BYTES, **kw)


def cost(us):
    return pl.CostEstimate(flops=int(us * 6e8), transcendentals=0, bytes_accessed=int(us * 3e6))


def whole():
    return pl.BlockSpec(memory_space=pltpu.VMEM)


def smem():
    return pl.BlockSpec(memory_space=pltpu.SMEM)


def dot(a, b, dims=((1,), (0,))):
    return lax.dot_general(a, b, (dims, ((), ())), preferred_element_type=F32)


def xor_pairs(size, k):
    return [(i, i ^ k) for i in range(size)]


def rms(values, gain):
    factor = lax.rsqrt(jnp.mean(values * values, axis=-1, keepdims=True) + EPSILON)
    return (values * factor * gain.astype(F32)).astype(BF16)


def turned(value, step):
    size = lax.axis_size("head")
    return lax.ppermute(value, "head", [(i, (i + step) % size) for i in range(size)])


def gather_rows(own):
    size = lax.axis_size("head")
    if size != 4:
        full = lax.all_gather(own, "head")
        here = lax.axis_index("head")
        return [[own]] + [
            [lax.dynamic_index_in_dim(full, (here + k) % size, 0, False)] for k in range(1, size)
        ]
    half = own.shape[0] // 2
    before, after = turned(own, 1), turned(own, -1)
    return [[own], [after], [turned(before[:half], 1), turned(after[half:], -1)], [before]]


def scatter_rows(far, near):
    size = lax.axis_size("head")
    if size != 4:
        here = lax.axis_index("head")
        full = jnp.stack([near()[0]] + list(far))
        full = jnp.stack(
            [lax.dynamic_index_in_dim(full, (d - here) % size, 0, False) for d in range(size)]
        )
        return [[lax.psum_scatter(full, "head", scatter_dimension=0, tiled=True)[0]]]
    from_before, from_after = turned(far[0], 1), turned(far[1], -1)
    own_upper, own_lower, next_upper, next_lower, prev_upper, prev_lower = near()
    lower_right, upper_left = turned(next_lower, 1), turned(prev_upper, -1)
    upper_right, lower_left = pass_on(next_upper, from_before, prev_lower, from_after)
    upper_right, lower_left = turned(upper_right, 1), turned(lower_left, -1)
    return [[own_upper, upper_right, upper_left], [own_lower, lower_right, lower_left]]


def pass_on_kernel(next_ref, before_ref, prev_ref, after_ref, right_ref, left_ref):
    right_ref[...] = (next_ref[...].astype(F32) + before_ref[...].astype(F32)).astype(BF16)
    left_ref[...] = (prev_ref[...].astype(F32) + after_ref[...].astype(F32)).astype(BF16)


def pass_on(next_upper, from_before, prev_lower, from_after):
    return pl.pallas_call(
        pass_on_kernel,
        in_specs=[whole()] * 4,
        out_specs=[whole()] * 2,
        out_shape=[jax.ShapeDtypeStruct(next_upper.shape, BF16)] * 2,
        compiler_params=params(),
        cost_estimate=cost(1.5),
        name="pass_on",
    )(next_upper, from_before, prev_lower, from_after)


def chunk_order(size):
    if size == 4:
        return [[0, 1, 3], [2]]
    return [[k] for k in range(size)]


def lookup_kernel(ids_ref, table_ref, *refs):
    outs, total = refs[:-1], refs[-1]
    step = pl.program_id(0)
    tile = table_ref.shape[0]
    count = ids_ref.shape[1]
    ids = jnp.transpose(jnp.broadcast_to(ids_ref[...], (8, count)))[:, 0:1] - step * tile
    hot = (lax.broadcasted_iota(jnp.int32, (count, tile), 1) == ids).astype(F32).astype(BF16)
    found = dot(hot, table_ref[...])

    @pl.when(step == 0)
    def _():
        total[...] = found

    @pl.when(step > 0)
    def _():
        total[...] += found

    @pl.when(step == pl.num_programs(0) - 1)
    def _():
        rows = outs[0].shape[0]
        for n, out in enumerate(outs):
            out[...] = total[n * rows : (n + 1) * rows].astype(BF16)


def lookup(ids, table, pieces):
    count = ids.shape[0]
    rows, width = table.shape
    tile = rows // 5
    return pl.pallas_call(
        lookup_kernel,
        grid=(rows // tile,),
        in_specs=[
            pl.BlockSpec((1, count), lambda i: (0, 0)),
            pl.BlockSpec((tile, width), lambda i: (i, 0)),
        ],
        out_specs=[pl.BlockSpec((count // pieces, width), lambda i: (0, 0))] * pieces,
        out_shape=[jax.ShapeDtypeStruct((count // pieces, width), BF16)] * pieces,
        scratch_shapes=[pltpu.VMEM((count, width), F32)],
        compiler_params=params(),
        cost_estimate=cost(8 * count / 512),
        name="lookup",
    )(ids.reshape(1, count), table)


def gathered_sum(refs, sizes):
    rows, at = [], 0
    for size in sizes:
        total = refs[at][...].astype(F32)
        for ref in refs[at + 1 : at + size]:
            total = total + ref[...].astype(F32)
        rows.append(total)
        at += size
    return rows[0] if len(rows) == 1 else jnp.concatenate(rows, axis=0)


def collect_kernel(sizes, *refs):
    ins, outs = refs[: sum(sizes)], refs[sum(sizes) :]
    rows = outs[0].shape[0]
    total = gathered_sum(ins, sizes)
    for n, out in enumerate(outs):
        out[...] = total[n * rows : (n + 1) * rows].astype(BF16)


def collect(terms, pieces):
    sizes = [len(part) for part in terms]
    parts = [term for part in terms for term in part]
    rows, width = sum(part[0].shape[0] for part in terms), parts[0].shape[1]
    return pl.pallas_call(
        functools.partial(collect_kernel, sizes),
        in_specs=[whole()] * len(parts),
        out_specs=[whole()] * pieces,
        out_shape=[jax.ShapeDtypeStruct((rows // pieces, width), BF16)] * pieces,
        compiler_params=params(),
        cost_estimate=cost(2),
        name="collect",
    )(*parts)


def begin_kernel(pieces, order_ref, gain_ref, *refs):
    ins, (embedded_ref, units_ref, held) = refs[:pieces], refs[pieces:]
    width = ins[0].shape[1]
    for n in range(pieces):
        held[order_ref[n]] = ins[n][...]
    values = jnp.concatenate([held[n] for n in range(pieces)], axis=1)
    embedded_ref[...] = values
    units_ref[...] = rms(values.astype(F32), gain_ref[...])


def begin(order, gain, pieces):
    rows, width = pieces[0].shape
    full = jax.ShapeDtypeStruct((rows, width * len(pieces)), BF16)
    return pl.pallas_call(
        functools.partial(begin_kernel, len(pieces)),
        in_specs=[smem()] + [whole()] * (1 + len(pieces)),
        out_specs=[whole()] * 2,
        out_shape=[full, full],
        scratch_shapes=[pltpu.VMEM((len(pieces), rows, width), BF16)],
        compiler_params=params(),
        cost_estimate=cost(2),
        name="begin",
    )(order, gain.reshape(1, -1), *pieces)


def finish_kernel(sizes, last, residual_ref, gain_ref, *refs):
    parts = sum(sizes)
    total = gathered_sum(refs[:parts], sizes) + residual_ref[...].astype(F32)
    if not last:
        total = total.astype(BF16)
        refs[parts + 1][...] = total
    refs[parts][...] = rms(total.astype(F32), gain_ref[...])


def finish(residual, gain, terms, last):
    full = jax.ShapeDtypeStruct(residual.shape, BF16)
    parts = [term for part in terms for term in part]
    return pl.pallas_call(
        functools.partial(finish_kernel, [len(part) for part in terms], last),
        in_specs=[whole()] * (2 + len(parts)),
        out_specs=[whole()] * (1 if last else 2),
        out_shape=[full] * (1 if last else 2),
        compiler_params=params(),
        cost_estimate=cost(2.5),
        name="finish",
    )(residual, gain.reshape(1, -1), *parts)


def selectors():
    pairs = [(r, s) for r in range(FEAT) for s in range(r, FEAT)]
    picks = np.zeros((2, 2, LANES, WIDE), np.float32)
    extra = np.zeros((3, WIDE), np.float32)
    extra[0:2, 0] = 1.0
    extra[1, 1 : 1 + FEAT] = 1.0
    extra[2] = 1.0
    for kind in range(2):
        first = kind * FEAT
        for r in range(FEAT):
            picks[kind, 0, first + r, 1 + r] = FEAT ** (-0.25)
        for n, (r, s) in enumerate(pairs):
            picks[kind, 0, first + r, 1 + FEAT + n] = FEAT ** (-0.25)
            picks[kind, 1, first + s, 1 + FEAT + n] = FEAT ** (-0.25)
    for n, (r, s) in enumerate(pairs):
        extra[2, 1 + FEAT + n] = 0.5**0.5 if r == s else 1.0
    return jnp.asarray(np.concatenate([picks, picks], axis=2), BF16), jnp.asarray(extra)


def place_column(places_ref, slots, rows):
    inner = lax.broadcasted_iota(jnp.int32, (rows, 1), 0)
    return jnp.concatenate([inner + places_ref[slot] for slot in slots], axis=0)


def place_row(places_ref, slots, rows):
    inner = lax.broadcasted_iota(jnp.int32, (1, rows), 1)
    return jnp.concatenate([inner + places_ref[slot] for slot in slots], axis=1)


def project_kernel(heads, slots, chunk, count, pieces, more, last, bound_ref, places_ref, *refs):
    units = jnp.concatenate([ref[...] for ref in refs[:pieces]], axis=0)
    weight_ref, pick_ref, extra_ref = refs[pieces : pieces + 3]
    fq_ref, fk_ref, v_ref, state_ref = refs[-4:]
    projected = dot(units, weight_ref[...])
    rows, width = projected.shape
    needed = (heads - 1) * LANES + WIDE
    if needed > width:
        projected = jnp.pad(projected, ((0, 0), (0, needed - width)))
    bound = bound_ref[0]
    place = place_column(places_ref, slots, chunk)
    kept = ((place >= bound) | (bound == count)).astype(F32)
    ones = jnp.ones((8, rows), BF16)
    shift = 2 * FEAT
    for head in range(heads):
        part = projected[:, head * LANES : head * LANES + WIDE]
        narrow = part if head == 0 else pltpu.roll(part, WIDE - shift * head, 1)
        narrow = narrow[:, :LANES]
        values = pltpu.roll(part, WIDE - shift * (head + 1), 1)[:, :HEAD_DIM].astype(BF16)
        v_ref[:, head * HEAD_DIM : (head + 1) * HEAD_DIM] = values
        upper = narrow.astype(BF16)
        lower = (narrow - upper.astype(F32)).astype(BF16)
        both = jnp.concatenate([upper, lower], axis=1)
        feats = []
        for kind in range(2):
            one = dot(both, pick_ref[kind, 0]) + extra_ref[0:1]
            two = dot(both, pick_ref[kind, 1]) + extra_ref[1:2]
            feats.append((one * two * extra_ref[2:3]).astype(BF16))
        fq_ref[head] = feats[0]
        fk_ref[head] = feats[1]
        keys = (feats[1].astype(F32) * kept).astype(BF16)
        state = dot(keys, values, ((0,), (0,)))
        total = dot(ones, keys)
        tail = jnp.concatenate([total[0:1, :LANES], total[0:1, LANES:], jnp.zeros((14, LANES), F32)], axis=0)
        state = jnp.concatenate([state[0:STATE_ROWS], tail], axis=0)
        if more:
            state = state + refs[pieces + 3][head]
        state_ref[head] = state.astype(BF16) if last else state


def project(bound, places, slots, chunk, count, pieces, weight, constants, earlier, last, heads):
    rows = sum(piece.shape[0] for piece in pieces)
    extra = [] if earlier is None else [earlier]
    return pl.pallas_call(
        functools.partial(project_kernel, heads, slots, chunk, count, len(pieces), bool(extra), last),
        in_specs=[smem(), smem()] + [whole()] * (len(pieces) + 3 + len(extra)),
        out_specs=[whole()] * 4,
        out_shape=[
            jax.ShapeDtypeStruct((heads, rows, WIDE), BF16),
            jax.ShapeDtypeStruct((heads, rows, WIDE), BF16),
            jax.ShapeDtypeStruct((rows, heads * HEAD_DIM), BF16),
            jax.ShapeDtypeStruct((heads, BUFFER_ROWS, HEAD_DIM), BF16 if last else F32),
        ],
        compiler_params=params(),
        cost_estimate=cost(5),
        name="project",
    )(bound, places, *pieces, weight, *constants, *extra)


def within_kernel(heads, slots, chunk, sets, bound_ref, places_ref, *refs):
    fqs, fks, vs = refs[:sets], refs[sets : 2 * sets], refs[2 * sets : 3 * sets]
    num_ref, den_ref = refs[3 * sets :]
    bound = bound_ref[0]
    row = place_column(places_ref, slots, chunk)
    col = place_row(places_ref, slots, chunk)
    allowed = (row >= col) & ((row >= bound) == (col >= bound))
    for head in range(heads):
        query = jnp.concatenate([ref[head] for ref in fqs], axis=0)
        keys = jnp.concatenate([ref[head] for ref in fks], axis=0)
        values = jnp.concatenate(
            [ref[:, head * HEAD_DIM : (head + 1) * HEAD_DIM] for ref in vs], axis=0
        )
        weights = dot(query, keys, ((1,), (1,)))
        weights = jnp.where(allowed, weights, 0.0)
        den_ref[head] = jnp.broadcast_to(
            jnp.sum(weights, axis=-1, keepdims=True), (row.shape[0], 8)
        )
        num_ref[head] = dot(weights.astype(BF16), values)


def within(bound, places, slots, chunk, fqs, fks, vs, heads):
    count = len(slots) * chunk
    return pl.pallas_call(
        functools.partial(within_kernel, heads, slots, chunk, len(fqs)),
        in_specs=[smem(), smem()] + [whole()] * (3 * len(fqs)),
        out_specs=[whole()] * 2,
        out_shape=[
            jax.ShapeDtypeStruct((heads, count, HEAD_DIM), F32),
            jax.ShapeDtypeStruct((heads, count, 8), F32),
        ],
        compiler_params=params(),
        cost_estimate=cost(4.5),
        name="within",
    )(bound, places, *fqs, *fks, *vs)


def split_store(total, refs):
    rows = refs[0].shape[0]
    for n, ref in enumerate(refs):
        ref[...] = total[n * rows : (n + 1) * rows].astype(BF16)


def across_kernel(heads, slots, chunk, sets, earlier, near, bound_ref, places_ref, share_ref, *refs):
    fqs, refs = refs[:sets], refs[sets:]
    num_ref, den_ref, gain_ref, weight_ref = refs[:4]
    states, refs = refs[4 : 4 + earlier], refs[4 + earlier :]
    mixed_ref, fars = refs[0], refs[1:]
    bound = bound_ref[0]
    before = (place_column(places_ref, slots, chunk) < bound).astype(F32)
    for head in range(heads):
        carried = jnp.zeros((BUFFER_ROWS, HEAD_DIM), F32)
        for n in range(earlier):
            carried = carried + jnp.where(share_ref[n] > 0, states[n][head].astype(F32), 0.0)
        state = jnp.concatenate(
            [carried[0:STATE_ROWS], jnp.zeros((WIDE - STATE_ROWS, HEAD_DIM), F32)], axis=0
        ).astype(BF16)
        total = jnp.concatenate(
            [carried[STATE_ROWS : STATE_ROWS + 1], carried[STATE_ROWS + 1 : STATE_ROWS + 2]], axis=1
        )
        query = jnp.concatenate([ref[head] for ref in fqs], axis=0)
        numerator = num_ref[head] + before * dot(query, state)
        more = jnp.sum(query.astype(F32) * total, axis=-1, keepdims=True)
        denominator = den_ref[head][:, 0:1] + before * more
        lanes = slice(head * HEAD_DIM, (head + 1) * HEAD_DIM)
        mixed_ref[:, lanes] = (numerator / denominator * gain_ref[:, lanes].astype(F32)).astype(BF16)
    split_store(dot(mixed_ref[near * chunk :], weight_ref[...]), fars)


def across(bound, places, share, slots, chunk, near, far, fqs, num, den, gain, weight, states, heads):
    count = len(slots) * chunk
    rows = (count - near * chunk) // far
    return pl.pallas_call(
        functools.partial(across_kernel, heads, slots, chunk, len(fqs), len(states), near),
        in_specs=[smem()] * 3 + [whole()] * (len(fqs) + 4 + len(states)),
        out_specs=[whole()] * (1 + far),
        out_shape=[jax.ShapeDtypeStruct((count, heads * HEAD_DIM), BF16)]
        + [jax.ShapeDtypeStruct((rows, weight.shape[1]), BF16)] * far,
        compiler_params=params(),
        cost_estimate=cost(4.5),
        name="across",
    )(bound, places, share, *fqs, num, den, gain, weight, *states)


def near_kernel(rows, mixed_ref, weight_ref, *outs):
    split_store(dot(mixed_ref[0:rows], weight_ref[...]), outs)


def near_chunks(mixed, weight, near, chunk):
    pieces = 2 * near if near > 1 else 1
    rows = near * chunk
    return pl.pallas_call(
        functools.partial(near_kernel, rows),
        in_specs=[whole()] * 2,
        out_specs=[whole()] * pieces,
        out_shape=[jax.ShapeDtypeStruct((rows // pieces, weight.shape[1]), BF16)] * pieces,
        compiler_params=params(),
        cost_estimate=cost(4),
        name="near",
    )(mixed, weight)


def matmul_kernel(*refs):
    a = jnp.concatenate([ref[...] for ref in refs[:-2]], axis=0)
    refs[-1][...] = dot(a, refs[-2][...]).astype(BF16)


def matmul(pieces, b, tile):
    rows = sum(piece.shape[0] for piece in pieces)
    inner = b.shape[0]
    return pl.pallas_call(
        matmul_kernel,
        grid=(b.shape[1] // tile,),
        in_specs=[
            pl.BlockSpec(piece.shape, lambda n: (0, 0), pipeline_mode=pl.Buffered(1)) for piece in pieces
        ]
        + [pl.BlockSpec((inner, tile), lambda n: (0, n))],
        out_specs=pl.BlockSpec((rows, tile), lambda n: (0, n)),
        out_shape=jax.ShapeDtypeStruct((rows, b.shape[1]), BF16),
        compiler_params=params(),
        cost_estimate=cost(5),
        name="matmul",
    )(*pieces, b)


def attend(queries, keys, values, allowed):
    rows = queries[0].shape[0]
    scores = jnp.concatenate(
        [dot(q, k, ((1,), (1,))) for q, k in zip(queries, keys)], axis=0
    ) * HEAD_DIM ** (-0.5)
    allowed = jnp.concatenate([allowed.astype(F32)] * len(queries), axis=0) > 0
    scores = jnp.where(allowed, scores, NEGATIVE)
    peak = jnp.max(scores, axis=-1, keepdims=True)
    weights = jnp.where(allowed, jnp.exp(scores - peak), 0.0)
    probabilities = (weights * (1.0 / jnp.sum(weights, axis=-1, keepdims=True))).astype(BF16)
    return jnp.concatenate(
        [
            dot(probabilities[n * rows : (n + 1) * rows], value).astype(BF16)
            for n, value in enumerate(values)
        ],
        axis=1,
    )


def local_kernel(heads, slots, spots, chunk, sets, bound_ref, places_ref, *refs):
    qkvs, (result_ref, first_ref) = refs[:sets], refs[sets:]
    size = len(slots)
    reach = chunk + WINDOW
    bound = bound_ref[0]
    row = lax.broadcasted_iota(jnp.int32, (chunk, reach), 0)
    col = lax.broadcasted_iota(jnp.int32, (chunk, reach), 1)
    band = (col > row) & (col <= row + WINDOW)
    for slot in range(size):
        k = slots[slot]
        mine, at = spots[k]
        theirs, there = spots[(k - 1) % size]
        base = places_ref[slot]
        query_place = row + base
        key_place = col + (base - WINDOW)
        allowed = band & (key_place >= 0) & ((query_place >= bound) == (key_place >= bound))
        rows = slice(at, at + chunk)
        tail = slice(there + chunk - WINDOW, there + chunk)

        @pl.when(base == 0)
        def _():
            first_ref[...] = qkvs[mine][at : at + WINDOW]

        queries, keys, values = [], [], []
        for head in range(heads):
            lane = head * 3 * HEAD_DIM
            queries.append(qkvs[mine][rows, lane : lane + HEAD_DIM])
            for n, held in ((1, keys), (2, values)):
                lanes = slice(lane + n * HEAD_DIM, lane + (n + 1) * HEAD_DIM)
                held.append(jnp.concatenate([qkvs[theirs][tail, lanes], qkvs[mine][rows, lanes]], axis=0))
        result_ref[slot * chunk : (slot + 1) * chunk] = attend(queries, keys, values, allowed)


def local_window(bound, places, slots, spots, chunk, qkvs, heads):
    return pl.pallas_call(
        functools.partial(local_kernel, heads, slots, spots, chunk, len(qkvs)),
        in_specs=[smem(), smem()] + [whole()] * len(qkvs),
        out_specs=[whole()] * 2,
        out_shape=[
            jax.ShapeDtypeStruct((len(slots) * chunk, heads * HEAD_DIM), BF16),
            jax.ShapeDtypeStruct((WINDOW, qkvs[0].shape[1]), BF16),
        ],
        compiler_params=params(),
        cost_estimate=cost(8),
        name="local_window",
    )(bound, places, *qkvs)


def halo_kernel(heads, count, start, info_ref, local_ref, first_ref, halo_ref, weight_ref, result_ref, *fars):
    result_ref[...] = local_ref[...]
    bound, valid_from, spot = info_ref[0], info_ref[1], info_ref[2]
    row = lax.broadcasted_iota(jnp.int32, (WINDOW, 2 * WINDOW), 0)
    col = lax.broadcasted_iota(jnp.int32, (WINDOW, 2 * WINDOW), 1)
    key_place = col - WINDOW
    allowed = (col > row) & (col <= row + WINDOW) & ((row >= bound) == (key_place >= bound))
    allowed = allowed & ((key_place >= 0) | (key_place + count >= valid_from))
    spot = pl.multiple_of(spot, WINDOW)
    queries, keys, values = [], [], []
    for head in range(heads):
        lane = head * 3 * HEAD_DIM
        queries.append(first_ref[:, lane : lane + HEAD_DIM])
        for n, held in ((1, keys), (2, values)):
            lanes = slice(lane + n * HEAD_DIM, lane + (n + 1) * HEAD_DIM)
            held.append(jnp.concatenate([halo_ref[:, lanes], first_ref[:, lanes]], axis=0))
    result_ref[pl.ds(spot, WINDOW), :] = attend(queries, keys, values, allowed)
    split_store(dot(result_ref[start:], weight_ref[...]), fars)


def halo_window(info, near, chunk, far, local, first, halo, weight, heads):
    count = local.shape[0]
    rows = (count - near * chunk) // far
    return pl.pallas_call(
        functools.partial(halo_kernel, heads, count, near * chunk),
        in_specs=[smem()] + [whole()] * 4,
        out_specs=[whole()] * (1 + far),
        out_shape=[jax.ShapeDtypeStruct(local.shape, BF16)]
        + [jax.ShapeDtypeStruct((rows, weight.shape[1]), BF16)] * far,
        compiler_params=params(),
        cost_estimate=cost(4.5),
        name="halo_window",
    )(info, local, first, halo, weight)


def score_kernel(units_count, pieces, lots, tile, order_ref, *refs):
    units, refs = refs[:units_count], refs[units_count:]
    tables, (goal_ref, out_ref, turned_ref, held) = refs[: len(lots) * pieces], refs[len(lots) * pieces :]
    step = pl.program_id(0)
    width = tables[0].shape[1]
    count = goal_ref.shape[1]
    part = 128

    @pl.when(step == 0)
    def _():
        rows = jnp.concatenate([ref[...] for ref in units], axis=0)
        turned_ref[...] = jnp.transpose(rows)
        held[0] = jnp.full((8, count), NEGATIVE, F32)
        held[1] = jnp.zeros((8, count), F32)
        held[2] = jnp.zeros((8, count), F32)

    def run(mine):
        inner = lax.broadcasted_iota(jnp.int32, (part // 8, 8, count), 0) * 8
        inner = inner + lax.broadcasted_iota(jnp.int32, (part // 8, 8, count), 1)
        peak, total, picked = held[0], held[1], held[2]
        sides = [
            turned_ref[pl.ds(pl.multiple_of(order_ref[n] * width, width), width), :] for n in range(pieces)
        ]
        for at in range(0, tile, part):
            logits = None
            for n in range(pieces):
                more = dot(mine[n][at : at + part], sides[n])
                logits = more if logits is None else logits + more
            logits = logits.reshape(part // 8, 8, count)
            goal = (goal_ref[...] - (step * tile + at)).reshape(1, 1, count)
            old = peak
            peak = jnp.maximum(old, jnp.max(logits, axis=0))
            total = total * jnp.exp(old - peak) + jnp.sum(jnp.exp(logits - peak[None]), axis=0)
            picked = picked + jnp.sum(jnp.where(inner == goal, logits, 0.0), axis=0)
        held[0], held[1], held[2] = peak, total, picked

    for lot, (start, stop) in enumerate(lots):
        pl.when((step >= start) & (step < stop))(
            lambda lot=lot: run(tables[lot * pieces : (lot + 1) * pieces])
        )

    @pl.when(step == pl.num_programs(0) - 1)
    def _():
        peak = jnp.max(held[0], axis=0, keepdims=True)
        total = jnp.sum(held[1] * jnp.exp(held[0] - peak), axis=0, keepdims=True)
        picked = jnp.sum(held[2], axis=0, keepdims=True)
        out_ref[...] = jnp.concatenate([peak, total, picked, jnp.zeros((5, count), F32)], axis=0)


def scores(order, units, lots, goal):
    count = goal.shape[1]
    rows = lots[-1][1]
    tile = 640
    pieces = len(lots[0][2])
    specs, steps = [], []
    for first, last, tables in lots:
        start, stop = first // tile, last // tile
        steps.append((start, stop))
        for table in tables:
            shift = 0 if table.shape[0] == rows else start
            specs.append(
                pl.BlockSpec(
                    (tile, table.shape[1]),
                    lambda i, start=start, stop=stop, shift=shift: (jnp.clip(i, start, stop - 1) - shift, 0),
                )
            )
    return pl.pallas_call(
        functools.partial(score_kernel, len(units), pieces, steps, tile),
        in_specs=[smem()]
        + [pl.BlockSpec(piece.shape, lambda i: (0, 0), pipeline_mode=pl.Buffered(1)) for piece in units]
        + specs
        + [pl.BlockSpec((1, count), lambda i: (0, 0))],
        out_specs=pl.BlockSpec((8, count), lambda i: (0, 0)),
        grid=(rows // tile,),
        out_shape=jax.ShapeDtypeStruct((8, count), F32),
        scratch_shapes=[pltpu.VMEM((units[0].shape[1], count), BF16), pltpu.VMEM((3, 8, count), F32)],
        compiler_params=params(),
        cost_estimate=cost(20),
        name="scores",
    )(order, *units, *[table for lot in lots for table in lot[2]], goal)


def shards(
    token_ids,
    target_ids,
    doc_start,
    vocab_table,
    norm_gain_one,
    lin_qkv,
    lin_head_gain,
    lin_out,
    norm_gain_two,
    win_qkv,
    win_out,
    final_gain,
):
    head_count = lax.axis_size("head")
    seq_count = lax.axis_size("seq")
    head_index = lax.axis_index("head")
    seq_index = lax.axis_index("seq")
    tok_count = token_ids.shape[0]
    chunk = tok_count // head_count
    vocab_rows = vocab_table.shape[0]
    heads = lin_qkv.shape[1] // (2 * FEAT + HEAD_DIM)
    vocab_first = head_index * vocab_rows
    calls = chunk_order(head_count)
    slots = [k for call in calls for k in call]
    near = 3 if head_count == 4 else 1
    far = 2 if head_count == 4 else head_count - 1
    spots = {}
    for n, call in enumerate(calls):
        for at, k in enumerate(call):
            spots[k] = (n, at * chunk)
    held_at = (head_index + jnp.asarray(slots, jnp.int32)) % head_count
    places = held_at * chunk

    marks = jnp.concatenate([token_ids, jnp.broadcast_to(doc_start, (LANES,))])
    marks = jnp.stack(
        [marks] + [lax.ppermute(marks, "seq", xor_pairs(seq_count, k)) for k in range(1, seq_count)]
    )
    block = jnp.arange(seq_count, dtype=jnp.int32)
    order = seq_index ^ block
    starts = marks[:, tok_count]
    starts = jnp.sum(jnp.where(order[None, :] == block[:, None], starts[None, :], 0), axis=1)
    bound = doc_start.astype(jnp.int32)

    marks_at = [0, vocab_rows // 5, vocab_rows * 3 // 5, vocab_rows]
    lots = [vocab_table[i:j] for i, j in zip(marks_at[:-1], marks_at[1:])]

    ids = (marks[:, :tok_count] - vocab_first).reshape(seq_count, head_count, chunk)

    def ids_of(k):
        return lax.dynamic_index_in_dim(ids, (head_index + k) % head_count, 1, False).reshape(-1)

    if head_count == 4:
        outer = lookup(ids_of(2), vocab_table, 2)
        inner = lambda: (
            lookup(ids_of(0), vocab_table, 2)
            + lookup(jnp.concatenate([ids_of(1), ids_of(3)]), vocab_table, 4)
        )
    else:
        outer = [lookup(ids_of(k), vocab_table, 1)[0] for k in range(1, head_count)]
        inner = lambda: lookup(ids_of(0), vocab_table, 1)
    found, lots[:2] = lax.optimization_barrier((scatter_rows(outer, inner), lots[:2]))
    found = collect(found, seq_count)
    gathered = [found[0]] + [
        lax.ppermute(found[k], "seq", xor_pairs(seq_count, k)) for k in range(1, seq_count)
    ]
    lots[0], gathered = lax.optimization_barrier((lots[0], gathered))
    embedded, units = begin(order, norm_gain_one, gathered)
    across_x, corners = [None] * 3, [None] * 3

    constants = selectors()
    sets, state = [], None

    def project_call(n, pieces, state):
        first = sum(len(c) for c in calls[:n])
        return project(
            bound,
            places[first : first + len(calls[n])],
            list(range(len(calls[n]))),
            chunk,
            tok_count,
            pieces,
            lin_qkv,
            constants,
            state,
            n == len(calls) - 1,
            heads,
        )

    chunks = gather_rows(units)
    if seq_count == 4:
        across_x[0] = lax.ppermute(lots[0], "seq", xor_pairs(seq_count, 2))
        corners[0] = lax.ppermute(across_x[0], "seq", xor_pairs(seq_count, 1))
    for n, call in enumerate(calls):
        made = project_call(n, [piece for k in call for piece in chunks[k]], state)
        sets.append(made[:3])
        state = made[3]
    fqs, fks, vs = zip(*sets)
    if seq_count == 4:
        state, across_x[0] = lax.optimization_barrier((state, across_x[0]))
    states, shares = [], []
    for back in range(1, seq_count):
        states.append(
            lax.ppermute(state, "seq", [(i, i + back) for i in range(seq_count - back)])
        )
        between = (block > seq_index - back) & (block < seq_index)
        broken = jnp.sum(jnp.where(between & (starts != tok_count), 1, 0))
        shares.append(((broken == 0) & (seq_index >= back)).astype(jnp.int32))
    position = list(range(head_count))
    num, den = within(bound, places, position, chunk, fqs, fks, vs, heads)
    mixed, *outer = across(
        bound,
        places,
        jnp.stack(shares),
        position,
        chunk,
        near,
        far,
        fqs,
        num,
        den,
        lin_head_gain.reshape(1, -1),
        lin_out,
        states,
        heads,
    )
    parts = scatter_rows(outer, lambda: near_chunks(mixed, lin_out, near, chunk))
    parts, lots[2] = lax.optimization_barrier((parts, lots[2]))
    units, residual = finish(embedded, norm_gain_two, parts, False)

    if seq_count == 4:
        lots[1], _ = lax.optimization_barrier((lots[1], states))
        across_x[1] = lax.ppermute(lots[1], "seq", xor_pairs(seq_count, 2))
        corners[1] = lax.ppermute(across_x[1], "seq", xor_pairs(seq_count, 1))
        beside = lax.ppermute(vocab_table, "seq", xor_pairs(seq_count, 1))

    chunks = gather_rows(units)
    qkvs = []
    for call in calls:
        qkvs.append(matmul([piece for k in call for piece in chunks[k]], win_qkv, 3 * HEAD_DIM))
    tail = jnp.zeros((WINDOW, win_qkv.shape[1]), BF16)
    for slot, k in enumerate(slots):
        n, at = spots[k]
        tail = jnp.where(
            held_at[slot] == head_count - 1, qkvs[n][at + chunk - WINDOW : at + chunk], tail
        )
    if seq_count == 4:
        tail, across_x[1] = lax.optimization_barrier((tail, across_x[1]))
    halo = lax.ppermute(tail, "seq", [(i, i + 1) for i in range(seq_count - 1)])
    previous = jnp.sum(jnp.where(block == seq_index - 1, starts, 0))
    valid_from = jnp.where(
        seq_index == 0, tok_count, jnp.where(previous == tok_count, 0, previous)
    ).astype(jnp.int32)
    first_spot = jnp.sum(jnp.where(held_at == 0, jnp.arange(head_count) * chunk, 0)).astype(jnp.int32)
    local, first = local_window(bound, places, slots, spots, chunk, qkvs, heads)
    lots[2], local, halo = lax.optimization_barrier((lots[2], local, halo))
    info = jnp.stack([bound[0], valid_from, first_spot])
    mixed, *outer = halo_window(info, near, chunk, far, local, first, halo, win_out, heads)
    parts = scatter_rows(outer, lambda: near_chunks(mixed, win_out, near, chunk))
    units = finish(residual, final_gain, parts, True)[0]

    chunks = gather_rows(units)
    if seq_count == 4:
        across_x[2] = lax.ppermute(lots[2], "seq", xor_pairs(seq_count, 2))
        corner, _ = lax.optimization_barrier((across_x[2], (chunks[1][0], chunks[-1][0])))
        corners[2] = lax.ppermute(corner, "seq", xor_pairs(seq_count, 1))
        lots = [
            (marks_at[n], marks_at[n + 1], [vocab_table, beside, across_x[n], corners[n]])
            for n in range(3)
        ]
    else:
        lots = [(0, vocab_rows, [lax.all_gather(vocab_table, "seq", axis=1, tiled=True)])]
        order = jnp.zeros((1,), jnp.int32)
    goals = (target_ids - vocab_first).reshape(head_count, chunk)
    goal = jnp.concatenate(
        [lax.dynamic_index_in_dim(goals, (head_index + k) % head_count, 0, False) for k in slots]
    ).reshape(1, -1)
    triple = scores(order, [piece for k in slots for piece in chunks[k]], lots, goal)
    found = {k: triple[:3, at * chunk : (at + 1) * chunk] for at, k in enumerate(slots)}

    shares = jnp.stack([found[0]] + [turned(found[k], k) for k in range(1, head_count)])
    peak = jnp.max(shares[:, 0], axis=0)
    total = jnp.sum(shares[:, 1] * jnp.exp(shares[:, 0] - peak), axis=0)
    return jnp.sum(shares[:, 2], axis=0) - (peak + jnp.log(total))


def solution(mesh):
    return jax.shard_map(
        shards,
        mesh=mesh,
        in_specs=(
            P(("shadow", "seq")),
            P(("shadow", "seq")),
            P(("shadow", "seq")),
            P(("shadow", "head"), "seq"),
            P("shadow"),
            P("shadow", "head"),
            P(("shadow", "head")),
            P(("shadow", "head"), None),
            P("shadow"),
            P("shadow", "head"),
            P(("shadow", "head"), None),
            P("shadow"),
        ),
        out_specs=P(("shadow", "seq", "head")),
        check_vma=False,
    )
```

```python
import functools

import jax
import jax.numpy as jnp
import numpy as np
from jax import lax
from jax.experimental import pallas as pl
from jax.experimental.pallas import tpu as pltpu
from jax.sharding import PartitionSpec as P

FEAT = 16
WINDOW = 64
HEAD_DIM = 128
EPSILON = 1e-05
NEGATIVE = -1e30
LANES = 128
WIDE = 256
STATE_ROWS = 160
BUFFER_ROWS = 176
F32 = jnp.float32
BF16 = jnp.bfloat16
VMEM_BYTES = 56 * 1024 * 1024


def params(**kw):
    return pltpu.CompilerParams(vmem_limit_bytes=VMEM_BYTES, **kw)


def cost(us):
    return pl.CostEstimate(flops=int(us * 6e8), transcendentals=0, bytes_accessed=int(us * 3e6))


def whole():
    return pl.BlockSpec(memory_space=pltpu.VMEM)


def smem():
    return pl.BlockSpec(memory_space=pltpu.SMEM)


def dot(a, b, dims=((1,), (0,))):
    return lax.dot_general(a, b, (dims, ((), ())), preferred_element_type=F32)


def xor_pairs(size, k):
    return [(i, i ^ k) for i in range(size)]


def rms(values, gain):
    factor = lax.rsqrt(jnp.mean(values * values, axis=-1, keepdims=True) + EPSILON)
    return (values * factor * gain.astype(F32)).astype(BF16)


def turned(value, step):
    size = lax.axis_size("head")
    return lax.ppermute(value, "head", [(i, (i + step) % size) for i in range(size)])


def gather_rows(own):
    size = lax.axis_size("head")
    if size != 4:
        full = lax.all_gather(own, "head")
        here = lax.axis_index("head")
        return [[own]] + [
            [lax.dynamic_index_in_dim(full, (here + k) % size, 0, False)] for k in range(1, size)
        ]
    half = own.shape[0] // 2
    before, after = turned(own, 1), turned(own, -1)
    return [[own], [after], [turned(before[:half], 1), turned(after[half:], -1)], [before]]


def scatter_rows(far, near):
    size = lax.axis_size("head")
    if size != 4:
        here = lax.axis_index("head")
        full = jnp.stack([near()[0]] + list(far))
        full = jnp.stack(
            [lax.dynamic_index_in_dim(full, (d - here) % size, 0, False) for d in range(size)]
        )
        return [[lax.psum_scatter(full, "head", scatter_dimension=0, tiled=True)[0]]]
    from_before, from_after = turned(far[0], 1), turned(far[1], -1)
    own_upper, own_lower, next_upper, next_lower, prev_upper, prev_lower = near()
    lower_right, upper_left = turned(next_lower, 1), turned(prev_upper, -1)
    upper_right, lower_left = pass_on(next_upper, from_before, prev_lower, from_after)
    upper_right, lower_left = turned(upper_right, 1), turned(lower_left, -1)
    return [[own_upper, upper_right, upper_left], [own_lower, lower_right, lower_left]]


def pass_on_kernel(next_ref, before_ref, prev_ref, after_ref, right_ref, left_ref):
    right_ref[...] = (next_ref[...].astype(F32) + before_ref[...].astype(F32)).astype(BF16)
    left_ref[...] = (prev_ref[...].astype(F32) + after_ref[...].astype(F32)).astype(BF16)


def pass_on(next_upper, from_before, prev_lower, from_after):
    return pl.pallas_call(
        pass_on_kernel,
        in_specs=[whole()] * 4,
        out_specs=[whole()] * 2,
        out_shape=[jax.ShapeDtypeStruct(next_upper.shape, BF16)] * 2,
        compiler_params=params(),
        cost_estimate=cost(1.5),
        name="pass_on",
    )(next_upper, from_before, prev_lower, from_after)


def chunk_order(size):
    if size == 4:
        return [[0, 1, 3], [2]]
    return [[k] for k in range(size)]


def lookup_kernel(lots, ids_ref, table_ref, *refs):
    outs, copies, total = refs[: -1 - len(lots)], refs[-1 - len(lots) : -1], refs[-1]
    step = pl.program_id(0)
    for (start, stop), copy in zip(lots, copies):

        @pl.when((step >= start) & (step < stop))
        def _():
            copy[...] = table_ref[...]

    tile = table_ref.shape[0]
    count = ids_ref.shape[1]
    ids = jnp.transpose(jnp.broadcast_to(ids_ref[...], (8, count)))[:, 0:1] - step * tile
    hot = (lax.broadcasted_iota(jnp.int32, (count, tile), 1) == ids).astype(F32).astype(BF16)
    found = dot(hot, table_ref[...])

    @pl.when(step == 0)
    def _():
        total[...] = found

    @pl.when(step > 0)
    def _():
        total[...] += found

    @pl.when(step == pl.num_programs(0) - 1)
    def _():
        rows = outs[0].shape[0]
        for n, out in enumerate(outs):
            out[...] = total[n * rows : (n + 1) * rows].astype(BF16)


TABLE_STEPS = 5


def lookup(ids, table, pieces, lots=()):
    count = ids.shape[0]
    rows, width = table.shape
    tile = rows // TABLE_STEPS
    return pl.pallas_call(
        functools.partial(lookup_kernel, lots),
        grid=(TABLE_STEPS,),
        in_specs=[
            pl.BlockSpec((1, count), lambda i: (0, 0)),
            pl.BlockSpec((tile, width), lambda i: (i, 0)),
        ],
        out_specs=[pl.BlockSpec((count // pieces, width), lambda i: (0, 0))] * pieces
        + [
            pl.BlockSpec((tile, width), lambda i, start=start, stop=stop: (jnp.clip(i, start, stop - 1) - start, 0))
            for start, stop in lots
        ],
        out_shape=[jax.ShapeDtypeStruct((count // pieces, width), BF16)] * pieces
        + [jax.ShapeDtypeStruct(((stop - start) * tile, width), BF16) for start, stop in lots],
        scratch_shapes=[pltpu.VMEM((count, width), F32)],
        compiler_params=params(),
        cost_estimate=cost(8 * count / 512),
        name="lookup",
    )(ids.reshape(1, count), table)


def gathered_sum(refs, sizes):
    rows, at = [], 0
    for size in sizes:
        total = refs[at][...].astype(F32)
        for ref in refs[at + 1 : at + size]:
            total = total + ref[...].astype(F32)
        rows.append(total)
        at += size
    return rows[0] if len(rows) == 1 else jnp.concatenate(rows, axis=0)


def collect_kernel(sizes, *refs):
    ins, outs = refs[: sum(sizes)], refs[sum(sizes) :]
    rows = outs[0].shape[0]
    total = gathered_sum(ins, sizes)
    for n, out in enumerate(outs):
        out[...] = total[n * rows : (n + 1) * rows].astype(BF16)


def collect(terms, pieces):
    sizes = [len(part) for part in terms]
    parts = [term for part in terms for term in part]
    rows, width = sum(part[0].shape[0] for part in terms), parts[0].shape[1]
    return pl.pallas_call(
        functools.partial(collect_kernel, sizes),
        in_specs=[whole()] * len(parts),
        out_specs=[whole()] * pieces,
        out_shape=[jax.ShapeDtypeStruct((rows // pieces, width), BF16)] * pieces,
        compiler_params=params(),
        cost_estimate=cost(2),
        name="collect",
    )(*parts)


def begin_kernel(pieces, order_ref, gain_ref, *refs):
    ins, (embedded_ref, units_ref, held) = refs[:pieces], refs[pieces:]
    width = ins[0].shape[1]
    for n in range(pieces):
        held[order_ref[n]] = ins[n][...]
    values = jnp.concatenate([held[n] for n in range(pieces)], axis=1)
    embedded_ref[...] = values
    units_ref[...] = rms(values.astype(F32), gain_ref[...])


def begin(order, gain, pieces):
    rows, width = pieces[0].shape
    full = jax.ShapeDtypeStruct((rows, width * len(pieces)), BF16)
    return pl.pallas_call(
        functools.partial(begin_kernel, len(pieces)),
        in_specs=[smem()] + [whole()] * (1 + len(pieces)),
        out_specs=[whole()] * 2,
        out_shape=[full, full],
        scratch_shapes=[pltpu.VMEM((len(pieces), rows, width), BF16)],
        compiler_params=params(),
        cost_estimate=cost(2),
        name="begin",
    )(order, gain.reshape(1, -1), *pieces)


def finish_kernel(sizes, last, residual_ref, gain_ref, *refs):
    parts = sum(sizes)
    total = gathered_sum(refs[:parts], sizes) + residual_ref[...].astype(F32)
    if not last:
        total = total.astype(BF16)
        refs[parts + 1][...] = total
    refs[parts][...] = rms(total.astype(F32), gain_ref[...])


def finish(residual, gain, terms, last):
    full = jax.ShapeDtypeStruct(residual.shape, BF16)
    parts = [term for part in terms for term in part]
    return pl.pallas_call(
        functools.partial(finish_kernel, [len(part) for part in terms], last),
        in_specs=[whole()] * (2 + len(parts)),
        out_specs=[whole()] * (1 if last else 2),
        out_shape=[full] * (1 if last else 2),
        compiler_params=params(),
        cost_estimate=cost(2.5),
        name="finish",
    )(residual, gain.reshape(1, -1), *parts)


def selectors():
    pairs = [(r, s) for r in range(FEAT) for s in range(r, FEAT)]
    picks = np.zeros((2, 2, LANES, WIDE), np.float32)
    extra = np.zeros((3, WIDE), np.float32)
    extra[0:2, 0] = 1.0
    extra[1, 1 : 1 + FEAT] = 1.0
    extra[2] = 1.0
    for kind in range(2):
        first = kind * FEAT
        for r in range(FEAT):
            picks[kind, 0, first + r, 1 + r] = FEAT ** (-0.25)
        for n, (r, s) in enumerate(pairs):
            picks[kind, 0, first + r, 1 + FEAT + n] = FEAT ** (-0.25)
            picks[kind, 1, first + s, 1 + FEAT + n] = FEAT ** (-0.25)
    for n, (r, s) in enumerate(pairs):
        extra[2, 1 + FEAT + n] = 0.5**0.5 if r == s else 1.0
    return jnp.asarray(np.concatenate([picks, picks], axis=2), BF16), jnp.asarray(extra)


def place_column(places_ref, slots, rows):
    inner = lax.broadcasted_iota(jnp.int32, (rows, 1), 0)
    return jnp.concatenate([inner + places_ref[slot] for slot in slots], axis=0)


def place_row(places_ref, slots, rows):
    inner = lax.broadcasted_iota(jnp.int32, (1, rows), 1)
    return jnp.concatenate([inner + places_ref[slot] for slot in slots], axis=1)


def project_kernel(heads, slots, chunk, count, pieces, more, last, bound_ref, places_ref, *refs):
    units = jnp.concatenate([ref[...] for ref in refs[:pieces]], axis=0)
    weight_ref, pick_ref, extra_ref = refs[pieces : pieces + 3]
    fq_ref, fk_ref, v_ref, state_ref = refs[-4:]
    projected = dot(units, weight_ref[...])
    rows, width = projected.shape
    needed = (heads - 1) * LANES + WIDE
    if needed > width:
        projected = jnp.pad(projected, ((0, 0), (0, needed - width)))
    bound = bound_ref[0]
    place = place_column(places_ref, slots, chunk)
    kept = ((place >= bound) | (bound == count)).astype(F32)
    ones = jnp.ones((8, rows), BF16)
    shift = 2 * FEAT
    for head in range(heads):
        part = projected[:, head * LANES : head * LANES + WIDE]
        narrow = part if head == 0 else pltpu.roll(part, WIDE - shift * head, 1)
        narrow = narrow[:, :LANES]
        values = pltpu.roll(part, WIDE - shift * (head + 1), 1)[:, :HEAD_DIM].astype(BF16)
        v_ref[:, head * HEAD_DIM : (head + 1) * HEAD_DIM] = values
        upper = narrow.astype(BF16)
        lower = (narrow - upper.astype(F32)).astype(BF16)
        both = jnp.concatenate([upper, lower], axis=1)
        feats = []
        for kind in range(2):
            one = dot(both, pick_ref[kind, 0]) + extra_ref[0:1]
            two = dot(both, pick_ref[kind, 1]) + extra_ref[1:2]
            feats.append((one * two * extra_ref[2:3]).astype(BF16))
        fq_ref[head] = feats[0]
        fk_ref[head] = feats[1]
        keys = (feats[1].astype(F32) * kept).astype(BF16)
        state = dot(keys, values, ((0,), (0,)))
        total = dot(ones, keys)
        tail = jnp.concatenate([total[0:1, :LANES], total[0:1, LANES:], jnp.zeros((14, LANES), F32)], axis=0)
        state = jnp.concatenate([state[0:STATE_ROWS], tail], axis=0)
        if more:
            state = state + refs[pieces + 3][head]
        state_ref[head] = state.astype(BF16) if last else state


def project(bound, places, slots, chunk, count, pieces, weight, constants, earlier, last, heads):
    rows = sum(piece.shape[0] for piece in pieces)
    extra = [] if earlier is None else [earlier]
    return pl.pallas_call(
        functools.partial(project_kernel, heads, slots, chunk, count, len(pieces), bool(extra), last),
        in_specs=[smem(), smem()] + [whole()] * (len(pieces) + 3 + len(extra)),
        out_specs=[whole()] * 4,
        out_shape=[
            jax.ShapeDtypeStruct((heads, rows, WIDE), BF16),
            jax.ShapeDtypeStruct((heads, rows, WIDE), BF16),
            jax.ShapeDtypeStruct((rows, heads * HEAD_DIM), BF16),
            jax.ShapeDtypeStruct((heads, BUFFER_ROWS, HEAD_DIM), BF16 if last else F32),
        ],
        compiler_params=params(),
        cost_estimate=cost(5),
        name="project",
    )(bound, places, *pieces, weight, *constants, *extra)


def within_kernel(heads, slots, chunk, sets, bound_ref, places_ref, *refs):
    fqs, fks, vs = refs[:sets], refs[sets : 2 * sets], refs[2 * sets : 3 * sets]
    num_ref, den_ref = refs[3 * sets :]
    bound = bound_ref[0]
    row = place_column(places_ref, slots, chunk)
    col = place_row(places_ref, slots, chunk)
    allowed = (row >= col) & ((row >= bound) == (col >= bound))
    for head in range(heads):
        query = jnp.concatenate([ref[head] for ref in fqs], axis=0)
        keys = jnp.concatenate([ref[head] for ref in fks], axis=0)
        values = jnp.concatenate(
            [ref[:, head * HEAD_DIM : (head + 1) * HEAD_DIM] for ref in vs], axis=0
        )
        weights = dot(query, keys, ((1,), (1,)))
        weights = jnp.where(allowed, weights, 0.0)
        den_ref[head] = jnp.broadcast_to(
            jnp.sum(weights, axis=-1, keepdims=True), (row.shape[0], 8)
        )
        num_ref[head] = dot(weights.astype(BF16), values)


def within(bound, places, slots, chunk, fqs, fks, vs, heads):
    count = len(slots) * chunk
    return pl.pallas_call(
        functools.partial(within_kernel, heads, slots, chunk, len(fqs)),
        in_specs=[smem(), smem()] + [whole()] * (3 * len(fqs)),
        out_specs=[whole()] * 2,
        out_shape=[
            jax.ShapeDtypeStruct((heads, count, HEAD_DIM), F32),
            jax.ShapeDtypeStruct((heads, count, 8), F32),
        ],
        compiler_params=params(),
        cost_estimate=cost(4.5),
        name="within",
    )(bound, places, *fqs, *fks, *vs)


def split_store(total, refs):
    rows = refs[0].shape[0]
    for n, ref in enumerate(refs):
        ref[...] = total[n * rows : (n + 1) * rows].astype(BF16)


def across_kernel(heads, slots, chunk, sets, earlier, near, bound_ref, places_ref, share_ref, *refs):
    fqs, refs = refs[:sets], refs[sets:]
    num_ref, den_ref, gain_ref, weight_ref = refs[:4]
    states, refs = refs[4 : 4 + earlier], refs[4 + earlier :]
    mixed_ref, fars = refs[0], refs[1:]
    bound = bound_ref[0]
    before = (place_column(places_ref, slots, chunk) < bound).astype(F32)
    for head in range(heads):
        carried = jnp.zeros((BUFFER_ROWS, HEAD_DIM), F32)
        for n in range(earlier):
            carried = carried + jnp.where(share_ref[n] > 0, states[n][head].astype(F32), 0.0)
        state = jnp.concatenate(
            [carried[0:STATE_ROWS], jnp.zeros((WIDE - STATE_ROWS, HEAD_DIM), F32)], axis=0
        ).astype(BF16)
        total = jnp.concatenate(
            [carried[STATE_ROWS : STATE_ROWS + 1], carried[STATE_ROWS + 1 : STATE_ROWS + 2]], axis=1
        )
        query = jnp.concatenate([ref[head] for ref in fqs], axis=0)
        numerator = num_ref[head] + before * dot(query, state)
        more = jnp.sum(query.astype(F32) * total, axis=-1, keepdims=True)
        denominator = den_ref[head][:, 0:1] + before * more
        lanes = slice(head * HEAD_DIM, (head + 1) * HEAD_DIM)
        mixed_ref[:, lanes] = (numerator / denominator * gain_ref[:, lanes].astype(F32)).astype(BF16)
    split_store(dot(mixed_ref[near * chunk :], weight_ref[...]), fars)


def across(bound, places, share, slots, chunk, near, far, fqs, num, den, gain, weight, states, heads):
    count = len(slots) * chunk
    rows = (count - near * chunk) // far
    return pl.pallas_call(
        functools.partial(across_kernel, heads, slots, chunk, len(fqs), len(states), near),
        in_specs=[smem()] * 3 + [whole()] * (len(fqs) + 4 + len(states)),
        out_specs=[whole()] * (1 + far),
        out_shape=[jax.ShapeDtypeStruct((count, heads * HEAD_DIM), BF16)]
        + [jax.ShapeDtypeStruct((rows, weight.shape[1]), BF16)] * far,
        compiler_params=params(),
        cost_estimate=cost(4.5),
        name="across",
    )(bound, places, share, *fqs, num, den, gain, weight, *states)


def near_kernel(rows, mixed_ref, weight_ref, *outs):
    split_store(dot(mixed_ref[0:rows], weight_ref[...]), outs)


def near_chunks(mixed, weight, near, chunk):
    pieces = 2 * near if near > 1 else 1
    rows = near * chunk
    return pl.pallas_call(
        functools.partial(near_kernel, rows),
        in_specs=[whole()] * 2,
        out_specs=[whole()] * pieces,
        out_shape=[jax.ShapeDtypeStruct((rows // pieces, weight.shape[1]), BF16)] * pieces,
        compiler_params=params(),
        cost_estimate=cost(4),
        name="near",
    )(mixed, weight)


def matmul_kernel(*refs):
    a = jnp.concatenate([ref[...] for ref in refs[:-2]], axis=0)
    refs[-1][...] = dot(a, refs[-2][...]).astype(BF16)


def matmul(pieces, b, tile):
    rows = sum(piece.shape[0] for piece in pieces)
    inner = b.shape[0]
    return pl.pallas_call(
        matmul_kernel,
        grid=(b.shape[1] // tile,),
        in_specs=[
            pl.BlockSpec(piece.shape, lambda n: (0, 0), pipeline_mode=pl.Buffered(1)) for piece in pieces
        ]
        + [pl.BlockSpec((inner, tile), lambda n: (0, n))],
        out_specs=pl.BlockSpec((rows, tile), lambda n: (0, n)),
        out_shape=jax.ShapeDtypeStruct((rows, b.shape[1]), BF16),
        compiler_params=params(),
        cost_estimate=cost(5),
        name="matmul",
    )(*pieces, b)


def attend(queries, keys, values, allowed):
    rows = queries[0].shape[0]
    scores = jnp.concatenate(
        [dot(q, k, ((1,), (1,))) for q, k in zip(queries, keys)], axis=0
    ) * HEAD_DIM ** (-0.5)
    allowed = jnp.concatenate([allowed.astype(F32)] * len(queries), axis=0) > 0
    scores = jnp.where(allowed, scores, NEGATIVE)
    peak = jnp.max(scores, axis=-1, keepdims=True)
    weights = jnp.where(allowed, jnp.exp(scores - peak), 0.0)
    probabilities = (weights * (1.0 / jnp.sum(weights, axis=-1, keepdims=True))).astype(BF16)
    return jnp.concatenate(
        [
            dot(probabilities[n * rows : (n + 1) * rows], value).astype(BF16)
            for n, value in enumerate(values)
        ],
        axis=1,
    )


def local_kernel(heads, slots, spots, chunk, sets, bound_ref, places_ref, *refs):
    qkvs, (result_ref, first_ref) = refs[:sets], refs[sets:]
    size = len(slots)
    reach = chunk + WINDOW
    bound = bound_ref[0]
    row = lax.broadcasted_iota(jnp.int32, (chunk, reach), 0)
    col = lax.broadcasted_iota(jnp.int32, (chunk, reach), 1)
    band = (col > row) & (col <= row + WINDOW)
    for slot in range(size):
        k = slots[slot]
        mine, at = spots[k]
        theirs, there = spots[(k - 1) % size]
        base = places_ref[slot]
        query_place = row + base
        key_place = col + (base - WINDOW)
        allowed = band & (key_place >= 0) & ((query_place >= bound) == (key_place >= bound))
        rows = slice(at, at + chunk)
        tail = slice(there + chunk - WINDOW, there + chunk)

        @pl.when(base == 0)
        def _():
            first_ref[...] = qkvs[mine][at : at + WINDOW]

        queries, keys, values = [], [], []
        for head in range(heads):
            lane = head * 3 * HEAD_DIM
            queries.append(qkvs[mine][rows, lane : lane + HEAD_DIM])
            for n, held in ((1, keys), (2, values)):
                lanes = slice(lane + n * HEAD_DIM, lane + (n + 1) * HEAD_DIM)
                held.append(jnp.concatenate([qkvs[theirs][tail, lanes], qkvs[mine][rows, lanes]], axis=0))
        result_ref[slot * chunk : (slot + 1) * chunk] = attend(queries, keys, values, allowed)


def local_window(bound, places, slots, spots, chunk, qkvs, heads):
    return pl.pallas_call(
        functools.partial(local_kernel, heads, slots, spots, chunk, len(qkvs)),
        in_specs=[smem(), smem()] + [whole()] * len(qkvs),
        out_specs=[whole()] * 2,
        out_shape=[
            jax.ShapeDtypeStruct((len(slots) * chunk, heads * HEAD_DIM), BF16),
            jax.ShapeDtypeStruct((WINDOW, qkvs[0].shape[1]), BF16),
        ],
        compiler_params=params(),
        cost_estimate=cost(8),
        name="local_window",
    )(bound, places, *qkvs)


def halo_kernel(heads, count, start, info_ref, local_ref, first_ref, halo_ref, weight_ref, result_ref, *fars):
    result_ref[...] = local_ref[...]
    bound, valid_from, spot = info_ref[0], info_ref[1], info_ref[2]
    row = lax.broadcasted_iota(jnp.int32, (WINDOW, 2 * WINDOW), 0)
    col = lax.broadcasted_iota(jnp.int32, (WINDOW, 2 * WINDOW), 1)
    key_place = col - WINDOW
    allowed = (col > row) & (col <= row + WINDOW) & ((row >= bound) == (key_place >= bound))
    allowed = allowed & ((key_place >= 0) | (key_place + count >= valid_from))
    spot = pl.multiple_of(spot, WINDOW)
    queries, keys, values = [], [], []
    for head in range(heads):
        lane = head * 3 * HEAD_DIM
        queries.append(first_ref[:, lane : lane + HEAD_DIM])
        for n, held in ((1, keys), (2, values)):
            lanes = slice(lane + n * HEAD_DIM, lane + (n + 1) * HEAD_DIM)
            held.append(jnp.concatenate([halo_ref[:, lanes], first_ref[:, lanes]], axis=0))
    result_ref[pl.ds(spot, WINDOW), :] = attend(queries, keys, values, allowed)
    split_store(dot(result_ref[start:], weight_ref[...]), fars)


def halo_window(info, near, chunk, far, local, first, halo, weight, heads):
    count = local.shape[0]
    rows = (count - near * chunk) // far
    return pl.pallas_call(
        functools.partial(halo_kernel, heads, count, near * chunk),
        in_specs=[smem()] + [whole()] * 4,
        out_specs=[whole()] * (1 + far),
        out_shape=[jax.ShapeDtypeStruct(local.shape, BF16)]
        + [jax.ShapeDtypeStruct((rows, weight.shape[1]), BF16)] * far,
        compiler_params=params(),
        cost_estimate=cost(4.5),
        name="halo_window",
    )(info, local, first, halo, weight)


def score_kernel(units_count, pieces, lots, tile, order_ref, *refs):
    units, refs = refs[:units_count], refs[units_count:]
    tables, (goal_ref, out_ref, turned_ref, held) = refs[: len(lots) * pieces], refs[len(lots) * pieces :]
    step = pl.program_id(0)
    width = tables[0].shape[1]
    count = goal_ref.shape[1]
    part = 128

    @pl.when(step == 0)
    def _():
        rows = jnp.concatenate([ref[...] for ref in units], axis=0)
        turned_ref[...] = jnp.transpose(rows)
        held[0] = jnp.full((8, count), NEGATIVE, F32)
        held[1] = jnp.zeros((8, count), F32)
        held[2] = jnp.zeros((8, count), F32)

    def run(mine):
        inner = lax.broadcasted_iota(jnp.int32, (part // 8, 8, count), 0) * 8
        inner = inner + lax.broadcasted_iota(jnp.int32, (part // 8, 8, count), 1)
        peak, total, picked = held[0], held[1], held[2]
        sides = [
            turned_ref[pl.ds(pl.multiple_of(order_ref[n] * width, width), width), :] for n in range(pieces)
        ]
        for at in range(0, tile, part):
            logits = None
            for n in range(pieces):
                more = dot(mine[n][at : at + part], sides[n])
                logits = more if logits is None else logits + more
            logits = logits.reshape(part // 8, 8, count)
            goal = (goal_ref[...] - (step * tile + at)).reshape(1, 1, count)
            old = peak
            peak = jnp.maximum(old, jnp.max(logits, axis=0))
            total = total * jnp.exp(old - peak) + jnp.sum(jnp.exp(logits - peak[None]), axis=0)
            picked = picked + jnp.sum(jnp.where(inner == goal, logits, 0.0), axis=0)
        held[0], held[1], held[2] = peak, total, picked

    for lot, (start, stop) in enumerate(lots):
        pl.when((step >= start) & (step < stop))(
            lambda lot=lot: run(tables[lot * pieces : (lot + 1) * pieces])
        )

    @pl.when(step == pl.num_programs(0) - 1)
    def _():
        peak = jnp.max(held[0], axis=0, keepdims=True)
        total = jnp.sum(held[1] * jnp.exp(held[0] - peak), axis=0, keepdims=True)
        picked = jnp.sum(held[2], axis=0, keepdims=True)
        out_ref[...] = jnp.concatenate([peak, total, picked, jnp.zeros((5, count), F32)], axis=0)


def scores(order, units, lots, goal):
    count = goal.shape[1]
    rows = lots[-1][1]
    tile = 640
    pieces = len(lots[0][2])
    specs, steps = [], []
    for first, last, tables in lots:
        start, stop = first // tile, last // tile
        steps.append((start, stop))
        for table in tables:
            shift = 0 if table.shape[0] == rows else start
            specs.append(
                pl.BlockSpec(
                    (tile, table.shape[1]),
                    lambda i, start=start, stop=stop, shift=shift: (jnp.clip(i, start, stop - 1) - shift, 0),
                )
            )
    return pl.pallas_call(
        functools.partial(score_kernel, len(units), pieces, steps, tile),
        in_specs=[smem()]
        + [pl.BlockSpec(piece.shape, lambda i: (0, 0), pipeline_mode=pl.Buffered(1)) for piece in units]
        + specs
        + [pl.BlockSpec((1, count), lambda i: (0, 0))],
        out_specs=pl.BlockSpec((8, count), lambda i: (0, 0)),
        grid=(rows // tile,),
        out_shape=jax.ShapeDtypeStruct((8, count), F32),
        scratch_shapes=[pltpu.VMEM((units[0].shape[1], count), BF16), pltpu.VMEM((3, 8, count), F32)],
        compiler_params=params(),
        cost_estimate=cost(20),
        name="scores",
    )(order, *units, *[table for lot in lots for table in lot[2]], goal)


def shards(
    token_ids,
    target_ids,
    doc_start,
    vocab_table,
    norm_gain_one,
    lin_qkv,
    lin_head_gain,
    lin_out,
    norm_gain_two,
    win_qkv,
    win_out,
    final_gain,
):
    head_count = lax.axis_size("head")
    seq_count = lax.axis_size("seq")
    head_index = lax.axis_index("head")
    seq_index = lax.axis_index("seq")
    tok_count = token_ids.shape[0]
    chunk = tok_count // head_count
    vocab_rows = vocab_table.shape[0]
    heads = lin_qkv.shape[1] // (2 * FEAT + HEAD_DIM)
    vocab_first = head_index * vocab_rows
    calls = chunk_order(head_count)
    slots = [k for call in calls for k in call]
    near = 3 if head_count == 4 else 1
    far = 2 if head_count == 4 else head_count - 1
    spots = {}
    for n, call in enumerate(calls):
        for at, k in enumerate(call):
            spots[k] = (n, at * chunk)
    held_at = (head_index + jnp.asarray(slots, jnp.int32)) % head_count
    places = held_at * chunk

    marks = jnp.concatenate([token_ids, jnp.broadcast_to(doc_start, (LANES,))])
    marks = jnp.stack(
        [marks] + [lax.ppermute(marks, "seq", xor_pairs(seq_count, k)) for k in range(1, seq_count)]
    )
    block = jnp.arange(seq_count, dtype=jnp.int32)
    order = seq_index ^ block
    starts = marks[:, tok_count]
    starts = jnp.sum(jnp.where(order[None, :] == block[:, None], starts[None, :], 0), axis=1)
    bound = doc_start.astype(jnp.int32)

    steps = [(0, 1), (1, 3), (3, TABLE_STEPS)]
    marks_at = [start * (vocab_rows // TABLE_STEPS) for start, _ in steps] + [vocab_rows]
    lots = []

    ids = (marks[:, :tok_count] - vocab_first).reshape(seq_count, head_count, chunk)

    def ids_of(k):
        return lax.dynamic_index_in_dim(ids, (head_index + k) % head_count, 1, False).reshape(-1)

    if head_count == 4:
        outer = lookup(ids_of(2), vocab_table, 2)

        def inner():
            beside = lookup(jnp.concatenate([ids_of(1), ids_of(3)]), vocab_table, 4)
            own = lookup(ids_of(0), vocab_table, 2, steps)
            lots.extend(own[2:])
            return own[:2] + beside

    else:
        outer = [lookup(ids_of(k), vocab_table, 1)[0] for k in range(1, head_count)]

        def inner():
            own = lookup(ids_of(0), vocab_table, 1, steps)
            lots.extend(own[1:])
            return own[:1]

    found = collect(scatter_rows(outer, inner), seq_count)
    gathered = [found[0]] + [
        lax.ppermute(found[k], "seq", xor_pairs(seq_count, k)) for k in range(1, seq_count)
    ]
    lots[0], gathered = lax.optimization_barrier((lots[0], gathered))
    embedded, units = begin(order, norm_gain_one, gathered)
    across_x, corners = [None] * 3, [None] * 3

    constants = selectors()
    sets, state = [], None

    def project_call(n, pieces, state):
        first = sum(len(c) for c in calls[:n])
        return project(
            bound,
            places[first : first + len(calls[n])],
            list(range(len(calls[n]))),
            chunk,
            tok_count,
            pieces,
            lin_qkv,
            constants,
            state,
            n == len(calls) - 1,
            heads,
        )

    chunks = gather_rows(units)
    if seq_count == 4:
        across_x[0] = lax.ppermute(lots[0], "seq", xor_pairs(seq_count, 2))
        corners[0] = lax.ppermute(across_x[0], "seq", xor_pairs(seq_count, 1))
    for n, call in enumerate(calls):
        made = project_call(n, [piece for k in call for piece in chunks[k]], state)
        sets.append(made[:3])
        state = made[3]
    fqs, fks, vs = zip(*sets)
    if seq_count == 4:
        state, across_x[0] = lax.optimization_barrier((state, across_x[0]))
    states, shares = [], []
    for back in range(1, seq_count):
        states.append(
            lax.ppermute(state, "seq", [(i, i + back) for i in range(seq_count - back)])
        )
        between = (block > seq_index - back) & (block < seq_index)
        broken = jnp.sum(jnp.where(between & (starts != tok_count), 1, 0))
        shares.append(((broken == 0) & (seq_index >= back)).astype(jnp.int32))
    position = list(range(head_count))
    num, den = within(bound, places, position, chunk, fqs, fks, vs, heads)
    mixed, *outer = across(
        bound,
        places,
        jnp.stack(shares),
        position,
        chunk,
        near,
        far,
        fqs,
        num,
        den,
        lin_head_gain.reshape(1, -1),
        lin_out,
        states,
        heads,
    )
    parts = scatter_rows(outer, lambda: near_chunks(mixed, lin_out, near, chunk))
    units, residual = finish(embedded, norm_gain_two, parts, False)

    if seq_count == 4:
        lots[1], _ = lax.optimization_barrier((lots[1], (states, num)))
        across_x[1] = lax.ppermute(lots[1], "seq", xor_pairs(seq_count, 2))
        corners[1] = lax.ppermute(across_x[1], "seq", xor_pairs(seq_count, 1))
        beside = lax.ppermute(vocab_table, "seq", xor_pairs(seq_count, 1))

    chunks = gather_rows(units)
    qkvs = []
    for call in calls:
        qkvs.append(matmul([piece for k in call for piece in chunks[k]], win_qkv, 3 * HEAD_DIM))
    tail = jnp.zeros((WINDOW, win_qkv.shape[1]), BF16)
    for slot, k in enumerate(slots):
        n, at = spots[k]
        tail = jnp.where(
            held_at[slot] == head_count - 1, qkvs[n][at + chunk - WINDOW : at + chunk], tail
        )
    if seq_count == 4:
        tail, across_x[1], corners[0], beside = lax.optimization_barrier(
            (tail, across_x[1], corners[0], beside)
        )
    halo = lax.ppermute(tail, "seq", [(i, i + 1) for i in range(seq_count - 1)])
    previous = jnp.sum(jnp.where(block == seq_index - 1, starts, 0))
    valid_from = jnp.where(
        seq_index == 0, tok_count, jnp.where(previous == tok_count, 0, previous)
    ).astype(jnp.int32)
    first_spot = jnp.sum(jnp.where(held_at == 0, jnp.arange(head_count) * chunk, 0)).astype(jnp.int32)
    local, first = local_window(bound, places, slots, spots, chunk, qkvs, heads)
    lots[2], local, halo = lax.optimization_barrier((lots[2], local, halo))
    info = jnp.stack([bound[0], valid_from, first_spot])
    mixed, *outer = halo_window(info, near, chunk, far, local, first, halo, win_out, heads)
    parts = scatter_rows(outer, lambda: near_chunks(mixed, win_out, near, chunk))
    if seq_count == 4:
        parts, corners[1] = lax.optimization_barrier((parts, corners[1]))
    units = finish(residual, final_gain, parts, True)[0]

    chunks = gather_rows(units)
    if seq_count == 4:
        across_x[2] = lax.ppermute(lots[2], "seq", xor_pairs(seq_count, 2))
        corner, _ = lax.optimization_barrier((across_x[2], (chunks[1][0], chunks[-1][0])))
        corners[2] = lax.ppermute(corner, "seq", xor_pairs(seq_count, 1))
        lots = [
            (marks_at[n], marks_at[n + 1], [vocab_table, beside, across_x[n], corners[n]])
            for n in range(3)
        ]
    else:
        lots = [(0, vocab_rows, [lax.all_gather(vocab_table, "seq", axis=1, tiled=True)])]
        order = jnp.zeros((1,), jnp.int32)
    goals = (target_ids - vocab_first).reshape(head_count, chunk)
    goal = jnp.concatenate(
        [lax.dynamic_index_in_dim(goals, (head_index + k) % head_count, 0, False) for k in slots]
    ).reshape(1, -1)
    triple = scores(order, [piece for k in slots for piece in chunks[k]], lots, goal)
    found = {k: triple[:3, at * chunk : (at + 1) * chunk] for at, k in enumerate(slots)}

    shares = jnp.stack([found[0]] + [turned(found[k], k) for k in range(1, head_count)])
    peak = jnp.max(shares[:, 0], axis=0)
    total = jnp.sum(shares[:, 1] * jnp.exp(shares[:, 0] - peak), axis=0)
    return jnp.sum(shares[:, 2], axis=0) - (peak + jnp.log(total))


def solution(mesh):
    return jax.shard_map(
        shards,
        mesh=mesh,
        in_specs=(
            P(("shadow", "seq")),
            P(("shadow", "seq")),
            P(("shadow", "seq")),
            P(("shadow", "head"), "seq"),
            P("shadow"),
            P("shadow", "head"),
            P(("shadow", "head")),
            P(("shadow", "head"), None),
            P("shadow"),
            P("shadow", "head"),
            P(("shadow", "head"), None),
            P("shadow"),
        ),
        out_specs=P(("shadow", "seq", "head")),
        check_vma=False,
    )
```

```python
import functools

import jax
import jax.numpy as jnp
import numpy as np
from jax import lax
from jax.experimental import pallas as pl
from jax.experimental.pallas import tpu as pltpu
from jax.sharding import PartitionSpec as P

FEAT = 16
WINDOW = 64
HEAD_DIM = 128
EPSILON = 1e-05
NEGATIVE = -1e30
LANES = 128
WIDE = 256
STATE_ROWS = 160
BUFFER_ROWS = 176
F32 = jnp.float32
BF16 = jnp.bfloat16
VMEM_BYTES = 56 * 1024 * 1024


def params(**kw):
    return pltpu.CompilerParams(vmem_limit_bytes=VMEM_BYTES, **kw)


def cost(us):
    return pl.CostEstimate(flops=int(us * 6e8), transcendentals=0, bytes_accessed=int(us * 3e6))


def whole():
    return pl.BlockSpec(memory_space=pltpu.VMEM)


def smem():
    return pl.BlockSpec(memory_space=pltpu.SMEM)


def dot(a, b, dims=((1,), (0,))):
    return lax.dot_general(a, b, (dims, ((), ())), preferred_element_type=F32)


def xor_pairs(size, k):
    return [(i, i ^ k) for i in range(size)]


def rms(values, gain):
    factor = lax.rsqrt(jnp.mean(values * values, axis=-1, keepdims=True) + EPSILON)
    return (values * factor * gain.astype(F32)).astype(BF16)


def turned(value, step):
    size = lax.axis_size("head")
    return lax.ppermute(value, "head", [(i, (i + step) % size) for i in range(size)])


def gather_rows(own):
    size = lax.axis_size("head")
    if size != 4:
        full = lax.all_gather(own, "head")
        here = lax.axis_index("head")
        return [[own]] + [
            [lax.dynamic_index_in_dim(full, (here + k) % size, 0, False)] for k in range(1, size)
        ]
    half = own.shape[0] // 2
    before, after = turned(own, 1), turned(own, -1)
    return [[own], [after], [turned(before[:half], 1), turned(after[half:], -1)], [before]]


def scatter_rows(far, near):
    size = lax.axis_size("head")
    if size != 4:
        here = lax.axis_index("head")
        full = jnp.stack([near()[0]] + list(far))
        full = jnp.stack(
            [lax.dynamic_index_in_dim(full, (d - here) % size, 0, False) for d in range(size)]
        )
        return [[lax.psum_scatter(full, "head", scatter_dimension=0, tiled=True)[0]]]
    from_before, from_after = turned(far[0], 1), turned(far[1], -1)
    own_upper, own_lower, next_upper, next_lower, prev_upper, prev_lower = near()
    lower_right, upper_left = turned(next_lower, 1), turned(prev_upper, -1)
    upper_right, lower_left = pass_on(next_upper, from_before, prev_lower, from_after)
    upper_right, lower_left = turned(upper_right, 1), turned(lower_left, -1)
    return [[own_upper, upper_right, upper_left], [own_lower, lower_right, lower_left]]


def pass_on_kernel(next_ref, before_ref, prev_ref, after_ref, right_ref, left_ref):
    right_ref[...] = (next_ref[...].astype(F32) + before_ref[...].astype(F32)).astype(BF16)
    left_ref[...] = (prev_ref[...].astype(F32) + after_ref[...].astype(F32)).astype(BF16)


def pass_on(next_upper, from_before, prev_lower, from_after):
    return pl.pallas_call(
        pass_on_kernel,
        in_specs=[whole()] * 4,
        out_specs=[whole()] * 2,
        out_shape=[jax.ShapeDtypeStruct(next_upper.shape, BF16)] * 2,
        compiler_params=params(),
        cost_estimate=cost(1.5),
        name="pass_on",
    )(next_upper, from_before, prev_lower, from_after)


def chunk_order(size):
    if size == 4:
        return [[0, 1, 3], [2]]
    return [[k] for k in range(size)]


def lookup_kernel(lots, ids_ref, table_ref, *refs):
    outs, copies, total = refs[: -1 - len(lots)], refs[-1 - len(lots) : -1], refs[-1]
    step = pl.program_id(0)
    tile = table_ref.shape[0]
    for at in range(0, TABLE_STEPS * tile if lots else 0, tile):

        @pl.when(step == at // tile)
        def _():
            for (start, stop), copy in zip(lots, copies):
                low, high = max(start, at), min(stop, at + tile)
                if low < high:
                    copy[low - start : high - start] = table_ref[low - at : high - at]

    count = ids_ref.shape[1]
    ids = jnp.transpose(jnp.broadcast_to(ids_ref[...], (8, count)))[:, 0:1] - step * tile
    hot = (lax.broadcasted_iota(jnp.int32, (count, tile), 1) == ids).astype(F32).astype(BF16)
    found = dot(hot, table_ref[...])

    @pl.when(step == 0)
    def _():
        total[...] = found

    @pl.when(step > 0)
    def _():
        total[...] += found

    @pl.when(step == pl.num_programs(0) - 1)
    def _():
        rows = outs[0].shape[0]
        for n, out in enumerate(outs):
            out[...] = total[n * rows : (n + 1) * rows].astype(BF16)


TABLE_STEPS = 5


def lookup(ids, table, pieces, lots=()):
    count = ids.shape[0]
    rows, width = table.shape
    tile = rows // TABLE_STEPS
    return pl.pallas_call(
        functools.partial(lookup_kernel, lots),
        grid=(TABLE_STEPS,),
        in_specs=[
            pl.BlockSpec((1, count), lambda i: (0, 0)),
            pl.BlockSpec((tile, width), lambda i: (i, 0)),
        ],
        out_specs=[pl.BlockSpec((count // pieces, width), lambda i: (0, 0))] * pieces
        + [
            pl.BlockSpec((stop - start, width), lambda i: (0, 0), pipeline_mode=pl.Buffered(1))
            for start, stop in lots
        ],
        out_shape=[jax.ShapeDtypeStruct((count // pieces, width), BF16)] * pieces
        + [jax.ShapeDtypeStruct((stop - start, width), BF16) for start, stop in lots],
        scratch_shapes=[pltpu.VMEM((count, width), F32)],
        compiler_params=params(),
        cost_estimate=cost(8 * count / 512),
        name="lookup",
    )(ids.reshape(1, count), table)


def gathered_sum(refs, sizes):
    rows, at = [], 0
    for size in sizes:
        total = refs[at][...].astype(F32)
        for ref in refs[at + 1 : at + size]:
            total = total + ref[...].astype(F32)
        rows.append(total)
        at += size
    return rows[0] if len(rows) == 1 else jnp.concatenate(rows, axis=0)


def collect_kernel(sizes, *refs):
    ins, outs = refs[: sum(sizes)], refs[sum(sizes) :]
    rows = outs[0].shape[0]
    total = gathered_sum(ins, sizes)
    for n, out in enumerate(outs):
        out[...] = total[n * rows : (n + 1) * rows].astype(BF16)


def collect(terms, pieces):
    sizes = [len(part) for part in terms]
    parts = [term for part in terms for term in part]
    rows, width = sum(part[0].shape[0] for part in terms), parts[0].shape[1]
    return pl.pallas_call(
        functools.partial(collect_kernel, sizes),
        in_specs=[whole()] * len(parts),
        out_specs=[whole()] * pieces,
        out_shape=[jax.ShapeDtypeStruct((rows // pieces, width), BF16)] * pieces,
        compiler_params=params(),
        cost_estimate=cost(2),
        name="collect",
    )(*parts)


def begin_kernel(pieces, order_ref, gain_ref, *refs):
    ins, (embedded_ref, units_ref, held) = refs[:pieces], refs[pieces:]
    width = ins[0].shape[1]
    for n in range(pieces):
        held[order_ref[n]] = ins[n][...]
    values = jnp.concatenate([held[n] for n in range(pieces)], axis=1)
    embedded_ref[...] = values
    units_ref[...] = rms(values.astype(F32), gain_ref[...])


def begin(order, gain, pieces):
    rows, width = pieces[0].shape
    full = jax.ShapeDtypeStruct((rows, width * len(pieces)), BF16)
    return pl.pallas_call(
        functools.partial(begin_kernel, len(pieces)),
        in_specs=[smem()] + [whole()] * (1 + len(pieces)),
        out_specs=[whole()] * 2,
        out_shape=[full, full],
        scratch_shapes=[pltpu.VMEM((len(pieces), rows, width), BF16)],
        compiler_params=params(),
        cost_estimate=cost(2),
        name="begin",
    )(order, gain.reshape(1, -1), *pieces)


def finish_kernel(sizes, last, residual_ref, gain_ref, *refs):
    parts = sum(sizes)
    total = gathered_sum(refs[:parts], sizes) + residual_ref[...].astype(F32)
    if not last:
        total = total.astype(BF16)
        refs[parts + 1][...] = total
    refs[parts][...] = rms(total.astype(F32), gain_ref[...])


def finish(residual, gain, terms, last):
    full = jax.ShapeDtypeStruct(residual.shape, BF16)
    parts = [term for part in terms for term in part]
    return pl.pallas_call(
        functools.partial(finish_kernel, [len(part) for part in terms], last),
        in_specs=[whole()] * (2 + len(parts)),
        out_specs=[whole()] * (1 if last else 2),
        out_shape=[full] * (1 if last else 2),
        compiler_params=params(),
        cost_estimate=cost(2.5),
        name="finish",
    )(residual, gain.reshape(1, -1), *parts)


def selectors():
    pairs = [(r, s) for r in range(FEAT) for s in range(r, FEAT)]
    picks = np.zeros((2, 2, LANES, WIDE), np.float32)
    extra = np.zeros((3, WIDE), np.float32)
    extra[0:2, 0] = 1.0
    extra[1, 1 : 1 + FEAT] = 1.0
    extra[2] = 1.0
    for kind in range(2):
        first = kind * FEAT
        for r in range(FEAT):
            picks[kind, 0, first + r, 1 + r] = FEAT ** (-0.25)
        for n, (r, s) in enumerate(pairs):
            picks[kind, 0, first + r, 1 + FEAT + n] = FEAT ** (-0.25)
            picks[kind, 1, first + s, 1 + FEAT + n] = FEAT ** (-0.25)
    for n, (r, s) in enumerate(pairs):
        extra[2, 1 + FEAT + n] = 0.5**0.5 if r == s else 1.0
    return jnp.asarray(np.concatenate([picks, picks], axis=2), BF16), jnp.asarray(extra)


def place_column(places_ref, slots, rows):
    inner = lax.broadcasted_iota(jnp.int32, (rows, 1), 0)
    return jnp.concatenate([inner + places_ref[slot] for slot in slots], axis=0)


def place_row(places_ref, slots, rows):
    inner = lax.broadcasted_iota(jnp.int32, (1, rows), 1)
    return jnp.concatenate([inner + places_ref[slot] for slot in slots], axis=1)


def project_kernel(heads, slots, chunk, count, pieces, more, last, bound_ref, places_ref, *refs):
    units = jnp.concatenate([ref[...] for ref in refs[:pieces]], axis=0)
    weight_ref, pick_ref, extra_ref = refs[pieces : pieces + 3]
    fq_ref, fk_ref, v_ref, state_ref = refs[-4:]
    projected = dot(units, weight_ref[...])
    rows, width = projected.shape
    needed = (heads - 1) * LANES + WIDE
    if needed > width:
        projected = jnp.pad(projected, ((0, 0), (0, needed - width)))
    bound = bound_ref[0]
    place = place_column(places_ref, slots, chunk)
    kept = ((place >= bound) | (bound == count)).astype(F32)
    ones = jnp.ones((8, rows), BF16)
    shift = 2 * FEAT
    for head in range(heads):
        part = projected[:, head * LANES : head * LANES + WIDE]
        narrow = part if head == 0 else pltpu.roll(part, WIDE - shift * head, 1)
        narrow = narrow[:, :LANES]
        values = pltpu.roll(part, WIDE - shift * (head + 1), 1)[:, :HEAD_DIM].astype(BF16)
        v_ref[:, head * HEAD_DIM : (head + 1) * HEAD_DIM] = values
        upper = narrow.astype(BF16)
        lower = (narrow - upper.astype(F32)).astype(BF16)
        both = jnp.concatenate([upper, lower], axis=1)
        feats = []
        for kind in range(2):
            one = dot(both, pick_ref[kind, 0]) + extra_ref[0:1]
            two = dot(both, pick_ref[kind, 1]) + extra_ref[1:2]
            feats.append((one * two * extra_ref[2:3]).astype(BF16))
        fq_ref[head] = feats[0]
        fk_ref[head] = feats[1]
        keys = (feats[1].astype(F32) * kept).astype(BF16)
        state = dot(keys, values, ((0,), (0,)))
        total = dot(ones, keys)
        tail = jnp.concatenate([total[0:1, :LANES], total[0:1, LANES:], jnp.zeros((14, LANES), F32)], axis=0)
        state = jnp.concatenate([state[0:STATE_ROWS], tail], axis=0)
        if more:
            state = state + refs[pieces + 3][head]
        state_ref[head] = state.astype(BF16) if last else state


def project(bound, places, slots, chunk, count, pieces, weight, constants, earlier, last, heads):
    rows = sum(piece.shape[0] for piece in pieces)
    extra = [] if earlier is None else [earlier]
    return pl.pallas_call(
        functools.partial(project_kernel, heads, slots, chunk, count, len(pieces), bool(extra), last),
        in_specs=[smem(), smem()] + [whole()] * (len(pieces) + 3 + len(extra)),
        out_specs=[whole()] * 4,
        out_shape=[
            jax.ShapeDtypeStruct((heads, rows, WIDE), BF16),
            jax.ShapeDtypeStruct((heads, rows, WIDE), BF16),
            jax.ShapeDtypeStruct((rows, heads * HEAD_DIM), BF16),
            jax.ShapeDtypeStruct((heads, BUFFER_ROWS, HEAD_DIM), BF16 if last else F32),
        ],
        compiler_params=params(),
        cost_estimate=cost(5),
        name="project",
    )(bound, places, *pieces, weight, *constants, *extra)


def within_kernel(heads, slots, chunk, sets, bound_ref, places_ref, *refs):
    fqs, fks, vs = refs[:sets], refs[sets : 2 * sets], refs[2 * sets : 3 * sets]
    num_ref, den_ref = refs[3 * sets :]
    bound = bound_ref[0]
    row = place_column(places_ref, slots, chunk)
    col = place_row(places_ref, slots, chunk)
    allowed = (row >= col) & ((row >= bound) == (col >= bound))
    for head in range(heads):
        query = jnp.concatenate([ref[head] for ref in fqs], axis=0)
        keys = jnp.concatenate([ref[head] for ref in fks], axis=0)
        values = jnp.concatenate(
            [ref[:, head * HEAD_DIM : (head + 1) * HEAD_DIM] for ref in vs], axis=0
        )
        weights = dot(query, keys, ((1,), (1,)))
        weights = jnp.where(allowed, weights, 0.0)
        den_ref[head] = jnp.broadcast_to(
            jnp.sum(weights, axis=-1, keepdims=True), (row.shape[0], 8)
        )
        num_ref[head] = dot(weights.astype(BF16), values)


def within(bound, places, slots, chunk, fqs, fks, vs, heads):
    count = len(slots) * chunk
    return pl.pallas_call(
        functools.partial(within_kernel, heads, slots, chunk, len(fqs)),
        in_specs=[smem(), smem()] + [whole()] * (3 * len(fqs)),
        out_specs=[whole()] * 2,
        out_shape=[
            jax.ShapeDtypeStruct((heads, count, HEAD_DIM), F32),
            jax.ShapeDtypeStruct((heads, count, 8), F32),
        ],
        compiler_params=params(),
        cost_estimate=cost(4.5),
        name="within",
    )(bound, places, *fqs, *fks, *vs)


def split_store(total, refs):
    rows = refs[0].shape[0]
    for n, ref in enumerate(refs):
        ref[...] = total[n * rows : (n + 1) * rows].astype(BF16)


def across_kernel(heads, slots, chunk, sets, earlier, near, bound_ref, places_ref, share_ref, *refs):
    fqs, refs = refs[:sets], refs[sets:]
    num_ref, den_ref, gain_ref, weight_ref = refs[:4]
    states, refs = refs[4 : 4 + earlier], refs[4 + earlier :]
    mixed_ref, fars = refs[0], refs[1:]
    bound = bound_ref[0]
    before = (place_column(places_ref, slots, chunk) < bound).astype(F32)
    for head in range(heads):
        carried = jnp.zeros((BUFFER_ROWS, HEAD_DIM), F32)
        for n in range(earlier):
            carried = carried + jnp.where(share_ref[n] > 0, states[n][head].astype(F32), 0.0)
        state = jnp.concatenate(
            [carried[0:STATE_ROWS], jnp.zeros((WIDE - STATE_ROWS, HEAD_DIM), F32)], axis=0
        ).astype(BF16)
        total = jnp.concatenate(
            [carried[STATE_ROWS : STATE_ROWS + 1], carried[STATE_ROWS + 1 : STATE_ROWS + 2]], axis=1
        )
        query = jnp.concatenate([ref[head] for ref in fqs], axis=0)
        numerator = num_ref[head] + before * dot(query, state)
        more = jnp.sum(query.astype(F32) * total, axis=-1, keepdims=True)
        denominator = den_ref[head][:, 0:1] + before * more
        lanes = slice(head * HEAD_DIM, (head + 1) * HEAD_DIM)
        mixed_ref[:, lanes] = (numerator / denominator * gain_ref[:, lanes].astype(F32)).astype(BF16)
    split_store(dot(mixed_ref[near * chunk :], weight_ref[...]), fars)


def across(bound, places, share, slots, chunk, near, far, fqs, num, den, gain, weight, states, heads):
    count = len(slots) * chunk
    rows = (count - near * chunk) // far
    return pl.pallas_call(
        functools.partial(across_kernel, heads, slots, chunk, len(fqs), len(states), near),
        in_specs=[smem()] * 3 + [whole()] * (len(fqs) + 4 + len(states)),
        out_specs=[whole()] * (1 + far),
        out_shape=[jax.ShapeDtypeStruct((count, heads * HEAD_DIM), BF16)]
        + [jax.ShapeDtypeStruct((rows, weight.shape[1]), BF16)] * far,
        compiler_params=params(),
        cost_estimate=cost(4.5),
        name="across",
    )(bound, places, share, *fqs, num, den, gain, weight, *states)


def near_kernel(rows, mixed_ref, weight_ref, *outs):
    split_store(dot(mixed_ref[0:rows], weight_ref[...]), outs)


def near_chunks(mixed, weight, near, chunk):
    pieces = 2 * near if near > 1 else 1
    rows = near * chunk
    return pl.pallas_call(
        functools.partial(near_kernel, rows),
        in_specs=[whole()] * 2,
        out_specs=[whole()] * pieces,
        out_shape=[jax.ShapeDtypeStruct((rows // pieces, weight.shape[1]), BF16)] * pieces,
        compiler_params=params(),
        cost_estimate=cost(4),
        name="near",
    )(mixed, weight)


def matmul_kernel(*refs):
    a = jnp.concatenate([ref[...] for ref in refs[:-2]], axis=0)
    refs[-1][...] = dot(a, refs[-2][...]).astype(BF16)


def matmul(pieces, b, tile):
    rows = sum(piece.shape[0] for piece in pieces)
    inner = b.shape[0]
    return pl.pallas_call(
        matmul_kernel,
        grid=(b.shape[1] // tile,),
        in_specs=[
            pl.BlockSpec(piece.shape, lambda n: (0, 0), pipeline_mode=pl.Buffered(1)) for piece in pieces
        ]
        + [pl.BlockSpec((inner, tile), lambda n: (0, n))],
        out_specs=pl.BlockSpec((rows, tile), lambda n: (0, n)),
        out_shape=jax.ShapeDtypeStruct((rows, b.shape[1]), BF16),
        compiler_params=params(),
        cost_estimate=cost(5),
        name="matmul",
    )(*pieces, b)


def attend(queries, keys, values, allowed):
    rows = queries[0].shape[0]
    scores = jnp.concatenate(
        [dot(q, k, ((1,), (1,))) for q, k in zip(queries, keys)], axis=0
    ) * HEAD_DIM ** (-0.5)
    allowed = jnp.concatenate([allowed.astype(F32)] * len(queries), axis=0) > 0
    scores = jnp.where(allowed, scores, NEGATIVE)
    peak = jnp.max(scores, axis=-1, keepdims=True)
    weights = jnp.where(allowed, jnp.exp(scores - peak), 0.0)
    probabilities = (weights * (1.0 / jnp.sum(weights, axis=-1, keepdims=True))).astype(BF16)
    return jnp.concatenate(
        [
            dot(probabilities[n * rows : (n + 1) * rows], value).astype(BF16)
            for n, value in enumerate(values)
        ],
        axis=1,
    )


def local_kernel(heads, slots, spots, chunk, sets, bound_ref, places_ref, *refs):
    qkvs, (result_ref, first_ref) = refs[:sets], refs[sets:]
    size = len(slots)
    reach = chunk + WINDOW
    bound = bound_ref[0]
    row = lax.broadcasted_iota(jnp.int32, (chunk, reach), 0)
    col = lax.broadcasted_iota(jnp.int32, (chunk, reach), 1)
    band = (col > row) & (col <= row + WINDOW)
    for slot in range(size):
        k = slots[slot]
        mine, at = spots[k]
        theirs, there = spots[(k - 1) % size]
        base = places_ref[slot]
        query_place = row + base
        key_place = col + (base - WINDOW)
        allowed = band & (key_place >= 0) & ((query_place >= bound) == (key_place >= bound))
        rows = slice(at, at + chunk)
        tail = slice(there + chunk - WINDOW, there + chunk)

        @pl.when(base == 0)
        def _():
            first_ref[...] = qkvs[mine][at : at + WINDOW]

        queries, keys, values = [], [], []
        for head in range(heads):
            lane = head * 3 * HEAD_DIM
            queries.append(qkvs[mine][rows, lane : lane + HEAD_DIM])
            for n, held in ((1, keys), (2, values)):
                lanes = slice(lane + n * HEAD_DIM, lane + (n + 1) * HEAD_DIM)
                held.append(jnp.concatenate([qkvs[theirs][tail, lanes], qkvs[mine][rows, lanes]], axis=0))
        result_ref[slot * chunk : (slot + 1) * chunk] = attend(queries, keys, values, allowed)


def local_window(bound, places, slots, spots, chunk, qkvs, heads):
    return pl.pallas_call(
        functools.partial(local_kernel, heads, slots, spots, chunk, len(qkvs)),
        in_specs=[smem(), smem()] + [whole()] * len(qkvs),
        out_specs=[whole()] * 2,
        out_shape=[
            jax.ShapeDtypeStruct((len(slots) * chunk, heads * HEAD_DIM), BF16),
            jax.ShapeDtypeStruct((WINDOW, qkvs[0].shape[1]), BF16),
        ],
        compiler_params=params(),
        cost_estimate=cost(8),
        name="local_window",
    )(bound, places, *qkvs)


def halo_kernel(heads, count, start, info_ref, local_ref, first_ref, halo_ref, weight_ref, result_ref, *fars):
    result_ref[...] = local_ref[...]
    bound, valid_from, spot = info_ref[0], info_ref[1], info_ref[2]
    row = lax.broadcasted_iota(jnp.int32, (WINDOW, 2 * WINDOW), 0)
    col = lax.broadcasted_iota(jnp.int32, (WINDOW, 2 * WINDOW), 1)
    key_place = col - WINDOW
    allowed = (col > row) & (col <= row + WINDOW) & ((row >= bound) == (key_place >= bound))
    allowed = allowed & ((key_place >= 0) | (key_place + count >= valid_from))
    spot = pl.multiple_of(spot, WINDOW)
    queries, keys, values = [], [], []
    for head in range(heads):
        lane = head * 3 * HEAD_DIM
        queries.append(first_ref[:, lane : lane + HEAD_DIM])
        for n, held in ((1, keys), (2, values)):
            lanes = slice(lane + n * HEAD_DIM, lane + (n + 1) * HEAD_DIM)
            held.append(jnp.concatenate([halo_ref[:, lanes], first_ref[:, lanes]], axis=0))
    result_ref[pl.ds(spot, WINDOW), :] = attend(queries, keys, values, allowed)
    split_store(dot(result_ref[start:], weight_ref[...]), fars)


def halo_window(info, near, chunk, far, local, first, halo, weight, heads):
    count = local.shape[0]
    rows = (count - near * chunk) // far
    return pl.pallas_call(
        functools.partial(halo_kernel, heads, count, near * chunk),
        in_specs=[smem()] + [whole()] * 4,
        out_specs=[whole()] * (1 + far),
        out_shape=[jax.ShapeDtypeStruct(local.shape, BF16)]
        + [jax.ShapeDtypeStruct((rows, weight.shape[1]), BF16)] * far,
        compiler_params=params(),
        cost_estimate=cost(4.5),
        name="halo_window",
    )(info, local, first, halo, weight)


def turn_kernel(*refs):
    refs[-1][...] = jnp.transpose(jnp.concatenate([ref[...] for ref in refs[:-1]], axis=0))


def turn(pieces):
    rows, width = sum(piece.shape[0] for piece in pieces), pieces[0].shape[1]
    return pl.pallas_call(
        turn_kernel,
        in_specs=[whole()] * len(pieces),
        out_specs=whole(),
        out_shape=jax.ShapeDtypeStruct((width, rows), BF16),
        compiler_params=params(),
        cost_estimate=cost(3),
        name="turn",
    )(*pieces)


def score_kernel(ready, rest, common, pieces, lots, tile, order_ref, *refs):
    early, refs = refs[:ready], refs[ready:]
    units, refs = refs[:rest], refs[rest:]
    shared, refs = refs[:common], refs[common:]
    tables, (goal_ref, out_ref, turned_ref, held) = refs[: len(lots) * pieces], refs[len(lots) * pieces :]
    step = pl.program_id(0)
    width = (shared or tables)[0].shape[1]
    count = goal_ref.shape[1]
    part = 128

    @pl.when(step == 0)
    def _():
        at = 0
        for ref in early:
            at = ref.shape[1]
            turned_ref[:, 0:at] = ref[...]
        turned_ref[:, at:] = jnp.transpose(jnp.concatenate([ref[...] for ref in units], axis=0))
        held[0] = jnp.full((8, count), NEGATIVE, F32)
        held[1] = jnp.zeros((8, count), F32)
        held[2] = jnp.zeros((8, count), F32)

    def run(mine):
        inner = lax.broadcasted_iota(jnp.int32, (part // 8, 8, count), 0) * 8
        inner = inner + lax.broadcasted_iota(jnp.int32, (part // 8, 8, count), 1)
        peak, total, picked = held[0], held[1], held[2]
        sides = [
            turned_ref[pl.ds(pl.multiple_of(order_ref[n] * width, width), width), :] for n in range(len(mine))
        ]
        for at in range(0, tile, part):
            logits = None
            for table, side in zip(mine, sides):
                more = dot(table[at : at + part], side)
                logits = more if logits is None else logits + more
            logits = logits.reshape(part // 8, 8, count)
            goal = (goal_ref[...] - (step * tile + at)).reshape(1, 1, count)
            old = peak
            peak = jnp.maximum(old, jnp.max(logits, axis=0))
            total = total * jnp.exp(old - peak) + jnp.sum(jnp.exp(logits - peak[None]), axis=0)
            picked = picked + jnp.sum(jnp.where(inner == goal, logits, 0.0), axis=0)
        held[0], held[1], held[2] = peak, total, picked

    for lot, (start, stop) in enumerate(lots):
        pl.when((step >= start) & (step < stop))(
            lambda lot=lot: run(list(shared) + list(tables[lot * pieces : (lot + 1) * pieces]))
        )

    @pl.when(step == pl.num_programs(0) - 1)
    def _():
        peak = jnp.max(held[0], axis=0, keepdims=True)
        total = jnp.sum(held[1] * jnp.exp(held[0] - peak), axis=0, keepdims=True)
        picked = jnp.sum(held[2], axis=0, keepdims=True)
        out_ref[...] = jnp.concatenate([peak, total, picked, jnp.zeros((5, count), F32)], axis=0)


def scores(order, early, units, shared, lots, goal):
    count = goal.shape[1]
    rows = lots[-1][1]
    tile = 640
    specs = [pl.BlockSpec((tile, table.shape[1]), lambda i: (i, 0)) for table in shared]
    steps = []
    for first, last, tables in lots:
        start, stop = first // tile, last // tile
        steps.append((start, stop))
        for table in tables:
            specs.append(
                pl.BlockSpec(
                    (tile, table.shape[1]),
                    lambda i, start=start, stop=stop: (jnp.clip(i, start, stop - 1) - start, 0),
                )
            )
    still = [
        pl.BlockSpec(piece.shape, lambda i: (0, 0), pipeline_mode=pl.Buffered(1)) for piece in early + units
    ]
    return pl.pallas_call(
        functools.partial(
            score_kernel, len(early), len(units), len(shared), len(lots[0][2]), steps, tile
        ),
        in_specs=[smem()] + still + specs + [pl.BlockSpec((1, count), lambda i: (0, 0))],
        out_specs=pl.BlockSpec((8, count), lambda i: (0, 0)),
        grid=(rows // tile,),
        out_shape=jax.ShapeDtypeStruct((8, count), F32),
        scratch_shapes=[pltpu.VMEM((units[0].shape[1], count), BF16), pltpu.VMEM((3, 8, count), F32)],
        compiler_params=params(),
        cost_estimate=cost(20),
        name="scores",
    )(order, *early, *units, *shared, *[table for lot in lots for table in lot[2]], goal)


def shards(
    token_ids,
    target_ids,
    doc_start,
    vocab_table,
    norm_gain_one,
    lin_qkv,
    lin_head_gain,
    lin_out,
    norm_gain_two,
    win_qkv,
    win_out,
    final_gain,
):
    head_count = lax.axis_size("head")
    seq_count = lax.axis_size("seq")
    head_index = lax.axis_index("head")
    seq_index = lax.axis_index("seq")
    tok_count = token_ids.shape[0]
    chunk = tok_count // head_count
    vocab_rows = vocab_table.shape[0]
    heads = lin_qkv.shape[1] // (2 * FEAT + HEAD_DIM)
    vocab_first = head_index * vocab_rows
    calls = chunk_order(head_count)
    slots = [k for call in calls for k in call]
    near = 3 if head_count == 4 else 1
    far = 2 if head_count == 4 else head_count - 1
    spots = {}
    for n, call in enumerate(calls):
        for at, k in enumerate(call):
            spots[k] = (n, at * chunk)
    held_at = (head_index + jnp.asarray(slots, jnp.int32)) % head_count
    places = held_at * chunk

    marks = jnp.concatenate([token_ids, jnp.broadcast_to(doc_start, (LANES,))])
    marks = jnp.stack(
        [marks] + [lax.ppermute(marks, "seq", xor_pairs(seq_count, k)) for k in range(1, seq_count)]
    )
    block = jnp.arange(seq_count, dtype=jnp.int32)
    order = seq_index ^ block
    starts = marks[:, tok_count]
    starts = jnp.sum(jnp.where(order[None, :] == block[:, None], starts[None, :], 0), axis=1)
    bound = doc_start.astype(jnp.int32)

    marks_at = [part * (vocab_rows // 10) for part in (0, 3, 8, 10)]
    bounds = list(zip(marks_at[:-1], marks_at[1:])) if seq_count == 4 else []
    lots = []

    ids = (marks[:, :tok_count] - vocab_first).reshape(seq_count, head_count, chunk)

    def ids_of(k):
        return lax.dynamic_index_in_dim(ids, (head_index + k) % head_count, 1, False).reshape(-1)

    if head_count == 4:
        outer = lookup(ids_of(2), vocab_table, 2)

        def inner():
            after, before, _ = lax.optimization_barrier((ids_of(1), ids_of(3), outer))
            half = after.shape[0] // 2
            next_lower, prev_upper = lookup(jnp.concatenate([after[half:], before[:half]]), vocab_table, 2)
            next_upper, prev_lower = lookup(jnp.concatenate([after[:half], before[half:]]), vocab_table, 2)
            own = lookup(ids_of(0), vocab_table, 2, bounds)
            lots.extend(own[2:])
            return [own[0], own[1], next_upper, next_lower, prev_upper, prev_lower]

    else:
        outer = [lookup(ids_of(k), vocab_table, 1)[0] for k in range(1, head_count)]

        def inner():
            own = lookup(ids_of(0), vocab_table, 1, bounds)
            lots.extend(own[1:])
            return own[:1]

    found = collect(scatter_rows(outer, inner), seq_count)
    gathered = [found[0]] + [
        lax.ppermute(found[k], "seq", xor_pairs(seq_count, k)) for k in range(1, seq_count)
    ]
    if lots:
        lots[0], gathered = lax.optimization_barrier((lots[0], gathered))
    embedded, units = begin(order, norm_gain_one, gathered)
    across_x, corners = [None] * 3, [None] * 3

    constants = selectors()
    sets, state = [], None

    def project_call(n, pieces, state):
        first = sum(len(c) for c in calls[:n])
        return project(
            bound,
            places[first : first + len(calls[n])],
            list(range(len(calls[n]))),
            chunk,
            tok_count,
            pieces,
            lin_qkv,
            constants,
            state,
            n == len(calls) - 1,
            heads,
        )

    chunks = gather_rows(units)

    shares = []
    for back in range(1, seq_count):
        between = (block > seq_index - back) & (block < seq_index)
        broken = jnp.sum(jnp.where(between & (starts != tok_count), 1, 0))
        shares.append(((broken == 0) & (seq_index >= back)).astype(jnp.int32))
    shares = jnp.stack(shares)
    previous = jnp.sum(jnp.where(block == seq_index - 1, starts, 0))
    valid_from = jnp.where(
        seq_index == 0, tok_count, jnp.where(previous == tok_count, 0, previous)
    ).astype(jnp.int32)
    first_spot = jnp.sum(jnp.where(held_at == 0, jnp.arange(head_count) * chunk, 0)).astype(jnp.int32)
    info = jnp.stack([bound[0], valid_from, first_spot])
    goals = (target_ids - vocab_first).reshape(head_count, chunk)
    goal = jnp.concatenate(
        [lax.dynamic_index_in_dim(goals, (head_index + k) % head_count, 0, False) for k in slots]
    ).reshape(1, -1)
    chunks[slots[-1]], shares, info, goal = lax.optimization_barrier((chunks[slots[-1]], shares, info, goal))
    if seq_count == 4:
        across_x[0] = lax.ppermute(lots[0], "seq", xor_pairs(seq_count, 2))
        corners[0] = lax.ppermute(across_x[0], "seq", xor_pairs(seq_count, 1))
    for n, call in enumerate(calls):
        made = project_call(n, [piece for k in call for piece in chunks[k]], state)
        sets.append(made[:3])
        state = made[3]
    fqs, fks, vs = zip(*sets)
    if seq_count == 4:
        state, across_x[0] = lax.optimization_barrier((state, across_x[0]))
    states = [
        lax.ppermute(state, "seq", [(i, i + back) for i in range(seq_count - back)])
        for back in range(1, seq_count)
    ]
    position = list(range(head_count))
    num, den = within(bound, places, position, chunk, fqs, fks, vs, heads)
    mixed, *outer = across(
        bound,
        places,
        shares,
        position,
        chunk,
        near,
        far,
        fqs,
        num,
        den,
        lin_head_gain.reshape(1, -1),
        lin_out,
        states,
        heads,
    )
    far_rows = outer
    parts = scatter_rows(outer, lambda: near_chunks(mixed, lin_out, near, chunk))
    units, residual = finish(embedded, norm_gain_two, parts, False)

    if seq_count == 4:
        lots[1], _ = lax.optimization_barrier((lots[1], (states, far_rows)))
        across_x[1] = lax.ppermute(lots[1], "seq", xor_pairs(seq_count, 2))
        beside = lax.ppermute(vocab_table, "seq", xor_pairs(seq_count, 1))

    chunks = gather_rows(units)
    qkvs = []
    for call in calls:
        qkvs.append(matmul([piece for k in call for piece in chunks[k]], win_qkv, 3 * HEAD_DIM))
    tail = jnp.zeros((WINDOW, win_qkv.shape[1]), BF16)
    for slot, k in enumerate(slots):
        n, at = spots[k]
        tail = jnp.where(
            held_at[slot] == head_count - 1, qkvs[n][at + chunk - WINDOW : at + chunk], tail
        )
    if seq_count == 4:
        tail, across_x[1], corners[0], beside = lax.optimization_barrier(
            (tail, across_x[1], corners[0], beside)
        )
    halo = lax.ppermute(tail, "seq", [(i, i + 1) for i in range(seq_count - 1)])
    local, first = local_window(bound, places, slots, spots, chunk, qkvs, heads)
    if lots:
        lots[2], local, halo, across_x[1] = lax.optimization_barrier((lots[2], local, halo, across_x[1]))
        corners[1] = lax.ppermute(across_x[1], "seq", xor_pairs(seq_count, 1))
    mixed, *outer = halo_window(info, near, chunk, far, local, first, halo, win_out, heads)
    parts = scatter_rows(outer, lambda: near_chunks(mixed, win_out, near, chunk))
    if seq_count == 4:
        parts, corners[1] = lax.optimization_barrier((parts, corners[1]))
    units = finish(residual, final_gain, parts, True)[0]

    chunks = gather_rows(units)
    if seq_count == 4:
        across_x[2] = lax.ppermute(lots[2], "seq", xor_pairs(seq_count, 2))
        corner, _ = lax.optimization_barrier((across_x[2], parts))
        corners[2] = lax.ppermute(corner, "seq", xor_pairs(seq_count, 1))
        shared = [vocab_table, beside]
        lots = [(marks_at[n], marks_at[n + 1], [across_x[n], corners[n]]) for n in range(3)]
    else:
        shared = [lax.all_gather(vocab_table, "seq", axis=1, tiled=True)]
        lots = [(0, vocab_rows, [])]
        order = jnp.zeros((1,), jnp.int32)
    first = slots[:-1] if chunk % LANES == 0 else []
    rest = [piece for k in slots[len(first) :] for piece in chunks[k]]
    first = [turn([piece for k in first for piece in chunks[k]])] if first else []
    triple = scores(order, first, rest, shared, lots, goal)
    found = {k: triple[:3, at * chunk : (at + 1) * chunk] for at, k in enumerate(slots)}

    shares = jnp.stack([found[0]] + [turned(found[k], k) for k in range(1, head_count)])
    peak = jnp.max(shares[:, 0], axis=0)
    total = jnp.sum(shares[:, 1] * jnp.exp(shares[:, 0] - peak), axis=0)
    return jnp.sum(shares[:, 2], axis=0) - (peak + jnp.log(total))


def solution(mesh):
    return jax.shard_map(
        shards,
        mesh=mesh,
        in_specs=(
            P(("shadow", "seq")),
            P(("shadow", "seq")),
            P(("shadow", "seq")),
            P(("shadow", "head"), "seq"),
            P("shadow"),
            P("shadow", "head"),
            P(("shadow", "head")),
            P(("shadow", "head"), None),
            P("shadow"),
            P("shadow", "head"),
            P(("shadow", "head"), None),
            P("shadow"),
        ),
        out_specs=P(("shadow", "seq", "head")),
        check_vma=False,
    )
```

```python
import functools

import jax
import jax.numpy as jnp
import numpy as np
from jax import lax
from jax.experimental import pallas as pl
from jax.experimental.pallas import tpu as pltpu
from jax.sharding import PartitionSpec as P

FEAT = 16
WINDOW = 64
HEAD_DIM = 128
EPSILON = 1e-05
NEGATIVE = -1e30
LANES = 128
WIDE = 256
STATE_ROWS = 160
BUFFER_ROWS = 176
F32 = jnp.float32
BF16 = jnp.bfloat16
VMEM_BYTES = 56 * 1024 * 1024


def params(**kw):
    return pltpu.CompilerParams(vmem_limit_bytes=VMEM_BYTES, **kw)


def cost(us):
    return pl.CostEstimate(flops=int(us * 6e8), transcendentals=0, bytes_accessed=int(us * 3e6))


def whole():
    return pl.BlockSpec(memory_space=pltpu.VMEM)


def smem():
    return pl.BlockSpec(memory_space=pltpu.SMEM)


def dot(a, b, dims=((1,), (0,))):
    return lax.dot_general(a, b, (dims, ((), ())), preferred_element_type=F32)


def xor_pairs(size, k):
    return [(i, i ^ k) for i in range(size)]


def rms(values, gain):
    factor = lax.rsqrt(jnp.mean(values * values, axis=-1, keepdims=True) + EPSILON)
    return (values * factor * gain.astype(F32)).astype(BF16)


def turned(value, step):
    size = lax.axis_size("head")
    return lax.ppermute(value, "head", [(i, (i + step) % size) for i in range(size)])


def gather_rows(upper, lower):
    size = lax.axis_size("head")
    if size != 4:
        full = lax.all_gather(jnp.concatenate([upper, lower]), "head")
        here = lax.axis_index("head")
        return [[upper, lower]] + [
            [lax.dynamic_index_in_dim(full, (here + k) % size, 0, False)] for k in range(1, size)
        ]
    before_upper, after_upper = turned(upper, 1), turned(upper, -1)
    after_lower, before_lower = turned(lower, -1), turned(lower, 1)
    far = [turned(before_upper, 1), turned(after_lower, -1)]
    return [[upper, lower], [after_upper, after_lower], far, [before_upper, before_lower]]


def in_halves(terms):
    if len(terms) == 2:
        return terms
    half = terms[0][0].shape[0] // 2
    return [[term[:half] for term in terms[0]], [term[half:] for term in terms[0]]]


def scatter_rows(far, near):
    size = lax.axis_size("head")
    if size != 4:
        here = lax.axis_index("head")
        full = jnp.stack([near()[0]] + list(far))
        full = jnp.stack(
            [lax.dynamic_index_in_dim(full, (d - here) % size, 0, False) for d in range(size)]
        )
        return [[lax.psum_scatter(full, "head", scatter_dimension=0, tiled=True)[0]]]
    from_before, from_after = turned(far[0], 1), turned(far[1], -1)
    own_upper, own_lower, next_upper, next_lower, prev_upper, prev_lower = near()
    lower_right, upper_left = turned(next_lower, 1), turned(prev_upper, -1)
    upper_right, lower_left = pass_on(next_upper, from_before, prev_lower, from_after)
    upper_right, lower_left = turned(upper_right, 1), turned(lower_left, -1)
    return [[own_upper, upper_right, upper_left], [own_lower, lower_right, lower_left]]


def pass_on_kernel(next_ref, before_ref, prev_ref, after_ref, right_ref, left_ref):
    right_ref[...] = (next_ref[...].astype(F32) + before_ref[...].astype(F32)).astype(BF16)
    left_ref[...] = (prev_ref[...].astype(F32) + after_ref[...].astype(F32)).astype(BF16)


def pass_on(next_upper, from_before, prev_lower, from_after):
    return pl.pallas_call(
        pass_on_kernel,
        in_specs=[whole()] * 4,
        out_specs=[whole()] * 2,
        out_shape=[jax.ShapeDtypeStruct(next_upper.shape, BF16)] * 2,
        compiler_params=params(),
        cost_estimate=cost(1.5),
        name="pass_on",
    )(next_upper, from_before, prev_lower, from_after)


def chunk_order(size):
    if size == 4:
        return [[0, 1, 3], [2]]
    return [[k] for k in range(size)]


def lookup_kernel(lots, ids_ref, table_ref, *refs):
    outs, copies, total = refs[: -1 - len(lots)], refs[-1 - len(lots) : -1], refs[-1]
    step = pl.program_id(0)
    tile = table_ref.shape[0]
    for at in range(0, TABLE_STEPS * tile if lots else 0, tile):

        @pl.when(step == at // tile)
        def _():
            for (start, stop), copy in zip(lots, copies):
                low, high = max(start, at), min(stop, at + tile)
                if low < high:
                    copy[low - start : high - start] = table_ref[low - at : high - at]

    count = ids_ref.shape[1]
    ids = jnp.transpose(jnp.broadcast_to(ids_ref[...], (8, count)))[:, 0:1] - step * tile
    hot = (lax.broadcasted_iota(jnp.int32, (count, tile), 1) == ids).astype(F32).astype(BF16)
    found = dot(hot, table_ref[...])

    @pl.when(step == 0)
    def _():
        total[...] = found

    @pl.when(step > 0)
    def _():
        total[...] += found

    @pl.when(step == pl.num_programs(0) - 1)
    def _():
        rows = outs[0].shape[0]
        for n, out in enumerate(outs):
            out[...] = total[n * rows : (n + 1) * rows].astype(BF16)


TABLE_STEPS = 5


def lookup(ids, table, pieces, lots=()):
    count = ids.shape[0]
    rows, width = table.shape
    tile = rows // TABLE_STEPS
    return pl.pallas_call(
        functools.partial(lookup_kernel, lots),
        grid=(TABLE_STEPS,),
        in_specs=[
            pl.BlockSpec((1, count), lambda i: (0, 0)),
            pl.BlockSpec((tile, width), lambda i: (i, 0)),
        ],
        out_specs=[pl.BlockSpec((count // pieces, width), lambda i: (0, 0))] * pieces
        + [
            pl.BlockSpec((stop - start, width), lambda i: (0, 0), pipeline_mode=pl.Buffered(1))
            for start, stop in lots
        ],
        out_shape=[jax.ShapeDtypeStruct((count // pieces, width), BF16)] * pieces
        + [jax.ShapeDtypeStruct((stop - start, width), BF16) for start, stop in lots],
        scratch_shapes=[pltpu.VMEM((count, width), F32)],
        compiler_params=params(),
        cost_estimate=cost(8 * count / 512),
        name="lookup",
    )(ids.reshape(1, count), table)


def gathered_sum(refs, sizes):
    rows, at = [], 0
    for size in sizes:
        total = refs[at][...].astype(F32)
        for ref in refs[at + 1 : at + size]:
            total = total + ref[...].astype(F32)
        rows.append(total)
        at += size
    return rows[0] if len(rows) == 1 else jnp.concatenate(rows, axis=0)


def collect_kernel(sizes, *refs):
    ins, outs = refs[: sum(sizes)], refs[sum(sizes) :]
    rows = outs[0].shape[0]
    total = gathered_sum(ins, sizes)
    for n, out in enumerate(outs):
        out[...] = total[n * rows : (n + 1) * rows].astype(BF16)


def collect(terms, pieces):
    sizes = [len(part) for part in terms]
    parts = [term for part in terms for term in part]
    rows, width = sum(part[0].shape[0] for part in terms), parts[0].shape[1]
    return pl.pallas_call(
        functools.partial(collect_kernel, sizes),
        in_specs=[whole()] * len(parts),
        out_specs=[whole()] * pieces,
        out_shape=[jax.ShapeDtypeStruct((rows // pieces, width), BF16)] * pieces,
        compiler_params=params(),
        cost_estimate=cost(2),
        name="collect",
    )(*parts)


def begin_kernel(pieces, order_ref, gain_ref, *refs):
    ins, outs, held = refs[:pieces], refs[pieces:-1], refs[-1]
    for n in range(pieces):
        held[order_ref[n]] = ins[n][...]
    values = jnp.concatenate([held[n] for n in range(pieces)], axis=1)
    units = rms(values.astype(F32), gain_ref[...])
    half = outs[0].shape[0]
    for n in range(2):
        outs[n][...] = values[n * half : (n + 1) * half]
        outs[2 + n][...] = units[n * half : (n + 1) * half]


def begin(order, gain, pieces):
    rows, width = pieces[0].shape
    half = jax.ShapeDtypeStruct((rows // 2, width * len(pieces)), BF16)
    return pl.pallas_call(
        functools.partial(begin_kernel, len(pieces)),
        in_specs=[smem()] + [whole()] * (1 + len(pieces)),
        out_specs=[whole()] * 4,
        out_shape=[half] * 4,
        scratch_shapes=[pltpu.VMEM((len(pieces), rows, width), BF16)],
        compiler_params=params(),
        cost_estimate=cost(2),
        name="begin",
    )(order, gain.reshape(1, -1), *pieces)


def finish_kernel(parts, last, residual_ref, gain_ref, *refs):
    total = gathered_sum(refs[:parts], [parts]) + residual_ref[...].astype(F32)
    if not last:
        total = total.astype(BF16)
        refs[parts + 1][...] = total
    refs[parts][...] = rms(total.astype(F32), gain_ref[...])


def finish(residual, gain, terms, last):
    full = jax.ShapeDtypeStruct(residual.shape, BF16)
    return pl.pallas_call(
        functools.partial(finish_kernel, len(terms), last),
        in_specs=[whole()] * (2 + len(terms)),
        out_specs=[whole()] * (1 if last else 2),
        out_shape=[full] * (1 if last else 2),
        compiler_params=params(),
        cost_estimate=cost(2),
        name="finish",
    )(residual, gain, *terms)


def selectors():
    pairs = [(r, s) for r in range(FEAT) for s in range(r, FEAT)]
    picks = np.zeros((2, 2, LANES, WIDE), np.float32)
    extra = np.zeros((3, WIDE), np.float32)
    extra[0:2, 0] = 1.0
    extra[1, 1 : 1 + FEAT] = 1.0
    extra[2] = 1.0
    for kind in range(2):
        first = kind * FEAT
        for r in range(FEAT):
            picks[kind, 0, first + r, 1 + r] = FEAT ** (-0.25)
        for n, (r, s) in enumerate(pairs):
            picks[kind, 0, first + r, 1 + FEAT + n] = FEAT ** (-0.25)
            picks[kind, 1, first + s, 1 + FEAT + n] = FEAT ** (-0.25)
    for n, (r, s) in enumerate(pairs):
        extra[2, 1 + FEAT + n] = 0.5**0.5 if r == s else 1.0
    return jnp.asarray(np.concatenate([picks, picks], axis=2), BF16), jnp.asarray(extra)


def place_column(places_ref, slots, rows):
    inner = lax.broadcasted_iota(jnp.int32, (rows, 1), 0)
    return jnp.concatenate([inner + places_ref[slot] for slot in slots], axis=0)


def place_row(places_ref, slots, rows):
    inner = lax.broadcasted_iota(jnp.int32, (1, rows), 1)
    return jnp.concatenate([inner + places_ref[slot] for slot in slots], axis=1)


def project_kernel(heads, slots, chunk, count, pieces, more, last, bound_ref, places_ref, *refs):
    units = jnp.concatenate([ref[...] for ref in refs[:pieces]], axis=0)
    weight_ref, pick_ref, extra_ref = refs[pieces : pieces + 3]
    fq_ref, fk_ref, v_ref, state_ref = refs[-4:]
    projected = dot(units, weight_ref[...])
    rows, width = projected.shape
    needed = (heads - 1) * LANES + WIDE
    if needed > width:
        projected = jnp.pad(projected, ((0, 0), (0, needed - width)))
    bound = bound_ref[0]
    place = place_column(places_ref, slots, chunk)
    kept = ((place >= bound) | (bound == count)).astype(F32)
    ones = jnp.ones((8, rows), BF16)
    shift = 2 * FEAT
    for head in range(heads):
        part = projected[:, head * LANES : head * LANES + WIDE]
        narrow = part if head == 0 else pltpu.roll(part, WIDE - shift * head, 1)
        narrow = narrow[:, :LANES]
        values = pltpu.roll(part, WIDE - shift * (head + 1), 1)[:, :HEAD_DIM].astype(BF16)
        v_ref[:, head * HEAD_DIM : (head + 1) * HEAD_DIM] = values
        upper = narrow.astype(BF16)
        lower = (narrow - upper.astype(F32)).astype(BF16)
        both = jnp.concatenate([upper, lower], axis=1)
        feats = []
        for kind in range(2):
            one = dot(both, pick_ref[kind, 0]) + extra_ref[0:1]
            two = dot(both, pick_ref[kind, 1]) + extra_ref[1:2]
            feats.append((one * two * extra_ref[2:3]).astype(BF16))
        fq_ref[head] = feats[0]
        fk_ref[head] = feats[1]
        keys = (feats[1].astype(F32) * kept).astype(BF16)
        state = dot(keys, values, ((0,), (0,)))
        total = dot(ones, keys)
        tail = jnp.concatenate([total[0:1, :LANES], total[0:1, LANES:], jnp.zeros((14, LANES), F32)], axis=0)
        state = jnp.concatenate([state[0:STATE_ROWS], tail], axis=0)
        if more:
            state = state + refs[pieces + 3][head]
        state_ref[head] = state.astype(BF16) if last else state


def project(bound, places, slots, chunk, count, pieces, weight, constants, earlier, last, heads):
    rows = sum(piece.shape[0] for piece in pieces)
    extra = [] if earlier is None else [earlier]
    return pl.pallas_call(
        functools.partial(project_kernel, heads, slots, chunk, count, len(pieces), bool(extra), last),
        in_specs=[smem(), smem()] + [whole()] * (len(pieces) + 3 + len(extra)),
        out_specs=[whole()] * 4,
        out_shape=[
            jax.ShapeDtypeStruct((heads, rows, WIDE), BF16),
            jax.ShapeDtypeStruct((heads, rows, WIDE), BF16),
            jax.ShapeDtypeStruct((rows, heads * HEAD_DIM), BF16),
            jax.ShapeDtypeStruct((heads, BUFFER_ROWS, HEAD_DIM), BF16 if last else F32),
        ],
        compiler_params=params(),
        cost_estimate=cost(5),
        name="project",
    )(bound, places, *pieces, weight, *constants, *extra)


def within_kernel(heads, slots, chunk, sets, bound_ref, places_ref, *refs):
    fqs, fks, vs = refs[:sets], refs[sets : 2 * sets], refs[2 * sets : 3 * sets]
    num_ref, den_ref = refs[3 * sets :]
    bound = bound_ref[0]
    row = place_column(places_ref, slots, chunk)
    col = place_row(places_ref, slots, chunk)
    allowed = (row >= col) & ((row >= bound) == (col >= bound))
    for head in range(heads):
        query = jnp.concatenate([ref[head] for ref in fqs], axis=0)
        keys = jnp.concatenate([ref[head] for ref in fks], axis=0)
        values = jnp.concatenate(
            [ref[:, head * HEAD_DIM : (head + 1) * HEAD_DIM] for ref in vs], axis=0
        )
        weights = dot(query, keys, ((1,), (1,)))
        weights = jnp.where(allowed, weights, 0.0)
        den_ref[head] = jnp.broadcast_to(
            jnp.sum(weights, axis=-1, keepdims=True), (row.shape[0], 8)
        )
        num_ref[head] = dot(weights.astype(BF16), values)


def within(bound, places, slots, chunk, fqs, fks, vs, heads):
    count = len(slots) * chunk
    return pl.pallas_call(
        functools.partial(within_kernel, heads, slots, chunk, len(fqs)),
        in_specs=[smem(), smem()] + [whole()] * (3 * len(fqs)),
        out_specs=[whole()] * 2,
        out_shape=[
            jax.ShapeDtypeStruct((heads, count, HEAD_DIM), F32),
            jax.ShapeDtypeStruct((heads, count, 8), F32),
        ],
        compiler_params=params(),
        cost_estimate=cost(4.5),
        name="within",
    )(bound, places, *fqs, *fks, *vs)


def split_store(total, refs):
    rows = refs[0].shape[0]
    for n, ref in enumerate(refs):
        ref[...] = total[n * rows : (n + 1) * rows].astype(BF16)


def across_kernel(heads, slots, chunk, sets, earlier, near, bound_ref, places_ref, share_ref, *refs):
    fqs, refs = refs[:sets], refs[sets:]
    num_ref, den_ref, gain_ref, weight_ref = refs[:4]
    states, refs = refs[4 : 4 + earlier], refs[4 + earlier :]
    mixed_ref, fars = refs[0], refs[1:]
    bound = bound_ref[0]
    before = (place_column(places_ref, slots, chunk) < bound).astype(F32)
    for head in range(heads):
        carried = jnp.zeros((BUFFER_ROWS, HEAD_DIM), F32)
        for n in range(earlier):
            carried = carried + jnp.where(share_ref[n] > 0, states[n][head].astype(F32), 0.0)
        state = jnp.concatenate(
            [carried[0:STATE_ROWS], jnp.zeros((WIDE - STATE_ROWS, HEAD_DIM), F32)], axis=0
        ).astype(BF16)
        total = jnp.concatenate(
            [carried[STATE_ROWS : STATE_ROWS + 1], carried[STATE_ROWS + 1 : STATE_ROWS + 2]], axis=1
        )
        query = jnp.concatenate([ref[head] for ref in fqs], axis=0)
        numerator = num_ref[head] + before * dot(query, state)
        more = jnp.sum(query.astype(F32) * total, axis=-1, keepdims=True)
        denominator = den_ref[head][:, 0:1] + before * more
        lanes = slice(head * HEAD_DIM, (head + 1) * HEAD_DIM)
        mixed_ref[:, lanes] = (numerator / denominator * gain_ref[:, lanes].astype(F32)).astype(BF16)
    split_store(dot(mixed_ref[near * chunk :], weight_ref[...]), fars)


def across(bound, places, share, slots, chunk, near, far, fqs, num, den, gain, weight, states, heads):
    count = len(slots) * chunk
    rows = (count - near * chunk) // far
    return pl.pallas_call(
        functools.partial(across_kernel, heads, slots, chunk, len(fqs), len(states), near),
        in_specs=[smem()] * 3 + [whole()] * (len(fqs) + 4 + len(states)),
        out_specs=[whole()] * (1 + far),
        out_shape=[jax.ShapeDtypeStruct((count, heads * HEAD_DIM), BF16)]
        + [jax.ShapeDtypeStruct((rows, weight.shape[1]), BF16)] * far,
        compiler_params=params(),
        cost_estimate=cost(4.5),
        name="across",
    )(bound, places, share, *fqs, num, den, gain, weight, *states)


def near_kernel(rows, mixed_ref, weight_ref, *outs):
    split_store(dot(mixed_ref[0:rows], weight_ref[...]), outs)


def near_chunks(mixed, weight, near, chunk):
    pieces = 2 * near if near > 1 else 1
    rows = near * chunk
    return pl.pallas_call(
        functools.partial(near_kernel, rows),
        in_specs=[whole()] * 2,
        out_specs=[whole()] * pieces,
        out_shape=[jax.ShapeDtypeStruct((rows // pieces, weight.shape[1]), BF16)] * pieces,
        compiler_params=params(),
        cost_estimate=cost(4),
        name="near",
    )(mixed, weight)


def matmul_kernel(*refs):
    a = jnp.concatenate([ref[...] for ref in refs[:-2]], axis=0)
    refs[-1][...] = dot(a, refs[-2][...]).astype(BF16)


def matmul(pieces, b, tile):
    rows = sum(piece.shape[0] for piece in pieces)
    inner = b.shape[0]
    return pl.pallas_call(
        matmul_kernel,
        grid=(b.shape[1] // tile,),
        in_specs=[
            pl.BlockSpec(piece.shape, lambda n: (0, 0), pipeline_mode=pl.Buffered(1)) for piece in pieces
        ]
        + [pl.BlockSpec((inner, tile), lambda n: (0, n))],
        out_specs=pl.BlockSpec((rows, tile), lambda n: (0, n)),
        out_shape=jax.ShapeDtypeStruct((rows, b.shape[1]), BF16),
        compiler_params=params(),
        cost_estimate=cost(5),
        name="matmul",
    )(*pieces, b)


def attend(queries, keys, values, allowed):
    rows = queries[0].shape[0]
    scores = jnp.concatenate(
        [dot(q, k, ((1,), (1,))) for q, k in zip(queries, keys)], axis=0
    ) * HEAD_DIM ** (-0.5)
    allowed = jnp.concatenate([allowed.astype(F32)] * len(queries), axis=0) > 0
    scores = jnp.where(allowed, scores, NEGATIVE)
    peak = jnp.max(scores, axis=-1, keepdims=True)
    weights = jnp.where(allowed, jnp.exp(scores - peak), 0.0)
    probabilities = (weights * (1.0 / jnp.sum(weights, axis=-1, keepdims=True))).astype(BF16)
    return jnp.concatenate(
        [
            dot(probabilities[n * rows : (n + 1) * rows], value).astype(BF16)
            for n, value in enumerate(values)
        ],
        axis=1,
    )


def local_kernel(heads, slots, spots, chunk, sets, bound_ref, places_ref, *refs):
    qkvs, (result_ref, first_ref) = refs[:sets], refs[sets:]
    size = len(slots)
    reach = chunk + WINDOW
    bound = bound_ref[0]
    row = lax.broadcasted_iota(jnp.int32, (chunk, reach), 0)
    col = lax.broadcasted_iota(jnp.int32, (chunk, reach), 1)
    band = (col > row) & (col <= row + WINDOW)
    for slot in range(size):
        k = slots[slot]
        mine, at = spots[k]
        theirs, there = spots[(k - 1) % size]
        base = places_ref[slot]
        query_place = row + base
        key_place = col + (base - WINDOW)
        allowed = band & (key_place >= 0) & ((query_place >= bound) == (key_place >= bound))
        rows = slice(at, at + chunk)
        tail = slice(there + chunk - WINDOW, there + chunk)

        @pl.when(base == 0)
        def _():
            first_ref[...] = qkvs[mine][at : at + WINDOW]

        queries, keys, values = [], [], []
        for head in range(heads):
            lane = head * 3 * HEAD_DIM
            queries.append(qkvs[mine][rows, lane : lane + HEAD_DIM])
            for n, held in ((1, keys), (2, values)):
                lanes = slice(lane + n * HEAD_DIM, lane + (n + 1) * HEAD_DIM)
                held.append(jnp.concatenate([qkvs[theirs][tail, lanes], qkvs[mine][rows, lanes]], axis=0))
        result_ref[slot * chunk : (slot + 1) * chunk] = attend(queries, keys, values, allowed)


def local_window(bound, places, slots, spots, chunk, qkvs, heads):
    return pl.pallas_call(
        functools.partial(local_kernel, heads, slots, spots, chunk, len(qkvs)),
        in_specs=[smem(), smem()] + [whole()] * len(qkvs),
        out_specs=[whole()] * 2,
        out_shape=[
            jax.ShapeDtypeStruct((len(slots) * chunk, heads * HEAD_DIM), BF16),
            jax.ShapeDtypeStruct((WINDOW, qkvs[0].shape[1]), BF16),
        ],
        compiler_params=params(),
        cost_estimate=cost(8),
        name="local_window",
    )(bound, places, *qkvs)


def halo_kernel(heads, count, start, info_ref, local_ref, first_ref, halo_ref, weight_ref, result_ref, *fars):
    result_ref[...] = local_ref[...]
    bound, valid_from, spot = info_ref[0], info_ref[1], info_ref[2]
    row = lax.broadcasted_iota(jnp.int32, (WINDOW, 2 * WINDOW), 0)
    col = lax.broadcasted_iota(jnp.int32, (WINDOW, 2 * WINDOW), 1)
    key_place = col - WINDOW
    allowed = (col > row) & (col <= row + WINDOW) & ((row >= bound) == (key_place >= bound))
    allowed = allowed & ((key_place >= 0) | (key_place + count >= valid_from))
    spot = pl.multiple_of(spot, WINDOW)
    queries, keys, values = [], [], []
    for head in range(heads):
        lane = head * 3 * HEAD_DIM
        queries.append(first_ref[:, lane : lane + HEAD_DIM])
        for n, held in ((1, keys), (2, values)):
            lanes = slice(lane + n * HEAD_DIM, lane + (n + 1) * HEAD_DIM)
            held.append(jnp.concatenate([halo_ref[:, lanes], first_ref[:, lanes]], axis=0))
    result_ref[pl.ds(spot, WINDOW), :] = attend(queries, keys, values, allowed)
    split_store(dot(result_ref[start:], weight_ref[...]), fars)


def halo_window(info, near, chunk, far, local, first, halo, weight, heads):
    count = local.shape[0]
    rows = (count - near * chunk) // far
    return pl.pallas_call(
        functools.partial(halo_kernel, heads, count, near * chunk),
        in_specs=[smem()] + [whole()] * 4,
        out_specs=[whole()] * (1 + far),
        out_shape=[jax.ShapeDtypeStruct(local.shape, BF16)]
        + [jax.ShapeDtypeStruct((rows, weight.shape[1]), BF16)] * far,
        compiler_params=params(),
        cost_estimate=cost(4.5),
        name="halo_window",
    )(info, local, first, halo, weight)


def turn_kernel(*refs):
    refs[-1][...] = jnp.transpose(jnp.concatenate([ref[...] for ref in refs[:-1]], axis=0))


def turn(pieces):
    rows, width = sum(piece.shape[0] for piece in pieces), pieces[0].shape[1]
    return pl.pallas_call(
        turn_kernel,
        in_specs=[whole()] * len(pieces),
        out_specs=whole(),
        out_shape=jax.ShapeDtypeStruct((width, rows), BF16),
        compiler_params=params(),
        cost_estimate=cost(3),
        name="turn",
    )(*pieces)


def score_kernel(ready, rest, common, pieces, lots, tile, order_ref, *refs):
    early, refs = refs[:ready], refs[ready:]
    units, refs = refs[:rest], refs[rest:]
    shared, refs = refs[:common], refs[common:]
    tables, (goal_ref, out_ref, turned_ref, held) = refs[: len(lots) * pieces], refs[len(lots) * pieces :]
    step = pl.program_id(0)
    width = (shared or tables)[0].shape[1]
    count = goal_ref.shape[1]
    part = 128

    @pl.when(step == 0)
    def _():
        at = 0
        for ref in early:
            at = ref.shape[1]
            turned_ref[:, 0:at] = ref[...]
        turned_ref[:, at:] = jnp.transpose(jnp.concatenate([ref[...] for ref in units], axis=0))
        held[0] = jnp.full((8, count), NEGATIVE, F32)
        held[1] = jnp.zeros((8, count), F32)
        held[2] = jnp.zeros((8, count), F32)

    def run(mine):
        inner = lax.broadcasted_iota(jnp.int32, (part // 8, 8, count), 0) * 8
        inner = inner + lax.broadcasted_iota(jnp.int32, (part // 8, 8, count), 1)
        peak, total, picked = held[0], held[1], held[2]
        sides = [
            turned_ref[pl.ds(pl.multiple_of(order_ref[n] * width, width), width), :] for n in range(len(mine))
        ]
        for at in range(0, tile, part):
            logits = None
            for table, side in zip(mine, sides):
                more = dot(table[at : at + part], side)
                logits = more if logits is None else logits + more
            logits = logits.reshape(part // 8, 8, count)
            goal = (goal_ref[...] - (step * tile + at)).reshape(1, 1, count)
            old = peak
            peak = jnp.maximum(old, jnp.max(logits, axis=0))
            total = total * jnp.exp(old - peak) + jnp.sum(jnp.exp(logits - peak[None]), axis=0)
            picked = picked + jnp.sum(jnp.where(inner == goal, logits, 0.0), axis=0)
        held[0], held[1], held[2] = peak, total, picked

    for lot, (start, stop) in enumerate(lots):
        pl.when((step >= start) & (step < stop))(
            lambda lot=lot: run(list(shared) + list(tables[lot * pieces : (lot + 1) * pieces]))
        )

    @pl.when(step == pl.num_programs(0) - 1)
    def _():
        peak = jnp.max(held[0], axis=0, keepdims=True)
        total = jnp.sum(held[1] * jnp.exp(held[0] - peak), axis=0, keepdims=True)
        picked = jnp.sum(held[2], axis=0, keepdims=True)
        out_ref[...] = jnp.concatenate([peak, total, picked, jnp.zeros((5, count), F32)], axis=0)


def scores(order, early, units, shared, lots, goal):
    count = goal.shape[1]
    rows = lots[-1][1]
    tile = 640
    specs = [pl.BlockSpec((tile, table.shape[1]), lambda i: (i, 0)) for table in shared]
    steps = []
    for first, last, tables in lots:
        start, stop = first // tile, last // tile
        steps.append((start, stop))
        for table in tables:
            specs.append(
                pl.BlockSpec(
                    (tile, table.shape[1]),
                    lambda i, start=start, stop=stop: (jnp.clip(i, start, stop - 1) - start, 0),
                )
            )
    still = [
        pl.BlockSpec(piece.shape, lambda i: (0, 0), pipeline_mode=pl.Buffered(1)) for piece in early + units
    ]
    return pl.pallas_call(
        functools.partial(
            score_kernel, len(early), len(units), len(shared), len(lots[0][2]), steps, tile
        ),
        in_specs=[smem()] + still + specs + [pl.BlockSpec((1, count), lambda i: (0, 0))],
        out_specs=pl.BlockSpec((8, count), lambda i: (0, 0)),
        grid=(rows // tile,),
        out_shape=jax.ShapeDtypeStruct((8, count), F32),
        scratch_shapes=[pltpu.VMEM((units[0].shape[1], count), BF16), pltpu.VMEM((3, 8, count), F32)],
        compiler_params=params(),
        cost_estimate=cost(20),
        name="scores",
    )(order, *early, *units, *shared, *[table for lot in lots for table in lot[2]], goal)


def shards(
    token_ids,
    target_ids,
    doc_start,
    vocab_table,
    norm_gain_one,
    lin_qkv,
    lin_head_gain,
    lin_out,
    norm_gain_two,
    win_qkv,
    win_out,
    final_gain,
):
    head_count = lax.axis_size("head")
    seq_count = lax.axis_size("seq")
    head_index = lax.axis_index("head")
    seq_index = lax.axis_index("seq")
    tok_count = token_ids.shape[0]
    chunk = tok_count // head_count
    vocab_rows = vocab_table.shape[0]
    heads = lin_qkv.shape[1] // (2 * FEAT + HEAD_DIM)
    vocab_first = head_index * vocab_rows
    calls = chunk_order(head_count)
    slots = [k for call in calls for k in call]
    near = 3 if head_count == 4 else 1
    far = 2 if head_count == 4 else head_count - 1
    spots = {}
    for n, call in enumerate(calls):
        for at, k in enumerate(call):
            spots[k] = (n, at * chunk)
    held_at = (head_index + jnp.asarray(slots, jnp.int32)) % head_count
    places = held_at * chunk

    marks = jnp.concatenate([token_ids, jnp.broadcast_to(doc_start, (LANES,))])
    marks = jnp.stack(
        [marks] + [lax.ppermute(marks, "seq", xor_pairs(seq_count, k)) for k in range(1, seq_count)]
    )
    block = jnp.arange(seq_count, dtype=jnp.int32)
    order = seq_index ^ block
    starts = marks[:, tok_count]
    starts = jnp.sum(jnp.where(order[None, :] == block[:, None], starts[None, :], 0), axis=1)
    bound = doc_start.astype(jnp.int32)

    marks_at = [part * (vocab_rows // 10) for part in (0, 3, 8, 10)]
    bounds = list(zip(marks_at[:-1], marks_at[1:])) if seq_count == 4 else []
    lots = []

    ids = (marks[:, :tok_count] - vocab_first).reshape(seq_count, head_count, chunk)

    def ids_of(k):
        return lax.dynamic_index_in_dim(ids, (head_index + k) % head_count, 1, False).reshape(-1)

    if head_count == 4:
        outer = lookup(ids_of(2), vocab_table, 2)

        def inner():
            after, before, _ = lax.optimization_barrier((ids_of(1), ids_of(3), outer))
            half = after.shape[0] // 2
            next_lower, prev_upper = lookup(jnp.concatenate([after[half:], before[:half]]), vocab_table, 2)
            next_upper, prev_lower = lookup(jnp.concatenate([after[:half], before[half:]]), vocab_table, 2)
            own = lookup(ids_of(0), vocab_table, 2, bounds)
            lots.extend(own[2:])
            return [own[0], own[1], next_upper, next_lower, prev_upper, prev_lower]

    else:
        outer = [lookup(ids_of(k), vocab_table, 1)[0] for k in range(1, head_count)]

        def inner():
            own = lookup(ids_of(0), vocab_table, 1, bounds)
            lots.extend(own[1:])
            return own[:1]

    found = collect(scatter_rows(outer, inner), seq_count)
    gathered = [found[0]] + [
        lax.ppermute(found[k], "seq", xor_pairs(seq_count, k)) for k in range(1, seq_count)
    ]
    if lots:
        lots[0], gathered = lax.optimization_barrier((lots[0], gathered))
    *embedded, upper, lower = begin(order, norm_gain_one, gathered)
    across_x, corners = [None] * 3, [None] * 3

    constants = selectors()
    sets, state = [], None

    def project_call(n, pieces, state):
        first = sum(len(c) for c in calls[:n])
        return project(
            bound,
            places[first : first + len(calls[n])],
            list(range(len(calls[n]))),
            chunk,
            tok_count,
            pieces,
            lin_qkv,
            constants,
            state,
            n == len(calls) - 1,
            heads,
        )

    chunks = gather_rows(upper, lower)

    shares = []
    for back in range(1, seq_count):
        between = (block > seq_index - back) & (block < seq_index)
        broken = jnp.sum(jnp.where(between & (starts != tok_count), 1, 0))
        shares.append(((broken == 0) & (seq_index >= back)).astype(jnp.int32))
    shares = jnp.stack(shares)
    previous = jnp.sum(jnp.where(block == seq_index - 1, starts, 0))
    valid_from = jnp.where(
        seq_index == 0, tok_count, jnp.where(previous == tok_count, 0, previous)
    ).astype(jnp.int32)
    first_spot = jnp.sum(jnp.where(held_at == 0, jnp.arange(head_count) * chunk, 0)).astype(jnp.int32)
    info = jnp.stack([bound[0], valid_from, first_spot])
    goals = (target_ids - vocab_first).reshape(head_count, chunk)
    goal = jnp.concatenate(
        [lax.dynamic_index_in_dim(goals, (head_index + k) % head_count, 0, False) for k in slots]
    ).reshape(1, -1)
    gain_two, gain_three = norm_gain_two.reshape(1, -1), final_gain.reshape(1, -1)
    head_gain = lin_head_gain.reshape(1, -1)
    chunks[slots[-1]], shares, info, goal, gain_two, gain_three, head_gain = lax.optimization_barrier(
        (chunks[slots[-1]], shares, info, goal, gain_two, gain_three, head_gain)
    )
    if seq_count == 4:
        across_x[0] = lax.ppermute(lots[0], "seq", xor_pairs(seq_count, 2))
        corners[0] = lax.ppermute(across_x[0], "seq", xor_pairs(seq_count, 1))
    for n, call in enumerate(calls):
        made = project_call(n, [piece for k in call for piece in chunks[k]], state)
        sets.append(made[:3])
        state = made[3]
    fqs, fks, vs = zip(*sets)
    if seq_count == 4:
        state, across_x[0] = lax.optimization_barrier((state, across_x[0]))
    states = [
        lax.ppermute(state, "seq", [(i, i + back) for i in range(seq_count - back)])
        for back in range(1, seq_count)
    ]
    position = list(range(head_count))
    num, den = within(bound, places, position, chunk, fqs, fks, vs, heads)
    mixed, *outer = across(
        bound,
        places,
        shares,
        position,
        chunk,
        near,
        far,
        fqs,
        num,
        den,
        head_gain,
        lin_out,
        states,
        heads,
    )
    far_rows = outer
    parts = scatter_rows(outer, lambda: near_chunks(mixed, lin_out, near, chunk))
    parts = in_halves(parts)
    upper, residual_upper = finish(embedded[0], gain_two, parts[0], False)
    lower, residual_lower = finish(embedded[1], gain_two, parts[1], False)

    if seq_count == 4:
        lots[1], _ = lax.optimization_barrier((lots[1], (states, far_rows)))
        across_x[1] = lax.ppermute(lots[1], "seq", xor_pairs(seq_count, 2))
        beside = lax.ppermute(vocab_table, "seq", xor_pairs(seq_count, 1))

    chunks = gather_rows(upper, lower)
    qkvs = []
    for call in calls:
        qkvs.append(matmul([piece for k in call for piece in chunks[k]], win_qkv, 3 * HEAD_DIM))
    tail = jnp.zeros((WINDOW, win_qkv.shape[1]), BF16)
    for slot, k in enumerate(slots):
        n, at = spots[k]
        tail = jnp.where(
            held_at[slot] == head_count - 1, qkvs[n][at + chunk - WINDOW : at + chunk], tail
        )
    if seq_count == 4:
        tail, across_x[1], corners[0], beside = lax.optimization_barrier(
            (tail, across_x[1], corners[0], beside)
        )
    halo = lax.ppermute(tail, "seq", [(i, i + 1) for i in range(seq_count - 1)])
    local, first = local_window(bound, places, slots, spots, chunk, qkvs, heads)
    if lots:
        lots[2], local, halo, across_x[1] = lax.optimization_barrier((lots[2], local, halo, across_x[1]))
        corners[1] = lax.ppermute(across_x[1], "seq", xor_pairs(seq_count, 1))
    mixed, *outer = halo_window(info, near, chunk, far, local, first, halo, win_out, heads)
    parts = scatter_rows(outer, lambda: near_chunks(mixed, win_out, near, chunk))
    parts = in_halves(parts)
    if seq_count == 4:
        parts[1], corners[1] = lax.optimization_barrier((parts[1], corners[1]))
    upper = finish(residual_upper, gain_three, parts[0], True)[0]
    lower = finish(residual_lower, gain_three, parts[1], True)[0]

    chunks = gather_rows(upper, lower)
    if seq_count == 4:
        across_x[2] = lax.ppermute(lots[2], "seq", xor_pairs(seq_count, 2))
        corner, _ = lax.optimization_barrier((across_x[2], parts[1]))
        corners[2] = lax.ppermute(corner, "seq", xor_pairs(seq_count, 1))
        shared = [vocab_table, beside]
        lots = [(marks_at[n], marks_at[n + 1], [across_x[n], corners[n]]) for n in range(3)]
    else:
        shared = [lax.all_gather(vocab_table, "seq", axis=1, tiled=True)]
        lots = [(0, vocab_rows, [])]
        order = jnp.zeros((1,), jnp.int32)
    first = slots[:-1] if chunk % LANES == 0 else []
    rest = [piece for k in slots[len(first) :] for piece in chunks[k]]
    first = [turn([piece for k in first for piece in chunks[k]])] if first else []
    triple = scores(order, first, rest, shared, lots, goal)
    found = {k: triple[:3, at * chunk : (at + 1) * chunk] for at, k in enumerate(slots)}

    shares = jnp.stack([found[0]] + [turned(found[k], k) for k in range(1, head_count)])
    peak = jnp.max(shares[:, 0], axis=0)
    total = jnp.sum(shares[:, 1] * jnp.exp(shares[:, 0] - peak), axis=0)
    return jnp.sum(shares[:, 2], axis=0) - (peak + jnp.log(total))


def solution(mesh):
    return jax.shard_map(
        shards,
        mesh=mesh,
        in_specs=(
            P(("shadow", "seq")),
            P(("shadow", "seq")),
            P(("shadow", "seq")),
            P(("shadow", "head"), "seq"),
            P("shadow"),
            P("shadow", "head"),
            P(("shadow", "head")),
            P(("shadow", "head"), None),
            P("shadow"),
            P("shadow", "head"),
            P(("shadow", "head"), None),
            P("shadow"),
        ),
        out_specs=P(("shadow", "seq", "head")),
        check_vma=False,
    )
```

```python
import functools

import jax
import jax.numpy as jnp
import numpy as np
from jax import lax
from jax.experimental import pallas as pl
from jax.experimental.pallas import tpu as pltpu
from jax.sharding import PartitionSpec as P

FEAT = 16
WINDOW = 64
HEAD_DIM = 128
EPSILON = 1e-05
NEGATIVE = -1e30
LANES = 128
WIDE = 256
STATE_ROWS = 160
BUFFER_ROWS = 176
F32 = jnp.float32
BF16 = jnp.bfloat16
VMEM_BYTES = 56 * 1024 * 1024


def params(**kw):
    return pltpu.CompilerParams(vmem_limit_bytes=VMEM_BYTES, **kw)


def cost(us):
    return pl.CostEstimate(flops=int(us * 6e8), transcendentals=0, bytes_accessed=int(us * 3e6))


def whole():
    return pl.BlockSpec(memory_space=pltpu.VMEM)


def smem():
    return pl.BlockSpec(memory_space=pltpu.SMEM)


def dot(a, b, dims=((1,), (0,))):
    return lax.dot_general(a, b, (dims, ((), ())), preferred_element_type=F32)


def xor_pairs(size, k):
    return [(i, i ^ k) for i in range(size)]


def rms(values, gain):
    factor = lax.rsqrt(jnp.mean(values * values, axis=-1, keepdims=True) + EPSILON)
    return (values * factor * gain.astype(F32)).astype(BF16)


def turned(value, step):
    size = lax.axis_size("head")
    return lax.ppermute(value, "head", [(i, (i + step) % size) for i in range(size)])


def gather_rows(upper, lower):
    size = lax.axis_size("head")
    if size != 4:
        full = lax.all_gather(jnp.concatenate([upper, lower]), "head")
        here = lax.axis_index("head")
        return [[upper, lower]] + [
            [lax.dynamic_index_in_dim(full, (here + k) % size, 0, False)] for k in range(1, size)
        ]
    before_upper, after_upper = turned(upper, 1), turned(upper, -1)
    after_lower, before_lower = turned(lower, -1), turned(lower, 1)
    far = [turned(before_upper, 1), turned(after_lower, -1)]
    return [[upper, lower], [after_upper, after_lower], far, [before_upper, before_lower]]


def in_halves(terms):
    if len(terms) == 2:
        return terms
    half = terms[0][0].shape[0] // 2
    return [[term[:half] for term in terms[0]], [term[half:] for term in terms[0]]]


def scatter_rows(far, near):
    size = lax.axis_size("head")
    if size != 4:
        here = lax.axis_index("head")
        full = jnp.stack([near()[0]] + list(far))
        full = jnp.stack(
            [lax.dynamic_index_in_dim(full, (d - here) % size, 0, False) for d in range(size)]
        )
        return [[lax.psum_scatter(full, "head", scatter_dimension=0, tiled=True)[0]]]
    from_before, from_after = turned(far[0], 1), turned(far[1], -1)
    own_upper, own_lower, next_upper, next_lower, prev_upper, prev_lower = near()
    lower_right, upper_left = turned(next_lower, 1), turned(prev_upper, -1)
    upper_right, lower_left = pass_on(next_upper, from_before, prev_lower, from_after)
    upper_right, lower_left = turned(upper_right, 1), turned(lower_left, -1)
    return [[own_upper, upper_right, upper_left], [own_lower, lower_right, lower_left]]


def pass_on_kernel(next_ref, before_ref, prev_ref, after_ref, right_ref, left_ref):
    right_ref[...] = (next_ref[...].astype(F32) + before_ref[...].astype(F32)).astype(BF16)
    left_ref[...] = (prev_ref[...].astype(F32) + after_ref[...].astype(F32)).astype(BF16)


def pass_on(next_upper, from_before, prev_lower, from_after):
    return pl.pallas_call(
        pass_on_kernel,
        in_specs=[whole()] * 4,
        out_specs=[whole()] * 2,
        out_shape=[jax.ShapeDtypeStruct(next_upper.shape, BF16)] * 2,
        compiler_params=params(),
        cost_estimate=cost(1.5),
        name="pass_on",
    )(next_upper, from_before, prev_lower, from_after)


def chunk_order(size):
    if size == 4:
        return [[0, 1, 3], [2]]
    return [[k] for k in range(size)]


def lookup_kernel(lots, ids_ref, table_ref, *refs):
    outs, copies, total = refs[: -1 - len(lots)], refs[-1 - len(lots) : -1], refs[-1]
    step = pl.program_id(0)
    tile = table_ref.shape[0]
    for at in range(0, TABLE_STEPS * tile if lots else 0, tile):

        @pl.when(step == at // tile)
        def _():
            for (start, stop), copy in zip(lots, copies):
                low, high = max(start, at), min(stop, at + tile)
                if low < high:
                    copy[low - start : high - start] = table_ref[low - at : high - at]

    count = ids_ref.shape[1]
    ids = jnp.transpose(jnp.broadcast_to(ids_ref[...], (8, count)))[:, 0:1] - step * tile
    hot = (lax.broadcasted_iota(jnp.int32, (count, tile), 1) == ids).astype(F32).astype(BF16)
    found = dot(hot, table_ref[...])

    @pl.when(step == 0)
    def _():
        total[...] = found

    @pl.when(step > 0)
    def _():
        total[...] += found

    @pl.when(step == pl.num_programs(0) - 1)
    def _():
        rows = outs[0].shape[0]
        for n, out in enumerate(outs):
            out[...] = total[n * rows : (n + 1) * rows].astype(BF16)


TABLE_STEPS = 5


def lookup(ids, table, pieces, lots=()):
    count = ids.shape[0]
    rows, width = table.shape
    tile = rows // TABLE_STEPS
    return pl.pallas_call(
        functools.partial(lookup_kernel, lots),
        grid=(TABLE_STEPS,),
        in_specs=[
            pl.BlockSpec((1, count), lambda i: (0, 0)),
            pl.BlockSpec((tile, width), lambda i: (i, 0)),
        ],
        out_specs=[pl.BlockSpec((count // pieces, width), lambda i: (0, 0))] * pieces
        + [
            pl.BlockSpec((stop - start, width), lambda i: (0, 0), pipeline_mode=pl.Buffered(1))
            for start, stop in lots
        ],
        out_shape=[jax.ShapeDtypeStruct((count // pieces, width), BF16)] * pieces
        + [jax.ShapeDtypeStruct((stop - start, width), BF16) for start, stop in lots],
        scratch_shapes=[pltpu.VMEM((count, width), F32)],
        compiler_params=params(),
        cost_estimate=cost(8 * count / 512),
        name="lookup",
    )(ids.reshape(1, count), table)


def gathered_sum(refs, sizes):
    rows, at = [], 0
    for size in sizes:
        total = refs[at][...].astype(F32)
        for ref in refs[at + 1 : at + size]:
            total = total + ref[...].astype(F32)
        rows.append(total)
        at += size
    return rows[0] if len(rows) == 1 else jnp.concatenate(rows, axis=0)


def collect_kernel(sizes, *refs):
    ins, outs = refs[: sum(sizes)], refs[sum(sizes) :]
    rows = outs[0].shape[0]
    total = gathered_sum(ins, sizes)
    for n, out in enumerate(outs):
        out[...] = total[n * rows : (n + 1) * rows].astype(BF16)


def collect(terms, pieces):
    sizes = [len(part) for part in terms]
    parts = [term for part in terms for term in part]
    rows, width = sum(part[0].shape[0] for part in terms), parts[0].shape[1]
    return pl.pallas_call(
        functools.partial(collect_kernel, sizes),
        in_specs=[whole()] * len(parts),
        out_specs=[whole()] * pieces,
        out_shape=[jax.ShapeDtypeStruct((rows // pieces, width), BF16)] * pieces,
        compiler_params=params(),
        cost_estimate=cost(2),
        name="collect",
    )(*parts)


def begin_kernel(pieces, order_ref, gain_ref, *refs):
    ins, outs, held = refs[:pieces], refs[pieces:-1], refs[-1]
    for n in range(pieces):
        held[order_ref[n]] = ins[n][...]
    values = jnp.concatenate([held[n] for n in range(pieces)], axis=1)
    units = rms(values.astype(F32), gain_ref[...])
    half = outs[0].shape[0]
    for n in range(2):
        outs[n][...] = values[n * half : (n + 1) * half]
        outs[2 + n][...] = units[n * half : (n + 1) * half]


def begin(order, gain, pieces):
    rows, width = pieces[0].shape
    half = jax.ShapeDtypeStruct((rows // 2, width * len(pieces)), BF16)
    return pl.pallas_call(
        functools.partial(begin_kernel, len(pieces)),
        in_specs=[smem()] + [whole()] * (1 + len(pieces)),
        out_specs=[whole()] * 4,
        out_shape=[half] * 4,
        scratch_shapes=[pltpu.VMEM((len(pieces), rows, width), BF16)],
        compiler_params=params(),
        cost_estimate=cost(2),
        name="begin",
    )(order, gain.reshape(1, -1), *pieces)


def finish_kernel(parts, last, residual_ref, gain_ref, *refs):
    total = gathered_sum(refs[:parts], [parts]) + residual_ref[...].astype(F32)
    if not last:
        total = total.astype(BF16)
        refs[parts + 1][...] = total
    refs[parts][...] = rms(total.astype(F32), gain_ref[...])


def finish(residual, gain, terms, last):
    full = jax.ShapeDtypeStruct(residual.shape, BF16)
    return pl.pallas_call(
        functools.partial(finish_kernel, len(terms), last),
        in_specs=[whole()] * (2 + len(terms)),
        out_specs=[whole()] * (1 if last else 2),
        out_shape=[full] * (1 if last else 2),
        compiler_params=params(),
        cost_estimate=cost(2),
        name="finish",
    )(residual, gain, *terms)


def selectors():
    pairs = [(r, s) for r in range(FEAT) for s in range(r, FEAT)]
    picks = np.zeros((2, 2, LANES, WIDE), np.float32)
    extra = np.zeros((3, WIDE), np.float32)
    extra[0:2, 0] = 1.0
    extra[1, 1 : 1 + FEAT] = 1.0
    extra[2] = 1.0
    for kind in range(2):
        first = kind * FEAT
        for r in range(FEAT):
            picks[kind, 0, first + r, 1 + r] = FEAT ** (-0.25)
        for n, (r, s) in enumerate(pairs):
            picks[kind, 0, first + r, 1 + FEAT + n] = FEAT ** (-0.25)
            picks[kind, 1, first + s, 1 + FEAT + n] = FEAT ** (-0.25)
    for n, (r, s) in enumerate(pairs):
        extra[2, 1 + FEAT + n] = 0.5**0.5 if r == s else 1.0
    return jnp.asarray(np.concatenate([picks, picks], axis=2), BF16), jnp.asarray(extra)


def place_column(places_ref, slots, rows):
    inner = lax.broadcasted_iota(jnp.int32, (rows, 1), 0)
    return jnp.concatenate([inner + places_ref[slot] for slot in slots], axis=0)


def place_row(places_ref, slots, rows):
    inner = lax.broadcasted_iota(jnp.int32, (1, rows), 1)
    return jnp.concatenate([inner + places_ref[slot] for slot in slots], axis=1)


def project_kernel(heads, slots, chunk, count, pieces, more, last, bound_ref, places_ref, *refs):
    units = jnp.concatenate([ref[...] for ref in refs[:pieces]], axis=0)
    weight_ref, pick_ref, extra_ref = refs[pieces : pieces + 3]
    fq_ref, fk_ref, v_ref, state_ref = refs[-4:]
    projected = dot(units, weight_ref[...])
    rows, width = projected.shape
    needed = (heads - 1) * LANES + WIDE
    if needed > width:
        projected = jnp.pad(projected, ((0, 0), (0, needed - width)))
    bound = bound_ref[0]
    place = place_column(places_ref, slots, chunk)
    kept = ((place >= bound) | (bound == count)).astype(F32)
    ones = jnp.ones((8, rows), BF16)
    shift = 2 * FEAT
    for head in range(heads):
        part = projected[:, head * LANES : head * LANES + WIDE]
        narrow = part if head == 0 else pltpu.roll(part, WIDE - shift * head, 1)
        narrow = narrow[:, :LANES]
        values = pltpu.roll(part, WIDE - shift * (head + 1), 1)[:, :HEAD_DIM].astype(BF16)
        v_ref[:, head * HEAD_DIM : (head + 1) * HEAD_DIM] = values
        upper = narrow.astype(BF16)
        lower = (narrow - upper.astype(F32)).astype(BF16)
        both = jnp.concatenate([upper, lower], axis=1)
        feats = []
        for kind in range(2):
            one = dot(both, pick_ref[kind, 0]) + extra_ref[0:1]
            two = dot(both, pick_ref[kind, 1]) + extra_ref[1:2]
            feats.append((one * two * extra_ref[2:3]).astype(BF16))
        fq_ref[head] = feats[0]
        fk_ref[head] = feats[1]
        keys = (feats[1].astype(F32) * kept).astype(BF16)
        state = dot(keys, values, ((0,), (0,)))
        total = dot(ones, keys)
        tail = jnp.concatenate([total[0:1, :LANES], total[0:1, LANES:], jnp.zeros((14, LANES), F32)], axis=0)
        state = jnp.concatenate([state[0:STATE_ROWS], tail], axis=0)
        if more:
            state = state + refs[pieces + 3][head]
        state_ref[head] = state.astype(BF16) if last else state


def project(bound, places, slots, chunk, count, pieces, weight, constants, earlier, last, heads):
    rows = sum(piece.shape[0] for piece in pieces)
    extra = [] if earlier is None else [earlier]
    return pl.pallas_call(
        functools.partial(project_kernel, heads, slots, chunk, count, len(pieces), bool(extra), last),
        in_specs=[smem(), smem()] + [whole()] * (len(pieces) + 3 + len(extra)),
        out_specs=[whole()] * 4,
        out_shape=[
            jax.ShapeDtypeStruct((heads, rows, WIDE), BF16),
            jax.ShapeDtypeStruct((heads, rows, WIDE), BF16),
            jax.ShapeDtypeStruct((rows, heads * HEAD_DIM), BF16),
            jax.ShapeDtypeStruct((heads, BUFFER_ROWS, HEAD_DIM), BF16 if last else F32),
        ],
        compiler_params=params(),
        cost_estimate=cost(5),
        name="project",
    )(bound, places, *pieces, weight, *constants, *extra)


def within_kernel(heads, slots, chunk, sets, bound_ref, places_ref, *refs):
    fqs, fks, vs = refs[:sets], refs[sets : 2 * sets], refs[2 * sets : 3 * sets]
    num_ref, den_ref = refs[3 * sets :]
    bound = bound_ref[0]
    row = place_column(places_ref, slots, chunk)
    col = place_row(places_ref, slots, chunk)
    allowed = (row >= col) & ((row >= bound) == (col >= bound))
    for head in range(heads):
        query = jnp.concatenate([ref[head] for ref in fqs], axis=0)
        keys = jnp.concatenate([ref[head] for ref in fks], axis=0)
        values = jnp.concatenate(
            [ref[:, head * HEAD_DIM : (head + 1) * HEAD_DIM] for ref in vs], axis=0
        )
        weights = dot(query, keys, ((1,), (1,)))
        weights = jnp.where(allowed, weights, 0.0)
        den_ref[head] = jnp.broadcast_to(
            jnp.sum(weights, axis=-1, keepdims=True), (row.shape[0], 8)
        )
        num_ref[head] = dot(weights.astype(BF16), values)


def within(bound, places, slots, chunk, fqs, fks, vs, heads):
    count = len(slots) * chunk
    return pl.pallas_call(
        functools.partial(within_kernel, heads, slots, chunk, len(fqs)),
        in_specs=[smem(), smem()] + [whole()] * (3 * len(fqs)),
        out_specs=[whole()] * 2,
        out_shape=[
            jax.ShapeDtypeStruct((heads, count, HEAD_DIM), F32),
            jax.ShapeDtypeStruct((heads, count, 8), F32),
        ],
        compiler_params=params(),
        cost_estimate=cost(4.5),
        name="within",
    )(bound, places, *fqs, *fks, *vs)


def split_store(total, refs):
    rows = refs[0].shape[0]
    for n, ref in enumerate(refs):
        ref[...] = total[n * rows : (n + 1) * rows].astype(BF16)


def across_kernel(heads, slots, chunk, sets, earlier, near, bound_ref, places_ref, share_ref, *refs):
    fqs, refs = refs[:sets], refs[sets:]
    num_ref, den_ref, gain_ref, weight_ref = refs[:4]
    states, refs = refs[4 : 4 + earlier], refs[4 + earlier :]
    mixed_ref, fars = refs[0], refs[1:]
    bound = bound_ref[0]
    before = (place_column(places_ref, slots, chunk) < bound).astype(F32)
    for head in range(heads):
        carried = jnp.zeros((BUFFER_ROWS, HEAD_DIM), F32)
        for n in range(earlier):
            carried = carried + jnp.where(share_ref[n] > 0, states[n][head].astype(F32), 0.0)
        state = jnp.concatenate(
            [carried[0:STATE_ROWS], jnp.zeros((WIDE - STATE_ROWS, HEAD_DIM), F32)], axis=0
        ).astype(BF16)
        total = jnp.concatenate(
            [carried[STATE_ROWS : STATE_ROWS + 1], carried[STATE_ROWS + 1 : STATE_ROWS + 2]], axis=1
        )
        query = jnp.concatenate([ref[head] for ref in fqs], axis=0)
        numerator = num_ref[head] + before * dot(query, state)
        more = jnp.sum(query.astype(F32) * total, axis=-1, keepdims=True)
        denominator = den_ref[head][:, 0:1] + before * more
        lanes = slice(head * HEAD_DIM, (head + 1) * HEAD_DIM)
        mixed_ref[:, lanes] = (numerator / denominator * gain_ref[:, lanes].astype(F32)).astype(BF16)
    split_store(dot(mixed_ref[near * chunk :], weight_ref[...]), fars)


def across(bound, places, share, slots, chunk, near, far, fqs, num, den, gain, weight, states, heads):
    count = len(slots) * chunk
    rows = (count - near * chunk) // far
    return pl.pallas_call(
        functools.partial(across_kernel, heads, slots, chunk, len(fqs), len(states), near),
        in_specs=[smem()] * 3 + [whole()] * (len(fqs) + 4 + len(states)),
        out_specs=[whole()] * (1 + far),
        out_shape=[jax.ShapeDtypeStruct((count, heads * HEAD_DIM), BF16)]
        + [jax.ShapeDtypeStruct((rows, weight.shape[1]), BF16)] * far,
        compiler_params=params(),
        cost_estimate=cost(4.5),
        name="across",
    )(bound, places, share, *fqs, num, den, gain, weight, *states)


def near_kernel(rows, mixed_ref, weight_ref, *outs):
    split_store(dot(mixed_ref[0:rows], weight_ref[...]), outs)


def near_chunks(mixed, weight, near, chunk):
    pieces = 2 * near if near > 1 else 1
    rows = near * chunk
    return pl.pallas_call(
        functools.partial(near_kernel, rows),
        in_specs=[whole()] * 2,
        out_specs=[whole()] * pieces,
        out_shape=[jax.ShapeDtypeStruct((rows // pieces, weight.shape[1]), BF16)] * pieces,
        compiler_params=params(),
        cost_estimate=cost(4),
        name="near",
    )(mixed, weight)


def matmul_kernel(*refs):
    a = jnp.concatenate([ref[...] for ref in refs[:-2]], axis=0)
    refs[-1][...] = dot(a, refs[-2][...]).astype(BF16)


def matmul(pieces, b, tile):
    rows = sum(piece.shape[0] for piece in pieces)
    inner = b.shape[0]
    return pl.pallas_call(
        matmul_kernel,
        grid=(b.shape[1] // tile,),
        in_specs=[
            pl.BlockSpec(piece.shape, lambda n: (0, 0), pipeline_mode=pl.Buffered(1)) for piece in pieces
        ]
        + [pl.BlockSpec((inner, tile), lambda n: (0, n))],
        out_specs=pl.BlockSpec((rows, tile), lambda n: (0, n)),
        out_shape=jax.ShapeDtypeStruct((rows, b.shape[1]), BF16),
        compiler_params=params(),
        cost_estimate=cost(5),
        name="matmul",
    )(*pieces, b)


def attend(queries, keys, values, allowed):
    rows = queries[0].shape[0]
    scores = jnp.concatenate(
        [dot(q, k, ((1,), (1,))) for q, k in zip(queries, keys)], axis=0
    ) * HEAD_DIM ** (-0.5)
    allowed = jnp.concatenate([allowed.astype(F32)] * len(queries), axis=0) > 0
    scores = jnp.where(allowed, scores, NEGATIVE)
    peak = jnp.max(scores, axis=-1, keepdims=True)
    weights = jnp.where(allowed, jnp.exp(scores - peak), 0.0)
    probabilities = (weights * (1.0 / jnp.sum(weights, axis=-1, keepdims=True))).astype(BF16)
    return jnp.concatenate(
        [
            dot(probabilities[n * rows : (n + 1) * rows], value).astype(BF16)
            for n, value in enumerate(values)
        ],
        axis=1,
    )


def local_kernel(heads, slots, spots, chunk, sets, bound_ref, places_ref, *refs):
    qkvs, (result_ref, first_ref) = refs[:sets], refs[sets:]
    size = len(slots)
    reach = chunk + WINDOW
    bound = bound_ref[0]
    row = lax.broadcasted_iota(jnp.int32, (chunk, reach), 0)
    col = lax.broadcasted_iota(jnp.int32, (chunk, reach), 1)
    band = (col > row) & (col <= row + WINDOW)
    for slot in range(size):
        k = slots[slot]
        mine, at = spots[k]
        theirs, there = spots[(k - 1) % size]
        base = places_ref[slot]
        query_place = row + base
        key_place = col + (base - WINDOW)
        allowed = band & (key_place >= 0) & ((query_place >= bound) == (key_place >= bound))
        rows = slice(at, at + chunk)
        tail = slice(there + chunk - WINDOW, there + chunk)

        @pl.when(base == 0)
        def _():
            first_ref[...] = qkvs[mine][at : at + WINDOW]

        queries, keys, values = [], [], []
        for head in range(heads):
            lane = head * 3 * HEAD_DIM
            queries.append(qkvs[mine][rows, lane : lane + HEAD_DIM])
            for n, held in ((1, keys), (2, values)):
                lanes = slice(lane + n * HEAD_DIM, lane + (n + 1) * HEAD_DIM)
                held.append(jnp.concatenate([qkvs[theirs][tail, lanes], qkvs[mine][rows, lanes]], axis=0))
        result_ref[slot * chunk : (slot + 1) * chunk] = attend(queries, keys, values, allowed)


def local_window(bound, places, slots, spots, chunk, qkvs, heads):
    return pl.pallas_call(
        functools.partial(local_kernel, heads, slots, spots, chunk, len(qkvs)),
        in_specs=[smem(), smem()] + [whole()] * len(qkvs),
        out_specs=[whole()] * 2,
        out_shape=[
            jax.ShapeDtypeStruct((len(slots) * chunk, heads * HEAD_DIM), BF16),
            jax.ShapeDtypeStruct((WINDOW, qkvs[0].shape[1]), BF16),
        ],
        compiler_params=params(),
        cost_estimate=cost(8),
        name="local_window",
    )(bound, places, *qkvs)


def halo_kernel(heads, count, start, info_ref, local_ref, first_ref, halo_ref, weight_ref, result_ref, *fars):
    result_ref[...] = local_ref[...]
    bound, valid_from, spot = info_ref[0], info_ref[1], info_ref[2]
    row = lax.broadcasted_iota(jnp.int32, (WINDOW, 2 * WINDOW), 0)
    col = lax.broadcasted_iota(jnp.int32, (WINDOW, 2 * WINDOW), 1)
    key_place = col - WINDOW
    allowed = (col > row) & (col <= row + WINDOW) & ((row >= bound) == (key_place >= bound))
    allowed = allowed & ((key_place >= 0) | (key_place + count >= valid_from))
    spot = pl.multiple_of(spot, WINDOW)
    queries, keys, values = [], [], []
    for head in range(heads):
        lane = head * 3 * HEAD_DIM
        queries.append(first_ref[:, lane : lane + HEAD_DIM])
        for n, held in ((1, keys), (2, values)):
            lanes = slice(lane + n * HEAD_DIM, lane + (n + 1) * HEAD_DIM)
            held.append(jnp.concatenate([halo_ref[:, lanes], first_ref[:, lanes]], axis=0))
    result_ref[pl.ds(spot, WINDOW), :] = attend(queries, keys, values, allowed)
    split_store(dot(result_ref[start:], weight_ref[...]), fars)


def halo_window(info, near, chunk, far, local, first, halo, weight, heads):
    count = local.shape[0]
    rows = (count - near * chunk) // far
    return pl.pallas_call(
        functools.partial(halo_kernel, heads, count, near * chunk),
        in_specs=[smem()] + [whole()] * 4,
        out_specs=[whole()] * (1 + far),
        out_shape=[jax.ShapeDtypeStruct(local.shape, BF16)]
        + [jax.ShapeDtypeStruct((rows, weight.shape[1]), BF16)] * far,
        compiler_params=params(),
        cost_estimate=cost(4.5),
        name="halo_window",
    )(info, local, first, halo, weight)


def turn_kernel(*refs):
    refs[-1][...] = jnp.transpose(jnp.concatenate([ref[...] for ref in refs[:-1]], axis=0))


def turn(pieces):
    rows, width = sum(piece.shape[0] for piece in pieces), pieces[0].shape[1]
    return pl.pallas_call(
        turn_kernel,
        in_specs=[whole()] * len(pieces),
        out_specs=whole(),
        out_shape=jax.ShapeDtypeStruct((width, rows), BF16),
        compiler_params=params(),
        cost_estimate=cost(3),
        name="turn",
    )(*pieces)


def score_kernel(ready, rest, common, pieces, lots, tile, order_ref, *refs):
    early, refs = refs[:ready], refs[ready:]
    units, refs = refs[:rest], refs[rest:]
    shared, refs = refs[:common], refs[common:]
    tables, (goal_ref, out_ref, turned_ref, held) = refs[: len(lots) * pieces], refs[len(lots) * pieces :]
    step = pl.program_id(0)
    width = (shared or tables)[0].shape[1]
    count = goal_ref.shape[1]
    part = 128

    @pl.when(step == 0)
    def _():
        at = 0
        for ref in early:
            at = ref.shape[1]
            turned_ref[:, 0:at] = ref[...]
        turned_ref[:, at:] = jnp.transpose(jnp.concatenate([ref[...] for ref in units], axis=0))
        held[0] = jnp.full((8, count), NEGATIVE, F32)
        held[1] = jnp.zeros((8, count), F32)
        held[2] = jnp.zeros((8, count), F32)

    def run(mine):
        inner = lax.broadcasted_iota(jnp.int32, (part // 8, 8, count), 0) * 8
        inner = inner + lax.broadcasted_iota(jnp.int32, (part // 8, 8, count), 1)
        peak, total, picked = held[0], held[1], held[2]
        sides = [
            turned_ref[pl.ds(pl.multiple_of(order_ref[n] * width, width), width), :] for n in range(len(mine))
        ]
        for at in range(0, tile, part):
            logits = None
            for table, side in zip(mine, sides):
                more = dot(table[at : at + part], side)
                logits = more if logits is None else logits + more
            logits = logits.reshape(part // 8, 8, count)
            goal = (goal_ref[...] - (step * tile + at)).reshape(1, 1, count)
            old = peak
            peak = jnp.maximum(old, jnp.max(logits, axis=0))
            total = total * jnp.exp(old - peak) + jnp.sum(jnp.exp(logits - peak[None]), axis=0)
            picked = picked + jnp.sum(jnp.where(inner == goal, logits, 0.0), axis=0)
        held[0], held[1], held[2] = peak, total, picked

    for lot, (start, stop) in enumerate(lots):
        pl.when((step >= start) & (step < stop))(
            lambda lot=lot: run(list(shared) + list(tables[lot * pieces : (lot + 1) * pieces]))
        )

    @pl.when(step == pl.num_programs(0) - 1)
    def _():
        peak = jnp.max(held[0], axis=0, keepdims=True)
        total = jnp.sum(held[1] * jnp.exp(held[0] - peak), axis=0, keepdims=True)
        picked = jnp.sum(held[2], axis=0, keepdims=True)
        out_ref[...] = jnp.concatenate([peak, total, picked, jnp.zeros((5, count), F32)], axis=0)


def scores(order, early, units, shared, lots, goal):
    count = goal.shape[1]
    rows = lots[-1][1]
    tile = 640
    specs = [pl.BlockSpec((tile, table.shape[1]), lambda i: (i, 0)) for table in shared]
    steps = []
    for first, last, tables in lots:
        start, stop = first // tile, last // tile
        steps.append((start, stop))
        for table in tables:
            specs.append(
                pl.BlockSpec(
                    (tile, table.shape[1]),
                    lambda i, start=start, stop=stop: (jnp.clip(i, start, stop - 1) - start, 0),
                )
            )
    still = [
        pl.BlockSpec(piece.shape, lambda i: (0, 0), pipeline_mode=pl.Buffered(1)) for piece in early + units
    ]
    return pl.pallas_call(
        functools.partial(
            score_kernel, len(early), len(units), len(shared), len(lots[0][2]), steps, tile
        ),
        in_specs=[smem()] + still + specs + [pl.BlockSpec((1, count), lambda i: (0, 0))],
        out_specs=pl.BlockSpec((8, count), lambda i: (0, 0)),
        grid=(rows // tile,),
        out_shape=jax.ShapeDtypeStruct((8, count), F32),
        scratch_shapes=[pltpu.VMEM((units[0].shape[1], count), BF16), pltpu.VMEM((3, 8, count), F32)],
        compiler_params=params(),
        cost_estimate=cost(20),
        name="scores",
    )(order, *early, *units, *shared, *[table for lot in lots for table in lot[2]], goal)


def shards(
    token_ids,
    target_ids,
    doc_start,
    vocab_table,
    norm_gain_one,
    lin_qkv,
    lin_head_gain,
    lin_out,
    norm_gain_two,
    win_qkv,
    win_out,
    final_gain,
):
    head_count = lax.axis_size("head")
    seq_count = lax.axis_size("seq")
    head_index = lax.axis_index("head")
    seq_index = lax.axis_index("seq")
    tok_count = token_ids.shape[0]
    chunk = tok_count // head_count
    vocab_rows = vocab_table.shape[0]
    heads = lin_qkv.shape[1] // (2 * FEAT + HEAD_DIM)
    vocab_first = head_index * vocab_rows
    calls = chunk_order(head_count)
    slots = [k for call in calls for k in call]
    near = 3 if head_count == 4 else 1
    far = 2 if head_count == 4 else head_count - 1
    spots = {}
    for n, call in enumerate(calls):
        for at, k in enumerate(call):
            spots[k] = (n, at * chunk)
    held_at = (head_index + jnp.asarray(slots, jnp.int32)) % head_count
    places = held_at * chunk

    marks = jnp.concatenate([token_ids, jnp.broadcast_to(doc_start, (LANES,))])
    marks = jnp.stack(
        [marks] + [lax.ppermute(marks, "seq", xor_pairs(seq_count, k)) for k in range(1, seq_count)]
    )
    block = jnp.arange(seq_count, dtype=jnp.int32)
    order = seq_index ^ block
    starts = marks[:, tok_count]
    starts = jnp.sum(jnp.where(order[None, :] == block[:, None], starts[None, :], 0), axis=1)
    bound = doc_start.astype(jnp.int32)

    marks_at = [part * (vocab_rows // 10) for part in (0, 3, 8, 10)]
    bounds = list(zip(marks_at[:-1], marks_at[1:])) if seq_count == 4 else []
    lots = []

    ids = (marks[:, :tok_count] - vocab_first).reshape(seq_count, head_count, chunk)

    def ids_of(k):
        return lax.dynamic_index_in_dim(ids, (head_index + k) % head_count, 1, False).reshape(-1)

    if head_count == 4:
        outer = lookup(ids_of(2), vocab_table, 2)

        def inner():
            after, before, _ = lax.optimization_barrier((ids_of(1), ids_of(3), outer))
            half = after.shape[0] // 2
            next_lower, prev_upper = lookup(jnp.concatenate([after[half:], before[:half]]), vocab_table, 2)
            next_upper, prev_lower = lookup(jnp.concatenate([after[:half], before[half:]]), vocab_table, 2)
            own = lookup(ids_of(0), vocab_table, 2, bounds)
            lots.extend(own[2:])
            return [own[0], own[1], next_upper, next_lower, prev_upper, prev_lower]

    else:
        outer = [lookup(ids_of(k), vocab_table, 1)[0] for k in range(1, head_count)]

        def inner():
            own = lookup(ids_of(0), vocab_table, 1, bounds)
            lots.extend(own[1:])
            return own[:1]

    found = collect(scatter_rows(outer, inner), seq_count)
    gathered = [found[0]] + [
        lax.ppermute(found[k], "seq", xor_pairs(seq_count, k)) for k in range(1, seq_count)
    ]
    if lots:
        lots[0], gathered = lax.optimization_barrier((lots[0], gathered))
    *embedded, upper, lower = begin(order, norm_gain_one, gathered)
    across_x, corners = [None] * 3, [None] * 3

    constants = selectors()
    sets, state = [], None

    def project_call(n, pieces, state):
        first = sum(len(c) for c in calls[:n])
        return project(
            bound,
            places[first : first + len(calls[n])],
            list(range(len(calls[n]))),
            chunk,
            tok_count,
            pieces,
            lin_qkv,
            constants,
            state,
            n == len(calls) - 1,
            heads,
        )

    chunks = gather_rows(upper, lower)

    shares = []
    for back in range(1, seq_count):
        between = (block > seq_index - back) & (block < seq_index)
        broken = jnp.sum(jnp.where(between & (starts != tok_count), 1, 0))
        shares.append(((broken == 0) & (seq_index >= back)).astype(jnp.int32))
    shares = jnp.stack(shares)
    previous = jnp.sum(jnp.where(block == seq_index - 1, starts, 0))
    valid_from = jnp.where(
        seq_index == 0, tok_count, jnp.where(previous == tok_count, 0, previous)
    ).astype(jnp.int32)
    first_spot = jnp.sum(jnp.where(held_at == 0, jnp.arange(head_count) * chunk, 0)).astype(jnp.int32)
    info = jnp.stack([bound[0], valid_from, first_spot])
    goals = (target_ids - vocab_first).reshape(head_count, chunk)
    goal = jnp.concatenate(
        [lax.dynamic_index_in_dim(goals, (head_index + k) % head_count, 0, False) for k in slots]
    ).reshape(1, -1)
    gain_two, gain_three = norm_gain_two.reshape(1, -1), final_gain.reshape(1, -1)
    head_gain = lin_head_gain.reshape(1, -1)
    chunks[slots[-1]], shares, info, goal, gain_two, gain_three, head_gain = lax.optimization_barrier(
        (chunks[slots[-1]], shares, info, goal, gain_two, gain_three, head_gain)
    )
    if seq_count == 4:
        across_x[0] = lax.ppermute(lots[0], "seq", xor_pairs(seq_count, 2))
        corners[0] = lax.ppermute(across_x[0], "seq", xor_pairs(seq_count, 1))
    for n, call in enumerate(calls):
        made = project_call(n, [piece for k in call for piece in chunks[k]], state)
        sets.append(made[:3])
        state = made[3]
    fqs, fks, vs = zip(*sets)
    if seq_count == 4:
        state, across_x[0] = lax.optimization_barrier((state, across_x[0]))
    states = [
        lax.ppermute(state, "seq", [(i, i + back) for i in range(seq_count - back)])
        for back in range(1, seq_count)
    ]
    position = list(range(head_count))
    num, den = within(bound, places, position, chunk, fqs, fks, vs, heads)
    mixed, *outer = across(
        bound,
        places,
        shares,
        position,
        chunk,
        near,
        far,
        fqs,
        num,
        den,
        head_gain,
        lin_out,
        states,
        heads,
    )
    far_rows = outer
    parts = scatter_rows(outer, lambda: near_chunks(mixed, lin_out, near, chunk))
    parts = in_halves(parts)
    upper, residual_upper = finish(embedded[0], gain_two, parts[0], False)
    lower, residual_lower = finish(embedded[1], gain_two, parts[1], False)

    if seq_count == 4:
        lots[1], _ = lax.optimization_barrier((lots[1], (states, far_rows)))
        across_x[1] = lax.ppermute(lots[1], "seq", xor_pairs(seq_count, 2))
        beside = lax.ppermute(vocab_table, "seq", xor_pairs(seq_count, 1))

    chunks = gather_rows(upper, lower)
    qkvs = []
    for call in calls:
        qkvs.append(matmul([piece for k in call for piece in chunks[k]], win_qkv, 3 * HEAD_DIM))
    tail = jnp.zeros((WINDOW, win_qkv.shape[1]), BF16)
    for slot, k in enumerate(slots):
        n, at = spots[k]
        tail = jnp.where(
            held_at[slot] == head_count - 1, qkvs[n][at + chunk - WINDOW : at + chunk], tail
        )
    if seq_count == 4:
        tail, across_x[1], corners[0], beside = lax.optimization_barrier(
            (tail, across_x[1], corners[0], beside)
        )
    halo = lax.ppermute(tail, "seq", [(i, i + 1) for i in range(seq_count - 1)])
    local, first = local_window(bound, places, slots, spots, chunk, qkvs, heads)
    if lots:
        lots[2], local, halo, across_x[1] = lax.optimization_barrier((lots[2], local, halo, across_x[1]))
        corners[1] = lax.ppermute(across_x[1], "seq", xor_pairs(seq_count, 1))
    mixed, *outer = halo_window(info, near, chunk, far, local, first, halo, win_out, heads)
    if seq_count == 4:
        mixed, corners[1] = lax.optimization_barrier((mixed, corners[1]))
    parts = scatter_rows(outer, lambda: near_chunks(mixed, win_out, near, chunk))
    parts = in_halves(parts)
    upper = finish(residual_upper, gain_three, parts[0], True)[0]
    lower = finish(residual_lower, gain_three, parts[1], True)[0]

    chunks = gather_rows(upper, lower)
    if seq_count == 4:
        across_x[2] = lax.ppermute(lots[2], "seq", xor_pairs(seq_count, 2))
        corner, _ = lax.optimization_barrier((across_x[2], chunks[1:]))
        corners[2] = lax.ppermute(corner, "seq", xor_pairs(seq_count, 1))
        shared = [vocab_table, beside]
        lots = [(marks_at[n], marks_at[n + 1], [across_x[n], corners[n]]) for n in range(3)]
    else:
        shared = [lax.all_gather(vocab_table, "seq", axis=1, tiled=True)]
        lots = [(0, vocab_rows, [])]
        order = jnp.zeros((1,), jnp.int32)
    first = slots[:-1] if chunk % LANES == 0 else []
    rest = [piece for k in slots[len(first) :] for piece in chunks[k]]
    first = [turn([piece for k in first for piece in chunks[k]])] if first else []
    triple = scores(order, first, rest, shared, lots, goal)
    found = {k: triple[:3, at * chunk : (at + 1) * chunk] for at, k in enumerate(slots)}

    shares = jnp.stack([found[0]] + [turned(found[k], k) for k in range(1, head_count)])
    peak = jnp.max(shares[:, 0], axis=0)
    total = jnp.sum(shares[:, 1] * jnp.exp(shares[:, 0] - peak), axis=0)
    return jnp.sum(shares[:, 2], axis=0) - (peak + jnp.log(total))


def solution(mesh):
    return jax.shard_map(
        shards,
        mesh=mesh,
        in_specs=(
            P(("shadow", "seq")),
            P(("shadow", "seq")),
            P(("shadow", "seq")),
            P(("shadow", "head"), "seq"),
            P("shadow"),
            P("shadow", "head"),
            P(("shadow", "head")),
            P(("shadow", "head"), None),
            P("shadow"),
            P("shadow", "head"),
            P(("shadow", "head"), None),
            P("shadow"),
        ),
        out_specs=P(("shadow", "seq", "head")),
        check_vma=False,
    )
```

```python
import functools

import jax
import jax.numpy as jnp
import numpy as np
from jax import lax
from jax.experimental import pallas as pl
from jax.experimental.pallas import tpu as pltpu
from jax.sharding import PartitionSpec as P

FEAT = 16
WINDOW = 64
HEAD_DIM = 128
EPSILON = 1e-05
NEGATIVE = -1e30
LANES = 128
WIDE = 256
STATE_ROWS = 160
BUFFER_ROWS = 176
F32 = jnp.float32
BF16 = jnp.bfloat16
VMEM_BYTES = 56 * 1024 * 1024


def params(**kw):
    return pltpu.CompilerParams(vmem_limit_bytes=VMEM_BYTES, **kw)


def cost(us):
    return pl.CostEstimate(flops=int(us * 6e8), transcendentals=0, bytes_accessed=int(us * 3e6))


def whole():
    return pl.BlockSpec(memory_space=pltpu.VMEM)


def smem():
    return pl.BlockSpec(memory_space=pltpu.SMEM)


def dot(a, b, dims=((1,), (0,))):
    return lax.dot_general(a, b, (dims, ((), ())), preferred_element_type=F32)


def xor_pairs(size, k):
    return [(i, i ^ k) for i in range(size)]


def rms(values, gain):
    factor = lax.rsqrt(jnp.mean(values * values, axis=-1, keepdims=True) + EPSILON)
    return (values * factor * gain.astype(F32)).astype(BF16)


def turned(value, step):
    size = lax.axis_size("head")
    return lax.ppermute(value, "head", [(i, (i + step) % size) for i in range(size)])


def gather_rows(upper, lower):
    size = lax.axis_size("head")
    if size != 4:
        full = lax.all_gather(jnp.concatenate([upper, lower]), "head")
        here = lax.axis_index("head")
        return [[upper, lower]] + [
            [lax.dynamic_index_in_dim(full, (here + k) % size, 0, False)] for k in range(1, size)
        ]
    before_upper, after_upper = turned(upper, 1), turned(upper, -1)
    after_lower, before_lower = turned(lower, -1), turned(lower, 1)
    far = [turned(before_upper, 1), turned(after_lower, -1)]
    return [[upper, lower], [after_upper, after_lower], far, [before_upper, before_lower]]


def in_halves(terms):
    if len(terms) == 2:
        return terms
    half = terms[0][0].shape[0] // 2
    return [[term[:half] for term in terms[0]], [term[half:] for term in terms[0]]]


def scatter_rows(far, near):
    size = lax.axis_size("head")
    if size != 4:
        here = lax.axis_index("head")
        full = jnp.stack([near()[0]] + list(far))
        full = jnp.stack(
            [lax.dynamic_index_in_dim(full, (d - here) % size, 0, False) for d in range(size)]
        )
        return [[lax.psum_scatter(full, "head", scatter_dimension=0, tiled=True)[0]]]
    from_before, from_after = turned(far[0], 1), turned(far[1], -1)
    own_upper, own_lower, next_upper, next_lower, prev_upper, prev_lower = near()
    lower_right, upper_left = turned(next_lower, 1), turned(prev_upper, -1)
    upper_right, lower_left = pass_on(next_upper, from_before, prev_lower, from_after)
    upper_right, lower_left = turned(upper_right, 1), turned(lower_left, -1)
    return [[own_upper, upper_right, upper_left], [own_lower, lower_right, lower_left]]


def pass_on_kernel(next_ref, before_ref, prev_ref, after_ref, right_ref, left_ref):
    right_ref[...] = (next_ref[...].astype(F32) + before_ref[...].astype(F32)).astype(BF16)
    left_ref[...] = (prev_ref[...].astype(F32) + after_ref[...].astype(F32)).astype(BF16)


def pass_on(next_upper, from_before, prev_lower, from_after):
    return pl.pallas_call(
        pass_on_kernel,
        in_specs=[whole()] * 4,
        out_specs=[whole()] * 2,
        out_shape=[jax.ShapeDtypeStruct(next_upper.shape, BF16)] * 2,
        compiler_params=params(),
        cost_estimate=cost(1.5),
        name="pass_on",
    )(next_upper, from_before, prev_lower, from_after)


def chunk_order(size):
    if size == 4:
        return [[0, 1, 3], [2]]
    return [[k] for k in range(size)]


def lookup_kernel(lots, ids_ref, table_ref, *refs):
    outs, copies, total = refs[: -1 - len(lots)], refs[-1 - len(lots) : -1], refs[-1]
    step = pl.program_id(0)
    tile = table_ref.shape[0]
    for at in range(0, TABLE_STEPS * tile if lots else 0, tile):

        @pl.when(step == at // tile)
        def _():
            for (start, stop), copy in zip(lots, copies):
                low, high = max(start, at), min(stop, at + tile)
                if low < high:
                    copy[low - start : high - start] = table_ref[low - at : high - at]

    count = ids_ref.shape[1]
    ids = jnp.transpose(jnp.broadcast_to(ids_ref[...], (8, count)))[:, 0:1] - step * tile
    hot = (lax.broadcasted_iota(jnp.int32, (count, tile), 1) == ids).astype(F32).astype(BF16)
    found = dot(hot, table_ref[...])

    @pl.when(step == 0)
    def _():
        total[...] = found

    @pl.when(step > 0)
    def _():
        total[...] += found

    @pl.when(step == pl.num_programs(0) - 1)
    def _():
        rows = outs[0].shape[0]
        for n, out in enumerate(outs):
            out[...] = total[n * rows : (n + 1) * rows].astype(BF16)


TABLE_STEPS = 5


def lookup(ids, table, pieces, lots=()):
    count = ids.shape[0]
    rows, width = table.shape
    tile = rows // TABLE_STEPS
    return pl.pallas_call(
        functools.partial(lookup_kernel, lots),
        grid=(TABLE_STEPS,),
        in_specs=[
            pl.BlockSpec((1, count), lambda i: (0, 0)),
            pl.BlockSpec((tile, width), lambda i: (i, 0)),
        ],
        out_specs=[pl.BlockSpec((count // pieces, width), lambda i: (0, 0))] * pieces
        + [
            pl.BlockSpec((stop - start, width), lambda i: (0, 0), pipeline_mode=pl.Buffered(1))
            for start, stop in lots
        ],
        out_shape=[jax.ShapeDtypeStruct((count // pieces, width), BF16)] * pieces
        + [jax.ShapeDtypeStruct((stop - start, width), BF16) for start, stop in lots],
        scratch_shapes=[pltpu.VMEM((count, width), F32)],
        compiler_params=params(),
        cost_estimate=cost(8 * count / 512),
        name="lookup",
    )(ids.reshape(1, count), table)


def gathered_sum(refs, sizes):
    rows, at = [], 0
    for size in sizes:
        total = refs[at][...].astype(F32)
        for ref in refs[at + 1 : at + size]:
            total = total + ref[...].astype(F32)
        rows.append(total)
        at += size
    return rows[0] if len(rows) == 1 else jnp.concatenate(rows, axis=0)


def collect_kernel(sizes, *refs):
    ins, outs = refs[: sum(sizes)], refs[sum(sizes) :]
    rows = outs[0].shape[0]
    total = gathered_sum(ins, sizes)
    for n, out in enumerate(outs):
        out[...] = total[n * rows : (n + 1) * rows].astype(BF16)


def collect(terms, pieces):
    sizes = [len(part) for part in terms]
    parts = [term for part in terms for term in part]
    rows, width = sum(part[0].shape[0] for part in terms), parts[0].shape[1]
    return pl.pallas_call(
        functools.partial(collect_kernel, sizes),
        in_specs=[whole()] * len(parts),
        out_specs=[whole()] * pieces,
        out_shape=[jax.ShapeDtypeStruct((rows // pieces, width), BF16)] * pieces,
        compiler_params=params(),
        cost_estimate=cost(2),
        name="collect",
    )(*parts)


def begin_kernel(pieces, order_ref, gain_ref, *refs):
    ins, outs, held = refs[:pieces], refs[pieces:-1], refs[-1]
    for n in range(pieces):
        held[order_ref[n]] = ins[n][...]
    values = jnp.concatenate([held[n] for n in range(pieces)], axis=1)
    units = rms(values.astype(F32), gain_ref[...])
    half = outs[0].shape[0]
    for n in range(2):
        outs[n][...] = values[n * half : (n + 1) * half]
        outs[2 + n][...] = units[n * half : (n + 1) * half]


def begin(order, gain, pieces):
    rows, width = pieces[0].shape
    half = jax.ShapeDtypeStruct((rows // 2, width * len(pieces)), BF16)
    return pl.pallas_call(
        functools.partial(begin_kernel, len(pieces)),
        in_specs=[smem()] + [whole()] * (1 + len(pieces)),
        out_specs=[whole()] * 4,
        out_shape=[half] * 4,
        scratch_shapes=[pltpu.VMEM((len(pieces), rows, width), BF16)],
        compiler_params=params(),
        cost_estimate=cost(2),
        name="begin",
    )(order, gain.reshape(1, -1), *pieces)


def finish_kernel(parts, last, residual_ref, gain_ref, *refs):
    total = gathered_sum(refs[:parts], [parts]) + residual_ref[...].astype(F32)
    if not last:
        total = total.astype(BF16)
        refs[parts + 1][...] = total
    refs[parts][...] = rms(total.astype(F32), gain_ref[...])


def finish(residual, gain, terms, last):
    full = jax.ShapeDtypeStruct(residual.shape, BF16)
    return pl.pallas_call(
        functools.partial(finish_kernel, len(terms), last),
        in_specs=[whole()] * (2 + len(terms)),
        out_specs=[whole()] * (1 if last else 2),
        out_shape=[full] * (1 if last else 2),
        compiler_params=params(),
        cost_estimate=cost(2),
        name="finish",
    )(residual, gain, *terms)


def selectors():
    pairs = [(r, s) for r in range(FEAT) for s in range(r, FEAT)]
    picks = np.zeros((2, 2, LANES, WIDE), np.float32)
    extra = np.zeros((3, WIDE), np.float32)
    extra[0:2, 0] = 1.0
    extra[1, 1 : 1 + FEAT] = 1.0
    extra[2] = 1.0
    for kind in range(2):
        first = kind * FEAT
        for r in range(FEAT):
            picks[kind, 0, first + r, 1 + r] = FEAT ** (-0.25)
        for n, (r, s) in enumerate(pairs):
            picks[kind, 0, first + r, 1 + FEAT + n] = FEAT ** (-0.25)
            picks[kind, 1, first + s, 1 + FEAT + n] = FEAT ** (-0.25)
    for n, (r, s) in enumerate(pairs):
        extra[2, 1 + FEAT + n] = 0.5**0.5 if r == s else 1.0
    return jnp.asarray(np.concatenate([picks, picks], axis=2), BF16), jnp.asarray(extra)


def place_column(places_ref, slots, rows):
    inner = lax.broadcasted_iota(jnp.int32, (rows, 1), 0)
    return jnp.concatenate([inner + places_ref[slot] for slot in slots], axis=0)


def place_row(places_ref, slots, rows):
    inner = lax.broadcasted_iota(jnp.int32, (1, rows), 1)
    return jnp.concatenate([inner + places_ref[slot] for slot in slots], axis=1)


def project_kernel(heads, slots, chunk, count, pieces, more, last, bound_ref, places_ref, *refs):
    units = jnp.concatenate([ref[...] for ref in refs[:pieces]], axis=0)
    weight_ref, pick_ref, extra_ref = refs[pieces : pieces + 3]
    fq_ref, fk_ref, v_ref, state_ref = refs[-4:]
    projected = dot(units, weight_ref[...])
    rows, width = projected.shape
    needed = (heads - 1) * LANES + WIDE
    if needed > width:
        projected = jnp.pad(projected, ((0, 0), (0, needed - width)))
    bound = bound_ref[0]
    place = place_column(places_ref, slots, chunk)
    kept = ((place >= bound) | (bound == count)).astype(F32)
    ones = jnp.ones((8, rows), BF16)
    shift = 2 * FEAT
    for head in range(heads):
        part = projected[:, head * LANES : head * LANES + WIDE]
        narrow = part if head == 0 else pltpu.roll(part, WIDE - shift * head, 1)
        narrow = narrow[:, :LANES]
        values = pltpu.roll(part, WIDE - shift * (head + 1), 1)[:, :HEAD_DIM].astype(BF16)
        v_ref[:, head * HEAD_DIM : (head + 1) * HEAD_DIM] = values
        upper = narrow.astype(BF16)
        lower = (narrow - upper.astype(F32)).astype(BF16)
        both = jnp.concatenate([upper, lower], axis=1)
        feats = []
        for kind in range(2):
            one = dot(both, pick_ref[kind, 0]) + extra_ref[0:1]
            two = dot(both, pick_ref[kind, 1]) + extra_ref[1:2]
            feats.append((one * two * extra_ref[2:3]).astype(BF16))
        fq_ref[head] = feats[0]
        fk_ref[head] = feats[1]
        keys = (feats[1].astype(F32) * kept).astype(BF16)
        state = dot(keys, values, ((0,), (0,)))
        total = dot(ones, keys)
        tail = jnp.concatenate([total[0:1, :LANES], total[0:1, LANES:], jnp.zeros((14, LANES), F32)], axis=0)
        state = jnp.concatenate([state[0:STATE_ROWS], tail], axis=0)
        if more:
            state = state + refs[pieces + 3][head]
        state_ref[head] = state.astype(BF16) if last else state


def project(bound, places, slots, chunk, count, pieces, weight, constants, earlier, last, heads):
    rows = sum(piece.shape[0] for piece in pieces)
    extra = [] if earlier is None else [earlier]
    return pl.pallas_call(
        functools.partial(project_kernel, heads, slots, chunk, count, len(pieces), bool(extra), last),
        in_specs=[smem(), smem()] + [whole()] * (len(pieces) + 3 + len(extra)),
        out_specs=[whole()] * 4,
        out_shape=[
            jax.ShapeDtypeStruct((heads, rows, WIDE), BF16),
            jax.ShapeDtypeStruct((heads, rows, WIDE), BF16),
            jax.ShapeDtypeStruct((rows, heads * HEAD_DIM), BF16),
            jax.ShapeDtypeStruct((heads, BUFFER_ROWS, HEAD_DIM), BF16 if last else F32),
        ],
        compiler_params=params(),
        cost_estimate=cost(5),
        name="project",
    )(bound, places, *pieces, weight, *constants, *extra)


def within_kernel(heads, slots, chunk, sets, bound_ref, places_ref, *refs):
    fqs, fks, vs = refs[:sets], refs[sets : 2 * sets], refs[2 * sets : 3 * sets]
    num_ref, den_ref = refs[3 * sets :]
    bound = bound_ref[0]
    row = place_column(places_ref, slots, chunk)
    col = place_row(places_ref, slots, chunk)
    allowed = (row >= col) & ((row >= bound) == (col >= bound))
    for head in range(heads):
        query = jnp.concatenate([ref[head] for ref in fqs], axis=0)
        keys = jnp.concatenate([ref[head] for ref in fks], axis=0)
        values = jnp.concatenate(
            [ref[:, head * HEAD_DIM : (head + 1) * HEAD_DIM] for ref in vs], axis=0
        )
        weights = dot(query, keys, ((1,), (1,)))
        weights = jnp.where(allowed, weights, 0.0)
        den_ref[head] = jnp.broadcast_to(
            jnp.sum(weights, axis=-1, keepdims=True), (row.shape[0], 8)
        )
        num_ref[head] = dot(weights.astype(BF16), values)


def within(bound, places, slots, chunk, fqs, fks, vs, heads):
    count = len(slots) * chunk
    return pl.pallas_call(
        functools.partial(within_kernel, heads, slots, chunk, len(fqs)),
        in_specs=[smem(), smem()] + [whole()] * (3 * len(fqs)),
        out_specs=[whole()] * 2,
        out_shape=[
            jax.ShapeDtypeStruct((heads, count, HEAD_DIM), F32),
            jax.ShapeDtypeStruct((heads, count, 8), F32),
        ],
        compiler_params=params(),
        cost_estimate=cost(4.5),
        name="within",
    )(bound, places, *fqs, *fks, *vs)


def split_store(total, refs):
    rows = refs[0].shape[0]
    for n, ref in enumerate(refs):
        ref[...] = total[n * rows : (n + 1) * rows].astype(BF16)


def across_kernel(heads, slots, chunk, sets, earlier, near, bound_ref, places_ref, share_ref, *refs):
    fqs, refs = refs[:sets], refs[sets:]
    num_ref, den_ref, gain_ref, weight_ref = refs[:4]
    states, refs = refs[4 : 4 + earlier], refs[4 + earlier :]
    mixed_ref, fars = refs[0], refs[1:]
    bound = bound_ref[0]
    before = (place_column(places_ref, slots, chunk) < bound).astype(F32)
    for head in range(heads):
        carried = jnp.zeros((BUFFER_ROWS, HEAD_DIM), F32)
        for n in range(earlier):
            carried = carried + jnp.where(share_ref[n] > 0, states[n][head].astype(F32), 0.0)
        state = jnp.concatenate(
            [carried[0:STATE_ROWS], jnp.zeros((WIDE - STATE_ROWS, HEAD_DIM), F32)], axis=0
        ).astype(BF16)
        total = jnp.concatenate(
            [carried[STATE_ROWS : STATE_ROWS + 1], carried[STATE_ROWS + 1 : STATE_ROWS + 2]], axis=1
        )
        query = jnp.concatenate([ref[head] for ref in fqs], axis=0)
        numerator = num_ref[head] + before * dot(query, state)
        more = jnp.sum(query.astype(F32) * total, axis=-1, keepdims=True)
        denominator = den_ref[head][:, 0:1] + before * more
        lanes = slice(head * HEAD_DIM, (head + 1) * HEAD_DIM)
        mixed_ref[:, lanes] = (numerator / denominator * gain_ref[:, lanes].astype(F32)).astype(BF16)
    split_store(dot(mixed_ref[near * chunk :], weight_ref[...]), fars)


def across(bound, places, share, slots, chunk, near, far, fqs, num, den, gain, weight, states, heads):
    count = len(slots) * chunk
    rows = (count - near * chunk) // far
    return pl.pallas_call(
        functools.partial(across_kernel, heads, slots, chunk, len(fqs), len(states), near),
        in_specs=[smem()] * 3 + [whole()] * (len(fqs) + 4 + len(states)),
        out_specs=[whole()] * (1 + far),
        out_shape=[jax.ShapeDtypeStruct((count, heads * HEAD_DIM), BF16)]
        + [jax.ShapeDtypeStruct((rows, weight.shape[1]), BF16)] * far,
        compiler_params=params(),
        cost_estimate=cost(4.5),
        name="across",
    )(bound, places, share, *fqs, num, den, gain, weight, *states)


def near_kernel(rows, mixed_ref, weight_ref, *outs):
    split_store(dot(mixed_ref[0:rows], weight_ref[...]), outs)


def near_chunks(mixed, weight, near, chunk):
    pieces = 2 * near if near > 1 else 1
    rows = near * chunk
    return pl.pallas_call(
        functools.partial(near_kernel, rows),
        in_specs=[whole()] * 2,
        out_specs=[whole()] * pieces,
        out_shape=[jax.ShapeDtypeStruct((rows // pieces, weight.shape[1]), BF16)] * pieces,
        compiler_params=params(),
        cost_estimate=cost(4),
        name="near",
    )(mixed, weight)


def matmul_kernel(*refs):
    a = jnp.concatenate([ref[...] for ref in refs[:-2]], axis=0)
    refs[-1][...] = dot(a, refs[-2][...]).astype(BF16)


def matmul(pieces, b, tile):
    rows = sum(piece.shape[0] for piece in pieces)
    inner = b.shape[0]
    return pl.pallas_call(
        matmul_kernel,
        grid=(b.shape[1] // tile,),
        in_specs=[
            pl.BlockSpec(piece.shape, lambda n: (0, 0), pipeline_mode=pl.Buffered(1)) for piece in pieces
        ]
        + [pl.BlockSpec((inner, tile), lambda n: (0, n))],
        out_specs=pl.BlockSpec((rows, tile), lambda n: (0, n)),
        out_shape=jax.ShapeDtypeStruct((rows, b.shape[1]), BF16),
        compiler_params=params(),
        cost_estimate=cost(5),
        name="matmul",
    )(*pieces, b)


def attend(queries, keys, values, allowed):
    rows = queries[0].shape[0]
    scores = jnp.concatenate(
        [dot(q, k, ((1,), (1,))) for q, k in zip(queries, keys)], axis=0
    ) * HEAD_DIM ** (-0.5)
    allowed = jnp.concatenate([allowed.astype(F32)] * len(queries), axis=0) > 0
    scores = jnp.where(allowed, scores, NEGATIVE)
    peak = jnp.max(scores, axis=-1, keepdims=True)
    weights = jnp.where(allowed, jnp.exp(scores - peak), 0.0)
    probabilities = (weights * (1.0 / jnp.sum(weights, axis=-1, keepdims=True))).astype(BF16)
    return jnp.concatenate(
        [
            dot(probabilities[n * rows : (n + 1) * rows], value).astype(BF16)
            for n, value in enumerate(values)
        ],
        axis=1,
    )


def local_kernel(heads, slots, spots, chunk, sets, bound_ref, places_ref, *refs):
    qkvs, (result_ref, first_ref) = refs[:sets], refs[sets:]
    size = len(slots)
    reach = chunk + WINDOW
    bound = bound_ref[0]
    row = lax.broadcasted_iota(jnp.int32, (chunk, reach), 0)
    col = lax.broadcasted_iota(jnp.int32, (chunk, reach), 1)
    band = (col > row) & (col <= row + WINDOW)
    for slot in range(size):
        k = slots[slot]
        mine, at = spots[k]
        theirs, there = spots[(k - 1) % size]
        base = places_ref[slot]
        query_place = row + base
        key_place = col + (base - WINDOW)
        allowed = band & (key_place >= 0) & ((query_place >= bound) == (key_place >= bound))
        rows = slice(at, at + chunk)
        tail = slice(there + chunk - WINDOW, there + chunk)

        @pl.when(base == 0)
        def _():
            first_ref[...] = qkvs[mine][at : at + WINDOW]

        queries, keys, values = [], [], []
        for head in range(heads):
            lane = head * 3 * HEAD_DIM
            queries.append(qkvs[mine][rows, lane : lane + HEAD_DIM])
            for n, held in ((1, keys), (2, values)):
                lanes = slice(lane + n * HEAD_DIM, lane + (n + 1) * HEAD_DIM)
                held.append(jnp.concatenate([qkvs[theirs][tail, lanes], qkvs[mine][rows, lanes]], axis=0))
        result_ref[slot * chunk : (slot + 1) * chunk] = attend(queries, keys, values, allowed)


def local_window(bound, places, slots, spots, chunk, qkvs, heads):
    return pl.pallas_call(
        functools.partial(local_kernel, heads, slots, spots, chunk, len(qkvs)),
        in_specs=[smem(), smem()] + [whole()] * len(qkvs),
        out_specs=[whole()] * 2,
        out_shape=[
            jax.ShapeDtypeStruct((len(slots) * chunk, heads * HEAD_DIM), BF16),
            jax.ShapeDtypeStruct((WINDOW, qkvs[0].shape[1]), BF16),
        ],
        compiler_params=params(),
        cost_estimate=cost(8),
        name="local_window",
    )(bound, places, *qkvs)


def halo_kernel(heads, count, start, info_ref, local_ref, first_ref, halo_ref, weight_ref, result_ref, *fars):
    result_ref[...] = local_ref[...]
    bound, valid_from, spot = info_ref[0], info_ref[1], info_ref[2]
    row = lax.broadcasted_iota(jnp.int32, (WINDOW, 2 * WINDOW), 0)
    col = lax.broadcasted_iota(jnp.int32, (WINDOW, 2 * WINDOW), 1)
    key_place = col - WINDOW
    allowed = (col > row) & (col <= row + WINDOW) & ((row >= bound) == (key_place >= bound))
    allowed = allowed & ((key_place >= 0) | (key_place + count >= valid_from))
    spot = pl.multiple_of(spot, WINDOW)
    queries, keys, values = [], [], []
    for head in range(heads):
        lane = head * 3 * HEAD_DIM
        queries.append(first_ref[:, lane : lane + HEAD_DIM])
        for n, held in ((1, keys), (2, values)):
            lanes = slice(lane + n * HEAD_DIM, lane + (n + 1) * HEAD_DIM)
            held.append(jnp.concatenate([halo_ref[:, lanes], first_ref[:, lanes]], axis=0))
    result_ref[pl.ds(spot, WINDOW), :] = attend(queries, keys, values, allowed)
    split_store(dot(result_ref[start:], weight_ref[...]), fars)


def halo_window(info, near, chunk, far, local, first, halo, weight, heads):
    count = local.shape[0]
    rows = (count - near * chunk) // far
    return pl.pallas_call(
        functools.partial(halo_kernel, heads, count, near * chunk),
        in_specs=[smem()] + [whole()] * 4,
        out_specs=[whole()] * (1 + far),
        out_shape=[jax.ShapeDtypeStruct(local.shape, BF16)]
        + [jax.ShapeDtypeStruct((rows, weight.shape[1]), BF16)] * far,
        compiler_params=params(),
        cost_estimate=cost(4.5),
        name="halo_window",
    )(info, local, first, halo, weight)


def turn_kernel(*refs):
    refs[-1][...] = jnp.transpose(jnp.concatenate([ref[...] for ref in refs[:-1]], axis=0))


def turn(pieces):
    rows, width = sum(piece.shape[0] for piece in pieces), pieces[0].shape[1]
    return pl.pallas_call(
        turn_kernel,
        in_specs=[whole()] * len(pieces),
        out_specs=whole(),
        out_shape=jax.ShapeDtypeStruct((width, rows), BF16),
        compiler_params=params(),
        cost_estimate=cost(3),
        name="turn",
    )(*pieces)


def score_kernel(ready, rest, common, pieces, lots, tile, order_ref, *refs):
    early, refs = refs[:ready], refs[ready:]
    units, refs = refs[:rest], refs[rest:]
    shared, refs = refs[:common], refs[common:]
    tables, (goal_ref, out_ref, turned_ref, held) = refs[: len(lots) * pieces], refs[len(lots) * pieces :]
    step = pl.program_id(0)
    width = (shared or tables)[0].shape[1]
    count = goal_ref.shape[1]
    part = 128

    @pl.when(step == 0)
    def _():
        at = 0
        for ref in early:
            at = ref.shape[1]
            turned_ref[:, 0:at] = ref[...]
        turned_ref[:, at:] = jnp.transpose(jnp.concatenate([ref[...] for ref in units], axis=0))
        held[0] = jnp.full((8, count), NEGATIVE, F32)
        held[1] = jnp.zeros((8, count), F32)
        held[2] = jnp.zeros((8, count), F32)

    def run(mine):
        inner = lax.broadcasted_iota(jnp.int32, (part // 8, 8, count), 0) * 8
        inner = inner + lax.broadcasted_iota(jnp.int32, (part // 8, 8, count), 1)
        peak, total, picked = held[0], held[1], held[2]
        sides = [
            turned_ref[pl.ds(pl.multiple_of(order_ref[n] * width, width), width), :] for n in range(len(mine))
        ]
        for at in range(0, tile, part):
            logits = None
            for table, side in zip(mine, sides):
                more = dot(table[at : at + part], side)
                logits = more if logits is None else logits + more
            logits = logits.reshape(part // 8, 8, count)
            goal = (goal_ref[...] - (step * tile + at)).reshape(1, 1, count)
            old = peak
            peak = jnp.maximum(old, jnp.max(logits, axis=0))
            total = total * jnp.exp(old - peak) + jnp.sum(jnp.exp(logits - peak[None]), axis=0)
            picked = picked + jnp.sum(jnp.where(inner == goal, logits, 0.0), axis=0)
        held[0], held[1], held[2] = peak, total, picked

    for lot, (start, stop) in enumerate(lots):
        pl.when((step >= start) & (step < stop))(
            lambda lot=lot: run(list(shared) + list(tables[lot * pieces : (lot + 1) * pieces]))
        )

    @pl.when(step == pl.num_programs(0) - 1)
    def _():
        peak = jnp.max(held[0], axis=0, keepdims=True)
        total = jnp.sum(held[1] * jnp.exp(held[0] - peak), axis=0, keepdims=True)
        picked = jnp.sum(held[2], axis=0, keepdims=True)
        out_ref[...] = jnp.concatenate([peak, total, picked, jnp.zeros((5, count), F32)], axis=0)


def scores(order, early, units, shared, lots, goal):
    count = goal.shape[1]
    rows = lots[-1][1]
    tile = 640
    specs = [pl.BlockSpec((tile, table.shape[1]), lambda i: (i, 0)) for table in shared]
    steps = []
    for first, last, tables in lots:
        start, stop = first // tile, last // tile
        steps.append((start, stop))
        for table in tables:
            specs.append(
                pl.BlockSpec(
                    (tile, table.shape[1]),
                    lambda i, start=start, stop=stop: (jnp.clip(i, start, stop - 1) - start, 0),
                )
            )
    still = [
        pl.BlockSpec(piece.shape, lambda i: (0, 0), pipeline_mode=pl.Buffered(1)) for piece in early + units
    ]
    return pl.pallas_call(
        functools.partial(
            score_kernel, len(early), len(units), len(shared), len(lots[0][2]), steps, tile
        ),
        in_specs=[smem()] + still + specs + [pl.BlockSpec((1, count), lambda i: (0, 0))],
        out_specs=pl.BlockSpec((8, count), lambda i: (0, 0)),
        grid=(rows // tile,),
        out_shape=jax.ShapeDtypeStruct((8, count), F32),
        scratch_shapes=[pltpu.VMEM((units[0].shape[1], count), BF16), pltpu.VMEM((3, 8, count), F32)],
        compiler_params=params(),
        cost_estimate=cost(20),
        name="scores",
    )(order, *early, *units, *shared, *[table for lot in lots for table in lot[2]], goal)


def shards(
    token_ids,
    target_ids,
    doc_start,
    vocab_table,
    norm_gain_one,
    lin_qkv,
    lin_head_gain,
    lin_out,
    norm_gain_two,
    win_qkv,
    win_out,
    final_gain,
):
    head_count = lax.axis_size("head")
    seq_count = lax.axis_size("seq")
    head_index = lax.axis_index("head")
    seq_index = lax.axis_index("seq")
    tok_count = token_ids.shape[0]
    chunk = tok_count // head_count
    vocab_rows = vocab_table.shape[0]
    heads = lin_qkv.shape[1] // (2 * FEAT + HEAD_DIM)
    vocab_first = head_index * vocab_rows
    calls = chunk_order(head_count)
    slots = [k for call in calls for k in call]
    near = 3 if head_count == 4 else 1
    far = 2 if head_count == 4 else head_count - 1
    spots = {}
    for n, call in enumerate(calls):
        for at, k in enumerate(call):
            spots[k] = (n, at * chunk)
    held_at = (head_index + jnp.asarray(slots, jnp.int32)) % head_count
    places = held_at * chunk

    marks = jnp.concatenate([token_ids, jnp.broadcast_to(doc_start, (LANES,))])
    marks = jnp.stack(
        [marks] + [lax.ppermute(marks, "seq", xor_pairs(seq_count, k)) for k in range(1, seq_count)]
    )
    block = jnp.arange(seq_count, dtype=jnp.int32)
    order = seq_index ^ block
    starts = marks[:, tok_count]
    starts = jnp.sum(jnp.where(order[None, :] == block[:, None], starts[None, :], 0), axis=1)
    bound = doc_start.astype(jnp.int32)

    marks_at = [part * (vocab_rows // 10) for part in (0, 3, 8, 10)]
    bounds = list(zip(marks_at[:-1], marks_at[1:])) if seq_count == 4 else []
    lots = []

    ids = (marks[:, :tok_count] - vocab_first).reshape(seq_count, head_count, chunk)

    def ids_of(k):
        return lax.dynamic_index_in_dim(ids, (head_index + k) % head_count, 1, False).reshape(-1)

    if head_count == 4:
        outer = lookup(ids_of(2), vocab_table, 2)

        def inner():
            after, before, _ = lax.optimization_barrier((ids_of(1), ids_of(3), outer))
            half = after.shape[0] // 2
            next_lower, prev_upper = lookup(jnp.concatenate([after[half:], before[:half]]), vocab_table, 2)
            next_upper, prev_lower = lookup(jnp.concatenate([after[:half], before[half:]]), vocab_table, 2)
            own = lookup(ids_of(0), vocab_table, 2, bounds)
            lots.extend(own[2:])
            return [own[0], own[1], next_upper, next_lower, prev_upper, prev_lower]

    else:
        outer = [lookup(ids_of(k), vocab_table, 1)[0] for k in range(1, head_count)]

        def inner():
            own = lookup(ids_of(0), vocab_table, 1, bounds)
            lots.extend(own[1:])
            return own[:1]

    found = collect(scatter_rows(outer, inner), seq_count)
    gathered = [found[0]] + [
        lax.ppermute(found[k], "seq", xor_pairs(seq_count, k)) for k in range(1, seq_count)
    ]
    if lots:
        lots[0], gathered = lax.optimization_barrier((lots[0], gathered))
    *embedded, upper, lower = begin(order, norm_gain_one, gathered)
    across_x, corners = [None] * 3, [None] * 3

    constants = selectors()
    sets, state = [], None

    def project_call(n, pieces, state):
        first = sum(len(c) for c in calls[:n])
        return project(
            bound,
            places[first : first + len(calls[n])],
            list(range(len(calls[n]))),
            chunk,
            tok_count,
            pieces,
            lin_qkv,
            constants,
            state,
            n == len(calls) - 1,
            heads,
        )

    chunks = gather_rows(upper, lower)

    shares = []
    for back in range(1, seq_count):
        between = (block > seq_index - back) & (block < seq_index)
        broken = jnp.sum(jnp.where(between & (starts != tok_count), 1, 0))
        shares.append(((broken == 0) & (seq_index >= back)).astype(jnp.int32))
    shares = jnp.stack(shares)
    previous = jnp.sum(jnp.where(block == seq_index - 1, starts, 0))
    valid_from = jnp.where(
        seq_index == 0, tok_count, jnp.where(previous == tok_count, 0, previous)
    ).astype(jnp.int32)
    first_spot = jnp.sum(jnp.where(held_at == 0, jnp.arange(head_count) * chunk, 0)).astype(jnp.int32)
    info = jnp.stack([bound[0], valid_from, first_spot])
    goals = (target_ids - vocab_first).reshape(head_count, chunk)
    goal = jnp.concatenate(
        [lax.dynamic_index_in_dim(goals, (head_index + k) % head_count, 0, False) for k in slots]
    ).reshape(1, -1)
    gain_two, gain_three = norm_gain_two.reshape(1, -1), final_gain.reshape(1, -1)
    head_gain = lin_head_gain.reshape(1, -1)
    chunks[slots[-1]], shares, info, goal, gain_two, gain_three, head_gain = lax.optimization_barrier(
        (chunks[slots[-1]], shares, info, goal, gain_two, gain_three, head_gain)
    )
    if seq_count == 4:
        across_x[0] = lax.ppermute(lots[0], "seq", xor_pairs(seq_count, 2))
        corners[0] = lax.ppermute(across_x[0], "seq", xor_pairs(seq_count, 1))
    for n, call in enumerate(calls):
        made = project_call(n, [piece for k in call for piece in chunks[k]], state)
        sets.append(made[:3])
        state = made[3]
    fqs, fks, vs = zip(*sets)
    if seq_count == 4:
        state, across_x[0] = lax.optimization_barrier((state, across_x[0]))
    states = [
        lax.ppermute(state, "seq", [(i, i + back) for i in range(seq_count - back)])
        for back in range(1, seq_count)
    ]
    position = list(range(head_count))
    num, den = within(bound, places, position, chunk, fqs, fks, vs, heads)
    mixed, *outer = across(
        bound,
        places,
        shares,
        position,
        chunk,
        near,
        far,
        fqs,
        num,
        den,
        head_gain,
        lin_out,
        states,
        heads,
    )
    far_rows = outer
    parts = scatter_rows(outer, lambda: near_chunks(mixed, lin_out, near, chunk))
    parts = in_halves(parts)
    upper, residual_upper = finish(embedded[0], gain_two, parts[0], False)
    lower, residual_lower = finish(embedded[1], gain_two, parts[1], False)

    if seq_count == 4:
        lots[1], _ = lax.optimization_barrier((lots[1], (states, far_rows)))
        across_x[1] = lax.ppermute(lots[1], "seq", xor_pairs(seq_count, 2))
        beside = lax.ppermute(vocab_table, "seq", xor_pairs(seq_count, 1))

    chunks = gather_rows(upper, lower)
    qkvs = []
    for call in calls:
        qkvs.append(matmul([piece for k in call for piece in chunks[k]], win_qkv, 3 * HEAD_DIM))
    tail = jnp.zeros((WINDOW, win_qkv.shape[1]), BF16)
    for slot, k in enumerate(slots):
        n, at = spots[k]
        tail = jnp.where(
            held_at[slot] == head_count - 1, qkvs[n][at + chunk - WINDOW : at + chunk], tail
        )
    if seq_count == 4:
        tail, across_x[1], corners[0], beside = lax.optimization_barrier(
            (tail, across_x[1], corners[0], beside)
        )
    halo = lax.ppermute(tail, "seq", [(i, i + 1) for i in range(seq_count - 1)])
    local, first = local_window(bound, places, slots, spots, chunk, qkvs, heads)
    if lots:
        lots[2], local, halo, across_x[1] = lax.optimization_barrier((lots[2], local, halo, across_x[1]))
        corners[1] = lax.ppermute(across_x[1], "seq", xor_pairs(seq_count, 1))
    mixed, *outer = halo_window(info, near, chunk, far, local, first, halo, win_out, heads)
    if seq_count == 4:
        mixed, corners[1] = lax.optimization_barrier((mixed, corners[1]))
    parts = scatter_rows(outer, lambda: near_chunks(mixed, win_out, near, chunk))
    parts = in_halves(parts)
    upper = finish(residual_upper, gain_three, parts[0], True)[0]
    lower = finish(residual_lower, gain_three, parts[1], True)[0]

    chunks = gather_rows(upper, lower)
    if seq_count == 4:
        across_x[2] = lax.ppermute(lots[2], "seq", xor_pairs(seq_count, 2))
        corners[2] = lax.ppermute(lots[2], "seq", xor_pairs(seq_count, 3))
        shared = [vocab_table, beside]
        lots = [(marks_at[n], marks_at[n + 1], [across_x[n], corners[n]]) for n in range(3)]
    else:
        shared = [lax.all_gather(vocab_table, "seq", axis=1, tiled=True)]
        lots = [(0, vocab_rows, [])]
        order = jnp.zeros((1,), jnp.int32)
    first = slots[:-1] if chunk % LANES == 0 else []
    rest = [piece for k in slots[len(first) :] for piece in chunks[k]]
    first = [turn([piece for k in first for piece in chunks[k]])] if first else []
    triple = scores(order, first, rest, shared, lots, goal)
    found = {k: triple[:3, at * chunk : (at + 1) * chunk] for at, k in enumerate(slots)}

    shares = jnp.stack([found[0]] + [turned(found[k], k) for k in range(1, head_count)])
    peak = jnp.max(shares[:, 0], axis=0)
    total = jnp.sum(shares[:, 1] * jnp.exp(shares[:, 0] - peak), axis=0)
    return jnp.sum(shares[:, 2], axis=0) - (peak + jnp.log(total))


def solution(mesh):
    return jax.shard_map(
        shards,
        mesh=mesh,
        in_specs=(
            P(("shadow", "seq")),
            P(("shadow", "seq")),
            P(("shadow", "seq")),
            P(("shadow", "head"), "seq"),
            P("shadow"),
            P("shadow", "head"),
            P(("shadow", "head")),
            P(("shadow", "head"), None),
            P("shadow"),
            P("shadow", "head"),
            P(("shadow", "head"), None),
            P("shadow"),
        ),
        out_specs=P(("shadow", "seq", "head")),
        check_vma=False,
    )
```

```python
import functools

import jax
import jax.numpy as jnp
import numpy as np
from jax import lax
from jax.experimental import pallas as pl
from jax.experimental.pallas import tpu as pltpu
from jax.sharding import PartitionSpec as P

FEAT = 16
WINDOW = 64
HEAD_DIM = 128
EPSILON = 1e-05
NEGATIVE = -1e30
LANES = 128
WIDE = 256
STATE_ROWS = 160
BUFFER_ROWS = 176
F32 = jnp.float32
BF16 = jnp.bfloat16
VMEM_BYTES = 56 * 1024 * 1024


def params(**kw):
    return pltpu.CompilerParams(vmem_limit_bytes=VMEM_BYTES, **kw)


def cost(us):
    return pl.CostEstimate(flops=int(us * 6e8), transcendentals=0, bytes_accessed=int(us * 3e6))


def whole():
    return pl.BlockSpec(memory_space=pltpu.VMEM)


def smem():
    return pl.BlockSpec(memory_space=pltpu.SMEM)


def dot(a, b, dims=((1,), (0,))):
    return lax.dot_general(a, b, (dims, ((), ())), preferred_element_type=F32)


def xor_pairs(size, k):
    return [(i, i ^ k) for i in range(size)]


def rms(values, gain):
    factor = lax.rsqrt(jnp.mean(values * values, axis=-1, keepdims=True) + EPSILON)
    return (values * factor * gain.astype(F32)).astype(BF16)


def turned(value, step):
    size = lax.axis_size("head")
    return lax.ppermute(value, "head", [(i, (i + step) % size) for i in range(size)])


def gather_rows(upper, lower):
    size = lax.axis_size("head")
    if size != 4:
        full = lax.all_gather(jnp.concatenate([upper, lower]), "head")
        here = lax.axis_index("head")
        return [[upper, lower]] + [
            [lax.dynamic_index_in_dim(full, (here + k) % size, 0, False)] for k in range(1, size)
        ]
    before_upper, after_upper = turned(upper, 1), turned(upper, -1)
    after_lower, before_lower = turned(lower, -1), turned(lower, 1)
    far = [turned(before_upper, 1), turned(after_lower, -1)]
    return [[upper, lower], [after_upper, after_lower], far, [before_upper, before_lower]]


def in_halves(terms):
    if len(terms) == 2:
        return terms
    half = terms[0][0].shape[0] // 2
    return [[term[:half] for term in terms[0]], [term[half:] for term in terms[0]]]


def scatter_rows(far, near):
    size = lax.axis_size("head")
    if size != 4:
        here = lax.axis_index("head")
        full = jnp.stack([near()[0]] + list(far))
        full = jnp.stack(
            [lax.dynamic_index_in_dim(full, (d - here) % size, 0, False) for d in range(size)]
        )
        return [[lax.psum_scatter(full, "head", scatter_dimension=0, tiled=True)[0]]]
    from_before, from_after = turned(far[0], 1), turned(far[1], -1)
    own_upper, own_lower, next_upper, next_lower, prev_upper, prev_lower = near()
    lower_right, upper_left = turned(next_lower, 1), turned(prev_upper, -1)
    upper_right, lower_left = pass_on(next_upper, from_before, prev_lower, from_after)
    upper_right, lower_left = turned(upper_right, 1), turned(lower_left, -1)
    return [[own_upper, upper_right, upper_left], [own_lower, lower_right, lower_left]]


def pass_on_kernel(next_ref, before_ref, prev_ref, after_ref, right_ref, left_ref):
    right_ref[...] = (next_ref[...].astype(F32) + before_ref[...].astype(F32)).astype(BF16)
    left_ref[...] = (prev_ref[...].astype(F32) + after_ref[...].astype(F32)).astype(BF16)


def pass_on(next_upper, from_before, prev_lower, from_after):
    return pl.pallas_call(
        pass_on_kernel,
        in_specs=[whole()] * 4,
        out_specs=[whole()] * 2,
        out_shape=[jax.ShapeDtypeStruct(next_upper.shape, BF16)] * 2,
        compiler_params=params(),
        cost_estimate=cost(1.5),
        name="pass_on",
    )(next_upper, from_before, prev_lower, from_after)


def chunk_order(size):
    if size == 4:
        return [[0, 1, 3], [2]]
    return [[k] for k in range(size)]


def lookup_kernel(lots, ids_ref, table_ref, *refs):
    outs, copies, total = refs[: -1 - len(lots)], refs[-1 - len(lots) : -1], refs[-1]
    step = pl.program_id(0)
    tile = table_ref.shape[0]
    for at in range(0, TABLE_STEPS * tile if lots else 0, tile):

        @pl.when(step == at // tile)
        def _():
            for (start, stop), copy in zip(lots, copies):
                low, high = max(start, at), min(stop, at + tile)
                if low < high:
                    copy[low - start : high - start] = table_ref[low - at : high - at]

    count = ids_ref.shape[1]
    ids = jnp.transpose(jnp.broadcast_to(ids_ref[...], (8, count)))[:, 0:1] - step * tile
    hot = (lax.broadcasted_iota(jnp.int32, (count, tile), 1) == ids).astype(F32).astype(BF16)
    found = dot(hot, table_ref[...])

    @pl.when(step == 0)
    def _():
        total[...] = found

    @pl.when(step > 0)
    def _():
        total[...] += found

    @pl.when(step == pl.num_programs(0) - 1)
    def _():
        rows = outs[0].shape[0]
        for n, out in enumerate(outs):
            out[...] = total[n * rows : (n + 1) * rows].astype(BF16)


TABLE_STEPS = 5


def lookup(ids, table, pieces, lots=()):
    count = ids.shape[0]
    rows, width = table.shape
    tile = rows // TABLE_STEPS
    return pl.pallas_call(
        functools.partial(lookup_kernel, lots),
        grid=(TABLE_STEPS,),
        in_specs=[
            pl.BlockSpec((1, count), lambda i: (0, 0)),
            pl.BlockSpec((tile, width), lambda i: (i, 0)),
        ],
        out_specs=[pl.BlockSpec((count // pieces, width), lambda i: (0, 0))] * pieces
        + [
            pl.BlockSpec((stop - start, width), lambda i: (0, 0), pipeline_mode=pl.Buffered(1))
            for start, stop in lots
        ],
        out_shape=[jax.ShapeDtypeStruct((count // pieces, width), BF16)] * pieces
        + [jax.ShapeDtypeStruct((stop - start, width), BF16) for start, stop in lots],
        scratch_shapes=[pltpu.VMEM((count, width), F32)],
        compiler_params=params(),
        cost_estimate=cost(8 * count / 512),
        name="lookup",
    )(ids.reshape(1, count), table)


def gathered_sum(refs, sizes):
    rows, at = [], 0
    for size in sizes:
        total = refs[at][...].astype(F32)
        for ref in refs[at + 1 : at + size]:
            total = total + ref[...].astype(F32)
        rows.append(total)
        at += size
    return rows[0] if len(rows) == 1 else jnp.concatenate(rows, axis=0)


def collect_kernel(sizes, *refs):
    ins, outs = refs[: sum(sizes)], refs[sum(sizes) :]
    rows = outs[0].shape[0]
    total = gathered_sum(ins, sizes)
    for n, out in enumerate(outs):
        out[...] = total[n * rows : (n + 1) * rows].astype(BF16)


def collect(terms, pieces):
    sizes = [len(part) for part in terms]
    parts = [term for part in terms for term in part]
    rows, width = sum(part[0].shape[0] for part in terms), parts[0].shape[1]
    return pl.pallas_call(
        functools.partial(collect_kernel, sizes),
        in_specs=[whole()] * len(parts),
        out_specs=[whole()] * pieces,
        out_shape=[jax.ShapeDtypeStruct((rows // pieces, width), BF16)] * pieces,
        compiler_params=params(),
        cost_estimate=cost(2),
        name="collect",
    )(*parts)


def begin_kernel(pieces, order_ref, gain_ref, *refs):
    ins, outs, held = refs[:pieces], refs[pieces:-1], refs[-1]
    for n in range(pieces):
        held[order_ref[n]] = ins[n][...]
    values = jnp.concatenate([held[n] for n in range(pieces)], axis=1)
    units = rms(values.astype(F32), gain_ref[...])
    half = outs[0].shape[0]
    for n in range(2):
        outs[n][...] = values[n * half : (n + 1) * half]
        outs[2 + n][...] = units[n * half : (n + 1) * half]


def begin(order, gain, pieces):
    rows, width = pieces[0].shape
    half = jax.ShapeDtypeStruct((rows // 2, width * len(pieces)), BF16)
    return pl.pallas_call(
        functools.partial(begin_kernel, len(pieces)),
        in_specs=[smem()] + [whole()] * (1 + len(pieces)),
        out_specs=[whole()] * 4,
        out_shape=[half] * 4,
        scratch_shapes=[pltpu.VMEM((len(pieces), rows, width), BF16)],
        compiler_params=params(),
        cost_estimate=cost(2),
        name="begin",
    )(order, gain.reshape(1, -1), *pieces)


def finish_kernel(parts, last, residual_ref, gain_ref, *refs):
    total = gathered_sum(refs[:parts], [parts]) + residual_ref[...].astype(F32)
    if not last:
        total = total.astype(BF16)
        refs[parts + 1][...] = total
    refs[parts][...] = rms(total.astype(F32), gain_ref[...])


def finish(residual, gain, terms, last):
    full = jax.ShapeDtypeStruct(residual.shape, BF16)
    return pl.pallas_call(
        functools.partial(finish_kernel, len(terms), last),
        in_specs=[whole()] * (2 + len(terms)),
        out_specs=[whole()] * (1 if last else 2),
        out_shape=[full] * (1 if last else 2),
        compiler_params=params(),
        cost_estimate=cost(2),
        name="finish",
    )(residual, gain, *terms)


def selectors():
    pairs = [(r, s) for r in range(FEAT) for s in range(r, FEAT)]
    picks = np.zeros((2, 2, LANES, WIDE), np.float32)
    extra = np.zeros((3, WIDE), np.float32)
    extra[0:2, 0] = 1.0
    extra[1, 1 : 1 + FEAT] = 1.0
    extra[2] = 1.0
    for kind in range(2):
        first = kind * FEAT
        for r in range(FEAT):
            picks[kind, 0, first + r, 1 + r] = FEAT ** (-0.25)
        for n, (r, s) in enumerate(pairs):
            picks[kind, 0, first + r, 1 + FEAT + n] = FEAT ** (-0.25)
            picks[kind, 1, first + s, 1 + FEAT + n] = FEAT ** (-0.25)
    for n, (r, s) in enumerate(pairs):
        extra[2, 1 + FEAT + n] = 0.5**0.5 if r == s else 1.0
    return jnp.asarray(np.concatenate([picks, picks], axis=2), BF16), jnp.asarray(extra)


def place_column(places_ref, slots, rows):
    inner = lax.broadcasted_iota(jnp.int32, (rows, 1), 0)
    return jnp.concatenate([inner + places_ref[slot] for slot in slots], axis=0)


def place_row(places_ref, slots, rows):
    inner = lax.broadcasted_iota(jnp.int32, (1, rows), 1)
    return jnp.concatenate([inner + places_ref[slot] for slot in slots], axis=1)


def project_kernel(heads, slots, chunk, count, pieces, more, last, bound_ref, places_ref, *refs):
    units = jnp.concatenate([ref[...] for ref in refs[:pieces]], axis=0)
    weight_ref, pick_ref, extra_ref = refs[pieces : pieces + 3]
    fq_ref, fk_ref, v_ref, state_ref = refs[-4:]
    projected = dot(units, weight_ref[...])
    rows, width = projected.shape
    needed = (heads - 1) * LANES + WIDE
    if needed > width:
        projected = jnp.pad(projected, ((0, 0), (0, needed - width)))
    bound = bound_ref[0]
    place = place_column(places_ref, slots, chunk)
    kept = ((place >= bound) | (bound == count)).astype(F32)
    ones = jnp.ones((8, rows), BF16)
    shift = 2 * FEAT
    for head in range(heads):
        part = projected[:, head * LANES : head * LANES + WIDE]
        narrow = part if head == 0 else pltpu.roll(part, WIDE - shift * head, 1)
        narrow = narrow[:, :LANES]
        values = pltpu.roll(part, WIDE - shift * (head + 1), 1)[:, :HEAD_DIM].astype(BF16)
        v_ref[:, head * HEAD_DIM : (head + 1) * HEAD_DIM] = values
        upper = narrow.astype(BF16)
        lower = (narrow - upper.astype(F32)).astype(BF16)
        both = jnp.concatenate([upper, lower], axis=1)
        feats = []
        for kind in range(2):
            one = dot(both, pick_ref[kind, 0]) + extra_ref[0:1]
            two = dot(both, pick_ref[kind, 1]) + extra_ref[1:2]
            feats.append((one * two * extra_ref[2:3]).astype(BF16))
        fq_ref[head] = feats[0]
        fk_ref[head] = feats[1]
        keys = (feats[1].astype(F32) * kept).astype(BF16)
        state = dot(keys, values, ((0,), (0,)))
        total = dot(ones, keys)
        tail = jnp.concatenate([total[0:1, :LANES], total[0:1, LANES:], jnp.zeros((14, LANES), F32)], axis=0)
        state = jnp.concatenate([state[0:STATE_ROWS], tail], axis=0)
        if more:
            state = state + refs[pieces + 3][head]
        state_ref[head] = state.astype(BF16) if last else state


def project(bound, places, slots, chunk, count, pieces, weight, constants, earlier, last, heads):
    rows = sum(piece.shape[0] for piece in pieces)
    extra = [] if earlier is None else [earlier]
    return pl.pallas_call(
        functools.partial(project_kernel, heads, slots, chunk, count, len(pieces), bool(extra), last),
        in_specs=[smem(), smem()] + [whole()] * (len(pieces) + 3 + len(extra)),
        out_specs=[whole()] * 4,
        out_shape=[
            jax.ShapeDtypeStruct((heads, rows, WIDE), BF16),
            jax.ShapeDtypeStruct((heads, rows, WIDE), BF16),
            jax.ShapeDtypeStruct((rows, heads * HEAD_DIM), BF16),
            jax.ShapeDtypeStruct((heads, BUFFER_ROWS, HEAD_DIM), BF16 if last else F32),
        ],
        compiler_params=params(),
        cost_estimate=cost(5),
        name="project",
    )(bound, places, *pieces, weight, *constants, *extra)


def within_kernel(heads, slots, chunk, sets, bound_ref, places_ref, *refs):
    fqs, fks, vs = refs[:sets], refs[sets : 2 * sets], refs[2 * sets : 3 * sets]
    num_ref, den_ref = refs[3 * sets :]
    bound = bound_ref[0]
    row = place_column(places_ref, slots, chunk)
    col = place_row(places_ref, slots, chunk)
    allowed = (row >= col) & ((row >= bound) == (col >= bound))
    for head in range(heads):
        query = jnp.concatenate([ref[head] for ref in fqs], axis=0)
        keys = jnp.concatenate([ref[head] for ref in fks], axis=0)
        values = jnp.concatenate(
            [ref[:, head * HEAD_DIM : (head + 1) * HEAD_DIM] for ref in vs], axis=0
        )
        weights = dot(query, keys, ((1,), (1,)))
        weights = jnp.where(allowed, weights, 0.0)
        den_ref[head] = jnp.broadcast_to(
            jnp.sum(weights, axis=-1, keepdims=True), (row.shape[0], 8)
        )
        num_ref[head] = dot(weights.astype(BF16), values)


def within(bound, places, slots, chunk, fqs, fks, vs, heads):
    count = len(slots) * chunk
    return pl.pallas_call(
        functools.partial(within_kernel, heads, slots, chunk, len(fqs)),
        in_specs=[smem(), smem()] + [whole()] * (3 * len(fqs)),
        out_specs=[whole()] * 2,
        out_shape=[
            jax.ShapeDtypeStruct((heads, count, HEAD_DIM), F32),
            jax.ShapeDtypeStruct((heads, count, 8), F32),
        ],
        compiler_params=params(),
        cost_estimate=cost(4.5),
        name="within",
    )(bound, places, *fqs, *fks, *vs)


def split_store(total, refs):
    rows = refs[0].shape[0]
    for n, ref in enumerate(refs):
        ref[...] = total[n * rows : (n + 1) * rows].astype(BF16)


def across_kernel(heads, slots, chunk, sets, earlier, near, bound_ref, places_ref, share_ref, *refs):
    fqs, refs = refs[:sets], refs[sets:]
    num_ref, den_ref, gain_ref, weight_ref = refs[:4]
    states, refs = refs[4 : 4 + earlier], refs[4 + earlier :]
    mixed_ref, fars = refs[0], refs[1:]
    bound = bound_ref[0]
    before = (place_column(places_ref, slots, chunk) < bound).astype(F32)
    for head in range(heads):
        carried = jnp.zeros((BUFFER_ROWS, HEAD_DIM), F32)
        for n in range(earlier):
            carried = carried + jnp.where(share_ref[n] > 0, states[n][head].astype(F32), 0.0)
        state = jnp.concatenate(
            [carried[0:STATE_ROWS], jnp.zeros((WIDE - STATE_ROWS, HEAD_DIM), F32)], axis=0
        ).astype(BF16)
        total = jnp.concatenate(
            [carried[STATE_ROWS : STATE_ROWS + 1], carried[STATE_ROWS + 1 : STATE_ROWS + 2]], axis=1
        )
        query = jnp.concatenate([ref[head] for ref in fqs], axis=0)
        numerator = num_ref[head] + before * dot(query, state)
        more = jnp.sum(query.astype(F32) * total, axis=-1, keepdims=True)
        denominator = den_ref[head][:, 0:1] + before * more
        lanes = slice(head * HEAD_DIM, (head + 1) * HEAD_DIM)
        mixed_ref[:, lanes] = (numerator / denominator * gain_ref[:, lanes].astype(F32)).astype(BF16)
    split_store(dot(mixed_ref[near * chunk :], weight_ref[...]), fars)


def across(bound, places, share, slots, chunk, near, far, fqs, num, den, gain, weight, states, heads):
    count = len(slots) * chunk
    rows = (count - near * chunk) // far
    return pl.pallas_call(
        functools.partial(across_kernel, heads, slots, chunk, len(fqs), len(states), near),
        in_specs=[smem()] * 3 + [whole()] * (len(fqs) + 4 + len(states)),
        out_specs=[whole()] * (1 + far),
        out_shape=[jax.ShapeDtypeStruct((count, heads * HEAD_DIM), BF16)]
        + [jax.ShapeDtypeStruct((rows, weight.shape[1]), BF16)] * far,
        compiler_params=params(),
        cost_estimate=cost(4.5),
        name="across",
    )(bound, places, share, *fqs, num, den, gain, weight, *states)


def near_kernel(rows, mixed_ref, weight_ref, *outs):
    split_store(dot(mixed_ref[0:rows], weight_ref[...]), outs)


def near_chunks(mixed, weight, near, chunk):
    pieces = 2 * near if near > 1 else 1
    rows = near * chunk
    return pl.pallas_call(
        functools.partial(near_kernel, rows),
        in_specs=[whole()] * 2,
        out_specs=[whole()] * pieces,
        out_shape=[jax.ShapeDtypeStruct((rows // pieces, weight.shape[1]), BF16)] * pieces,
        compiler_params=params(),
        cost_estimate=cost(4),
        name="near",
    )(mixed, weight)


def matmul_kernel(*refs):
    a = jnp.concatenate([ref[...] for ref in refs[:-2]], axis=0)
    refs[-1][...] = dot(a, refs[-2][...]).astype(BF16)


def matmul(pieces, b, tile):
    rows = sum(piece.shape[0] for piece in pieces)
    inner = b.shape[0]
    return pl.pallas_call(
        matmul_kernel,
        grid=(b.shape[1] // tile,),
        in_specs=[
            pl.BlockSpec(piece.shape, lambda n: (0, 0), pipeline_mode=pl.Buffered(1)) for piece in pieces
        ]
        + [pl.BlockSpec((inner, tile), lambda n: (0, n))],
        out_specs=pl.BlockSpec((rows, tile), lambda n: (0, n)),
        out_shape=jax.ShapeDtypeStruct((rows, b.shape[1]), BF16),
        compiler_params=params(),
        cost_estimate=cost(5),
        name="matmul",
    )(*pieces, b)


def attend(queries, keys, values, allowed):
    rows = queries[0].shape[0]
    scores = jnp.concatenate(
        [dot(q, k, ((1,), (1,))) for q, k in zip(queries, keys)], axis=0
    ) * HEAD_DIM ** (-0.5)
    allowed = jnp.concatenate([allowed.astype(F32)] * len(queries), axis=0) > 0
    scores = jnp.where(allowed, scores, NEGATIVE)
    peak = jnp.max(scores, axis=-1, keepdims=True)
    weights = jnp.where(allowed, jnp.exp(scores - peak), 0.0)
    probabilities = (weights * (1.0 / jnp.sum(weights, axis=-1, keepdims=True))).astype(BF16)
    return jnp.concatenate(
        [
            dot(probabilities[n * rows : (n + 1) * rows], value).astype(BF16)
            for n, value in enumerate(values)
        ],
        axis=1,
    )


def local_kernel(heads, slots, spots, chunk, sets, bound_ref, places_ref, *refs):
    qkvs, (result_ref, first_ref) = refs[:sets], refs[sets:]
    size = len(slots)
    reach = chunk + WINDOW
    bound = bound_ref[0]
    row = lax.broadcasted_iota(jnp.int32, (chunk, reach), 0)
    col = lax.broadcasted_iota(jnp.int32, (chunk, reach), 1)
    band = (col > row) & (col <= row + WINDOW)
    for slot in range(size):
        k = slots[slot]
        mine, at = spots[k]
        theirs, there = spots[(k - 1) % size]
        base = places_ref[slot]
        query_place = row + base
        key_place = col + (base - WINDOW)
        allowed = band & (key_place >= 0) & ((query_place >= bound) == (key_place >= bound))
        rows = slice(at, at + chunk)
        tail = slice(there + chunk - WINDOW, there + chunk)

        @pl.when(base == 0)
        def _():
            first_ref[...] = qkvs[mine][at : at + WINDOW]

        queries, keys, values = [], [], []
        for head in range(heads):
            lane = head * 3 * HEAD_DIM
            queries.append(qkvs[mine][rows, lane : lane + HEAD_DIM])
            for n, held in ((1, keys), (2, values)):
                lanes = slice(lane + n * HEAD_DIM, lane + (n + 1) * HEAD_DIM)
                held.append(jnp.concatenate([qkvs[theirs][tail, lanes], qkvs[mine][rows, lanes]], axis=0))
        result_ref[slot * chunk : (slot + 1) * chunk] = attend(queries, keys, values, allowed)


def local_window(bound, places, slots, spots, chunk, qkvs, heads):
    return pl.pallas_call(
        functools.partial(local_kernel, heads, slots, spots, chunk, len(qkvs)),
        in_specs=[smem(), smem()] + [whole()] * len(qkvs),
        out_specs=[whole()] * 2,
        out_shape=[
            jax.ShapeDtypeStruct((len(slots) * chunk, heads * HEAD_DIM), BF16),
            jax.ShapeDtypeStruct((WINDOW, qkvs[0].shape[1]), BF16),
        ],
        compiler_params=params(),
        cost_estimate=cost(8),
        name="local_window",
    )(bound, places, *qkvs)


def halo_kernel(heads, count, start, info_ref, local_ref, first_ref, halo_ref, weight_ref, result_ref, *fars):
    result_ref[...] = local_ref[...]
    bound, valid_from, spot = info_ref[0], info_ref[1], info_ref[2]
    row = lax.broadcasted_iota(jnp.int32, (WINDOW, 2 * WINDOW), 0)
    col = lax.broadcasted_iota(jnp.int32, (WINDOW, 2 * WINDOW), 1)
    key_place = col - WINDOW
    allowed = (col > row) & (col <= row + WINDOW) & ((row >= bound) == (key_place >= bound))
    allowed = allowed & ((key_place >= 0) | (key_place + count >= valid_from))
    spot = pl.multiple_of(spot, WINDOW)
    queries, keys, values = [], [], []
    for head in range(heads):
        lane = head * 3 * HEAD_DIM
        queries.append(first_ref[:, lane : lane + HEAD_DIM])
        for n, held in ((1, keys), (2, values)):
            lanes = slice(lane + n * HEAD_DIM, lane + (n + 1) * HEAD_DIM)
            held.append(jnp.concatenate([halo_ref[:, lanes], first_ref[:, lanes]], axis=0))
    result_ref[pl.ds(spot, WINDOW), :] = attend(queries, keys, values, allowed)
    split_store(dot(result_ref[start:], weight_ref[...]), fars)


def halo_window(info, near, chunk, far, local, first, halo, weight, heads):
    count = local.shape[0]
    rows = (count - near * chunk) // far
    return pl.pallas_call(
        functools.partial(halo_kernel, heads, count, near * chunk),
        in_specs=[smem()] + [whole()] * 4,
        out_specs=[whole()] * (1 + far),
        out_shape=[jax.ShapeDtypeStruct(local.shape, BF16)]
        + [jax.ShapeDtypeStruct((rows, weight.shape[1]), BF16)] * far,
        compiler_params=params(),
        cost_estimate=cost(4.5),
        name="halo_window",
    )(info, local, first, halo, weight)


def turn_kernel(*refs):
    refs[-1][...] = jnp.transpose(jnp.concatenate([ref[...] for ref in refs[:-1]], axis=0))


def turn(pieces):
    rows, width = sum(piece.shape[0] for piece in pieces), pieces[0].shape[1]
    return pl.pallas_call(
        turn_kernel,
        in_specs=[whole()] * len(pieces),
        out_specs=whole(),
        out_shape=jax.ShapeDtypeStruct((width, rows), BF16),
        compiler_params=params(),
        cost_estimate=cost(3),
        name="turn",
    )(*pieces)


def score_kernel(ready, rest, common, pieces, lots, tile, order_ref, *refs):
    early, refs = refs[:ready], refs[ready:]
    units, refs = refs[:rest], refs[rest:]
    shared, refs = refs[:common], refs[common:]
    tables, (goal_ref, out_ref, turned_ref, held) = refs[: len(lots) * pieces], refs[len(lots) * pieces :]
    step = pl.program_id(0)
    width = (shared or tables)[0].shape[1]
    count = goal_ref.shape[1]
    part = 128

    @pl.when(step == 0)
    def _():
        at = 0
        for ref in early:
            at = ref.shape[1]
            turned_ref[:, 0:at] = ref[...]
        turned_ref[:, at:] = jnp.transpose(jnp.concatenate([ref[...] for ref in units], axis=0))
        held[0] = jnp.full((8, count), NEGATIVE, F32)
        held[1] = jnp.zeros((8, count), F32)
        held[2] = jnp.zeros((8, count), F32)

    def run(mine):
        inner = lax.broadcasted_iota(jnp.int32, (part // 8, 8, count), 0) * 8
        inner = inner + lax.broadcasted_iota(jnp.int32, (part // 8, 8, count), 1)
        peak, total, picked = held[0], held[1], held[2]
        sides = [
            turned_ref[pl.ds(pl.multiple_of(order_ref[n] * width, width), width), :] for n in range(len(mine))
        ]
        for at in range(0, tile, part):
            logits = None
            for table, side in zip(mine, sides):
                more = dot(table[at : at + part], side)
                logits = more if logits is None else logits + more
            logits = logits.reshape(part // 8, 8, count)
            goal = (goal_ref[...] - (step * tile + at)).reshape(1, 1, count)
            old = peak
            peak = jnp.maximum(old, jnp.max(logits, axis=0))
            total = total * jnp.exp(old - peak) + jnp.sum(jnp.exp(logits - peak[None]), axis=0)
            picked = picked + jnp.sum(jnp.where(inner == goal, logits, 0.0), axis=0)
        held[0], held[1], held[2] = peak, total, picked

    for lot, (start, stop) in enumerate(lots):
        pl.when((step >= start) & (step < stop))(
            lambda lot=lot: run(list(shared) + list(tables[lot * pieces : (lot + 1) * pieces]))
        )

    @pl.when(step == pl.num_programs(0) - 1)
    def _():
        peak = jnp.max(held[0], axis=0, keepdims=True)
        total = jnp.sum(held[1] * jnp.exp(held[0] - peak), axis=0, keepdims=True)
        picked = jnp.sum(held[2], axis=0, keepdims=True)
        out_ref[...] = jnp.concatenate([peak, total, picked, jnp.zeros((5, count), F32)], axis=0)


def scores(order, early, units, shared, lots, goal):
    count = goal.shape[1]
    rows = lots[-1][1]
    tile = 640
    specs = [pl.BlockSpec((tile, table.shape[1]), lambda i: (i, 0)) for table in shared]
    steps = []
    for first, last, tables in lots:
        start, stop = first // tile, last // tile
        steps.append((start, stop))
        for table in tables:
            specs.append(
                pl.BlockSpec(
                    (tile, table.shape[1]),
                    lambda i, start=start, stop=stop: (jnp.clip(i, start, stop - 1) - start, 0),
                )
            )
    still = [
        pl.BlockSpec(piece.shape, lambda i: (0, 0), pipeline_mode=pl.Buffered(1)) for piece in early + units
    ]
    return pl.pallas_call(
        functools.partial(
            score_kernel, len(early), len(units), len(shared), len(lots[0][2]), steps, tile
        ),
        in_specs=[smem()] + still + specs + [pl.BlockSpec((1, count), lambda i: (0, 0))],
        out_specs=pl.BlockSpec((8, count), lambda i: (0, 0)),
        grid=(rows // tile,),
        out_shape=jax.ShapeDtypeStruct((8, count), F32),
        scratch_shapes=[pltpu.VMEM((units[0].shape[1], count), BF16), pltpu.VMEM((3, 8, count), F32)],
        compiler_params=params(),
        cost_estimate=cost(20),
        name="scores",
    )(order, *early, *units, *shared, *[table for lot in lots for table in lot[2]], goal)


def shards(
    token_ids,
    target_ids,
    doc_start,
    vocab_table,
    norm_gain_one,
    lin_qkv,
    lin_head_gain,
    lin_out,
    norm_gain_two,
    win_qkv,
    win_out,
    final_gain,
):
    head_count = lax.axis_size("head")
    seq_count = lax.axis_size("seq")
    head_index = lax.axis_index("head")
    seq_index = lax.axis_index("seq")
    tok_count = token_ids.shape[0]
    chunk = tok_count // head_count
    vocab_rows = vocab_table.shape[0]
    heads = lin_qkv.shape[1] // (2 * FEAT + HEAD_DIM)
    vocab_first = head_index * vocab_rows
    calls = chunk_order(head_count)
    slots = [k for call in calls for k in call]
    near = 3 if head_count == 4 else 1
    far = 2 if head_count == 4 else head_count - 1
    spots = {}
    for n, call in enumerate(calls):
        for at, k in enumerate(call):
            spots[k] = (n, at * chunk)
    held_at = (head_index + jnp.asarray(slots, jnp.int32)) % head_count
    places = held_at * chunk

    marks = jnp.concatenate([token_ids, jnp.broadcast_to(doc_start, (LANES,))])
    marks = jnp.stack(
        [marks] + [lax.ppermute(marks, "seq", xor_pairs(seq_count, k)) for k in range(1, seq_count)]
    )
    block = jnp.arange(seq_count, dtype=jnp.int32)
    order = seq_index ^ block
    starts = marks[:, tok_count]
    starts = jnp.sum(jnp.where(order[None, :] == block[:, None], starts[None, :], 0), axis=1)
    bound = doc_start.astype(jnp.int32)

    marks_at = [part * (vocab_rows // 10) for part in (0, 3, 8, 10)]
    bounds = list(zip(marks_at[:-1], marks_at[1:])) if seq_count == 4 else []
    lots = []

    ids = (marks[:, :tok_count] - vocab_first).reshape(seq_count, head_count, chunk)

    def ids_of(k):
        return lax.dynamic_index_in_dim(ids, (head_index + k) % head_count, 1, False).reshape(-1)

    if head_count == 4:
        outer = lookup(ids_of(2), vocab_table, 2)

        def inner():
            after, before, _ = lax.optimization_barrier((ids_of(1), ids_of(3), outer))
            half = after.shape[0] // 2
            next_lower, prev_upper = lookup(jnp.concatenate([after[half:], before[:half]]), vocab_table, 2)
            next_upper, prev_lower = lookup(jnp.concatenate([after[:half], before[half:]]), vocab_table, 2)
            own = lookup(ids_of(0), vocab_table, 2, bounds)
            lots.extend(own[2:])
            return [own[0], own[1], next_upper, next_lower, prev_upper, prev_lower]

    else:
        outer = [lookup(ids_of(k), vocab_table, 1)[0] for k in range(1, head_count)]

        def inner():
            own = lookup(ids_of(0), vocab_table, 1, bounds)
            lots.extend(own[1:])
            return own[:1]

    found = collect(scatter_rows(outer, inner), seq_count)
    gathered = [found[0]] + [
        lax.ppermute(found[k], "seq", xor_pairs(seq_count, k)) for k in range(1, seq_count)
    ]
    if lots:
        lots[0], gathered = lax.optimization_barrier((lots[0], gathered))
    *embedded, upper, lower = begin(order, norm_gain_one, gathered)
    across_x, corners = [None] * 3, [None] * 3

    constants = selectors()
    sets, state = [], None

    def project_call(n, pieces, state):
        first = sum(len(c) for c in calls[:n])
        return project(
            bound,
            places[first : first + len(calls[n])],
            list(range(len(calls[n]))),
            chunk,
            tok_count,
            pieces,
            lin_qkv,
            constants,
            state,
            n == len(calls) - 1,
            heads,
        )

    chunks = gather_rows(upper, lower)

    shares = []
    for back in range(1, seq_count):
        between = (block > seq_index - back) & (block < seq_index)
        broken = jnp.sum(jnp.where(between & (starts != tok_count), 1, 0))
        shares.append(((broken == 0) & (seq_index >= back)).astype(jnp.int32))
    shares = jnp.stack(shares)
    previous = jnp.sum(jnp.where(block == seq_index - 1, starts, 0))
    valid_from = jnp.where(
        seq_index == 0, tok_count, jnp.where(previous == tok_count, 0, previous)
    ).astype(jnp.int32)
    first_spot = jnp.sum(jnp.where(held_at == 0, jnp.arange(head_count) * chunk, 0)).astype(jnp.int32)
    info = jnp.stack([bound[0], valid_from, first_spot])
    goals = (target_ids - vocab_first).reshape(head_count, chunk)
    goal = jnp.concatenate(
        [lax.dynamic_index_in_dim(goals, (head_index + k) % head_count, 0, False) for k in slots]
    ).reshape(1, -1)
    gain_two, gain_three = norm_gain_two.reshape(1, -1), final_gain.reshape(1, -1)
    head_gain = lin_head_gain.reshape(1, -1)
    chunks[slots[-1]], shares, info, goal, gain_two, gain_three, head_gain = lax.optimization_barrier(
        (chunks[slots[-1]], shares, info, goal, gain_two, gain_three, head_gain)
    )
    if seq_count == 4:
        across_x[0] = lax.ppermute(lots[0], "seq", xor_pairs(seq_count, 2))
        corners[0] = lax.ppermute(across_x[0], "seq", xor_pairs(seq_count, 1))
    for n, call in enumerate(calls):
        made = project_call(n, [piece for k in call for piece in chunks[k]], state)
        sets.append(made[:3])
        state = made[3]
    fqs, fks, vs = zip(*sets)
    if seq_count == 4:
        state, across_x[0] = lax.optimization_barrier((state, across_x[0]))
    states = [
        lax.ppermute(state, "seq", [(i, i + back) for i in range(seq_count - back)])
        for back in range(1, seq_count)
    ]
    position = list(range(head_count))
    num, den = within(bound, places, position, chunk, fqs, fks, vs, heads)
    mixed, *outer = across(
        bound,
        places,
        shares,
        position,
        chunk,
        near,
        far,
        fqs,
        num,
        den,
        head_gain,
        lin_out,
        states,
        heads,
    )
    far_rows = outer
    parts = scatter_rows(outer, lambda: near_chunks(mixed, lin_out, near, chunk))
    parts = in_halves(parts)
    upper, residual_upper = finish(embedded[0], gain_two, parts[0], False)
    lower, residual_lower = finish(embedded[1], gain_two, parts[1], False)

    if seq_count == 4:
        lots[1], _ = lax.optimization_barrier((lots[1], (states, far_rows)))
        across_x[1] = lax.ppermute(lots[1], "seq", xor_pairs(seq_count, 2))
        beside = lax.ppermute(vocab_table, "seq", xor_pairs(seq_count, 1))

    chunks = gather_rows(upper, lower)
    qkvs = []
    for call in calls:
        qkvs.append(matmul([piece for k in call for piece in chunks[k]], win_qkv, 3 * HEAD_DIM))
    tail = jnp.zeros((WINDOW, win_qkv.shape[1]), BF16)
    for slot, k in enumerate(slots):
        n, at = spots[k]
        tail = jnp.where(
            held_at[slot] == head_count - 1, qkvs[n][at + chunk - WINDOW : at + chunk], tail
        )
    if seq_count == 4:
        tail, across_x[1], corners[0], beside = lax.optimization_barrier(
            (tail, across_x[1], corners[0], beside)
        )
    halo = lax.ppermute(tail, "seq", [(i, i + 1) for i in range(seq_count - 1)])
    local, first = local_window(bound, places, slots, spots, chunk, qkvs, heads)
    if lots:
        lots[2], local, halo, across_x[1] = lax.optimization_barrier((lots[2], local, halo, across_x[1]))
    mixed, *outer = halo_window(info, near, chunk, far, local, first, halo, win_out, heads)
    if seq_count == 4:
        across_x[1], lots[2], _ = lax.optimization_barrier((across_x[1], lots[2], outer))
        corners[1] = lax.ppermute(across_x[1], "seq", xor_pairs(seq_count, 1))
    parts = scatter_rows(outer, lambda: near_chunks(mixed, win_out, near, chunk))
    parts = in_halves(parts)
    upper = finish(residual_upper, gain_three, parts[0], True)[0]
    lower = finish(residual_lower, gain_three, parts[1], True)[0]

    chunks = gather_rows(upper, lower)
    if seq_count == 4:
        across_x[2] = lax.ppermute(lots[2], "seq", xor_pairs(seq_count, 2))
        corners[2] = lax.ppermute(lots[2], "seq", xor_pairs(seq_count, 3))
        shared = [vocab_table, beside]
        lots = [(marks_at[n], marks_at[n + 1], [across_x[n], corners[n]]) for n in range(3)]
    else:
        shared = [lax.all_gather(vocab_table, "seq", axis=1, tiled=True)]
        lots = [(0, vocab_rows, [])]
        order = jnp.zeros((1,), jnp.int32)
    first = slots[:-1] if chunk % LANES == 0 else []
    rest = [piece for k in slots[len(first) :] for piece in chunks[k]]
    first = [turn([piece for k in first for piece in chunks[k]])] if first else []
    triple = scores(order, first, rest, shared, lots, goal)
    found = {k: triple[:3, at * chunk : (at + 1) * chunk] for at, k in enumerate(slots)}

    shares = jnp.stack([found[0]] + [turned(found[k], k) for k in range(1, head_count)])
    peak = jnp.max(shares[:, 0], axis=0)
    total = jnp.sum(shares[:, 1] * jnp.exp(shares[:, 0] - peak), axis=0)
    return jnp.sum(shares[:, 2], axis=0) - (peak + jnp.log(total))


def solution(mesh):
    return jax.shard_map(
        shards,
        mesh=mesh,
        in_specs=(
            P(("shadow", "seq")),
            P(("shadow", "seq")),
            P(("shadow", "seq")),
            P(("shadow", "head"), "seq"),
            P("shadow"),
            P("shadow", "head"),
            P(("shadow", "head")),
            P(("shadow", "head"), None),
            P("shadow"),
            P("shadow", "head"),
            P(("shadow", "head"), None),
            P("shadow"),
        ),
        out_specs=P(("shadow", "seq", "head")),
        check_vma=False,
    )
```
